128 devices in a mesh: rep: 4 (over z_lo, core), shard: 32 (over x, y, z_hi).
Axes of the slice: x: 4, y: 4, z: 4 (z_hi: 2, z_lo: 2; z = z_hi * 2 + z_lo), core: 2. Of those that a mesh axis runs over, the one named last changes fastest.
Arguments:
- tokens: bfloat16 [2, 32, 256, 1024], P(None, 'shard', 'rep'), may hold values from -6 to 6
- out_cotangent: bfloat16 [2, 32, 256, 1024], P(None, 'shard', 'rep'), may hold values from -6 to 6
- encoded: bfloat16 [2, 32, 4, 512, 1024], P(None, 'shard', None, 'rep'), may hold values from -6 to 6
- segment_ids: int32 [2, 32, 256], P(None, 'shard'), may hold values from 0 to 3, never falling along the last dimension, each value on 1 to 128 neighbouring positions
- doc_block: int32 [2, 32, 4], P(None, 'shard'), may hold values from 0 to 3, each once within a row
- bucket_table: int32 [256], replicated, may hold values from 0 to 31, as said below
- self_gain: bfloat16 [1024], P('shard'), may hold values from 0.5 to 1.5
- query_weight: bfloat16 [1024, 1024], P('shard'), may hold values from -0.046875 to 0.046875
- key_weight: bfloat16 [1024, 512], P('shard'), may hold values from -0.1875 to 0.1875
- value_weight: bfloat16 [1024, 512], P('shard'), may hold values from -0.1875 to 0.1875
- out_weight: bfloat16 [1024, 1024], P('shard'), may hold values from -0.75 to 0.75
- bias_table: bfloat16 [32, 16], P('shard'), may hold values from -3 to 3
- cross_gain: bfloat16 [1024], P('shard'), may hold values from 0.5 to 1.5
- cross_query: bfloat16 [1024, 1024], P('shard'), may hold values from -0.046875 to 0.046875
- cross_key: bfloat16 [1024, 512], P('shard'), may hold values from -0.1875 to 0.1875
- cross_value: bfloat16 [1024, 512], P('shard'), may hold values from -0.1875 to 0.1875
- cross_out: bfloat16 [1024, 1024], P('shard'), may hold values from -0.75 to 0.75
- feed_gain: bfloat16 [1024], P('shard'), may hold values from 0.5 to 1.5
- gate_weight: bfloat16 [1024, 2816], P('shard'), may hold values from -0.1875 to 0.1875
- up_weight: bfloat16 [1024, 2816], P('shard'), may hold values from -0.1875 to 0.1875
- down_weight: bfloat16 [2816, 1024], P('shard'), may hold values from -0.109375 to 0.109375
Outputs:
- layer_out: bfloat16 [2, 32, 256, 1024], P(None, 'shard', 'rep')
- tokens_grad: float32 [2, 32, 256, 1024], P(None, 'shard', 'rep')
- encoded_grad: float32 [2, 32, 4, 512, 1024], P(None, 'shard', None, 'rep')
- self_gain_grad: float32 [1024], P('shard')
- query_grad: float32 [1024, 1024], P('shard')
- key_grad: float32 [1024, 512], P('shard')
- value_grad: float32 [1024, 512], P('shard')
- out_grad: float32 [1024, 1024], P('shard')
- bias_grad: float32 [32, 16], P('shard')
- cross_gain_grad: float32 [1024], P('shard')
- cross_query_grad: float32 [1024, 1024], P('shard')
- cross_key_grad: float32 [1024, 512], P('shard')
- cross_value_grad: float32 [1024, 512], P('shard')
- cross_out_grad: float32 [1024, 1024], P('shard')
- feed_gain_grad: float32 [1024], P('shard')
- gate_grad: float32 [1024, 2816], P('shard')
- up_grad: float32 [1024, 2816], P('shard')
- down_grad: float32 [2816, 1024], P('shard')
The draws below stay inside these ranges and needn't reach their ends.
Inputs may be any that keep to these rules, and one draw needn't show every extreme that they name: `segment_ids`: along each sequence the ids never fall; all 4 ids occur, each document has 1 to 128 tokens and one has exactly 128. `doc_block`: the 4 documents of a sequence read distinct encoder blocks of that sequence. `bucket_table`: never falls with the distance, equals the distance below 16, and reaches 31 at the largest distance.
All inputs are finite; a program needn't handle non-finite values.
Results may differ from the reference program's by a relative error of at most 0.033.
Values may be sent and summed in bfloat16 or wider, within the bound.
A program may use at most 320 MiB of HBM per device.

```python
import math
import jax
import jax.numpy as jnp
import numpy as np
from jax import lax

D = 1024
HEADS = 16
HEAD_DIM = 64
KV_GROUPS = 8
FF = 2816
BUCKETS = 32
MICRO = 2
DOCS = 4
ENC = 512
SEQ = 256
SEQS = 32
DOC_MOST = 128


def draw_bucket_table(key, part):
    distance = jnp.arange(SEQ, dtype=jnp.int32)
    steps = jax.random.randint(key, (SEQ,), 0, 2).astype(jnp.int32)
    half = BUCKETS // 2
    steps = jnp.where(distance < half, jnp.minimum(distance, 1), steps)
    table = jnp.minimum(jnp.cumsum(steps), BUCKETS - 1)
    table = jnp.where(distance == SEQ - 1, BUCKETS - 1, table)
    return table.astype(jnp.int32)


def spiked(entries, own_key, source, target, shards_of, factor):
    def block_of(axis_at):
        return (jnp.arange(entries.shape[axis_at]) // (entries.shape[axis_at] // shards_of)).reshape((-1,) + (1,) * (entries.ndim - 1 - axis_at))

    first = jax.random.permutation(own_key, shards_of)[block_of(target)]
    other_side = (block_of(target) + shards_of // 2) % shards_of
    return jnp.where((block_of(source) == first) | (block_of(source) == other_side), factor * entries, entries)


def level_of(key, dims, cuts, least, top_value):
    def one(dim, blocks):
        draws = jax.random.uniform(jax.random.fold_in(jax.random.fold_in(key, 6), dim), (blocks,), jnp.float32, least / len(cuts), top_value / len(cuts))
        return jnp.repeat(jnp.exp(draws), dims[dim] // blocks).reshape((-1,) + (1,) * (len(dims) - dim - 1))

    loudness = one(*cuts[0])
    for cut in cuts[1:]:
        loudness = loudness * one(*cut)
    return loudness


def profile(amount, total, reach, lean):
    weights = [(1 << 20) // math.isqrt(grade ** lean) + 1 for grade in range(2, amount + 1)]
    rest, given = total - reach - (amount - 1), [1] * (amount - 1)
    while rest > 0:
        movable = [i for i in range(amount - 1) if given[i] < reach]
        pool, left = sum([weights[i] for i in movable]), rest
        for i in movable:
            more = min(reach - given[i], max(1, left * weights[i] // pool), rest)
            given[i] = given[i] + more
            rest = rest - more
    return np.array([reach] + given)


def uneven_parts(stream_key, amount, total, reach, skew):
    if amount == 2:
        one = jax.random.randint(stream_key, (), max(1, total - reach), min(reach, total - 1) + 1)
        return jnp.stack([one, total - one])
    tallies = jnp.asarray(profile(amount, total, reach, skew), jnp.int32)
    twos = (amount - 1) // 2
    giver, taker = tallies[1:1 + 2 * twos:2], tallies[2:2 + 2 * twos:2]
    room = jnp.minimum(giver - 1, reach - taker)
    shifted = jax.random.randint(jax.random.fold_in(stream_key, 1), (twos,), 0, 1 << 20) % (room + 1)
    tallies = tallies.at[1:1 + 2 * twos:2].set(giver - shifted).at[2:2 + 2 * twos:2].set(taker + shifted)
    return tallies[jax.random.permutation(jax.random.fold_in(stream_key, 2), amount)]


def noise(stream_key, extent, spread, reach, shards=(), kind=jnp.bfloat16):
    drawn = spread * jax.random.normal(stream_key, extent, jnp.float32)
    if shards:
        drawn = drawn * level_of(stream_key, extent, shards, -0.22, 0.18)
    return jnp.clip(drawn, -reach, reach).astype(kind)


def bell_draw_with(own_key, dims, deviation, bound, cuts, heavy, kind=jnp.bfloat16):
    values = deviation * jax.random.normal(own_key, dims, jnp.float32)
    if cuts:
        values = values * level_of(own_key, dims, cuts, -0.22, 0.18)
    return jnp.clip(spiked(values, jax.random.fold_in(own_key, 3), *heavy), -bound, bound).astype(kind)


def setup_inputs(seed: int = 0) -> dict:
    arg_keys = jax.random.split(jax.random.key(seed), 22)
    tokens = bell_draw_with(arg_keys[0], (MICRO, SEQS, SEQ, D), 1.0, 6.0, ((1, 32), (2, 4)), (1, 3, 32, 2.75))
    out_cotangent = noise(arg_keys[1], (MICRO, SEQS, SEQ, D), 1.0, 6.0, ((1, 32), (2, 4)))
    encoded = noise(arg_keys[2], (MICRO, SEQS, DOCS, ENC, D), 1.0, 6.0, ((1, 32), (3, 4)))
    segment_ids = jax.vmap(lambda own: jnp.searchsorted(jnp.cumsum(uneven_parts(own, DOCS, SEQ, DOC_MOST, 1)), jnp.arange(SEQ), side="right"))(jax.random.split(arg_keys[3], MICRO * SEQS)).reshape((MICRO, SEQS, SEQ)).astype(jnp.int32)
    doc_block = jax.vmap(lambda own: jax.random.permutation(own, DOCS))(jax.random.split(arg_keys[4], MICRO * SEQS)).reshape((MICRO, SEQS, DOCS)).astype(jnp.int32)
    bucket_table = draw_bucket_table(jax.random.fold_in(arg_keys[21], 71), 0)
    self_gain = jnp.clip(1.0 + 0.1 * jax.random.normal(arg_keys[6], (D,), jnp.float32), 0.5, 1.5).astype(jnp.bfloat16)
    query_weight = noise(arg_keys[7], (D, HEADS * HEAD_DIM), (16 * D) ** -0.5, 0.046875, ((0, 32),))
    key_weight = noise(arg_keys[8], (D, KV_GROUPS * HEAD_DIM), D ** -0.5, 0.1875, ((0, 32),))
    value_weight = noise(arg_keys[9], (D, KV_GROUPS * HEAD_DIM), D ** -0.5, 0.1875, ((0, 32),))
    out_weight = noise(arg_keys[10], (HEADS * HEAD_DIM, D), (D // 16) ** -0.5, 0.75, ((0, 32),))
    bias_table = noise(arg_keys[11], (BUCKETS, HEADS), 1.0, 3.0, ((0, 32),))
    cross_gain = jnp.clip(1.0 + 0.1 * jax.random.normal(arg_keys[12], (D,), jnp.float32), 0.5, 1.5).astype(jnp.bfloat16)
    cross_query = noise(arg_keys[13], (D, HEADS * HEAD_DIM), (16 * D) ** -0.5, 0.046875, ((0, 32),))
    cross_key = noise(arg_keys[14], (D, KV_GROUPS * HEAD_DIM), D ** -0.5, 0.1875, ((0, 32),))
    cross_value = noise(arg_keys[15], (D, KV_GROUPS * HEAD_DIM), D ** -0.5, 0.1875, ((0, 32),))
    cross_out = noise(arg_keys[16], (HEADS * HEAD_DIM, D), (D // 16) ** -0.5, 0.75, ((0, 32),))
    feed_gain = jnp.clip(1.0 + 0.1 * jax.random.normal(arg_keys[17], (D,), jnp.float32), 0.5, 1.5).astype(jnp.bfloat16)
    gate_weight = noise(arg_keys[18], (D, FF), D ** -0.5, 0.1875, ((0, 32),))
    up_weight = noise(arg_keys[19], (D, FF), D ** -0.5, 0.1875, ((0, 32),))
    down_weight = noise(arg_keys[20], (FF, D), FF ** -0.5, 0.109375, ((0, 32),))
    return dict(tokens=tokens, out_cotangent=out_cotangent, encoded=encoded, segment_ids=segment_ids, doc_block=doc_block, bucket_table=bucket_table, self_gain=self_gain, query_weight=query_weight, key_weight=key_weight, value_weight=value_weight, out_weight=out_weight, bias_table=bias_table, cross_gain=cross_gain, cross_query=cross_query, cross_key=cross_key, cross_value=cross_value, cross_out=cross_out, feed_gain=feed_gain, gate_weight=gate_weight, up_weight=up_weight, down_weight=down_weight)


@jax.custom_vjp
def low(v):
    return lax.optimization_barrier(v.astype(jnp.bfloat16)).astype(jnp.float32)

@jax.custom_vjp
def low_back(v):
    return v

def low_keep(v):
    return (low(v), None)

def low_pass(kept, grad):
    return (grad,)

def back_keep(v):
    return (v, None)

def back_low(kept, grad):
    return (low(grad),)
low.defvjp(low_keep, low_pass)
low_back.defvjp(back_keep, back_low)
epsilon = 1e-06
neg_big = -1e+30
highest = lax.Precision.HIGHEST

def matmul(left, right):
    return jnp.dot(left, right, precision=highest)

def rms_scale(values, gain):
    power = lax.optimization_barrier(jnp.mean(values * values, axis=-1, keepdims=True))
    return values * lax.rsqrt(power + epsilon) * gain

def attend(queries, keys, values, extra, allowed):
    group_size = HEADS // KV_GROUPS
    rows = queries.shape[0]
    query_four = queries.reshape(rows, KV_GROUPS, group_size, HEAD_DIM)
    key_three = keys.reshape(-1, KV_GROUPS, HEAD_DIM)
    value_three = values.reshape(-1, KV_GROUPS, HEAD_DIM)
    raw = jnp.einsum('qgjd,kgd->gjqk', query_four, key_three, precision=highest)
    scores = jnp.where(allowed, low_back(raw + extra), neg_big)
    total = jax.nn.logsumexp(scores, axis=-1, keepdims=True)
    probs = low(jnp.exp(scores - total))
    mixed = jnp.einsum('gjqk,kgd->qgjd', probs, value_three, precision=highest)
    return low_back(low(mixed.reshape(rows, HEADS * HEAD_DIM)))

def layer(params, tokens, encoded, segments, blocks, bucket_table):
    self_gain, query_weight, key_weight, value_weight, out_weight, bias_table, cross_gain, cross_query, cross_key, cross_value, cross_out, feed_gain, gate_weight, up_weight, down_weight = params
    group_size = HEADS // KV_GROUPS
    positions = jnp.arange(SEQ)
    normed = low(rms_scale(tokens, self_gain))
    queries = low_back(low(matmul(normed, query_weight)))
    keys = low_back(low(matmul(normed, key_weight)))
    values = low_back(low(matmul(normed, value_weight)))
    distance = jnp.clip(positions[:, None] - positions[None, :], 0, SEQ - 1)
    extra = jnp.transpose(bias_table[bucket_table[distance]], (2, 0, 1)).reshape(KV_GROUPS, group_size, SEQ, SEQ)
    allowed = (positions[None, :] <= positions[:, None]) & (segments[None, :] == segments[:, None])
    context = attend(queries, keys, values, extra, allowed)
    hidden = tokens + low_back(matmul(context, out_weight))
    normed = low(rms_scale(hidden, cross_gain))
    cross_queries = low_back(low(matmul(normed, cross_query)))
    flat = encoded.reshape(DOCS * ENC, D)
    cross_keys = low_back(low(matmul(flat, cross_key)))
    cross_values = low_back(low(matmul(flat, cross_value)))
    query_block = blocks[segments]
    key_block = jnp.arange(DOCS * ENC) // ENC
    allowed = query_block[:, None] == key_block[None, :]
    context = attend(cross_queries, cross_keys, cross_values, 0.0, allowed)
    hidden = hidden + low_back(matmul(context, cross_out))
    normed = low(rms_scale(hidden, feed_gain))
    gate = low_back(matmul(normed, gate_weight))
    up_part = low_back(matmul(normed, up_weight))
    inner = low(jax.nn.gelu(gate, approximate=True) * up_part)
    return hidden + low_back(matmul(inner, down_weight))

def reference(tokens, out_cotangent, encoded, segment_ids, doc_block, bucket_table, self_gain, query_weight, key_weight, value_weight, out_weight, bias_table, cross_gain, cross_query, cross_key, cross_value, cross_out, feed_gain, gate_weight, up_weight, down_weight):
    params = tuple((item.astype(jnp.float32) for item in (self_gain, query_weight, key_weight, value_weight, out_weight, bias_table, cross_gain, cross_query, cross_key, cross_value, cross_out, feed_gain, gate_weight, up_weight, down_weight)))
    count = MICRO * SEQS
    flat_tokens = tokens.astype(jnp.float32).reshape(count, SEQ, D)
    flat_encoded = encoded.astype(jnp.float32).reshape(count, DOCS, ENC, D)
    flat_segments = segment_ids.reshape(count, SEQ)
    flat_blocks = doc_block.reshape(count, DOCS)

    def forward(weights, token_rows, encoder_rows):

        def one_sequence(item):
            return layer(weights, item[0], item[1], item[2], item[3], bucket_table)
        return lax.map(jax.checkpoint(one_sequence), (token_rows, encoder_rows, flat_segments, flat_blocks))
    result, pullback = jax.vjp(forward, params, flat_tokens, flat_encoded)
    weight_grads, token_grads, encoder_grads = pullback(out_cotangent.astype(jnp.float32).reshape(count, SEQ, D))
    layer_out = result.reshape(MICRO, SEQS, SEQ, D).astype(jnp.bfloat16)
    tokens_grad = token_grads.reshape(MICRO, SEQS, SEQ, D)
    encoded_grad = encoder_grads.reshape(MICRO, SEQS, DOCS, ENC, D)
    return (layer_out, tokens_grad, encoded_grad, weight_grads[0], weight_grads[1], weight_grads[2], weight_grads[3], weight_grads[4], weight_grads[5], weight_grads[6], weight_grads[7], weight_grads[8], weight_grads[9], weight_grads[10], weight_grads[11], weight_grads[12], weight_grads[13], weight_grads[14])
```

```python
import jax
import jax.numpy as jnp
from jax import lax
from jax.experimental import pallas as pl
from jax.experimental.pallas import tpu as pltpu
from jax.sharding import PartitionSpec as P

D = 1024
HEADS = 16
HEAD_DIM = 64
KV_GROUPS = 8
FF = 2816
BUCKETS = 32
ENC = 512
SEQ = 256
DOCS = 4
MICRO = 2

REP = 4
SHARDS = 32
ROWS = SEQ // REP
OWN_HEADS = HEADS // REP
OWN_GROUPS = KV_GROUPS // REP
QW = OWN_HEADS * HEAD_DIM
KW = OWN_GROUPS * HEAD_DIM
OWN_FF = FF // REP
WINDOW = 144

epsilon = 1e-06
neg_big = -1e30
f32 = jnp.float32
bf16 = jnp.bfloat16
vmem_limit = 40 * 1024 * 1024


def matmul(left, right):
    return jnp.dot(left, right, preferred_element_type=f32)


def left_contract(left, right):
    return lax.dot_general(left, right, (((0,), (0,)), ((), ())), preferred_element_type=f32)


def right_contract(left, right):
    return lax.dot_general(left, right, (((1,), (1,)), ((), ())), preferred_element_type=f32)


def skewed(row):
    n = row.shape[1]
    out = jnp.broadcast_to(row, (n, n))
    at = lax.broadcasted_iota(jnp.int32, (n, n), 0)
    step = 1
    while step < n:
        out = jnp.where((at & step) != 0, pltpu.roll(out, step, 1), out)
        step *= 2
    return out


def unskewed_sum(square):
    n = square.shape[1]
    at = lax.broadcasted_iota(jnp.int32, (n, n), 0)
    step = 1
    while step < n:
        square = jnp.where((at & step) != 0, pltpu.roll(square, n - step, 1), square)
        step *= 2
    return jnp.sum(square, axis=0, keepdims=True)


def softmax_parts(scores):
    top = jnp.max(scores, axis=-1, keepdims=True)
    raised = jnp.exp(scores - top)
    return raised * (1.0 / jnp.sum(raised, axis=-1, keepdims=True))


def self_mask(seg_col, seg_row):
    at_query = lax.broadcasted_iota(jnp.int32, (SEQ, SEQ), 0)
    at_key = lax.broadcasted_iota(jnp.int32, (SEQ, SEQ), 1)
    return (at_key <= at_query) & (seg_col == seg_row)


def fill_bias(curve_ref, bias_ref):
    for head in range(OWN_HEADS):
        bias_ref[head] = skewed(curve_ref[head : head + 1, :])


def self_forward_kernel(qkv_ref, seg_col_ref, seg_row_ref, curve_ref, out_ref, bias_ref):
    @pl.when(pl.program_id(0) == 0)
    def _():
        fill_bias(curve_ref, bias_ref)

    whole = qkv_ref[...].reshape(SEQ, QW + 2 * KW)
    allowed = self_mask(seg_col_ref[0], seg_row_ref[0])
    mixed = []
    for head in range(OWN_HEADS):
        group = head * OWN_GROUPS // OWN_HEADS
        query = whole[:, head * HEAD_DIM : (head + 1) * HEAD_DIM]
        key = whole[:, QW + group * HEAD_DIM : QW + (group + 1) * HEAD_DIM]
        value = whole[:, QW + KW + group * HEAD_DIM : QW + KW + (group + 1) * HEAD_DIM]
        scores = jnp.where(allowed, right_contract(query, key) + bias_ref[head], neg_big)
        probs = softmax_parts(scores).astype(bf16)
        mixed.append(matmul(probs, value))
    out_ref[...] = jnp.concatenate(mixed, axis=1).astype(bf16).reshape(out_ref.shape)


def self_backward_kernel(
    qkv_ref, grad_ref, seg_col_ref, seg_row_ref, curve_ref, out_ref, curve_grad_ref, bias_ref, sum_ref
):
    @pl.when(pl.program_id(0) == 0)
    def _():
        fill_bias(curve_ref, bias_ref)
        sum_ref[...] = jnp.zeros_like(sum_ref)

    whole = qkv_ref[...].reshape(SEQ, QW + 2 * KW)
    grads = grad_ref[...].reshape(SEQ, QW)
    allowed = self_mask(seg_col_ref[0], seg_row_ref[0])
    query_grads = []
    key_grads = [None] * OWN_GROUPS
    value_grads = [None] * OWN_GROUPS
    for head in range(OWN_HEADS):
        group = head * OWN_GROUPS // OWN_HEADS
        query = whole[:, head * HEAD_DIM : (head + 1) * HEAD_DIM]
        key = whole[:, QW + group * HEAD_DIM : QW + (group + 1) * HEAD_DIM]
        value = whole[:, QW + KW + group * HEAD_DIM : QW + KW + (group + 1) * HEAD_DIM]
        grad = grads[:, head * HEAD_DIM : (head + 1) * HEAD_DIM]
        scores = jnp.where(allowed, right_contract(query, key) + bias_ref[head], neg_big)
        probs = softmax_parts(scores)
        prob_grad = right_contract(grad, value)
        centred = prob_grad - jnp.sum(probs * prob_grad, axis=-1, keepdims=True)
        score_grad = (probs * centred).astype(bf16)
        sum_ref[head] += score_grad.astype(f32)
        query_grads.append(matmul(score_grad, key))
        key_part = left_contract(score_grad, query)
        value_part = left_contract(probs.astype(bf16), grad)
        if key_grads[group] is None:
            key_grads[group] = key_part
            value_grads[group] = value_part
        else:
            key_grads[group] = key_grads[group] + key_part
            value_grads[group] = value_grads[group] + value_part
    joined = jnp.concatenate(query_grads + key_grads + value_grads, axis=1)
    out_ref[...] = joined.astype(bf16).reshape(out_ref.shape)

    @pl.when(pl.program_id(0) == MICRO - 1)
    def _():
        curve_grad_ref[...] = jnp.zeros_like(curve_grad_ref)
        for head in range(OWN_HEADS):
            curve_grad_ref[head : head + 1, :] = unskewed_sum(sum_ref[head])


def cross_forward_kernel(block_ref, start_ref, q_ref, kv_ref, seg_ref, out_ref, query_ref, mixed_ref):
    at = pl.program_id(0) * DOCS + pl.program_id(1)

    @pl.when(pl.program_id(1) == 0)
    def _():
        query_ref[...] = q_ref[...].reshape(SEQ, QW)

    start = pl.multiple_of(start_ref[at], 16)
    rows = query_ref[pl.ds(start, WINDOW), :]
    mine = seg_ref[0, pl.ds(start, WINDOW), :] == pl.program_id(1)
    both = kv_ref[...].reshape(ENC, 2 * KW)
    mixed = []
    for head in range(OWN_HEADS):
        group = head * OWN_GROUPS // OWN_HEADS
        query = rows[:, head * HEAD_DIM : (head + 1) * HEAD_DIM]
        key = both[:, group * HEAD_DIM : (group + 1) * HEAD_DIM]
        value = both[:, KW + group * HEAD_DIM : KW + (group + 1) * HEAD_DIM]
        probs = softmax_parts(right_contract(query, key)).astype(bf16)
        mixed.append(matmul(probs, value))
    fresh = jnp.concatenate(mixed, axis=1)
    mixed_ref[pl.ds(start, WINDOW), :] = jnp.where(mine, fresh, mixed_ref[pl.ds(start, WINDOW), :])

    @pl.when(pl.program_id(1) == DOCS - 1)
    def _():
        out_ref[...] = mixed_ref[...].astype(bf16).reshape(out_ref.shape)


def cross_backward_kernel(
    block_ref, start_ref, q_ref, kv_ref, grad_ref, seg_ref, out_ref, kv_grad_ref, query_ref, given_ref, mixed_ref
):
    at = pl.program_id(0) * DOCS + pl.program_id(1)

    @pl.when(pl.program_id(1) == 0)
    def _():
        query_ref[...] = q_ref[...].reshape(SEQ, QW)
        given_ref[...] = grad_ref[...].reshape(SEQ, QW)

    start = pl.multiple_of(start_ref[at], 16)
    rows = query_ref[pl.ds(start, WINDOW), :]
    grads = given_ref[pl.ds(start, WINDOW), :]
    mine = seg_ref[0, pl.ds(start, WINDOW), :] == pl.program_id(1)
    both = kv_ref[...].reshape(ENC, 2 * KW)
    query_grads = []
    key_grads = [None] * OWN_GROUPS
    value_grads = [None] * OWN_GROUPS
    for head in range(OWN_HEADS):
        group = head * OWN_GROUPS // OWN_HEADS
        query = rows[:, head * HEAD_DIM : (head + 1) * HEAD_DIM]
        key = both[:, group * HEAD_DIM : (group + 1) * HEAD_DIM]
        value = both[:, KW + group * HEAD_DIM : KW + (group + 1) * HEAD_DIM]
        grad = grads[:, head * HEAD_DIM : (head + 1) * HEAD_DIM]
        probs = jnp.where(mine, softmax_parts(right_contract(query, key)), 0.0)
        prob_grad = right_contract(grad, value)
        centred = prob_grad - jnp.sum(probs * prob_grad, axis=-1, keepdims=True)
        score_grad = (probs * centred).astype(bf16)
        query_grads.append(matmul(score_grad, key))
        key_part = left_contract(score_grad, query)
        value_part = left_contract(probs.astype(bf16), grad)
        if key_grads[group] is None:
            key_grads[group] = key_part
            value_grads[group] = value_part
        else:
            key_grads[group] = key_grads[group] + key_part
            value_grads[group] = value_grads[group] + value_part
    fresh = jnp.concatenate(query_grads, axis=1)
    mixed_ref[pl.ds(start, WINDOW), :] = jnp.where(mine, fresh, mixed_ref[pl.ds(start, WINDOW), :])
    joined = jnp.concatenate(key_grads + value_grads, axis=1)
    kv_grad_ref[...] = joined.astype(bf16).reshape(kv_grad_ref.shape)

    @pl.when(pl.program_id(1) == DOCS - 1)
    def _():
        out_ref[...] = mixed_ref[...].astype(bf16).reshape(out_ref.shape)


def rows_block(width):
    return pl.BlockSpec((REP, 1, ROWS, width), lambda m, *rest: (0, m, 0, 0))


def fixed_block(shape):
    return pl.BlockSpec(shape, lambda *at: (0,) * len(shape))


def micro_block(shape):
    return pl.BlockSpec((1,) + shape, lambda m, *rest: (m,) + (0,) * len(shape))


def estimate(flops, moved, raised):
    return pl.CostEstimate(flops=flops, bytes_accessed=moved, transcendentals=raised)


self_pairs = MICRO * OWN_HEADS * SEQ * SEQ
cross_pairs = MICRO * OWN_HEADS * DOCS * WINDOW * ENC


def self_forward(qkv, seg_col, seg_row, curve):
    return pl.pallas_call(
        self_forward_kernel,
        name="self_forward",
        grid=(MICRO,),
        in_specs=[
            rows_block(QW + 2 * KW),
            micro_block((SEQ, 1)),
            micro_block((1, SEQ)),
            fixed_block((8, SEQ)),
        ],
        out_specs=rows_block(QW),
        out_shape=jax.ShapeDtypeStruct((REP, MICRO, ROWS, QW), bf16),
        scratch_shapes=[pltpu.VMEM((OWN_HEADS, SEQ, SEQ), f32)],
        compiler_params=pltpu.CompilerParams(vmem_limit_bytes=vmem_limit),
        cost_estimate=estimate(self_pairs * 256, 2 << 20, self_pairs),
    )(qkv, seg_col, seg_row, curve)


def self_backward(qkv, grads, seg_col, seg_row, curve):
    return pl.pallas_call(
        self_backward_kernel,
        name="self_backward",
        grid=(MICRO,),
        in_specs=[
            rows_block(QW + 2 * KW),
            rows_block(QW),
            micro_block((SEQ, 1)),
            micro_block((1, SEQ)),
            fixed_block((8, SEQ)),
        ],
        out_specs=[rows_block(QW + 2 * KW), fixed_block((8, SEQ))],
        out_shape=[
            jax.ShapeDtypeStruct((REP, MICRO, ROWS, QW + 2 * KW), bf16),
            jax.ShapeDtypeStruct((8, SEQ), f32),
        ],
        scratch_shapes=[
            pltpu.VMEM((OWN_HEADS, SEQ, SEQ), f32),
            pltpu.VMEM((OWN_HEADS, SEQ, SEQ), f32),
        ],
        compiler_params=pltpu.CompilerParams(vmem_limit_bytes=vmem_limit),
        cost_estimate=estimate(self_pairs * 640, 3 << 20, self_pairs),
    )(qkv, grads, seg_col, seg_row, curve)


def cross_rows():
    return pl.BlockSpec((REP, 1, ROWS, QW), lambda m, d, block, start: (0, m, 0, 0))


def cross_keys():
    return pl.BlockSpec(
        (REP, 1, 1, ENC // REP, 2 * KW),
        lambda m, d, block, start: (0, m, block[m * DOCS + d], 0, 0),
    )


def cross_segs():
    return pl.BlockSpec((1, SEQ, 1), lambda m, d, block, start: (m, 0, 0))


def cross_forward(blocks, starts, queries, kv, seg_col):
    return pl.pallas_call(
        cross_forward_kernel,
        name="cross_forward",
        grid_spec=pltpu.PrefetchScalarGridSpec(
            num_scalar_prefetch=2,
            grid=(MICRO, DOCS),
            in_specs=[cross_rows(), cross_keys(), cross_segs()],
            out_specs=cross_rows(),
            scratch_shapes=[pltpu.VMEM((SEQ, QW), bf16), pltpu.VMEM((SEQ, QW), f32)],
        ),
        out_shape=jax.ShapeDtypeStruct((REP, MICRO, ROWS, QW), bf16),
        compiler_params=pltpu.CompilerParams(vmem_limit_bytes=vmem_limit),
        cost_estimate=estimate(cross_pairs * 256, 3 << 20, cross_pairs),
    )(blocks, starts, queries, kv, seg_col)


def cross_backward(blocks, starts, queries, kv, grads, seg_col):
    return pl.pallas_call(
        cross_backward_kernel,
        name="cross_backward",
        grid_spec=pltpu.PrefetchScalarGridSpec(
            num_scalar_prefetch=2,
            grid=(MICRO, DOCS),
            in_specs=[cross_rows(), cross_keys(), cross_rows(), cross_segs()],
            out_specs=[cross_rows(), cross_keys()],
            scratch_shapes=[
                pltpu.VMEM((SEQ, QW), bf16),
                pltpu.VMEM((SEQ, QW), bf16),
                pltpu.VMEM((SEQ, QW), f32),
            ],
        ),
        out_shape=[
            jax.ShapeDtypeStruct((REP, MICRO, ROWS, QW), bf16),
            jax.ShapeDtypeStruct((REP, MICRO, DOCS, ENC // REP, 2 * KW), bf16),
        ],
        compiler_params=pltpu.CompilerParams(vmem_limit_bytes=vmem_limit),
        cost_estimate=estimate(cross_pairs * 640, 6 << 20, cross_pairs),
    )(blocks, starts, queries, kv, grads, seg_col)


swap_chip = [(i, i ^ 2) for i in range(REP)]
swap_core = [(i, i ^ 1) for i in range(REP)]
spread_rows = [
    (q * SHARDS + 8 * r + a, r * SHARDS + 4 * a + q)
    for q in range(REP)
    for r in range(REP)
    for a in range(SHARDS // REP)
]
collect_rows = [(there, here) for here, there in spread_rows]


def other_chip(value):
    return lax.ppermute(value, "rep", swap_chip)


def other_core(value):
    return lax.ppermute(value, "rep", swap_core)


def in_order(flag, own, other, axis):
    return jnp.where(flag == 0, jnp.stack([own, other], axis), jnp.stack([other, own], axis))


def gather_rep(value):
    rep = lax.axis_index("rep")
    pair = in_order(rep // 2, value, other_chip(value), 0)
    whole = in_order(rep % 2, pair, other_core(pair), 1)
    return whole.reshape((REP,) + value.shape)


def scatter_rep(parts):
    rep = lax.axis_index("rep")
    chip, core = rep // 2, rep % 2
    four = parts.reshape((2, 2) + parts.shape[1:])
    given = lax.dynamic_index_in_dim(four, 1 - core, 1, keepdims=False).astype(bf16)
    kept = lax.dynamic_index_in_dim(four, core, 1, keepdims=False)
    pair = kept + other_core(given).astype(f32)
    given = lax.dynamic_index_in_dim(pair, 1 - chip, 0, keepdims=False).astype(bf16)
    kept = lax.dynamic_index_in_dim(pair, chip, 0, keepdims=False)
    return kept + other_chip(given).astype(f32)


def gather_shard(block):
    return lax.all_to_all(
        jnp.broadcast_to(block[None], (SHARDS,) + block.shape), "shard", 0, 0, tiled=True
    )


def scatter_shard(parts):
    sent = lax.all_to_all(parts.astype(bf16), "shard", 0, 0, tiled=True)
    return jnp.sum(sent.astype(f32), axis=0)


def norm_parts(values):
    return lax.rsqrt(jnp.mean(values * values, axis=-1, keepdims=True) + epsilon)


def norm_backward(values, rho, gain, upstream):
    scaled = gain * upstream
    inner = jnp.mean(values * scaled, axis=-1, keepdims=True)
    back = rho * scaled - values * (rho * rho * rho * inner)
    return back, jnp.sum(values * rho * upstream, axis=0)


def local(
    tokens,
    out_cotangent,
    encoded,
    segment_ids,
    doc_block,
    bucket_table,
    self_gain,
    query_weight,
    key_weight,
    value_weight,
    out_weight,
    bias_table,
    cross_gain,
    cross_query,
    cross_key,
    cross_value,
    cross_out,
    feed_gain,
    gate_weight,
    up_weight,
    down_weight,
):
    rep = lax.axis_index("rep")
    own = MICRO * ROWS
    enc_rows = MICRO * DOCS * ENC // REP

    def columns(weight, width):
        return lax.dynamic_slice_in_dim(weight, rep * width, width, 1)

    def piece(weight, rows):
        return lax.dynamic_slice_in_dim(weight, rep * rows, rows, 0)

    qkv_block = jnp.concatenate(
        [columns(query_weight, QW), columns(key_weight, KW), columns(value_weight, KW)], axis=1
    )
    small = jnp.concatenate([self_gain, cross_gain, feed_gain, bias_table[0], jnp.zeros((16,), bf16)])
    small = jnp.broadcast_to(small[None], (8, 128))
    small = gather_shard(small)[:, 0]
    w_qkv = gather_shard(qkv_block).reshape(D, QW + 2 * KW)
    down_padded = jnp.pad(down_weight, ((0, 8), (0, 0)))
    rows_piece = jnp.concatenate([piece(out_weight, 8), piece(cross_out, 8), piece(down_padded, 24)], axis=0)
    rows_piece = lax.ppermute(rows_piece, ("rep", "shard"), spread_rows)
    ckv_block = jnp.stack(
        [cross_key.reshape(-1, REP, KW), cross_value.reshape(-1, REP, KW)], axis=2
    ).reshape(-1, 2 * REP * KW)
    w_ckv = gather_shard(ckv_block).reshape(D, 2 * REP * KW)
    w_out = gather_shard(rows_piece[0:8]).reshape(QW, D)
    w_cq = gather_shard(columns(cross_query, QW)).reshape(D, QW)
    w_cout = gather_shard(rows_piece[8:16]).reshape(QW, D)
    w_gate = gather_shard(columns(gate_weight, OWN_FF)).reshape(D, OWN_FF)
    w_up = gather_shard(columns(up_weight, OWN_FF)).reshape(D, OWN_FF)
    w_down = gather_shard(rows_piece[16:40]).reshape(8, 96, D)[:, :88].reshape(OWN_FF, D)
    self_factor = small[:, 0:32].reshape(D).astype(f32)
    cross_factor = small[:, 32:64].reshape(D).astype(f32)
    feed_factor = small[:, 64:96].reshape(D).astype(f32)
    table = small[:, 96:112]

    segments = segment_ids[:, 0]
    seg_col = segments[:, :, None]
    seg_row = segments[:, None, :]
    blocks = doc_block[:, 0].reshape(-1)
    doc_ids = jnp.arange(DOCS, dtype=jnp.int32)
    starts = jnp.sum((segments[:, None, :] < doc_ids[None, :, None]).astype(jnp.int32), axis=2)
    starts = jnp.minimum(starts // 16 * 16, SEQ - WINDOW).reshape(-1)
    turned = jnp.roll(bucket_table[::-1], 1)
    hot = (turned[None, :] == jnp.arange(BUCKETS, dtype=jnp.int32)[:, None]).astype(bf16)
    own_table = lax.dynamic_slice_in_dim(table, rep * OWN_HEADS, OWN_HEADS, 1)
    curve = left_contract(own_table, hot)
    curve = jnp.pad(curve, ((0, 4), (0, 0)))

    own_tokens = tokens.reshape(own, D)
    own_cotangent = out_cotangent.reshape(own, D)
    all_tokens = gather_rep(own_tokens).reshape(REP * own, D).astype(f32)
    all_grad = gather_rep(own_cotangent).reshape(REP * own, D)

    normed = (all_tokens * norm_parts(all_tokens) * self_factor).astype(bf16)
    qkv = matmul(normed, w_qkv).astype(bf16).reshape(REP, MICRO, ROWS, QW + 2 * KW)
    enc = encoded.reshape(enc_rows, D)
    ckv = jnp.stack(
        [matmul(enc, w_ckv[:, 2 * KW * r : 2 * KW * (r + 1)]).astype(bf16) for r in range(REP)]
    )
    kv = lax.all_to_all(ckv, "rep", 0, 0, tiled=True)
    kv = kv.reshape(REP, MICRO, DOCS, ENC // REP, 2 * KW)
    context = self_forward(qkv, seg_col, seg_row, curve).reshape(REP * own, QW)
    own_float = own_tokens.astype(f32)
    hidden = own_float + scatter_rep(matmul(context, w_out).reshape(REP, own, D))
    cross_rho = norm_parts(hidden)
    cross_normed = gather_rep((hidden * cross_rho * cross_factor).astype(bf16)).reshape(REP * own, D)
    cross_queries = matmul(cross_normed, w_cq).astype(bf16).reshape(REP, MICRO, ROWS, QW)
    cross_context = cross_forward(blocks, starts, cross_queries, kv, seg_col).reshape(REP * own, QW)
    hidden_two = hidden + scatter_rep(matmul(cross_context, w_cout).reshape(REP, own, D))
    feed_rho = norm_parts(hidden_two)
    feed_normed = gather_rep((hidden_two * feed_rho * feed_factor).astype(bf16)).reshape(REP * own, D)
    gate = matmul(feed_normed, w_gate)
    up_part = matmul(feed_normed, w_up)
    inner_grad = right_contract(all_grad, w_down)

    def gated(gate, up_part):
        return jax.nn.gelu(gate, approximate=True) * up_part

    inner, gated_back = jax.vjp(gated, gate, up_part)
    inner = inner.astype(bf16)
    gate_part, up_grad_part = gated_back(inner_grad)
    gate_low = gate_part.astype(bf16)
    up_low = up_grad_part.astype(bf16)

    own_grad = own_cotangent.astype(f32)
    feed_upstream = scatter_rep(
        (right_contract(gate_low, w_gate) + right_contract(up_low, w_up)).reshape(REP, own, D)
    )
    hidden_grad, feed_acc = norm_backward(hidden_two, feed_rho, feed_factor, feed_upstream)
    hidden_grad = hidden_grad + own_grad
    branch = gather_rep(hidden_grad.astype(bf16)).reshape(REP * own, D)
    layer_out = hidden_two + scatter_rep(matmul(inner, w_down).reshape(REP, own, D))
    gate_acc = scatter_shard(left_contract(feed_normed, gate_low).reshape(SHARDS, 32, OWN_FF))
    up_acc = scatter_shard(left_contract(feed_normed, up_low).reshape(SHARDS, 32, OWN_FF))
    down_part = left_contract(inner, all_grad).reshape(8, 88, D)
    down_part = jnp.pad(down_part.astype(bf16), ((0, 0), (0, 8), (0, 0)))
    down_acc = scatter_shard(down_part.reshape(SHARDS, 24, D))

    context_grad = right_contract(branch, w_cout).astype(bf16).reshape(REP, MICRO, ROWS, QW)
    cq_grad, kv_grad = cross_backward(blocks, starts, cross_queries, kv, context_grad, seg_col)
    cq_grad = cq_grad.reshape(REP * own, QW)
    cross_upstream = scatter_rep(right_contract(cq_grad, w_cq).reshape(REP, own, D))
    hidden_part, cross_acc = norm_backward(hidden, cross_rho, cross_factor, cross_upstream)
    hidden_grad = hidden_grad + hidden_part
    first_branch = gather_rep(hidden_grad.astype(bf16)).reshape(REP * own, D)
    cout_acc = scatter_shard(left_contract(cross_context, branch).reshape(SHARDS, 8, D))
    cq_acc = scatter_shard(left_contract(cross_normed, cq_grad).reshape(SHARDS, 32, QW))

    ckv_grad = lax.all_to_all(kv_grad.reshape(REP, enc_rows, 2 * KW), "rep", 0, 0, tiled=True)
    ckv_grad = jnp.concatenate([ckv_grad[r] for r in range(REP)], axis=1)
    encoder_grad = right_contract(ckv_grad, w_ckv)
    core = rep % 2
    half = REP * KW
    ckv_part = left_contract(enc, ckv_grad)
    given = lax.dynamic_slice_in_dim(ckv_part, (1 - core) * half, half, 1).astype(bf16)
    kept = lax.dynamic_slice_in_dim(ckv_part, core * half, half, 1)
    ckv_acc = scatter_shard((kept + other_core(given).astype(f32)).reshape(SHARDS, 32, half))

    context_grad = right_contract(first_branch, w_out).astype(bf16).reshape(REP, MICRO, ROWS, QW)
    qkv_grad, curve_grad = self_backward(qkv, context_grad, seg_col, seg_row, curve)
    qkv_grad = qkv_grad.reshape(REP * own, QW + 2 * KW)
    out_acc = scatter_shard(left_contract(context, first_branch).reshape(SHARDS, 8, D))
    qkv_acc = scatter_shard(left_contract(normed, qkv_grad).reshape(SHARDS, 32, QW + 2 * KW))
    self_upstream = scatter_rep(right_contract(qkv_grad, w_qkv).reshape(REP, own, D))
    self_rho = norm_parts(own_float)
    token_part, self_acc = norm_backward(own_float, self_rho, self_factor, self_upstream)
    tokens_grad = hidden_grad + token_part

    table_part = lax.dot_general(
        hot.astype(f32), curve_grad[:OWN_HEADS], (((1,), (1,)), ((), ())), precision=lax.Precision.HIGHEST
    )
    table_part = lax.dynamic_update_slice(jnp.zeros((BUCKETS, HEADS), f32), table_part, (0, rep * OWN_HEADS))
    small_part = jnp.concatenate(
        [
            self_acc.reshape(SHARDS, 32),
            cross_acc.reshape(SHARDS, 32),
            feed_acc.reshape(SHARDS, 32),
            table_part,
            jnp.zeros((SHARDS, 16), f32),
        ],
        axis=1,
    )
    small_sent = lax.all_to_all(
        jnp.broadcast_to(small_part[:, None], (SHARDS, 8, 128)), "shard", 0, 0, tiled=True
    )
    small_sum = jnp.sum(small_sent, axis=0)
    small_sum = small_sum + other_chip(small_sum)
    small_sum = (small_sum + other_core(small_sum))[0]

    def all_columns(value):
        whole = gather_rep(value.astype(bf16)).astype(f32)
        return jnp.concatenate([whole[r] for r in range(REP)], axis=1)

    rows_back = jnp.concatenate([out_acc, cout_acc, down_acc], axis=0).astype(bf16)
    rows_back = gather_rep(lax.ppermute(rows_back, ("rep", "shard"), collect_rows)).astype(f32)
    out_grad = rows_back[:, 0:8].reshape(32, D)
    cout_grad = rows_back[:, 8:16].reshape(32, D)
    down_grad = rows_back[:, 16:40].reshape(96, D)[:88]
    qkv_all = gather_rep(qkv_acc.astype(bf16)).astype(f32)
    query_grad = jnp.concatenate([qkv_all[r, :, :QW] for r in range(REP)], axis=1)
    key_grad = jnp.concatenate([qkv_all[r, :, QW : QW + KW] for r in range(REP)], axis=1)
    value_grad = jnp.concatenate([qkv_all[r, :, QW + KW :] for r in range(REP)], axis=1)
    cq_all = all_columns(cq_acc)
    gate_all = all_columns(gate_acc)
    up_all = all_columns(up_acc)
    ckv_acc = ckv_acc + other_chip(ckv_acc.astype(bf16)).astype(f32)
    ckv_acc = ckv_acc.astype(bf16)
    ckv_all = in_order(core, ckv_acc, other_core(ckv_acc), 1).astype(f32)
    ckv_all = ckv_all.reshape(32, REP, 2, KW)
    ck_grad = ckv_all[:, :, 0].reshape(32, REP * KW)
    cv_grad = ckv_all[:, :, 1].reshape(32, REP * KW)

    return (
        layer_out.astype(bf16).reshape(tokens.shape),
        tokens_grad.reshape(tokens.shape),
        encoder_grad.reshape(encoded.shape),
        small_sum[0:32],
        query_grad,
        key_grad,
        value_grad,
        out_grad,
        small_sum[96:112].reshape(1, HEADS),
        small_sum[32:64],
        cq_all,
        ck_grad,
        cv_grad,
        cout_grad,
        small_sum[64:96],
        gate_all,
        up_all,
        down_grad,
    )


def solution(mesh):
    rows = P("shard", None)
    gain = P("shard")
    acts = P(None, "shard", "rep", None)
    encs = P(None, "shard", None, "rep", None)
    ids = P(None, "shard", None)
    weights = (gain, rows, rows, rows, rows, rows, gain, rows, rows, rows, rows, gain, rows, rows, rows)
    return jax.shard_map(
        local,
        mesh=mesh,
        in_specs=(acts, acts, encs, ids, ids, P()) + weights,
        out_specs=(acts, acts, encs) + weights,
        check_vma=False,
    )
```

```python
import jax
import jax.numpy as jnp
from jax import lax
from jax.experimental import pallas as pl
from jax.experimental.pallas import tpu as pltpu
from jax.sharding import PartitionSpec as P

D = 1024
HEADS = 16
HEAD_DIM = 64
KV_GROUPS = 8
FF = 2816
BUCKETS = 32
ENC = 512
SEQ = 256
DOCS = 4
MICRO = 2

REP = 4
SHARDS = 32
ROWS = SEQ // REP
OWN_HEADS = HEADS // REP
OWN_GROUPS = KV_GROUPS // REP
QW = OWN_HEADS * HEAD_DIM
KW = OWN_GROUPS * HEAD_DIM
OWN_FF = FF // REP
WINDOW = 144

epsilon = 1e-06
neg_big = -1e30
f32 = jnp.float32
bf16 = jnp.bfloat16
vmem_limit = 40 * 1024 * 1024


def matmul(left, right):
    return jnp.dot(left, right, preferred_element_type=f32)


def left_contract(left, right):
    return lax.dot_general(left, right, (((0,), (0,)), ((), ())), preferred_element_type=f32)


def right_contract(left, right):
    return lax.dot_general(left, right, (((1,), (1,)), ((), ())), preferred_element_type=f32)


def skewed(row):
    n = row.shape[1]
    out = jnp.broadcast_to(row, (n, n))
    at = lax.broadcasted_iota(jnp.int32, (n, n), 0)
    step = 1
    while step < n:
        out = jnp.where((at & step) != 0, pltpu.roll(out, step, 1), out)
        step *= 2
    return out


def unskewed_sum(square):
    n = square.shape[1]
    at = lax.broadcasted_iota(jnp.int32, (n, n), 0)
    step = 1
    while step < n:
        square = jnp.where((at & step) != 0, pltpu.roll(square, n - step, 1), square)
        step *= 2
    return jnp.sum(square, axis=0, keepdims=True)


def softmax_parts(scores):
    top = jnp.max(scores, axis=-1, keepdims=True)
    raised = jnp.exp(scores - top)
    return raised * (1.0 / jnp.sum(raised, axis=-1, keepdims=True))


def self_mask(seg_col, seg_row):
    at_query = lax.broadcasted_iota(jnp.int32, (SEQ, SEQ), 0)
    at_key = lax.broadcasted_iota(jnp.int32, (SEQ, SEQ), 1)
    return (at_key <= at_query) & (seg_col == seg_row)


def fill_bias(curve_ref, bias_ref):
    for head in range(OWN_HEADS):
        bias_ref[head] = skewed(curve_ref[head : head + 1, :])


def self_forward_kernel(qkv_ref, seg_col_ref, seg_row_ref, curve_ref, out_ref, bias_ref):
    @pl.when(pl.program_id(0) == 0)
    def _():
        fill_bias(curve_ref, bias_ref)

    whole = qkv_ref[...].reshape(SEQ, QW + 2 * KW)
    allowed = self_mask(seg_col_ref[0], seg_row_ref[0])
    mixed = []
    for head in range(OWN_HEADS):
        group = head * OWN_GROUPS // OWN_HEADS
        query = whole[:, head * HEAD_DIM : (head + 1) * HEAD_DIM]
        key = whole[:, QW + group * HEAD_DIM : QW + (group + 1) * HEAD_DIM]
        value = whole[:, QW + KW + group * HEAD_DIM : QW + KW + (group + 1) * HEAD_DIM]
        scores = jnp.where(allowed, right_contract(query, key) + bias_ref[head], neg_big)
        probs = softmax_parts(scores).astype(bf16)
        mixed.append(matmul(probs, value))
    out_ref[...] = jnp.concatenate(mixed, axis=1).astype(bf16).reshape(out_ref.shape)


def self_backward_kernel(
    qkv_ref, grad_ref, seg_col_ref, seg_row_ref, curve_ref, out_ref, curve_grad_ref, bias_ref, sum_ref
):
    @pl.when(pl.program_id(0) == 0)
    def _():
        fill_bias(curve_ref, bias_ref)
        sum_ref[...] = jnp.zeros_like(sum_ref)

    whole = qkv_ref[...].reshape(SEQ, QW + 2 * KW)
    grads = grad_ref[...].reshape(SEQ, QW)
    allowed = self_mask(seg_col_ref[0], seg_row_ref[0])
    query_grads = []
    key_grads = [None] * OWN_GROUPS
    value_grads = [None] * OWN_GROUPS
    for head in range(OWN_HEADS):
        group = head * OWN_GROUPS // OWN_HEADS
        query = whole[:, head * HEAD_DIM : (head + 1) * HEAD_DIM]
        key = whole[:, QW + group * HEAD_DIM : QW + (group + 1) * HEAD_DIM]
        value = whole[:, QW + KW + group * HEAD_DIM : QW + KW + (group + 1) * HEAD_DIM]
        grad = grads[:, head * HEAD_DIM : (head + 1) * HEAD_DIM]
        scores = jnp.where(allowed, right_contract(query, key) + bias_ref[head], neg_big)
        probs = softmax_parts(scores)
        prob_grad = right_contract(grad, value)
        centred = prob_grad - jnp.sum(probs * prob_grad, axis=-1, keepdims=True)
        score_grad = (probs * centred).astype(bf16)
        sum_ref[head] += score_grad.astype(f32)
        query_grads.append(matmul(score_grad, key))
        key_part = left_contract(score_grad, query)
        value_part = left_contract(probs.astype(bf16), grad)
        if key_grads[group] is None:
            key_grads[group] = key_part
            value_grads[group] = value_part
        else:
            key_grads[group] = key_grads[group] + key_part
            value_grads[group] = value_grads[group] + value_part
    joined = jnp.concatenate(query_grads + key_grads + value_grads, axis=1)
    out_ref[...] = joined.astype(bf16).reshape(out_ref.shape)

    @pl.when(pl.program_id(0) == MICRO - 1)
    def _():
        curve_grad_ref[...] = jnp.zeros_like(curve_grad_ref)
        for head in range(OWN_HEADS):
            curve_grad_ref[head : head + 1, :] = unskewed_sum(sum_ref[head])


def cross_forward_kernel(block_ref, start_ref, q_ref, kv_ref, seg_ref, out_ref, query_ref, mixed_ref):
    at = pl.program_id(0) * DOCS + pl.program_id(1)

    @pl.when(pl.program_id(1) == 0)
    def _():
        query_ref[...] = q_ref[...].reshape(SEQ, QW)

    start = pl.multiple_of(start_ref[at], 16)
    rows = query_ref[pl.ds(start, WINDOW), :]
    mine = seg_ref[0, pl.ds(start, WINDOW), :] == pl.program_id(1)
    both = kv_ref[...].reshape(ENC, 2 * KW)
    mixed = []
    for head in range(OWN_HEADS):
        group = head * OWN_GROUPS // OWN_HEADS
        query = rows[:, head * HEAD_DIM : (head + 1) * HEAD_DIM]
        key = both[:, group * HEAD_DIM : (group + 1) * HEAD_DIM]
        value = both[:, KW + group * HEAD_DIM : KW + (group + 1) * HEAD_DIM]
        probs = softmax_parts(right_contract(query, key)).astype(bf16)
        mixed.append(matmul(probs, value))
    fresh = jnp.concatenate(mixed, axis=1)
    mixed_ref[pl.ds(start, WINDOW), :] = jnp.where(mine, fresh, mixed_ref[pl.ds(start, WINDOW), :])

    @pl.when(pl.program_id(1) == DOCS - 1)
    def _():
        out_ref[...] = mixed_ref[...].astype(bf16).reshape(out_ref.shape)


def cross_backward_kernel(
    block_ref, start_ref, q_ref, kv_ref, grad_ref, seg_ref, out_ref, kv_grad_ref, query_ref, given_ref, mixed_ref
):
    at = pl.program_id(0) * DOCS + pl.program_id(1)

    @pl.when(pl.program_id(1) == 0)
    def _():
        query_ref[...] = q_ref[...].reshape(SEQ, QW)
        given_ref[...] = grad_ref[...].reshape(SEQ, QW)

    start = pl.multiple_of(start_ref[at], 16)
    rows = query_ref[pl.ds(start, WINDOW), :]
    grads = given_ref[pl.ds(start, WINDOW), :]
    mine = seg_ref[0, pl.ds(start, WINDOW), :] == pl.program_id(1)
    both = kv_ref[...].reshape(ENC, 2 * KW)
    query_grads = []
    key_grads = [None] * OWN_GROUPS
    value_grads = [None] * OWN_GROUPS
    for head in range(OWN_HEADS):
        group = head * OWN_GROUPS // OWN_HEADS
        query = rows[:, head * HEAD_DIM : (head + 1) * HEAD_DIM]
        key = both[:, group * HEAD_DIM : (group + 1) * HEAD_DIM]
        value = both[:, KW + group * HEAD_DIM : KW + (group + 1) * HEAD_DIM]
        grad = grads[:, head * HEAD_DIM : (head + 1) * HEAD_DIM]
        probs = jnp.where(mine, softmax_parts(right_contract(query, key)), 0.0)
        prob_grad = right_contract(grad, value)
        centred = prob_grad - jnp.sum(probs * prob_grad, axis=-1, keepdims=True)
        score_grad = (probs * centred).astype(bf16)
        query_grads.append(matmul(score_grad, key))
        key_part = left_contract(score_grad, query)
        value_part = left_contract(probs.astype(bf16), grad)
        if key_grads[group] is None:
            key_grads[group] = key_part
            value_grads[group] = value_part
        else:
            key_grads[group] = key_grads[group] + key_part
            value_grads[group] = value_grads[group] + value_part
    fresh = jnp.concatenate(query_grads, axis=1)
    mixed_ref[pl.ds(start, WINDOW), :] = jnp.where(mine, fresh, mixed_ref[pl.ds(start, WINDOW), :])
    joined = jnp.concatenate(key_grads + value_grads, axis=1)
    kv_grad_ref[...] = joined.astype(bf16).reshape(kv_grad_ref.shape)

    @pl.when(pl.program_id(1) == DOCS - 1)
    def _():
        out_ref[...] = mixed_ref[...].astype(bf16).reshape(out_ref.shape)


def rows_block(width):
    return pl.BlockSpec((REP, 1, ROWS, width), lambda m, *rest: (0, m, 0, 0))


def fixed_block(shape):
    return pl.BlockSpec(shape, lambda *at: (0,) * len(shape))


def micro_block(shape):
    return pl.BlockSpec((1,) + shape, lambda m, *rest: (m,) + (0,) * len(shape))


def estimate(flops, moved, raised):
    return pl.CostEstimate(flops=flops, bytes_accessed=moved, transcendentals=raised)


self_pairs = MICRO * OWN_HEADS * SEQ * SEQ
cross_pairs = MICRO * OWN_HEADS * DOCS * WINDOW * ENC


def self_forward(qkv, seg_col, seg_row, curve):
    return pl.pallas_call(
        self_forward_kernel,
        name="self_forward",
        grid=(MICRO,),
        in_specs=[
            rows_block(QW + 2 * KW),
            micro_block((SEQ, 1)),
            micro_block((1, SEQ)),
            fixed_block((8, SEQ)),
        ],
        out_specs=rows_block(QW),
        out_shape=jax.ShapeDtypeStruct((REP, MICRO, ROWS, QW), bf16),
        scratch_shapes=[pltpu.VMEM((OWN_HEADS, SEQ, SEQ), f32)],
        compiler_params=pltpu.CompilerParams(vmem_limit_bytes=vmem_limit),
        cost_estimate=estimate(self_pairs * 256, 2 << 20, self_pairs),
    )(qkv, seg_col, seg_row, curve)


def self_backward(qkv, grads, seg_col, seg_row, curve):
    return pl.pallas_call(
        self_backward_kernel,
        name="self_backward",
        grid=(MICRO,),
        in_specs=[
            rows_block(QW + 2 * KW),
            rows_block(QW),
            micro_block((SEQ, 1)),
            micro_block((1, SEQ)),
            fixed_block((8, SEQ)),
        ],
        out_specs=[rows_block(QW + 2 * KW), fixed_block((8, SEQ))],
        out_shape=[
            jax.ShapeDtypeStruct((REP, MICRO, ROWS, QW + 2 * KW), bf16),
            jax.ShapeDtypeStruct((8, SEQ), f32),
        ],
        scratch_shapes=[
            pltpu.VMEM((OWN_HEADS, SEQ, SEQ), f32),
            pltpu.VMEM((OWN_HEADS, SEQ, SEQ), f32),
        ],
        compiler_params=pltpu.CompilerParams(vmem_limit_bytes=vmem_limit),
        cost_estimate=estimate(self_pairs * 640, 3 << 20, self_pairs),
    )(qkv, grads, seg_col, seg_row, curve)


def cross_rows():
    return pl.BlockSpec((REP, 1, ROWS, QW), lambda m, d, block, start: (0, m, 0, 0))


def cross_keys():
    return pl.BlockSpec(
        (REP, 1, 1, ENC // REP, 2 * KW),
        lambda m, d, block, start: (0, m, block[m * DOCS + d], 0, 0),
    )


def cross_segs():
    return pl.BlockSpec((1, SEQ, 1), lambda m, d, block, start: (m, 0, 0))


def cross_forward(blocks, starts, queries, kv, seg_col):
    return pl.pallas_call(
        cross_forward_kernel,
        name="cross_forward",
        grid_spec=pltpu.PrefetchScalarGridSpec(
            num_scalar_prefetch=2,
            grid=(MICRO, DOCS),
            in_specs=[cross_rows(), cross_keys(), cross_segs()],
            out_specs=cross_rows(),
            scratch_shapes=[pltpu.VMEM((SEQ, QW), bf16), pltpu.VMEM((SEQ, QW), f32)],
        ),
        out_shape=jax.ShapeDtypeStruct((REP, MICRO, ROWS, QW), bf16),
        compiler_params=pltpu.CompilerParams(vmem_limit_bytes=vmem_limit),
        cost_estimate=estimate(cross_pairs * 256, 3 << 20, cross_pairs),
    )(blocks, starts, queries, kv, seg_col)


def cross_backward(blocks, starts, queries, kv, grads, seg_col):
    return pl.pallas_call(
        cross_backward_kernel,
        name="cross_backward",
        grid_spec=pltpu.PrefetchScalarGridSpec(
            num_scalar_prefetch=2,
            grid=(MICRO, DOCS),
            in_specs=[cross_rows(), cross_keys(), cross_rows(), cross_segs()],
            out_specs=[cross_rows(), cross_keys()],
            scratch_shapes=[
                pltpu.VMEM((SEQ, QW), bf16),
                pltpu.VMEM((SEQ, QW), bf16),
                pltpu.VMEM((SEQ, QW), f32),
            ],
        ),
        out_shape=[
            jax.ShapeDtypeStruct((REP, MICRO, ROWS, QW), bf16),
            jax.ShapeDtypeStruct((REP, MICRO, DOCS, ENC // REP, 2 * KW), bf16),
        ],
        compiler_params=pltpu.CompilerParams(vmem_limit_bytes=vmem_limit),
        cost_estimate=estimate(cross_pairs * 640, 6 << 20, cross_pairs),
    )(blocks, starts, queries, kv, grads, seg_col)


swap_chip = [(i, i ^ 2) for i in range(REP)]
swap_core = [(i, i ^ 1) for i in range(REP)]
spread_rows = [
    (q * SHARDS + 8 * r + a, r * SHARDS + 4 * a + q)
    for q in range(REP)
    for r in range(REP)
    for a in range(SHARDS // REP)
]
collect_rows = [(there, here) for here, there in spread_rows]


def other_chip(value):
    return lax.ppermute(value, "rep", swap_chip)


def other_core(value):
    return lax.ppermute(value, "rep", swap_core)


def in_order(flag, own, other, axis):
    return jnp.where(flag == 0, jnp.stack([own, other], axis), jnp.stack([other, own], axis))


def gather_rep(value):
    rep = lax.axis_index("rep")
    pair = in_order(rep // 2, value, other_chip(value), 0)
    whole = in_order(rep % 2, pair, other_core(pair), 1)
    return whole.reshape((REP,) + value.shape)


def scatter_rep(parts):
    rep = lax.axis_index("rep")
    chip, core = rep // 2, rep % 2
    four = parts.reshape((2, 2) + parts.shape[1:])
    given = lax.dynamic_index_in_dim(four, 1 - core, 1, keepdims=False).astype(bf16)
    kept = lax.dynamic_index_in_dim(four, core, 1, keepdims=False)
    pair = kept + other_core(given).astype(f32)
    given = lax.dynamic_index_in_dim(pair, 1 - chip, 0, keepdims=False).astype(bf16)
    kept = lax.dynamic_index_in_dim(pair, chip, 0, keepdims=False)
    return kept + other_chip(given).astype(f32)


def gather_shard(block):
    return lax.all_to_all(
        jnp.broadcast_to(block[None], (SHARDS,) + block.shape), "shard", 0, 0, tiled=True
    )


def scatter_shard(parts):
    sent = lax.all_to_all(parts.astype(bf16), "shard", 0, 0, tiled=True)
    return jnp.sum(sent.astype(f32), axis=0)


MESH = pl.DeviceIdType.MESH


def remote(source, target, send_sem, recv_sem, device):
    return pltpu.make_async_remote_copy(
        src_ref=source,
        dst_ref=target,
        send_sem=send_sem,
        recv_sem=recv_sem,
        device_id=device,
        device_id_type=MESH,
    )


def meet(devices):
    barrier = pltpu.get_barrier_semaphore()
    for device in devices:
        pl.semaphore_signal(barrier, inc=1, device_id=device, device_id_type=MESH)
    pl.semaphore_wait(barrier, len(devices))


class Ring:
    def __init__(self, group, half, me, device_at, send_sems, recv_sems):
        right, left = lax.rem(me + 1, 4), lax.rem(me + 3, 4)
        to_right, to_left = device_at(right), device_at(left)

        def copy(ref, device, i):
            return remote(ref, ref, send_sems.at[i], recv_sems.at[i], device)

        self.direct = [copy(group(me), to_right, 0), copy(group(me), to_left, 1)]
        self.passed = [copy(half(left, 0), to_right, 2), copy(half(right, 1), to_left, 3)]

    def start(self):
        for copy in self.direct:
            copy.start()

    def forward(self):
        for arrived, onward in zip(self.direct, self.passed):
            arrived.wait_recv()
            onward.start()

    def finish(self):
        for copy in self.passed:
            copy.wait_recv()

    def drain(self):
        for copy in self.direct + self.passed:
            copy.wait_send()


def gather_kernel(first_x, split, n_rep, *refs):
    n = len(first_x)
    blocks, own_rows = refs[:n], refs[n : n + n_rep]
    wholes, all_rows = refs[n + n_rep : 2 * n + n_rep], refs[2 * n + n_rep : 2 * n + 2 * n_rep]
    local_sems, pair_send, pair_recv, ring_send, ring_recv, rep_send, rep_recv = refs[2 * n + 2 * n_rep :]
    at = lax.axis_index("shard")
    rep = lax.axis_index("rep")
    x, y, z = lax.div(at, 8), lax.rem(lax.div(at, 2), 4), lax.rem(at, 2)
    chip, core = lax.div(rep, 2), lax.rem(rep, 2)
    pair = {"shard": at + 1 - 2 * z}
    far = {"rep": (1 - chip) * 2 + core}
    near = {"rep": chip * 2 + 1 - core}

    def on_x(i):
        return {"shard": i * 8 + y * 2 + z}

    def on_y(i):
        return {"shard": x * 8 + i * 2 + z}

    meet(
        [pair, far, near]
        + [on_x(lax.rem(x + d, 4)) for d in (1, 3)]
        + [on_y(lax.rem(y + d, 4)) for d in (1, 3)]
    )
    locals_, pairs, small_rings, large_rings = [], [], [], []
    for i in range(n):
        whole = wholes[i].at[core] if split[i] else wholes[i]
        slot = whole.at[x, y, z]
        locals_.append(pltpu.make_async_copy(blocks[i], slot, local_sems.at[i]))
        pairs.append(remote(blocks[i], slot, pair_send.at[i], pair_recv.at[i], pair))

        def x_small(j, whole=whole):
            return whole.at[j, y]

        def x_small_half(j, h, whole=whole):
            return whole.at[j, y, h]

        def y_small(j, whole=whole):
            return whole.at[x, j]

        def y_small_half(j, h, whole=whole):
            return whole.at[x, j, h]

        def x_large(j, whole=whole):
            return whole.at[j]

        def x_large_half(j, h, whole=whole):
            return whole.at[j, pl.ds(2 * h, 2)]

        def y_large(j, whole=whole):
            return whole.at[:, j]

        def y_large_half(j, h, whole=whole):
            return whole.at[pl.ds(2 * h, 2), j]

        small, large = ring_send.at[i, 0], ring_send.at[i, 1]
        small_in, large_in = ring_recv.at[i, 0], ring_recv.at[i, 1]
        if first_x[i]:
            small_rings.append(Ring(x_small, x_small_half, x, on_x, small, small_in))
            large_rings.append(Ring(y_large, y_large_half, y, on_y, large, large_in))
        else:
            small_rings.append(Ring(y_small, y_small_half, y, on_y, small, small_in))
            large_rings.append(Ring(x_large, x_large_half, x, on_x, large, large_in))
    for i in range(n):
        locals_[i].start()
        pairs[i].start()
    rep_local, rep_first, rep_second = [], [], []
    for i in range(n_rep):
        mine = all_rows[i].at[rep]
        theirs = all_rows[i].at[(1 - chip) * 2 + core]
        rep_local.append(pltpu.make_async_copy(own_rows[i], mine, local_sems.at[n + i]))
        rep_first.append(remote(own_rows[i], mine, rep_send.at[i, 0], rep_recv.at[i, 0], far))
        rep_second.append(remote(own_rows[i], mine, rep_send.at[i, 1], rep_recv.at[i, 1], near))
        rep_second.append(remote(theirs, theirs, rep_send.at[i, 2], rep_recv.at[i, 2], near))
        rep_local[i].start()
        rep_first[i].start()
        rep_second[2 * i].start()
    for i in range(n):
        locals_[i].wait()
        pairs[i].wait_recv()
        small_rings[i].start()
    for i in range(n):
        small_rings[i].forward()
    for i in range(n):
        small_rings[i].finish()
        large_rings[i].start()
    for i in range(n_rep):
        rep_first[i].wait_recv()
        rep_second[2 * i + 1].start()
    for i in range(n):
        large_rings[i].forward()
    swaps = []
    for i in range(n):
        large_rings[i].finish()
        if split[i]:
            half = wholes[i].at[core]
            swaps.append(remote(half, half, rep_send.at[n_rep, 0], rep_recv.at[n_rep, 0], near))
            swaps[-1].start()
    for i in range(n):
        pairs[i].wait_send()
        small_rings[i].drain()
        large_rings[i].drain()
    for i in range(n_rep):
        rep_local[i].wait()
        rep_first[i].wait_send()
        for copy in rep_second[2 * i : 2 * i + 2]:
            copy.wait()
    for copy in swaps:
        copy.wait()


def gather_weights(blocks, first_x, split, rows):
    n, n_rep = len(blocks), len(rows)
    shapes = [
        jax.ShapeDtypeStruct(((2,) if split[i] else ()) + (4, 4, 2) + blocks[i].shape, blocks[i].dtype)
        for i in range(n)
    ] + [jax.ShapeDtypeStruct((REP,) + value.shape, value.dtype) for value in rows]
    anywhere = pl.BlockSpec(memory_space=pl.ANY)
    dma = pltpu.SemaphoreType.DMA
    results = pl.pallas_call(
        lambda *refs: gather_kernel(first_x, split, n_rep, *refs),
        name="gather_weights",
        in_specs=[anywhere] * (n + n_rep),
        out_specs=[anywhere] * (n + n_rep),
        out_shape=shapes,
        scratch_shapes=[
            dma((n + n_rep,)),
            dma((n,)),
            dma((n,)),
            dma((n, 2, 4)),
            dma((n, 2, 4)),
            dma((n_rep + 1, 3)),
            dma((n_rep + 1, 3)),
        ],
        compiler_params=pltpu.CompilerParams(collective_id=0, has_side_effects=True),
        cost_estimate=estimate(0, 64 << 20, 0),
    )(*blocks, *rows)
    return results[:n], results[n:]


def norm_parts(values):
    return lax.rsqrt(jnp.mean(values * values, axis=-1, keepdims=True) + epsilon)


def norm_backward(values, rho, gain, upstream):
    scaled = gain * upstream
    inner = jnp.mean(values * scaled, axis=-1, keepdims=True)
    back = rho * scaled - values * (rho * rho * rho * inner)
    return back, jnp.sum(values * rho * upstream, axis=0)


def local(
    tokens,
    out_cotangent,
    encoded,
    segment_ids,
    doc_block,
    bucket_table,
    self_gain,
    query_weight,
    key_weight,
    value_weight,
    out_weight,
    bias_table,
    cross_gain,
    cross_query,
    cross_key,
    cross_value,
    cross_out,
    feed_gain,
    gate_weight,
    up_weight,
    down_weight,
):
    rep = lax.axis_index("rep")
    own = MICRO * ROWS
    enc_rows = MICRO * DOCS * ENC // REP

    def columns(weight, width):
        return lax.dynamic_slice_in_dim(weight, rep * width, width, 1)

    def piece(weight, rows):
        return lax.dynamic_slice_in_dim(weight, rep * rows, rows, 0)

    qkv_block = jnp.concatenate(
        [columns(query_weight, QW), columns(key_weight, KW), columns(value_weight, KW)], axis=1
    )
    small = jnp.concatenate([self_gain, cross_gain, feed_gain, bias_table[0], jnp.zeros((16,), bf16)])
    small = jnp.broadcast_to(small[None], (8, 128))
    down_padded = jnp.pad(down_weight, ((0, 8), (0, 0)))
    rows_piece = jnp.concatenate([piece(out_weight, 8), piece(cross_out, 8), piece(down_padded, 24)], axis=0)
    rows_piece = lax.ppermute(rows_piece, ("rep", "shard"), spread_rows)
    ckv_block = jnp.stack(
        [cross_key.reshape(-1, REP, KW), cross_value.reshape(-1, REP, KW)], axis=2
    ).reshape(-1, 2 * REP * KW)
    ckv_block = lax.dynamic_slice_in_dim(ckv_block, rep % 2 * REP * KW, REP * KW, 1)
    own_tokens = tokens.reshape(own, D)
    own_cotangent = out_cotangent.reshape(own, D)
    blocks = [
        qkv_block,
        small,
        rows_piece[0:8],
        ckv_block,
        columns(cross_query, QW),
        rows_piece[8:16],
        columns(gate_weight, OWN_FF),
        columns(up_weight, OWN_FF),
        rows_piece[16:40],
    ]
    first_x = [True, False, False, True, True, False, True, False, False]
    split = [False, False, False, True, False, False, False, False, False]
    (w_qkv, small, w_out, w_ckv, w_cq, w_cout, w_gate, w_up, w_down), (all_tokens, all_grad) = gather_weights(
        blocks, first_x, split, [own_tokens, own_cotangent]
    )
    w_qkv = w_qkv.reshape(D, QW + 2 * KW)
    small = small.reshape(SHARDS, 8, 128)[:, 0]
    w_out = w_out.reshape(QW, D)
    w_ckv = w_ckv.reshape(2, D, REP * KW)
    w_cq = w_cq.reshape(D, QW)
    w_cout = w_cout.reshape(QW, D)
    w_gate = w_gate.reshape(D, OWN_FF)
    w_up = w_up.reshape(D, OWN_FF)
    w_down = w_down.reshape(8, 96, D)[:, :88].reshape(OWN_FF, D)
    self_factor = small[:, 0:32].reshape(D).astype(f32)
    cross_factor = small[:, 32:64].reshape(D).astype(f32)
    feed_factor = small[:, 64:96].reshape(D).astype(f32)
    table = small[:, 96:112]

    segments = segment_ids[:, 0]
    seg_col = segments[:, :, None]
    seg_row = segments[:, None, :]
    blocks = doc_block[:, 0].reshape(-1)
    doc_ids = jnp.arange(DOCS, dtype=jnp.int32)
    starts = jnp.sum((segments[:, None, :] < doc_ids[None, :, None]).astype(jnp.int32), axis=2)
    starts = jnp.minimum(starts // 16 * 16, SEQ - WINDOW).reshape(-1)
    turned = jnp.roll(bucket_table[::-1], 1)
    hot = (turned[None, :] == jnp.arange(BUCKETS, dtype=jnp.int32)[:, None]).astype(bf16)
    own_table = lax.dynamic_slice_in_dim(table, rep * OWN_HEADS, OWN_HEADS, 1)
    curve = left_contract(own_table, hot)
    curve = jnp.pad(curve, ((0, 4), (0, 0)))

    all_tokens = all_tokens.reshape(REP * own, D).astype(f32)
    all_grad = all_grad.reshape(REP * own, D)

    normed = (all_tokens * norm_parts(all_tokens) * self_factor).astype(bf16)
    qkv = matmul(normed, w_qkv).astype(bf16).reshape(REP, MICRO, ROWS, QW + 2 * KW)
    enc = encoded.reshape(enc_rows, D)
    ckv = jnp.stack(
        [
            matmul(enc, w_ckv[r // 2, :, 2 * KW * (r % 2) : 2 * KW * (r % 2 + 1)]).astype(bf16)
            for r in range(REP)
        ]
    )
    kv = lax.all_to_all(ckv, "rep", 0, 0, tiled=True)
    kv = kv.reshape(REP, MICRO, DOCS, ENC // REP, 2 * KW)
    context = self_forward(qkv, seg_col, seg_row, curve).reshape(REP * own, QW)
    own_float = own_tokens.astype(f32)
    hidden = own_float + scatter_rep(matmul(context, w_out).reshape(REP, own, D))
    cross_rho = norm_parts(hidden)
    cross_normed = gather_rep((hidden * cross_rho * cross_factor).astype(bf16)).reshape(REP * own, D)
    cross_queries = matmul(cross_normed, w_cq).astype(bf16).reshape(REP, MICRO, ROWS, QW)
    cross_context = cross_forward(blocks, starts, cross_queries, kv, seg_col).reshape(REP * own, QW)
    hidden_two = hidden + scatter_rep(matmul(cross_context, w_cout).reshape(REP, own, D))
    feed_rho = norm_parts(hidden_two)
    feed_normed = gather_rep((hidden_two * feed_rho * feed_factor).astype(bf16)).reshape(REP * own, D)
    gate = matmul(feed_normed, w_gate)
    up_part = matmul(feed_normed, w_up)
    inner_grad = right_contract(all_grad, w_down)

    def gated(gate, up_part):
        return jax.nn.gelu(gate, approximate=True) * up_part

    inner, gated_back = jax.vjp(gated, gate, up_part)
    inner = inner.astype(bf16)
    gate_part, up_grad_part = gated_back(inner_grad)
    gate_low = gate_part.astype(bf16)
    up_low = up_grad_part.astype(bf16)

    own_grad = own_cotangent.astype(f32)
    feed_upstream = scatter_rep(
        (right_contract(gate_low, w_gate) + right_contract(up_low, w_up)).reshape(REP, own, D)
    )
    hidden_grad, feed_acc = norm_backward(hidden_two, feed_rho, feed_factor, feed_upstream)
    hidden_grad = hidden_grad + own_grad
    branch = gather_rep(hidden_grad.astype(bf16)).reshape(REP * own, D)
    layer_out = hidden_two + scatter_rep(matmul(inner, w_down).reshape(REP, own, D))
    gate_acc = scatter_shard(left_contract(feed_normed, gate_low).reshape(SHARDS, 32, OWN_FF))
    up_acc = scatter_shard(left_contract(feed_normed, up_low).reshape(SHARDS, 32, OWN_FF))
    down_part = left_contract(inner, all_grad).reshape(8, 88, D)
    down_part = jnp.pad(down_part.astype(bf16), ((0, 0), (0, 8), (0, 0)))
    down_acc = scatter_shard(down_part.reshape(SHARDS, 24, D))

    context_grad = right_contract(branch, w_cout).astype(bf16).reshape(REP, MICRO, ROWS, QW)
    cq_grad, kv_grad = cross_backward(blocks, starts, cross_queries, kv, context_grad, seg_col)
    cq_grad = cq_grad.reshape(REP * own, QW)
    cross_upstream = scatter_rep(right_contract(cq_grad, w_cq).reshape(REP, own, D))
    hidden_part, cross_acc = norm_backward(hidden, cross_rho, cross_factor, cross_upstream)
    hidden_grad = hidden_grad + hidden_part
    first_branch = gather_rep(hidden_grad.astype(bf16)).reshape(REP * own, D)
    cout_acc = scatter_shard(left_contract(cross_context, branch).reshape(SHARDS, 8, D))
    cq_acc = scatter_shard(left_contract(cross_normed, cq_grad).reshape(SHARDS, 32, QW))

    ckv_grad = lax.all_to_all(kv_grad.reshape(REP, enc_rows, 2 * KW), "rep", 0, 0, tiled=True)
    ckv_grad = jnp.concatenate([ckv_grad[r] for r in range(REP)], axis=1)
    core = rep % 2
    half = REP * KW
    encoder_grad = right_contract(ckv_grad[:, :half], w_ckv[0]) + right_contract(ckv_grad[:, half:], w_ckv[1])
    ckv_part = left_contract(enc, ckv_grad)
    given = lax.dynamic_slice_in_dim(ckv_part, (1 - core) * half, half, 1).astype(bf16)
    kept = lax.dynamic_slice_in_dim(ckv_part, core * half, half, 1)
    ckv_acc = scatter_shard((kept + other_core(given).astype(f32)).reshape(SHARDS, 32, half))

    context_grad = right_contract(first_branch, w_out).astype(bf16).reshape(REP, MICRO, ROWS, QW)
    qkv_grad, curve_grad = self_backward(qkv, context_grad, seg_col, seg_row, curve)
    qkv_grad = qkv_grad.reshape(REP * own, QW + 2 * KW)
    out_acc = scatter_shard(left_contract(context, first_branch).reshape(SHARDS, 8, D))
    qkv_acc = scatter_shard(left_contract(normed, qkv_grad).reshape(SHARDS, 32, QW + 2 * KW))
    self_upstream = scatter_rep(right_contract(qkv_grad, w_qkv).reshape(REP, own, D))
    self_rho = norm_parts(own_float)
    token_part, self_acc = norm_backward(own_float, self_rho, self_factor, self_upstream)
    tokens_grad = hidden_grad + token_part

    table_part = lax.dot_general(
        hot.astype(f32), curve_grad[:OWN_HEADS], (((1,), (1,)), ((), ())), precision=lax.Precision.HIGHEST
    )
    table_part = lax.dynamic_update_slice(jnp.zeros((BUCKETS, HEADS), f32), table_part, (0, rep * OWN_HEADS))
    small_part = jnp.concatenate(
        [
            self_acc.reshape(SHARDS, 32),
            cross_acc.reshape(SHARDS, 32),
            feed_acc.reshape(SHARDS, 32),
            table_part,
            jnp.zeros((SHARDS, 16), f32),
        ],
        axis=1,
    )
    small_sent = lax.all_to_all(
        jnp.broadcast_to(small_part[:, None], (SHARDS, 8, 128)), "shard", 0, 0, tiled=True
    )
    small_sum = jnp.sum(small_sent, axis=0)
    small_sum = small_sum + other_chip(small_sum)
    small_sum = (small_sum + other_core(small_sum))[0]

    def all_columns(value):
        whole = gather_rep(value.astype(bf16)).astype(f32)
        return jnp.concatenate([whole[r] for r in range(REP)], axis=1)

    rows_back = jnp.concatenate([out_acc, cout_acc, down_acc], axis=0).astype(bf16)
    rows_back = gather_rep(lax.ppermute(rows_back, ("rep", "shard"), collect_rows)).astype(f32)
    out_grad = rows_back[:, 0:8].reshape(32, D)
    cout_grad = rows_back[:, 8:16].reshape(32, D)
    down_grad = rows_back[:, 16:40].reshape(96, D)[:88]
    qkv_all = gather_rep(qkv_acc.astype(bf16)).astype(f32)
    query_grad = jnp.concatenate([qkv_all[r, :, :QW] for r in range(REP)], axis=1)
    key_grad = jnp.concatenate([qkv_all[r, :, QW : QW + KW] for r in range(REP)], axis=1)
    value_grad = jnp.concatenate([qkv_all[r, :, QW + KW :] for r in range(REP)], axis=1)
    cq_all = all_columns(cq_acc)
    gate_all = all_columns(gate_acc)
    up_all = all_columns(up_acc)
    ckv_acc = ckv_acc + other_chip(ckv_acc.astype(bf16)).astype(f32)
    ckv_acc = ckv_acc.astype(bf16)
    ckv_all = in_order(core, ckv_acc, other_core(ckv_acc), 1).astype(f32)
    ckv_all = ckv_all.reshape(32, REP, 2, KW)
    ck_grad = ckv_all[:, :, 0].reshape(32, REP * KW)
    cv_grad = ckv_all[:, :, 1].reshape(32, REP * KW)

    return (
        layer_out.astype(bf16).reshape(tokens.shape),
        tokens_grad.reshape(tokens.shape),
        encoder_grad.reshape(encoded.shape),
        small_sum[0:32],
        query_grad,
        key_grad,
        value_grad,
        out_grad,
        small_sum[96:112].reshape(1, HEADS),
        small_sum[32:64],
        cq_all,
        ck_grad,
        cv_grad,
        cout_grad,
        small_sum[64:96],
        gate_all,
        up_all,
        down_grad,
    )


def solution(mesh):
    rows = P("shard", None)
    gain = P("shard")
    acts = P(None, "shard", "rep", None)
    encs = P(None, "shard", None, "rep", None)
    ids = P(None, "shard", None)
    weights = (gain, rows, rows, rows, rows, rows, gain, rows, rows, rows, rows, gain, rows, rows, rows)
    return jax.shard_map(
        local,
        mesh=mesh,
        in_specs=(acts, acts, encs, ids, ids, P()) + weights,
        out_specs=(acts, acts, encs) + weights,
        check_vma=False,
    )
```

```python
import jax
import jax.numpy as jnp
from jax import lax
from jax.experimental import pallas as pl
from jax.experimental.pallas import tpu as pltpu
from jax.sharding import PartitionSpec as P

D = 1024
HEADS = 16
HEAD_DIM = 64
KV_GROUPS = 8
FF = 2816
BUCKETS = 32
ENC = 512
SEQ = 256
DOCS = 4
MICRO = 2

REP = 4
SHARDS = 32
ROWS = SEQ // REP
OWN_HEADS = HEADS // REP
OWN_GROUPS = KV_GROUPS // REP
QW = OWN_HEADS * HEAD_DIM
KW = OWN_GROUPS * HEAD_DIM
OWN_FF = FF // REP
WINDOW = 144

epsilon = 1e-06
neg_big = -1e30
f32 = jnp.float32
bf16 = jnp.bfloat16
vmem_limit = 40 * 1024 * 1024


def matmul(left, right):
    return jnp.dot(left, right, preferred_element_type=f32)


def left_contract(left, right):
    return lax.dot_general(left, right, (((0,), (0,)), ((), ())), preferred_element_type=f32)


def right_contract(left, right):
    return lax.dot_general(left, right, (((1,), (1,)), ((), ())), preferred_element_type=f32)


def skewed(row):
    n = row.shape[1]
    out = jnp.broadcast_to(row, (n, n))
    at = lax.broadcasted_iota(jnp.int32, (n, n), 0)
    step = 1
    while step < n:
        out = jnp.where((at & step) != 0, pltpu.roll(out, step, 1), out)
        step *= 2
    return out


def unskewed_sum(square):
    n = square.shape[1]
    at = lax.broadcasted_iota(jnp.int32, (n, n), 0)
    step = 1
    while step < n:
        square = jnp.where((at & step) != 0, pltpu.roll(square, n - step, 1), square)
        step *= 2
    return jnp.sum(square, axis=0, keepdims=True)


def softmax_parts(scores):
    top = jnp.max(scores, axis=-1, keepdims=True)
    raised = jnp.exp(scores - top)
    return raised * (1.0 / jnp.sum(raised, axis=-1, keepdims=True))


def self_mask(seg_col, seg_row):
    at_query = lax.broadcasted_iota(jnp.int32, (SEQ, SEQ), 0)
    at_key = lax.broadcasted_iota(jnp.int32, (SEQ, SEQ), 1)
    return (at_key <= at_query) & (seg_col == seg_row)


def fill_bias(curve_ref, bias_ref):
    for head in range(OWN_HEADS):
        bias_ref[head] = skewed(curve_ref[head : head + 1, :])


def self_forward_kernel(qkv_ref, seg_col_ref, seg_row_ref, curve_ref, out_ref, bias_ref):
    @pl.when(pl.program_id(0) == 0)
    def _():
        fill_bias(curve_ref, bias_ref)

    whole = qkv_ref[...].reshape(SEQ, QW + 2 * KW)
    allowed = self_mask(seg_col_ref[0], seg_row_ref[0])
    mixed = []
    for head in range(OWN_HEADS):
        group = head * OWN_GROUPS // OWN_HEADS
        query = whole[:, head * HEAD_DIM : (head + 1) * HEAD_DIM]
        key = whole[:, QW + group * HEAD_DIM : QW + (group + 1) * HEAD_DIM]
        value = whole[:, QW + KW + group * HEAD_DIM : QW + KW + (group + 1) * HEAD_DIM]
        scores = jnp.where(allowed, right_contract(query, key) + bias_ref[head], neg_big)
        probs = softmax_parts(scores).astype(bf16)
        mixed.append(matmul(probs, value))
    out_ref[...] = jnp.concatenate(mixed, axis=1).astype(bf16).reshape(out_ref.shape)


def self_backward_kernel(
    qkv_ref, grad_ref, seg_col_ref, seg_row_ref, curve_ref, out_ref, curve_grad_ref, bias_ref, sum_ref
):
    @pl.when(pl.program_id(0) == 0)
    def _():
        fill_bias(curve_ref, bias_ref)
        sum_ref[...] = jnp.zeros_like(sum_ref)

    whole = qkv_ref[...].reshape(SEQ, QW + 2 * KW)
    grads = grad_ref[...].reshape(SEQ, QW)
    allowed = self_mask(seg_col_ref[0], seg_row_ref[0])
    query_grads = []
    key_grads = [None] * OWN_GROUPS
    value_grads = [None] * OWN_GROUPS
    for head in range(OWN_HEADS):
        group = head * OWN_GROUPS // OWN_HEADS
        query = whole[:, head * HEAD_DIM : (head + 1) * HEAD_DIM]
        key = whole[:, QW + group * HEAD_DIM : QW + (group + 1) * HEAD_DIM]
        value = whole[:, QW + KW + group * HEAD_DIM : QW + KW + (group + 1) * HEAD_DIM]
        grad = grads[:, head * HEAD_DIM : (head + 1) * HEAD_DIM]
        scores = jnp.where(allowed, right_contract(query, key) + bias_ref[head], neg_big)
        probs = softmax_parts(scores)
        prob_grad = right_contract(grad, value)
        centred = prob_grad - jnp.sum(probs * prob_grad, axis=-1, keepdims=True)
        score_grad = (probs * centred).astype(bf16)
        sum_ref[head] += score_grad.astype(f32)
        query_grads.append(matmul(score_grad, key))
        key_part = left_contract(score_grad, query)
        value_part = left_contract(probs.astype(bf16), grad)
        if key_grads[group] is None:
            key_grads[group] = key_part
            value_grads[group] = value_part
        else:
            key_grads[group] = key_grads[group] + key_part
            value_grads[group] = value_grads[group] + value_part
    joined = jnp.concatenate(query_grads + key_grads + value_grads, axis=1)
    out_ref[...] = joined.astype(bf16).reshape(out_ref.shape)

    @pl.when(pl.program_id(0) == MICRO - 1)
    def _():
        curve_grad_ref[...] = jnp.zeros_like(curve_grad_ref)
        for head in range(OWN_HEADS):
            curve_grad_ref[head : head + 1, :] = unskewed_sum(sum_ref[head])


def cross_forward_kernel(block_ref, start_ref, q_ref, kv_ref, seg_ref, out_ref, query_ref, mixed_ref):
    at = pl.program_id(0) * DOCS + pl.program_id(1)

    @pl.when(pl.program_id(1) == 0)
    def _():
        query_ref[...] = q_ref[...].reshape(SEQ, QW)

    start = pl.multiple_of(start_ref[at], 16)
    rows = query_ref[pl.ds(start, WINDOW), :]
    mine = seg_ref[0, pl.ds(start, WINDOW), :] == pl.program_id(1)
    both = kv_ref[...].reshape(ENC, 2 * KW)
    mixed = []
    for head in range(OWN_HEADS):
        group = head * OWN_GROUPS // OWN_HEADS
        query = rows[:, head * HEAD_DIM : (head + 1) * HEAD_DIM]
        key = both[:, group * HEAD_DIM : (group + 1) * HEAD_DIM]
        value = both[:, KW + group * HEAD_DIM : KW + (group + 1) * HEAD_DIM]
        probs = softmax_parts(right_contract(query, key)).astype(bf16)
        mixed.append(matmul(probs, value))
    fresh = jnp.concatenate(mixed, axis=1)
    mixed_ref[pl.ds(start, WINDOW), :] = jnp.where(mine, fresh, mixed_ref[pl.ds(start, WINDOW), :])

    @pl.when(pl.program_id(1) == DOCS - 1)
    def _():
        out_ref[...] = mixed_ref[...].astype(bf16).reshape(out_ref.shape)


def cross_backward_kernel(
    block_ref, start_ref, q_ref, kv_ref, grad_ref, seg_ref, out_ref, kv_grad_ref, query_ref, given_ref, mixed_ref
):
    at = pl.program_id(0) * DOCS + pl.program_id(1)

    @pl.when(pl.program_id(1) == 0)
    def _():
        query_ref[...] = q_ref[...].reshape(SEQ, QW)
        given_ref[...] = grad_ref[...].reshape(SEQ, QW)

    start = pl.multiple_of(start_ref[at], 16)
    rows = query_ref[pl.ds(start, WINDOW), :]
    grads = given_ref[pl.ds(start, WINDOW), :]
    mine = seg_ref[0, pl.ds(start, WINDOW), :] == pl.program_id(1)
    both = kv_ref[...].reshape(ENC, 2 * KW)
    query_grads = []
    key_grads = [None] * OWN_GROUPS
    value_grads = [None] * OWN_GROUPS
    for head in range(OWN_HEADS):
        group = head * OWN_GROUPS // OWN_HEADS
        query = rows[:, head * HEAD_DIM : (head + 1) * HEAD_DIM]
        key = both[:, group * HEAD_DIM : (group + 1) * HEAD_DIM]
        value = both[:, KW + group * HEAD_DIM : KW + (group + 1) * HEAD_DIM]
        grad = grads[:, head * HEAD_DIM : (head + 1) * HEAD_DIM]
        probs = jnp.where(mine, softmax_parts(right_contract(query, key)), 0.0)
        prob_grad = right_contract(grad, value)
        centred = prob_grad - jnp.sum(probs * prob_grad, axis=-1, keepdims=True)
        score_grad = (probs * centred).astype(bf16)
        query_grads.append(matmul(score_grad, key))
        key_part = left_contract(score_grad, query)
        value_part = left_contract(probs.astype(bf16), grad)
        if key_grads[group] is None:
            key_grads[group] = key_part
            value_grads[group] = value_part
        else:
            key_grads[group] = key_grads[group] + key_part
            value_grads[group] = value_grads[group] + value_part
    fresh = jnp.concatenate(query_grads, axis=1)
    mixed_ref[pl.ds(start, WINDOW), :] = jnp.where(mine, fresh, mixed_ref[pl.ds(start, WINDOW), :])
    joined = jnp.concatenate(key_grads + value_grads, axis=1)
    kv_grad_ref[...] = joined.astype(bf16).reshape(kv_grad_ref.shape)

    @pl.when(pl.program_id(1) == DOCS - 1)
    def _():
        out_ref[...] = mixed_ref[...].astype(bf16).reshape(out_ref.shape)


def rows_block(width):
    return pl.BlockSpec((REP, 1, ROWS, width), lambda m, *rest: (0, m, 0, 0))


def fixed_block(shape):
    return pl.BlockSpec(shape, lambda *at: (0,) * len(shape))


def micro_block(shape):
    return pl.BlockSpec((1,) + shape, lambda m, *rest: (m,) + (0,) * len(shape))


def estimate(flops, moved, raised):
    return pl.CostEstimate(flops=flops, bytes_accessed=moved, transcendentals=raised)


self_pairs = MICRO * OWN_HEADS * SEQ * SEQ
cross_pairs = MICRO * OWN_HEADS * DOCS * WINDOW * ENC


def self_forward(qkv, seg_col, seg_row, curve):
    return pl.pallas_call(
        self_forward_kernel,
        name="self_forward",
        grid=(MICRO,),
        in_specs=[
            rows_block(QW + 2 * KW),
            micro_block((SEQ, 1)),
            micro_block((1, SEQ)),
            fixed_block((8, SEQ)),
        ],
        out_specs=rows_block(QW),
        out_shape=jax.ShapeDtypeStruct((REP, MICRO, ROWS, QW), bf16),
        scratch_shapes=[pltpu.VMEM((OWN_HEADS, SEQ, SEQ), f32)],
        compiler_params=pltpu.CompilerParams(vmem_limit_bytes=vmem_limit),
        cost_estimate=estimate(self_pairs * 256, 2 << 20, self_pairs),
    )(qkv, seg_col, seg_row, curve)


def self_backward(qkv, grads, seg_col, seg_row, curve):
    return pl.pallas_call(
        self_backward_kernel,
        name="self_backward",
        grid=(MICRO,),
        in_specs=[
            rows_block(QW + 2 * KW),
            rows_block(QW),
            micro_block((SEQ, 1)),
            micro_block((1, SEQ)),
            fixed_block((8, SEQ)),
        ],
        out_specs=[rows_block(QW + 2 * KW), fixed_block((8, SEQ))],
        out_shape=[
            jax.ShapeDtypeStruct((REP, MICRO, ROWS, QW + 2 * KW), bf16),
            jax.ShapeDtypeStruct((8, SEQ), f32),
        ],
        scratch_shapes=[
            pltpu.VMEM((OWN_HEADS, SEQ, SEQ), f32),
            pltpu.VMEM((OWN_HEADS, SEQ, SEQ), f32),
        ],
        compiler_params=pltpu.CompilerParams(vmem_limit_bytes=vmem_limit),
        cost_estimate=estimate(self_pairs * 640, 3 << 20, self_pairs),
    )(qkv, grads, seg_col, seg_row, curve)


def cross_rows():
    return pl.BlockSpec((REP, 1, ROWS, QW), lambda m, d, block, start: (0, m, 0, 0))


def cross_keys():
    return pl.BlockSpec(
        (REP, 1, 1, ENC // REP, 2 * KW),
        lambda m, d, block, start: (0, m, block[m * DOCS + d], 0, 0),
    )


def cross_segs():
    return pl.BlockSpec((1, SEQ, 1), lambda m, d, block, start: (m, 0, 0))


def cross_forward(blocks, starts, queries, kv, seg_col):
    return pl.pallas_call(
        cross_forward_kernel,
        name="cross_forward",
        grid_spec=pltpu.PrefetchScalarGridSpec(
            num_scalar_prefetch=2,
            grid=(MICRO, DOCS),
            in_specs=[cross_rows(), cross_keys(), cross_segs()],
            out_specs=cross_rows(),
            scratch_shapes=[pltpu.VMEM((SEQ, QW), bf16), pltpu.VMEM((SEQ, QW), f32)],
        ),
        out_shape=jax.ShapeDtypeStruct((REP, MICRO, ROWS, QW), bf16),
        compiler_params=pltpu.CompilerParams(vmem_limit_bytes=vmem_limit),
        cost_estimate=estimate(cross_pairs * 256, 3 << 20, cross_pairs),
    )(blocks, starts, queries, kv, seg_col)


def cross_backward(blocks, starts, queries, kv, grads, seg_col):
    return pl.pallas_call(
        cross_backward_kernel,
        name="cross_backward",
        grid_spec=pltpu.PrefetchScalarGridSpec(
            num_scalar_prefetch=2,
            grid=(MICRO, DOCS),
            in_specs=[cross_rows(), cross_keys(), cross_rows(), cross_segs()],
            out_specs=[cross_rows(), cross_keys()],
            scratch_shapes=[
                pltpu.VMEM((SEQ, QW), bf16),
                pltpu.VMEM((SEQ, QW), bf16),
                pltpu.VMEM((SEQ, QW), f32),
            ],
        ),
        out_shape=[
            jax.ShapeDtypeStruct((REP, MICRO, ROWS, QW), bf16),
            jax.ShapeDtypeStruct((REP, MICRO, DOCS, ENC // REP, 2 * KW), bf16),
        ],
        compiler_params=pltpu.CompilerParams(vmem_limit_bytes=vmem_limit),
        cost_estimate=estimate(cross_pairs * 640, 6 << 20, cross_pairs),
    )(blocks, starts, queries, kv, grads, seg_col)


MESH = pl.DeviceIdType.MESH


def remote(source, target, send_sem, recv_sem, device):
    return pltpu.make_async_remote_copy(
        src_ref=source,
        dst_ref=target,
        send_sem=send_sem,
        recv_sem=recv_sem,
        device_id=device,
        device_id_type=MESH,
    )


class Ring:
    def __init__(self, group, half, me, device_at, send_sems, recv_sems):
        right, left = lax.rem(me + 1, 4), lax.rem(me + 3, 4)
        to_right, to_left = device_at(right), device_at(left)

        def copy(ref, device, i):
            return remote(ref, ref, send_sems.at[i], recv_sems.at[i], device)

        self.direct = [copy(group(me), to_right, 0), copy(group(me), to_left, 1)]
        self.passed = [copy(half(left, 0), to_right, 2), copy(half(right, 1), to_left, 3)]

    def start(self):
        for copy in self.direct:
            copy.start()

    def forward(self):
        for arrived, onward in zip(self.direct, self.passed):
            arrived.wait_recv()
            onward.start()

    def finish(self):
        for copy in self.passed:
            copy.wait_recv()

    def drain(self):
        for copy in self.direct + self.passed:
            copy.wait_send()


class Place:
    def __init__(self):
        self.at = at = lax.axis_index("shard")
        self.rep = rep = lax.axis_index("rep")
        self.x, self.y, self.z = lax.div(at, 8), lax.rem(lax.div(at, 2), 4), lax.rem(at, 2)
        self.chip, self.core = chip, core = lax.div(rep, 2), lax.rem(rep, 2)
        self.pair = {"shard": at + 1 - 2 * self.z}
        self.theirs = (1 - chip) * 2 + core
        self.far = {"rep": self.theirs}
        self.near = {"rep": chip * 2 + 1 - core}
        self.across = {"rep": (1 - chip) * 2 + 1 - core}

    def on_x(self, i):
        return {"shard": i * 8 + self.y * 2 + self.z}

    def on_y(self, i):
        return {"shard": self.x * 8 + i * 2 + self.z}

    def neighbours(self):
        return [self.on_x(lax.rem(self.x + d, 4)) for d in (1, 3)] + [
            self.on_y(lax.rem(self.y + d, 4)) for d in (1, 3)
        ]


GATHER_BLOCKS = (
    (32, QW + 2 * KW, True),
    (32, 2 * KW, True),
    (32, QW, True),
    (32, OWN_FF, True),
    (8, 128, True),
    (32, OWN_FF, False),
    (24, D, False),
    (8, D, False),
    (8, D, False),
)
GATHER_ROWS = ((MICRO * ROWS, 1), (MICRO * DOCS * ENC // REP, 4), (MICRO * ROWS, 1))
GATHER_CHUNKS = sum(parts for _, parts in GATHER_ROWS)


def gather_kernel(*refs):
    query, key, value, cross_key, cross_value, cross_query, gate, small, up, down, out, cross_out = refs[:12]
    n, n_rows = len(GATHER_BLOCKS), len(GATHER_ROWS)
    own_rows = refs[12 : 12 + n_rows]
    wholes = refs[12 + n_rows : 12 + n_rows + n]
    all_rows = refs[12 + n_rows + n : 12 + 2 * n_rows + n]
    local_sems, piece_send, piece_recv, pair_send, pair_recv, ring_send, ring_recv, rep_send, rep_recv = refs[
        12 + 2 * n_rows + n :
    ]
    place = Place()
    at, rep, x, y, z = place.at, place.rep, place.x, place.y, place.z
    barrier = pltpu.get_barrier_semaphore()
    devices = [place.pair, place.far, place.near] + place.neighbours()
    for device in devices:
        pl.semaphore_signal(barrier, inc=1, device_id=device, device_id_type=MESH)
    goal = 4 * lax.rem(at, 8) + rep
    stays = (x == rep) & (goal == at)
    source = {"rep": lax.rem(at, 4), "shard": 8 * rep + lax.div(at, 4)}

    @pl.when(jnp.logical_not(stays))
    def _():
        pl.semaphore_signal(barrier, inc=1, device_id=source, device_id_type=MESH)

    pl.semaphore_wait(barrier, len(devices) + 1 - stays.astype(jnp.int32))

    slots = [whole.at[x, y, z] for whole in wholes]
    count = [0]

    def own(source_ref, target):
        count[0] += 1
        return pltpu.make_async_copy(source_ref, target, local_sems.at[count[0] - 1])

    def part(ref, width):
        return ref.at[:, pl.ds(pl.multiple_of(rep * width, 128), width)]

    fills = [
        [
            own(part(query, QW), slots[0].at[:, pl.ds(0, QW)]),
            own(part(key, KW), slots[0].at[:, pl.ds(QW, KW)]),
            own(part(value, KW), slots[0].at[:, pl.ds(QW + KW, KW)]),
        ],
        [
            own(part(cross_key, KW), slots[1].at[:, pl.ds(0, KW)]),
            own(part(cross_value, KW), slots[1].at[:, pl.ds(KW, KW)]),
        ],
        [own(part(cross_query, QW), slots[2])],
        [own(gate, slots[3])],
        [own(small, slots[4])],
        [own(up, slots[5])],
    ]
    firsts = [pl.multiple_of(24 * rep - 8 * lax.div(rep, 3), 8)] + [pl.multiple_of(8 * rep, 8)] * 2
    pieces = []
    for i, ref in enumerate((down, out, cross_out)):
        rows = ref.at[pl.ds(firsts[i], GATHER_BLOCKS[6 + i][0])]
        landing = wholes[6 + i].at[lax.div(goal, 8), lax.rem(lax.div(goal, 2), 4), lax.rem(goal, 2)]
        sent = remote(rows, landing, piece_send.at[i], piece_recv.at[i], {"rep": x, "shard": goal})
        pieces.append((sent, own(rows, landing)))
    for sent, stay in pieces:
        pl.when(jnp.logical_not(stays))(sent.start)
        pl.when(stays)(stay.start)
    for fill in fills:
        for copy in fill:
            copy.start()

    rep_first, rep_second, rep_local = [], [], []
    for i, (rows, parts) in enumerate(GATHER_ROWS):
        mine = all_rows[i].at[rep]
        rep_local.append(own(own_rows[i], mine))
        rep_local[i].start()
        for p in range(parts):
            span = pl.ds(p * (rows // parts), rows // parts)
            j = len(rep_first)
            here, there = all_rows[i].at[rep, span], all_rows[i].at[place.theirs, span]
            rep_first.append(remote(own_rows[i].at[span], here, rep_send.at[j, 0], rep_recv.at[j, 0], place.far))
            direct = remote(own_rows[i].at[span], here, rep_send.at[j, 1], rep_recv.at[j, 1], place.near)
            onward = remote(there, there, rep_send.at[j, 2], rep_recv.at[j, 2], place.near)
            rep_second.append((direct, onward))

    pairs, small_rings, large_rings = [], [], []
    for i, (_, _, first_x) in enumerate(GATHER_BLOCKS):
        whole = wholes[i]
        pairs.append(remote(slots[i], slots[i], pair_send.at[i], pair_recv.at[i], place.pair))

        def x_small(j, whole=whole):
            return whole.at[j, y]

        def x_small_half(j, h, whole=whole):
            return whole.at[j, y, h]

        def y_small(j, whole=whole):
            return whole.at[x, j]

        def y_small_half(j, h, whole=whole):
            return whole.at[x, j, h]

        def x_large(j, whole=whole):
            return whole.at[j]

        def x_large_half(j, h, whole=whole):
            return whole.at[j, pl.ds(2 * h, 2)]

        def y_large(j, whole=whole):
            return whole.at[:, j]

        def y_large_half(j, h, whole=whole):
            return whole.at[pl.ds(2 * h, 2), j]

        near_sems = ring_send.at[i, 0], ring_recv.at[i, 0]
        wide_sems = ring_send.at[i, 1], ring_recv.at[i, 1]
        if first_x:
            small_rings.append(Ring(x_small, x_small_half, x, place.on_x, *near_sems))
            large_rings.append(Ring(y_large, y_large_half, y, place.on_y, *wide_sems))
        else:
            small_rings.append(Ring(y_small, y_small_half, y, place.on_y, *near_sems))
            large_rings.append(Ring(x_large, x_large_half, x, place.on_x, *wide_sems))
    for i in range(n):
        if i < 6:
            for copy in fills[i]:
                copy.wait()
        else:
            sent, stay = pieces[i - 6]
            pl.when(jnp.logical_not(stays))(sent.wait_recv)
            pl.when(stays)(stay.wait)
        pairs[i].start()
    for first, (direct, _) in zip(rep_first, rep_second):
        first.start()
        direct.start()
    for i in range(n):
        pairs[i].wait_recv()
        small_rings[i].start()
    for i in range(n):
        small_rings[i].forward()
    for i in range(n):
        small_rings[i].finish()
        large_rings[i].start()
    passed = 0

    def pass_on(upto):
        nonlocal passed
        while passed < upto:
            rep_first[passed].wait_recv()
            rep_second[passed][1].start()
            passed += 1

    pass_on(3)
    for i in range(n):
        large_rings[i].forward()
    for i in range(n):
        large_rings[i].finish()
    pass_on(GATHER_CHUNKS)
    for sent, _ in pieces:
        pl.when(jnp.logical_not(stays))(sent.wait_send)
    for i in range(n):
        pairs[i].wait_send()
        small_rings[i].drain()
        large_rings[i].drain()
    for copy in rep_local:
        copy.wait()
    for j in range(GATHER_CHUNKS):
        rep_first[j].wait_send()
        for copy in rep_second[j]:
            copy.wait()


def gather_weights(weights, rows):
    n = len(GATHER_BLOCKS)
    shapes = [jax.ShapeDtypeStruct((4, 4, 2, r, c), bf16) for r, c, _ in GATHER_BLOCKS]
    shapes += [jax.ShapeDtypeStruct((REP,) + value.shape, value.dtype) for value in rows]
    anywhere = pl.BlockSpec(memory_space=pl.ANY)
    dma = pltpu.SemaphoreType.DMA
    results = pl.pallas_call(
        gather_kernel,
        name="gather_weights",
        in_specs=[anywhere] * (len(weights) + len(rows)),
        out_specs=[anywhere] * len(shapes),
        out_shape=shapes,
        scratch_shapes=[
            dma((9 + 3 + len(rows),)),
            dma((3,)),
            dma((3,)),
            dma((n,)),
            dma((n,)),
            dma((n, 2, 4)),
            dma((n, 2, 4)),
            dma((GATHER_CHUNKS, 3)),
            dma((GATHER_CHUNKS, 3)),
        ],
        compiler_params=pltpu.CompilerParams(collective_id=0, has_side_effects=True),
        cost_estimate=estimate(0, 64 << 20, 0),
    )(*weights, *rows)
    return results[:n], results[n:]


class ReduceRing:
    def __init__(self, half, whole_half, me, device_at, first, second, send_sems, recv_sems):
        right, left, far = lax.rem(me + 1, 4), lax.rem(me + 3, 4), lax.rem(me + 2, 4)
        to_right, to_left = device_at(right), device_at(left)

        def copy(source, target, device, i):
            return remote(source, target, send_sems.at[i], recv_sems.at[i], device)

        self.half, self.me, self.right, self.left = half, me, right, left
        self.first, self.second = first, second
        self.opening = [
            copy(whole_half(far, 0), first.at[0], to_right, 0),
            copy(whole_half(far, 1), first.at[1], to_left, 1),
        ]
        self.plain = [
            copy(whole_half(right, 1), second.at[0, 1], to_right, 2),
            copy(whole_half(left, 0), second.at[1, 0], to_left, 3),
        ]
        self.summed = [
            copy(first.at[0], second.at[0, 0], to_right, 4),
            copy(first.at[1], second.at[1, 1], to_left, 5),
        ]

    def start(self):
        for copy in self.opening + self.plain:
            copy.start()

    def middle(self, each):
        for h, group in enumerate((self.right, self.left)):
            self.opening[h].wait_recv()

            def add(*k, h=h, group=group):
                mixed = self.first[(h, *k)].astype(f32) + self.half(group, h, *k).astype(f32)
                self.first[(h, *k)] = mixed.astype(self.first.dtype)

            each(add)
            self.summed[h].start()

    def finish(self, each, store):
        for h in range(2):
            (self.plain[1] if h == 0 else self.plain[0]).wait_recv()
            self.summed[h].wait_recv()

            def add(*k, h=h):
                mixed = self.second[(0, h, *k)].astype(f32) + self.second[(1, h, *k)].astype(f32)
                store(h, *k, mixed + self.half(self.me, h, *k).astype(f32))

            each(add)

    def drain(self):
        for copy in self.opening + self.plain + self.summed:
            copy.wait_send()


def each_of_four(body):
    def step(i, carry):
        body(lax.div(i, 2), lax.rem(i, 2))
        return carry

    lax.fori_loop(0, 4, step, 0)


def just_once(body):
    body()


REDUCE_BLOCKS = (
    (32, QW + 2 * KW, True, bf16),
    (32, 2 * KW, True, bf16),
    (32, QW, True, bf16),
    (32, OWN_FF, True, bf16),
    (32, OWN_FF, False, bf16),
    (24, D, False, bf16),
    (8, D, False, bf16),
    (8, D, False, bf16),
    (8, 128, True, f32),
)
COLUMN_BLOCKS = (0, 1, 2, 3, 4)
PIECE_BLOCKS = (5, 6, 7)
SMALL_BLOCK = 8
REDUCE_SCRATCH = 8


def reduce_kernel(*refs):
    n = len(REDUCE_BLOCKS)
    own = MICRO * ROWS
    grads, refs = refs[:n], refs[n:]
    kv_grad, w_ckv, layer_part, hidden, *refs = refs
    alls, refs = refs[: len(COLUMN_BLOCKS)], refs[len(COLUMN_BLOCKS) :]
    gathered, refs = refs[: len(PIECE_BLOCKS)], refs[len(PIECE_BLOCKS) :]
    small_out, kv_all, w_all, layer_out, *refs = refs
    scratch = [refs[REDUCE_SCRATCH * i : REDUCE_SCRATCH * (i + 1)] for i in range(n)]
    refs = refs[REDUCE_SCRATCH * n :]
    (small_far, small_near, core_recv, far_send, far_recv, near_sum) = refs[:6]
    (ring_send, ring_recv, pair_send, pair_recv, rep_send, rep_recv, piece_send, piece_recv, more_send, more_recv,
     local_sems) = refs[6:]
    place = Place()
    at, rep, x, y, z, theirs = place.at, place.rep, place.x, place.y, place.z, place.theirs
    barrier = pltpu.get_barrier_semaphore()
    devices = [place.pair, place.far, place.near, place.across] + place.neighbours()
    for device in devices:
        pl.semaphore_signal(barrier, inc=1, device_id=device, device_id_type=MESH)
    owner = 8 * rep + lax.div(at, 4)
    slot = lax.rem(at, 4)
    stays = owner == at

    def from_self(q):
        return (x == rep) & (4 * lax.rem(at, 8) + q == at)

    for q in range(REP):
        giver = {"rep": x, "shard": 4 * lax.rem(at, 8) + q}

        @pl.when(jnp.logical_not(from_self(q)))
        def _(giver=giver):
            pl.semaphore_signal(barrier, inc=1, device_id=giver, device_id_type=MESH)

    pl.semaphore_wait(barrier, len(devices) + REP - stays.astype(jnp.int32))

    large, small = [], []
    for i, (_, _, on_y, dtype) in enumerate(REDUCE_BLOCKS):
        grad = grads[i]
        first, second, mid, first_small, second_small, low, arrived, result = scratch[i]
        if on_y:

            def half(j, h, a, b, grad=grad):
                return grad[2 * h + a, j, b]

            def whole_half(j, h, grad=grad):
                return grad.at[pl.ds(2 * h, 2), j]
        else:

            def half(j, h, a, b, grad=grad):
                return grad[j, 2 * h + a, b]

            def whole_half(j, h, grad=grad):
                return grad.at[j, pl.ds(2 * h, 2)]

        def half_small(j, h, mid=mid):
            return mid[j, h]

        def whole_half_small(j, h, mid=mid):
            return mid.at[j, h]

        wide = (y, place.on_y) if on_y else (x, place.on_x)
        narrow = (x, place.on_x) if on_y else (y, place.on_y)
        large.append(ReduceRing(half, whole_half, *wide, first, second, ring_send.at[i, 0], ring_recv.at[i, 0]))
        small.append(
            ReduceRing(
                half_small, whole_half_small, *narrow, first_small, second_small, ring_send.at[i, 1], ring_recv.at[i, 1]
            )
        )
    for ring in large:
        ring.start()

    to_core = [
        remote(
            layer_part.at[there * 2 + 1 - place.core], core_recv.at[i], more_send.at[i], more_recv.at[i], place.near
        )
        for i, there in enumerate((1 - place.chip, place.chip))
    ]
    for copy in to_core:
        copy.start()

    def lanes(r):
        return pl.ds(pl.multiple_of(r * 2 * KW, 128), 2 * KW)

    locals_ = [
        pltpu.make_async_copy(kv_grad.at[rep], kv_all.at[:, lanes(rep)], local_sems.at[0]),
        pltpu.make_async_copy(w_ckv, w_all.at[:, lanes(rep)], local_sems.at[1]),
    ]
    for copy in locals_:
        copy.start()

    to_core[0].wait_recv()
    far_send[...] = (layer_part[theirs].astype(f32) + core_recv[0].astype(f32)).astype(bf16)
    to_far = remote(far_send, far_recv, more_send.at[2], more_recv.at[2], place.far)
    to_far.start()
    exchanged = [
        remote(w_ckv, w_all.at[:, lanes(rep)], more_send.at[3], more_recv.at[3], place.far),
        remote(w_ckv, w_all.at[:, lanes(rep)], more_send.at[4], more_recv.at[4], place.near),
    ]
    passed_on = remote(
        w_all.at[:, lanes(theirs)], w_all.at[:, lanes(theirs)], more_send.at[5], more_recv.at[5], place.near
    )
    for i, there in enumerate((place.far, place.across, place.near)):
        exchanged.append(
            remote(
                kv_grad.at[there["rep"]], kv_all.at[:, lanes(rep)], more_send.at[6 + i], more_recv.at[6 + i], there
            )
        )
    for copy in exchanged:
        copy.start()
    to_core[1].wait_recv()
    near_sum[...] = hidden[...] + layer_part[rep].astype(f32) + core_recv[1].astype(f32)

    for ring in large:
        ring.middle(each_of_four)
    for i, ring in enumerate(large):
        mid = scratch[i][2]

        def store(h, a, b, total, mid=mid):
            mid[2 * h + a, b] = total.astype(mid.dtype)

        ring.finish(each_of_four, store)
        small[i].start()
    exchanged[0].wait_recv()
    passed_on.start()
    to_far.wait_recv()
    layer_out[...] = (near_sum[...] + far_recv[...].astype(f32)).astype(bf16)
    for ring in small:
        ring.middle(just_once)
    pairs = []
    for i, ring in enumerate(small):
        low = scratch[i][5]

        def store(h, total, low=low):
            low[h] = total.astype(low.dtype)

        ring.finish(just_once, store)
        pairs.append(remote(low.at[1 - z], scratch[i][6], pair_send.at[i], pair_recv.at[i], place.pair))
        pairs[i].start()
    spread, onward, given = [], [], []
    for i in range(n):
        low, arrived, result = scratch[i][5:8]
        pairs[i].wait_recv()
        total = (low[z].astype(f32) + arrived[...].astype(f32)).astype(low.dtype)
        if i in COLUMN_BLOCKS:
            j = COLUMN_BLOCKS.index(i)
            alls[j][rep] = total
            mine, other = alls[j].at[rep], alls[j].at[theirs]
            spread.append(
                [
                    remote(mine, mine, rep_send.at[j, 0], rep_recv.at[j, 0], place.far),
                    remote(mine, mine, rep_send.at[j, 1], rep_recv.at[j, 1], place.near),
                ]
            )
            onward.append(remote(other, other, rep_send.at[j, 2], rep_recv.at[j, 2], place.near))
            for copy in spread[j]:
                copy.start()
        elif i in PIECE_BLOCKS:
            j = PIECE_BLOCKS.index(i)
            result[...] = total
            for k in range(REP):
                copy = remote(
                    result,
                    gathered[j].at[slot],
                    piece_send.at[j, k],
                    piece_recv.at[j, slot],
                    {"rep": jnp.int32(k), "shard": owner},
                )
                own_piece = stays & (rep == k)
                given.append((own_piece, copy))
                pl.when(jnp.logical_not(own_piece))(copy.start)

            @pl.when(stays)
            def _(j=j, total=total):
                gathered[j][slot] = total
        else:
            result[...] = total
    result = scratch[SMALL_BLOCK][7]
    small_first = remote(result, small_far, more_send.at[9], more_recv.at[9], place.far)
    small_first.start()
    for j in range(len(onward)):
        spread[j][0].wait_recv()
        onward[j].start()
    small_first.wait()
    result[...] = result[...] + small_far[...]
    small_second = remote(result, small_near, more_send.at[10], more_recv.at[10], place.near)
    small_second.start()
    small_second.wait()
    small_out[...] = result[...] + small_near[...]
    for j in range(len(onward)):
        spread[j][1].wait_recv()
        onward[j].wait_recv()
    for j in range(len(PIECE_BLOCKS)):
        for q in range(REP):
            landed = gathered[j].at[q]
            arrival = remote(
                landed, landed, piece_send.at[j, q], piece_recv.at[j, q], {"rep": x, "shard": 4 * lax.rem(at, 8) + q}
            )
            pl.when(jnp.logical_not(from_self(q)))(arrival.wait_recv)
    for copy in exchanged[1:]:
        copy.wait_recv()
    passed_on.wait_recv()
    for copy in locals_:
        copy.wait()
    for ring in large + small:
        ring.drain()
    for own_piece, copy in given:
        pl.when(jnp.logical_not(own_piece))(copy.wait_send)
    for copy in to_core + [to_far, passed_on] + exchanged + pairs + onward + [one for two in spread for one in two]:
        copy.wait_send()


def reduce_grads(grads, kv_grad, w_ckv, layer_part, hidden):
    n = len(REDUCE_BLOCKS)
    own = MICRO * ROWS
    enc_rows = kv_grad.shape[1]
    shapes = [jax.ShapeDtypeStruct((REP,) + REDUCE_BLOCKS[i][:2], bf16) for i in COLUMN_BLOCKS + PIECE_BLOCKS]
    shapes += [
        jax.ShapeDtypeStruct((8, 128), f32),
        jax.ShapeDtypeStruct((enc_rows, REP * 2 * KW), bf16),
        jax.ShapeDtypeStruct((D, REP * 2 * KW), bf16),
        jax.ShapeDtypeStruct((own, D), bf16),
    ]
    anywhere = pl.BlockSpec(memory_space=pl.ANY)
    here = pl.BlockSpec(memory_space=pltpu.VMEM)
    dma = pltpu.SemaphoreType.DMA
    scratch = []
    for rows, width, _, dtype in REDUCE_BLOCKS:
        for lead in ((2, 2, 2), (2, 2, 2, 2), (4, 2), (2,), (2, 2), (2,), (), ()):
            scratch.append(pltpu.VMEM(lead + (rows, width), dtype))
    scratch += [
        pltpu.VMEM((8, 128), f32),
        pltpu.VMEM((8, 128), f32),
        pltpu.VMEM((2, own, D), bf16),
        pltpu.VMEM((own, D), bf16),
        pltpu.VMEM((own, D), bf16),
        pltpu.VMEM((own, D), f32),
    ]
    scratch += [dma((n, 2, 6)), dma((n, 2, 6)), dma((n,)), dma((n,)), dma((5, 3)), dma((5, 3))]
    scratch += [dma((3, REP)), dma((3, REP)), dma((11,)), dma((11,)), dma((2,))]
    results = pl.pallas_call(
        reduce_kernel,
        name="reduce_grads",
        in_specs=[here] * n + [anywhere, anywhere, here, here],
        out_specs=[here] * (len(COLUMN_BLOCKS) + len(PIECE_BLOCKS) + 1) + [anywhere, anywhere, here],
        out_shape=shapes,
        scratch_shapes=scratch,
        compiler_params=pltpu.CompilerParams(
            collective_id=6, has_side_effects=True, vmem_limit_bytes=vmem_limit
        ),
        cost_estimate=estimate(0, 128 << 20, 0),
    )(*grads, kv_grad, w_ckv, layer_part, hidden)
    return results


def norm_parts(values):
    return lax.rsqrt(jnp.mean(values * values, axis=-1, keepdims=True) + epsilon)


def boundary_kernel(n_pairs, turned, forward, gathers, *refs):
    pairs = [(refs[2 * i], refs[2 * i + 1]) for i in range(n_pairs)]
    rest = refs[2 * n_pairs :]
    if forward:
        hidden_ref, gain_ref, out_ref, *rest = rest
    else:
        values_ref, hidden_ref, gain_ref, out_ref, acc_ref, *rest = rest
    if gathers:
        all_ref, *rest = rest
    core_send, core_recv, far_send, far_recv, near_sum, send_sems, recv_sems = rest
    rep = lax.axis_index("rep")
    chip, core = lax.div(rep, 2), lax.rem(rep, 2)
    theirs = (1 - chip) * 2 + core
    far = {"rep": theirs}
    near = {"rep": chip * 2 + 1 - core}
    barrier = pltpu.get_barrier_semaphore()
    for device in (far, near):
        pl.semaphore_signal(barrier, inc=1, device_id=device, device_id_type=MESH)

    def partial(r):
        product = right_contract if turned else matmul
        total = product(pairs[0][0][r], pairs[0][1][...])
        for left, right in pairs[1:]:
            total = total + product(left[r], right[...])
        return total

    def copy(source, target, i, device):
        return remote(source, target, send_sems.at[i], recv_sems.at[i], device)

    half = ROWS
    chunks = [pl.ds(c * half, half) for c in range(MICRO)]
    to_core = []
    for i, there in enumerate((1 - chip, chip)):
        core_send[i] = partial(there * 2 + 1 - core).astype(bf16)
        to_core.append(copy(core_send.at[i], core_recv.at[i], i, near))
        if i == 0:
            pl.semaphore_wait(barrier, 2)
        to_core[i].start()
    far_own = partial(theirs)
    to_core[0].wait_recv()
    far_send[...] = (far_own + core_recv[0].astype(f32)).astype(bf16)
    to_far = [copy(far_send.at[rows], far_recv.at[rows], 2 + c, far) for c, rows in enumerate(chunks)]
    for sent in to_far:
        sent.start()
    near_own = partial(rep)
    to_core[1].wait_recv()
    near_sum[...] = near_own + core_recv[1].astype(f32)
    spread, onward = [], []
    acc = None
    for c, rows in enumerate(chunks):
        to_far[c].wait_recv()
        total = near_sum[rows, :] + far_recv[rows, :].astype(f32)
        gain = gain_ref[...]
        if forward:
            fresh = hidden_ref[rows, :].astype(f32) + total
            sent = (fresh * norm_parts(fresh) * gain).astype(bf16)
        else:
            values = values_ref[rows, :].astype(f32)
            rho = norm_parts(values)
            scaled = gain * total
            inner = jnp.mean(values * scaled, axis=-1, keepdims=True)
            fresh = hidden_ref[rows, :].astype(f32) + rho * scaled - values * (rho * rho * rho * inner)
            part = jnp.sum(values * rho * total, axis=0, keepdims=True)
            acc = part if acc is None else acc + part
            sent = fresh.astype(bf16)
        out_ref[rows, :] = fresh
        if gathers:
            all_ref[rep, rows, :] = sent
            mine = all_ref.at[rep, rows]
            other = all_ref.at[theirs, rows]
            spread.append((copy(mine, mine, 4 + c, far), copy(mine, mine, 6 + c, near)))
            onward.append(copy(other, other, 8 + c, near))
            for one in spread[c]:
                one.start()
    if not forward:
        acc_ref[...] = acc
    for c in range(len(onward)):
        spread[c][0].wait_recv()
        onward[c].start()
    for c in range(len(onward)):
        spread[c][1].wait_recv()
        onward[c].wait_recv()
    for sent in to_core + to_far + [one for two in spread for one in two] + onward:
        sent.wait_send()


def boundary(name, identity, pairs, turned, hidden, gain, values=None, gathers=True):
    own = MICRO * ROWS
    forward = values is None
    operands = [a.reshape(REP, own, -1) if i == 0 else a for pair in pairs for i, a in enumerate(pair)]
    operands += ([] if forward else [values]) + [hidden, gain.reshape(1, D)]
    shapes = [jax.ShapeDtypeStruct((own, D), f32)]
    if not forward:
        shapes.append(jax.ShapeDtypeStruct((1, D), f32))
    if gathers:
        shapes.append(jax.ShapeDtypeStruct((REP, own, D), bf16))
    here = pl.BlockSpec(memory_space=pltpu.VMEM)
    dma = pltpu.SemaphoreType.DMA
    return pl.pallas_call(
        lambda *refs: boundary_kernel(len(pairs), turned, forward, gathers, *refs),
        name=name,
        in_specs=[here] * len(operands),
        out_specs=[here] * len(shapes),
        out_shape=shapes,
        scratch_shapes=[
            pltpu.VMEM((2, own, D), bf16),
            pltpu.VMEM((2, own, D), bf16),
            pltpu.VMEM((own, D), bf16),
            pltpu.VMEM((own, D), bf16),
            pltpu.VMEM((own, D), f32),
            dma((10,)),
            dma((10,)),
        ],
        compiler_params=pltpu.CompilerParams(
            collective_id=identity, has_side_effects=True, vmem_limit_bytes=vmem_limit
        ),
        cost_estimate=estimate(1 << 30, 32 << 20, 0),
    )(*operands)


def local(
    tokens,
    out_cotangent,
    encoded,
    segment_ids,
    doc_block,
    bucket_table,
    self_gain,
    query_weight,
    key_weight,
    value_weight,
    out_weight,
    bias_table,
    cross_gain,
    cross_query,
    cross_key,
    cross_value,
    cross_out,
    feed_gain,
    gate_weight,
    up_weight,
    down_weight,
):
    rep = lax.axis_index("rep")
    own = MICRO * ROWS
    enc_rows = MICRO * DOCS * ENC // REP

    def columns(weight, width):
        return lax.dynamic_slice_in_dim(weight, rep * width, width, 1)

    small = jnp.concatenate([self_gain, cross_gain, feed_gain, bias_table[0], jnp.zeros((16,), bf16)])
    small = jnp.broadcast_to(small[None], (8, 128))
    own_tokens = tokens.reshape(own, D)
    own_cotangent = out_cotangent.reshape(own, D)
    wholes, (all_tokens, all_enc, all_grad) = gather_weights(
        [
            query_weight,
            key_weight,
            value_weight,
            cross_key,
            cross_value,
            cross_query,
            columns(gate_weight, OWN_FF),
            small,
            columns(up_weight, OWN_FF),
            down_weight,
            out_weight,
            cross_out,
        ],
        [own_tokens, encoded.reshape(enc_rows, D), own_cotangent],
    )
    w_qkv, w_ckv, w_cq, w_gate, small, w_up, w_down, w_out, w_cout = wholes
    w_qkv = w_qkv.reshape(D, QW + 2 * KW)
    small = small.reshape(SHARDS, 8, 128)[:, 0]
    w_out = w_out.reshape(QW, D)
    w_ckv = w_ckv.reshape(D, 2 * KW)
    w_cq = w_cq.reshape(D, QW)
    w_cout = w_cout.reshape(QW, D)
    w_gate = w_gate.reshape(D, OWN_FF)
    w_up = w_up.reshape(D, OWN_FF)
    w_down = w_down.reshape(8, 96, D)
    w_down = jnp.concatenate([w_down[:, :72], w_down[:, 80:]], axis=1).reshape(OWN_FF, D)
    self_factor = small[:, 0:32].reshape(D).astype(f32)
    cross_factor = small[:, 32:64].reshape(D).astype(f32)
    feed_factor = small[:, 64:96].reshape(D).astype(f32)
    table = small[:, 96:112]

    segments = segment_ids[:, 0]
    seg_col = segments[:, :, None]
    seg_row = segments[:, None, :]
    blocks = doc_block[:, 0].reshape(-1)
    doc_ids = jnp.arange(DOCS, dtype=jnp.int32)
    starts = jnp.sum((segments[:, None, :] < doc_ids[None, :, None]).astype(jnp.int32), axis=2)
    starts = jnp.minimum(starts // 16 * 16, SEQ - WINDOW).reshape(-1)
    turned = jnp.roll(bucket_table[::-1], 1)
    hot = (turned[None, :] == jnp.arange(BUCKETS, dtype=jnp.int32)[:, None]).astype(bf16)
    own_table = lax.dynamic_slice_in_dim(table, rep * OWN_HEADS, OWN_HEADS, 1)
    curve = left_contract(own_table, hot)
    curve = jnp.pad(curve, ((0, 4), (0, 0)))

    all_tokens = all_tokens.reshape(REP * own, D).astype(f32)
    all_enc = all_enc.reshape(REP * enc_rows, D)
    all_grad = all_grad.reshape(REP * own, D)

    normed = (all_tokens * norm_parts(all_tokens) * self_factor).astype(bf16)
    qkv = matmul(normed, w_qkv).astype(bf16).reshape(REP, MICRO, ROWS, QW + 2 * KW)
    kv = matmul(all_enc, w_ckv).astype(bf16).reshape(REP, MICRO, DOCS, ENC // REP, 2 * KW)
    context = self_forward(qkv, seg_col, seg_row, curve).reshape(REP * own, QW)
    hidden, cross_normed = boundary("after_self", 1, [(context, w_out)], False, own_tokens, cross_factor)
    cross_normed = cross_normed.reshape(REP * own, D)
    cross_queries = matmul(cross_normed, w_cq).astype(bf16).reshape(REP, MICRO, ROWS, QW)
    cross_context = cross_forward(blocks, starts, cross_queries, kv, seg_col).reshape(REP * own, QW)
    hidden_two, feed_normed = boundary("after_cross", 2, [(cross_context, w_cout)], False, hidden, feed_factor)
    feed_normed = feed_normed.reshape(REP * own, D)
    gate = matmul(feed_normed, w_gate)
    up_part = matmul(feed_normed, w_up)
    inner_grad = right_contract(all_grad, w_down)

    def gated(gate, up_part):
        return jax.nn.gelu(gate, approximate=True) * up_part

    inner, gated_back = jax.vjp(gated, gate, up_part)
    inner = inner.astype(bf16)
    gate_low, up_low = (grad.astype(bf16) for grad in gated_back(inner_grad))

    hidden_grad, feed_acc, branch = boundary(
        "before_feed", 3, [(gate_low, w_gate), (up_low, w_up)], True, own_cotangent, feed_factor, hidden_two
    )
    branch = branch.reshape(REP * own, D)
    layer_part = matmul(inner, w_down).astype(bf16).reshape(REP, own, D)
    gate_part = left_contract(feed_normed, gate_low)
    up_part = left_contract(feed_normed, up_low)
    down_part = left_contract(inner, all_grad).astype(bf16).reshape(8, 88, D)
    down_part = jnp.concatenate([down_part[:, :72], down_part[:, 64:]], axis=1)

    context_grad = right_contract(branch, w_cout).astype(bf16).reshape(REP, MICRO, ROWS, QW)
    cq_grad, kv_grad = cross_backward(blocks, starts, cross_queries, kv, context_grad, seg_col)
    cq_grad = cq_grad.reshape(REP * own, QW)
    hidden_grad, cross_acc, first_branch = boundary(
        "before_cross", 4, [(cq_grad, w_cq)], True, hidden_grad, cross_factor, hidden
    )
    first_branch = first_branch.reshape(REP * own, D)
    cout_part = left_contract(cross_context, branch)
    cq_part = left_contract(cross_normed, cq_grad)
    kv_grad = kv_grad.reshape(REP, enc_rows, 2 * KW)
    ckv_part = left_contract(all_enc, kv_grad.reshape(REP * enc_rows, 2 * KW))

    context_grad = right_contract(first_branch, w_out).astype(bf16).reshape(REP, MICRO, ROWS, QW)
    qkv_grad, curve_grad = self_backward(qkv, context_grad, seg_col, seg_row, curve)
    qkv_grad = qkv_grad.reshape(REP * own, QW + 2 * KW)
    out_part = left_contract(context, first_branch)
    qkv_part = left_contract(normed, qkv_grad)
    tokens_grad, self_acc = boundary(
        "before_self", 5, [(qkv_grad, w_qkv)], True, hidden_grad, self_factor, own_tokens, False
    )

    table_part = lax.dot_general(
        hot.astype(f32), curve_grad[:OWN_HEADS], (((1,), (1,)), ((), ())), precision=lax.Precision.HIGHEST
    )
    table_part = lax.dynamic_update_slice(jnp.zeros((BUCKETS, HEADS), f32), table_part, (0, rep * OWN_HEADS))
    small_part = jnp.concatenate(
        [
            self_acc.reshape(SHARDS, 32),
            cross_acc.reshape(SHARDS, 32),
            feed_acc.reshape(SHARDS, 32),
            table_part,
            jnp.zeros((SHARDS, 16), f32),
        ],
        axis=1,
    )
    small_part = jnp.broadcast_to(small_part[:, None], (SHARDS, 8, 128))

    parts = [qkv_part, ckv_part, cq_part, gate_part, up_part, down_part, out_part, cout_part, small_part]
    parts = [
        part.astype(dtype).reshape(4, 4, 2, rows, width)
        for part, (rows, width, _, dtype) in zip(parts, REDUCE_BLOCKS)
    ]
    *whole, small_sum, kv_all, w_all, layer_out = reduce_grads(parts, kv_grad, w_ckv, layer_part, hidden_two)
    qkv_all, ckv_all, cq_all, gate_all, up_all, down_all, out_all, cout_all = [part.astype(f32) for part in whole]
    encoder_grad = right_contract(kv_all, w_all)
    small_sum = small_sum[0]

    def joined(value, first, width):
        return jnp.concatenate([value[r, :, first : first + width] for r in range(REP)], axis=1)

    return (
        layer_out.reshape(tokens.shape),
        tokens_grad.reshape(tokens.shape),
        encoder_grad.reshape(encoded.shape),
        small_sum[0:32],
        joined(qkv_all, 0, QW),
        joined(qkv_all, QW, KW),
        joined(qkv_all, QW + KW, KW),
        out_all.reshape(32, D),
        small_sum[96:112].reshape(1, HEADS),
        small_sum[32:64],
        joined(cq_all, 0, QW),
        joined(ckv_all, 0, KW),
        joined(ckv_all, KW, KW),
        cout_all.reshape(32, D),
        small_sum[64:96],
        joined(gate_all, 0, OWN_FF),
        joined(up_all, 0, OWN_FF),
        jnp.concatenate([down_all[:3].reshape(72, D), down_all[3, 8:]], axis=0),
    )


def solution(mesh):
    rows = P("shard", None)
    gain = P("shard")
    acts = P(None, "shard", "rep", None)
    encs = P(None, "shard", None, "rep", None)
    ids = P(None, "shard", None)
    weights = (gain, rows, rows, rows, rows, rows, gain, rows, rows, rows, rows, gain, rows, rows, rows)
    return jax.shard_map(
        local,
        mesh=mesh,
        in_specs=(acts, acts, encs, ids, ids, P()) + weights,
        out_specs=(acts, acts, encs) + weights,
        check_vma=False,
    )
```

```python
import jax
import jax.numpy as jnp
from jax import lax
from jax.experimental import pallas as pl
from jax.experimental.pallas import tpu as pltpu
from jax.sharding import PartitionSpec as P

D = 1024
HEADS = 16
HEAD_DIM = 64
KV_GROUPS = 8
FF = 2816
BUCKETS = 32
ENC = 512
SEQ = 256
DOCS = 4
MICRO = 2

REP = 4
SHARDS = 32
ROWS = SEQ // REP
OWN_HEADS = HEADS // REP
OWN_GROUPS = KV_GROUPS // REP
QW = OWN_HEADS * HEAD_DIM
KW = OWN_GROUPS * HEAD_DIM
OWN_FF = FF // REP
WINDOW = 144
NARROW = 80

epsilon = 1e-06
neg_big = -1e30
f32 = jnp.float32
bf16 = jnp.bfloat16
mebibyte = 1024 * 1024


def matmul(left, right):
    return jnp.dot(left, right, preferred_element_type=f32)


def left_contract(left, right):
    return lax.dot_general(left, right, (((0,), (0,)), ((), ())), preferred_element_type=f32)


def right_contract(left, right):
    return lax.dot_general(left, right, (((1,), (1,)), ((), ())), preferred_element_type=f32)


def skewed(row):
    n = row.shape[1]
    out = jnp.broadcast_to(row, (n, n))
    at = lax.broadcasted_iota(jnp.int32, (n, n), 0)
    step = 1
    while step < n:
        out = jnp.where((at & step) != 0, pltpu.roll(out, step, 1), out)
        step *= 2
    return out


def unskewed_sum(square):
    n = square.shape[1]
    at = lax.broadcasted_iota(jnp.int32, (n, n), 0)
    step = 1
    while step < n:
        square = jnp.where((at & step) != 0, pltpu.roll(square, n - step, 1), square)
        step *= 2
    return jnp.sum(square, axis=0, keepdims=True)


def raised_parts(scores):
    raised = jnp.exp(scores - jnp.max(scores, axis=-1, keepdims=True))
    return raised, 1.0 / jnp.sum(raised, axis=-1, keepdims=True)


def group_rows(rows, group):
    first = group * OWN_HEADS // OWN_GROUPS
    heads = range(first, first + OWN_HEADS // OWN_GROUPS)
    return jnp.concatenate([rows[:, h * HEAD_DIM : (h + 1) * HEAD_DIM] for h in heads], axis=0)


def group_lanes(stacked):
    n = stacked.shape[0] * OWN_GROUPS // OWN_HEADS
    return [stacked[i * n : (i + 1) * n] for i in range(OWN_HEADS // OWN_GROUPS)]


def lanes_of(values, first, group):
    return values[:, first + group * HEAD_DIM : first + (group + 1) * HEAD_DIM]


def stacked_twice(value):
    return jnp.concatenate([value] * (OWN_HEADS // OWN_GROUPS), axis=0)


def attend_back(scores, query, key, value, grad):
    raised, shrink = raised_parts(scores)
    grad = (grad.astype(f32) * shrink).astype(bf16)
    prob_grad = right_contract(grad, value)
    centre = jnp.sum(raised * prob_grad, axis=-1, keepdims=True) * shrink
    score_grad = (raised * (prob_grad - centre)).astype(bf16)
    return score_grad, matmul(score_grad, key), left_contract(score_grad, query), left_contract(raised.astype(bf16), grad)


def self_mask(seg_col, seg_row):
    at_query = lax.broadcasted_iota(jnp.int32, (SEQ, SEQ), 0)
    at_key = lax.broadcasted_iota(jnp.int32, (SEQ, SEQ), 1)
    return (at_key <= at_query) & (seg_col == seg_row)


def fill_bias(curve_ref, bias_ref):
    for head in range(OWN_HEADS):
        bias_ref[head] = skewed(curve_ref[head : head + 1, :])


def self_forward_kernel(qkv_ref, seg_col_ref, seg_row_ref, curve_ref, out_ref, bias_ref):
    @pl.when(pl.program_id(0) == 0)
    def _():
        fill_bias(curve_ref, bias_ref)

    whole = qkv_ref[...].reshape(SEQ, QW + 2 * KW)
    allowed = stacked_twice(self_mask(seg_col_ref[0], seg_row_ref[0]).astype(jnp.int32)) != 0
    mixed = []
    for group in range(OWN_GROUPS):
        query = group_rows(whole, group)
        scores = right_contract(query, lanes_of(whole, QW, group))
        scores = jnp.where(allowed, scores + bias_ref[2 * group : 2 * group + 2].reshape(2 * SEQ, SEQ), neg_big)
        raised, shrink = raised_parts(scores)
        mixed += group_lanes(matmul(raised.astype(bf16), lanes_of(whole, QW + KW, group)) * shrink)
    out_ref[...] = jnp.concatenate(mixed, axis=1).astype(bf16).reshape(out_ref.shape)


def self_backward_kernel(
    qkv_ref, grad_ref, seg_col_ref, seg_row_ref, curve_ref, out_ref, curve_grad_ref, bias_ref, sum_ref
):
    @pl.when(pl.program_id(0) == 0)
    def _():
        fill_bias(curve_ref, bias_ref)
        sum_ref[...] = jnp.zeros_like(sum_ref)

    whole = qkv_ref[...].reshape(SEQ, QW + 2 * KW)
    grads = grad_ref[...].reshape(SEQ, QW)
    allowed = stacked_twice(self_mask(seg_col_ref[0], seg_row_ref[0]).astype(jnp.int32)) != 0
    query_grads, key_grads, value_grads = [], [], []
    for group in range(OWN_GROUPS):
        query = group_rows(whole, group)
        key = lanes_of(whole, QW, group)
        scores = right_contract(query, key)
        scores = jnp.where(allowed, scores + bias_ref[2 * group : 2 * group + 2].reshape(2 * SEQ, SEQ), neg_big)
        score_grad, query_grad, key_grad, value_grad = attend_back(
            scores, query, key, lanes_of(whole, QW + KW, group), group_rows(grads, group)
        )
        sum_ref[2 * group : 2 * group + 2] += score_grad.astype(f32).reshape(2, SEQ, SEQ)
        query_grads += group_lanes(query_grad)
        key_grads.append(key_grad)
        value_grads.append(value_grad)
    joined = jnp.concatenate(query_grads + key_grads + value_grads, axis=1)
    out_ref[...] = joined.astype(bf16).reshape(out_ref.shape)

    @pl.when(pl.program_id(0) == MICRO - 1)
    def _():
        curve_grad_ref[...] = jnp.zeros_like(curve_grad_ref)
        for head in range(OWN_HEADS):
            curve_grad_ref[head : head + 1, :] = unskewed_sum(sum_ref[head])


def by_window(at, wide_ref, body):
    pl.when(wide_ref[at] == 0)(lambda: body(NARROW))
    pl.when(wide_ref[at] != 0)(lambda: body(WINDOW))


def cross_forward_kernel(block_ref, start_ref, wide_ref, q_ref, kv_ref, seg_ref, out_ref, query_ref, mixed_ref):
    at = pl.program_id(0) * DOCS + pl.program_id(1)

    @pl.when(pl.program_id(1) == 0)
    def _():
        query_ref[...] = q_ref[...].reshape(SEQ, QW)

    start = pl.multiple_of(start_ref[at], 16)

    def body(window):
        rows = query_ref[pl.ds(start, window), :]
        mine = seg_ref[0, pl.ds(start, window), :] == pl.program_id(1)
        both = kv_ref[...].reshape(ENC, 2 * KW)
        mixed = []
        for group in range(OWN_GROUPS):
            raised, shrink = raised_parts(right_contract(group_rows(rows, group), lanes_of(both, 0, group)))
            mixed += group_lanes(matmul(raised.astype(bf16), lanes_of(both, KW, group)) * shrink)
        fresh = jnp.concatenate(mixed, axis=1)
        mixed_ref[pl.ds(start, window), :] = jnp.where(mine, fresh, mixed_ref[pl.ds(start, window), :])

    by_window(at, wide_ref, body)

    @pl.when(pl.program_id(1) == DOCS - 1)
    def _():
        out_ref[...] = mixed_ref[...].astype(bf16).reshape(out_ref.shape)


def cross_backward_kernel(
    block_ref, start_ref, wide_ref, q_ref, kv_ref, grad_ref, seg_ref, out_ref, kv_grad_ref, query_ref, given_ref, mixed_ref
):
    at = pl.program_id(0) * DOCS + pl.program_id(1)

    @pl.when(pl.program_id(1) == 0)
    def _():
        query_ref[...] = q_ref[...].reshape(SEQ, QW)
        given_ref[...] = grad_ref[...].reshape(SEQ, QW)

    start = pl.multiple_of(start_ref[at], 16)

    def body(window):
        rows = query_ref[pl.ds(start, window), :]
        mine = seg_ref[0, pl.ds(start, window), :] == pl.program_id(1)
        grads = jnp.where(mine, given_ref[pl.ds(start, window), :].astype(f32), 0.0)
        both = kv_ref[...].reshape(ENC, 2 * KW)
        query_grads, key_grads, value_grads = [], [], []
        for group in range(OWN_GROUPS):
            query, key = group_rows(rows, group), lanes_of(both, 0, group)
            _, query_grad, key_grad, value_grad = attend_back(
                right_contract(query, key), query, key, lanes_of(both, KW, group), group_rows(grads, group)
            )
            query_grads += group_lanes(query_grad)
            key_grads.append(key_grad)
            value_grads.append(value_grad)
        fresh = jnp.concatenate(query_grads, axis=1)
        mixed_ref[pl.ds(start, window), :] = jnp.where(mine, fresh, mixed_ref[pl.ds(start, window), :])
        joined = jnp.concatenate(key_grads + value_grads, axis=1)
        kv_grad_ref[...] = joined.astype(bf16).reshape(kv_grad_ref.shape)

    by_window(at, wide_ref, body)

    @pl.when(pl.program_id(1) == DOCS - 1)
    def _():
        out_ref[...] = mixed_ref[...].astype(bf16).reshape(out_ref.shape)


def rows_block(width):
    return pl.BlockSpec((REP, 1, ROWS, width), lambda m, *rest: (0, m, 0, 0))


def fixed_block(shape):
    return pl.BlockSpec(shape, lambda *at: (0,) * len(shape))


def micro_block(shape):
    return pl.BlockSpec((1,) + shape, lambda m, *rest: (m,) + (0,) * len(shape))


def estimate(flops, moved, raised):
    return pl.CostEstimate(flops=flops, bytes_accessed=moved, transcendentals=raised)


self_pairs = MICRO * OWN_HEADS * SEQ * SEQ
cross_pairs = MICRO * OWN_HEADS * DOCS * WINDOW * ENC


def self_forward(qkv, seg_col, seg_row, curve):
    return pl.pallas_call(
        self_forward_kernel,
        name="self_forward",
        grid=(MICRO,),
        in_specs=[
            rows_block(QW + 2 * KW),
            micro_block((SEQ, 1)),
            micro_block((1, SEQ)),
            fixed_block((8, SEQ)),
        ],
        out_specs=rows_block(QW),
        out_shape=jax.ShapeDtypeStruct((REP, MICRO, ROWS, QW), bf16),
        scratch_shapes=[pltpu.VMEM((OWN_HEADS, SEQ, SEQ), f32)],
        compiler_params=pltpu.CompilerParams(vmem_limit_bytes=14 * mebibyte),
        cost_estimate=estimate(self_pairs * 256, 2 << 20, self_pairs),
    )(qkv, seg_col, seg_row, curve)


def self_backward(qkv, grads, seg_col, seg_row, curve):
    return pl.pallas_call(
        self_backward_kernel,
        name="self_backward",
        grid=(MICRO,),
        in_specs=[
            rows_block(QW + 2 * KW),
            rows_block(QW),
            micro_block((SEQ, 1)),
            micro_block((1, SEQ)),
            fixed_block((8, SEQ)),
        ],
        out_specs=[rows_block(QW + 2 * KW), fixed_block((8, SEQ))],
        out_shape=[
            jax.ShapeDtypeStruct((REP, MICRO, ROWS, QW + 2 * KW), bf16),
            jax.ShapeDtypeStruct((8, SEQ), f32),
        ],
        scratch_shapes=[
            pltpu.VMEM((OWN_HEADS, SEQ, SEQ), f32),
            pltpu.VMEM((OWN_HEADS, SEQ, SEQ), f32),
        ],
        compiler_params=pltpu.CompilerParams(vmem_limit_bytes=18 * mebibyte),
        cost_estimate=estimate(self_pairs * 640, 3 << 20, self_pairs),
    )(qkv, grads, seg_col, seg_row, curve)


def cross_rows():
    return pl.BlockSpec((REP, 1, ROWS, QW), lambda m, d, block, start, wide: (0, m, 0, 0))


def cross_keys():
    return pl.BlockSpec(
        (REP, 1, 1, ENC // REP, 2 * KW),
        lambda m, d, block, start, wide: (0, m, block[m * DOCS + d], 0, 0),
    )


def cross_segs():
    return pl.BlockSpec((1, SEQ, 1), lambda m, d, block, start, wide: (m, 0, 0))


def cross_forward(blocks, starts, wides, queries, kv, seg_col):
    return pl.pallas_call(
        cross_forward_kernel,
        name="cross_forward",
        grid_spec=pltpu.PrefetchScalarGridSpec(
            num_scalar_prefetch=3,
            grid=(MICRO, DOCS),
            in_specs=[cross_rows(), cross_keys(), cross_segs()],
            out_specs=cross_rows(),
            scratch_shapes=[pltpu.VMEM((SEQ, QW), bf16), pltpu.VMEM((SEQ, QW), f32)],
        ),
        out_shape=jax.ShapeDtypeStruct((REP, MICRO, ROWS, QW), bf16),
        compiler_params=pltpu.CompilerParams(vmem_limit_bytes=16 * mebibyte),
        cost_estimate=estimate(cross_pairs * 256, 3 << 20, cross_pairs),
    )(blocks, starts, wides, queries, kv, seg_col)


def cross_backward(blocks, starts, wides, queries, kv, grads, seg_col):
    return pl.pallas_call(
        cross_backward_kernel,
        name="cross_backward",
        grid_spec=pltpu.PrefetchScalarGridSpec(
            num_scalar_prefetch=3,
            grid=(MICRO, DOCS),
            in_specs=[cross_rows(), cross_keys(), cross_rows(), cross_segs()],
            out_specs=[cross_rows(), cross_keys()],
            scratch_shapes=[
                pltpu.VMEM((SEQ, QW), bf16),
                pltpu.VMEM((SEQ, QW), bf16),
                pltpu.VMEM((SEQ, QW), f32),
            ],
        ),
        out_shape=[
            jax.ShapeDtypeStruct((REP, MICRO, ROWS, QW), bf16),
            jax.ShapeDtypeStruct((REP, MICRO, DOCS, ENC // REP, 2 * KW), bf16),
        ],
        compiler_params=pltpu.CompilerParams(vmem_limit_bytes=20 * mebibyte),
        cost_estimate=estimate(cross_pairs * 640, 6 << 20, cross_pairs),
    )(blocks, starts, wides, queries, kv, grads, seg_col)


MESH = pl.DeviceIdType.MESH


def remote(source, target, send_sem, recv_sem, device):
    return pltpu.make_async_remote_copy(
        src_ref=source,
        dst_ref=target,
        send_sem=send_sem,
        recv_sem=recv_sem,
        device_id=device,
        device_id_type=MESH,
    )


class Ring:
    def __init__(self, group, half, me, device_at, send_sems, recv_sems):
        right, left = lax.rem(me + 1, 4), lax.rem(me + 3, 4)
        to_right, to_left = device_at(right), device_at(left)

        def copy(ref, device, i):
            return remote(ref, ref, send_sems.at[i], recv_sems.at[i], device)

        self.direct = [copy(group(me), to_right, 0), copy(group(me), to_left, 1)]
        self.passed = [copy(half(left, 0), to_right, 2), copy(half(right, 1), to_left, 3)]

    def start(self):
        for copy in self.direct:
            copy.start()

    def forward(self):
        for arrived, onward in zip(self.direct, self.passed):
            arrived.wait_recv()
            onward.start()

    def finish(self):
        for copy in self.passed:
            copy.wait_recv()

    def drain(self):
        for copy in self.direct + self.passed:
            copy.wait_send()


class Place:
    def __init__(self):
        self.at = at = lax.axis_index("shard")
        self.rep = rep = lax.axis_index("rep")
        self.x, self.y, self.z = lax.div(at, 8), lax.rem(lax.div(at, 2), 4), lax.rem(at, 2)
        self.chip, self.core = chip, core = lax.div(rep, 2), lax.rem(rep, 2)
        self.pair = {"shard": at + 1 - 2 * self.z}
        self.theirs = (1 - chip) * 2 + core
        self.far = {"rep": self.theirs}
        self.near = {"rep": chip * 2 + 1 - core}
        self.across = {"rep": (1 - chip) * 2 + 1 - core}

    def on_x(self, i):
        return {"shard": i * 8 + self.y * 2 + self.z}

    def on_y(self, i):
        return {"shard": self.x * 8 + i * 2 + self.z}

    def neighbours(self):
        return [self.on_x(lax.rem(self.x + d, 4)) for d in (1, 3)] + [
            self.on_y(lax.rem(self.y + d, 4)) for d in (1, 3)
        ]


GATHER_BLOCKS = (
    (32, QW + 2 * KW, True),
    (32, 2 * KW, True),
    (32, QW, True),
    (32, OWN_FF, True),
    (8, 128, True),
    (32, OWN_FF, False),
    (24, D, False),
    (8, D, False),
    (8, D, False),
)
GATHER_ROWS = ((MICRO * ROWS, 1), (MICRO * DOCS * ENC // REP, 4), (MICRO * ROWS, 1))
GATHER_CHUNKS = sum(parts for _, parts in GATHER_ROWS)


def gather_kernel(*refs):
    query, key, value, cross_key, cross_value, cross_query, gate, small, up, down, out, cross_out = refs[:12]
    n, n_rows = len(GATHER_BLOCKS), len(GATHER_ROWS)
    own_rows = refs[12 : 12 + n_rows]
    wholes = refs[12 + n_rows : 12 + n_rows + n]
    all_rows = refs[12 + n_rows + n : 12 + 2 * n_rows + n]
    (local_sems, out_sems, piece_send, piece_recv, pair_send, pair_recv, ring_send, ring_recv, rep_send, rep_recv,
     *held) = refs[12 + 2 * n_rows + n :]
    held, held_rows = held[:6], held[6:]
    place = Place()
    at, rep, x, y, z = place.at, place.rep, place.x, place.y, place.z
    barrier = pltpu.get_barrier_semaphore()
    devices = [place.pair, place.far, place.near] + place.neighbours()
    for device in devices:
        pl.semaphore_signal(barrier, inc=1, device_id=device, device_id_type=MESH)
    goal = 4 * lax.rem(at, 8) + rep
    stays = (x == rep) & (goal == at)
    source = {"rep": lax.rem(at, 4), "shard": 8 * rep + lax.div(at, 4)}

    @pl.when(jnp.logical_not(stays))
    def _():
        pl.semaphore_signal(barrier, inc=1, device_id=source, device_id_type=MESH)

    pl.semaphore_wait(barrier, len(devices) + 1 - stays.astype(jnp.int32))

    slots = [whole.at[x, y, z] for whole in wholes]
    count = [0]

    def own(source_ref, target):
        count[0] += 1
        return pltpu.make_async_copy(source_ref, target, local_sems.at[count[0] - 1])

    def part(ref, width):
        return ref.at[:, pl.ds(pl.multiple_of(rep * width, 128), width)]

    fills = [
        [
            own(part(query, QW), held[0].at[:, pl.ds(0, QW)]),
            own(part(key, KW), held[0].at[:, pl.ds(QW, KW)]),
            own(part(value, KW), held[0].at[:, pl.ds(QW + KW, KW)]),
        ],
        [
            own(part(cross_key, KW), held[1].at[:, pl.ds(0, KW)]),
            own(part(cross_value, KW), held[1].at[:, pl.ds(KW, KW)]),
        ],
        [own(part(cross_query, QW), held[2])],
        [own(gate, held[3])],
        [own(small, held[4])],
        [own(up, held[5])],
    ]
    firsts = [pl.multiple_of(24 * rep - 8 * lax.div(rep, 3), 8)] + [pl.multiple_of(8 * rep, 8)] * 2
    pieces = []
    for i, ref in enumerate((down, out, cross_out)):
        rows = ref.at[pl.ds(firsts[i], GATHER_BLOCKS[6 + i][0])]
        landing = wholes[6 + i].at[lax.div(goal, 8), lax.rem(lax.div(goal, 2), 4), lax.rem(goal, 2)]
        sent = remote(rows, landing, piece_send.at[i], piece_recv.at[i], {"rep": x, "shard": goal})
        pieces.append((sent, own(rows, landing)))
    for sent, stay in pieces:
        pl.when(jnp.logical_not(stays))(sent.start)
        pl.when(stays)(stay.start)
    for fill in fills:
        for copy in fill:
            copy.start()

    rep_first, rep_second, rep_local = [], [], []
    for i, (rows, parts) in enumerate(GATHER_ROWS):
        mine = all_rows[i].at[rep]
        rep_local.append((own(own_rows[i], held_rows[i]), pltpu.make_async_copy(held_rows[i], mine, out_sems.at[6 + i])))
        rep_local[i][0].start()
        for p in range(parts):
            span = pl.ds(p * (rows // parts), rows // parts)
            j = len(rep_first)
            here, there = all_rows[i].at[rep, span], all_rows[i].at[place.theirs, span]
            rep_first.append(remote(own_rows[i].at[span], here, rep_send.at[j, 0], rep_recv.at[j, 0], place.far))
            direct = remote(own_rows[i].at[span], here, rep_send.at[j, 1], rep_recv.at[j, 1], place.near)
            onward = remote(there, there, rep_send.at[j, 2], rep_recv.at[j, 2], place.near)
            rep_second.append((direct, onward))

    pairs, small_rings, large_rings = [], [], []
    for i, (_, _, first_x) in enumerate(GATHER_BLOCKS):
        whole = wholes[i]
        block = held[i] if i < 6 else slots[i]
        pairs.append(remote(block, slots[i], pair_send.at[i], pair_recv.at[i], place.pair))

        def x_small(j, whole=whole):
            return whole.at[j, y]

        def x_small_half(j, h, whole=whole):
            return whole.at[j, y, h]

        def y_small(j, whole=whole):
            return whole.at[x, j]

        def y_small_half(j, h, whole=whole):
            return whole.at[x, j, h]

        def x_large(j, whole=whole):
            return whole.at[j]

        def x_large_half(j, h, whole=whole):
            return whole.at[j, pl.ds(2 * h, 2)]

        def y_large(j, whole=whole):
            return whole.at[:, j]

        def y_large_half(j, h, whole=whole):
            return whole.at[pl.ds(2 * h, 2), j]

        near_sems = ring_send.at[i, 0], ring_recv.at[i, 0]
        wide_sems = ring_send.at[i, 1], ring_recv.at[i, 1]
        if first_x:
            small_rings.append(Ring(x_small, x_small_half, x, place.on_x, *near_sems))
            large_rings.append(Ring(y_large, y_large_half, y, place.on_y, *wide_sems))
        else:
            small_rings.append(Ring(y_small, y_small_half, y, place.on_y, *near_sems))
            large_rings.append(Ring(x_large, x_large_half, x, place.on_x, *wide_sems))
    settled = []
    for i in range(n):
        if i < 6:
            for copy in fills[i]:
                copy.wait()
            settled.append(pltpu.make_async_copy(held[i], slots[i], out_sems.at[i]))
            settled[i].start()
        else:
            sent, stay = pieces[i - 6]
            pl.when(jnp.logical_not(stays))(sent.wait_recv)
            pl.when(stays)(stay.wait)
        pairs[i].start()
    for first, (direct, _) in zip(rep_first, rep_second):
        first.start()
        direct.start()
    for inward, outward in rep_local:
        inward.wait()
        outward.start()
    for i in range(n):
        if i < 6:
            settled[i].wait()
        pairs[i].wait_recv()
        small_rings[i].start()
    for i in range(n):
        small_rings[i].forward()
    for i in range(n):
        small_rings[i].finish()
        large_rings[i].start()
    passed = 0

    def pass_on(upto):
        nonlocal passed
        while passed < upto:
            rep_first[passed].wait_recv()
            rep_second[passed][1].start()
            passed += 1

    pass_on(3)
    for i in range(n):
        large_rings[i].forward()
    for i in range(n):
        large_rings[i].finish()
    pass_on(GATHER_CHUNKS)
    for sent, _ in pieces:
        pl.when(jnp.logical_not(stays))(sent.wait_send)
    for i in range(n):
        pairs[i].wait_send()
        small_rings[i].drain()
        large_rings[i].drain()
    for _, outward in rep_local:
        outward.wait()
    for j in range(GATHER_CHUNKS):
        rep_first[j].wait_send()
        for copy in rep_second[j]:
            copy.wait()


def gather_weights(weights, rows):
    n = len(GATHER_BLOCKS)
    shapes = [jax.ShapeDtypeStruct((4, 4, 2, r, c), bf16) for r, c, _ in GATHER_BLOCKS]
    shapes += [jax.ShapeDtypeStruct((REP,) + value.shape, value.dtype) for value in rows]
    anywhere = pl.BlockSpec(memory_space=pltpu.HBM)
    dma = pltpu.SemaphoreType.DMA
    results = pl.pallas_call(
        gather_kernel,
        name="gather_weights",
        in_specs=[anywhere] * (len(weights) + len(rows)),
        out_specs=[anywhere] * len(shapes),
        out_shape=shapes,
        scratch_shapes=[
            dma((9 + 3 + len(rows),)),
            dma((6 + len(rows),)),
            dma((3,)),
            dma((3,)),
            dma((n,)),
            dma((n,)),
            dma((n, 2, 4)),
            dma((n, 2, 4)),
            dma((GATHER_CHUNKS, 3)),
            dma((GATHER_CHUNKS, 3)),
        ]
        + [pltpu.VMEM((r, c), bf16) for r, c, _ in GATHER_BLOCKS[:6]]
        + [pltpu.VMEM(value.shape, value.dtype) for value in rows],
        compiler_params=pltpu.CompilerParams(collective_id=0, has_side_effects=True, vmem_limit_bytes=56 * mebibyte),
        cost_estimate=estimate(0, 64 << 20, 0),
    )(*weights, *rows)
    return results[:n], results[n:]


class ReduceRing:
    def __init__(self, half, whole_half, me, device_at, first, second, send_sems, recv_sems):
        right, left, far = lax.rem(me + 1, 4), lax.rem(me + 3, 4), lax.rem(me + 2, 4)
        to_right, to_left = device_at(right), device_at(left)

        def copy(source, target, device, i):
            return remote(source, target, send_sems.at[i], recv_sems.at[i], device)

        self.half, self.me, self.right, self.left = half, me, right, left
        self.first, self.second = first, second
        self.opening = [
            copy(whole_half(far, 0), first.at[0], to_right, 0),
            copy(whole_half(far, 1), first.at[1], to_left, 1),
        ]
        self.plain = [
            copy(whole_half(right, 1), second.at[0, 1], to_right, 2),
            copy(whole_half(left, 0), second.at[1, 0], to_left, 3),
        ]
        self.summed = [
            copy(first.at[0], second.at[0, 0], to_right, 4),
            copy(first.at[1], second.at[1, 1], to_left, 5),
        ]

    def start(self):
        for copy in self.opening + self.plain:
            copy.start()

    def middle(self, each):
        for h, group in enumerate((self.right, self.left)):
            self.opening[h].wait_recv()

            def add(*k, h=h, group=group):
                mixed = self.first[(h, *k)].astype(f32) + self.half(group, h, *k).astype(f32)
                self.first[(h, *k)] = mixed.astype(self.first.dtype)

            each(add)
            self.summed[h].start()

    def finish(self, each, store):
        for h in range(2):
            (self.plain[1] if h == 0 else self.plain[0]).wait_recv()
            self.summed[h].wait_recv()

            def add(*k, h=h):
                mixed = self.second[(0, h, *k)].astype(f32) + self.second[(1, h, *k)].astype(f32)
                store(h, *k, mixed + self.half(self.me, h, *k).astype(f32))

            each(add)

    def drain(self):
        for copy in self.opening + self.plain + self.summed:
            copy.wait_send()


def each_of_four(body):
    def step(i, carry):
        body(lax.div(i, 2), lax.rem(i, 2))
        return carry

    lax.fori_loop(0, 4, step, 0)


def just_once(body):
    body()


REDUCE_BLOCKS = (
    (32, QW + 2 * KW, True, bf16),
    (32, 2 * KW, True, bf16),
    (32, QW, True, bf16),
    (32, OWN_FF, True, bf16),
    (32, OWN_FF, False, bf16),
    (24, D, False, bf16),
    (8, D, False, bf16),
    (8, D, False, bf16),
    (8, 128, True, f32),
)
COLUMN_BLOCKS = (0, 1, 2, 3, 4)
PIECE_BLOCKS = (5, 6, 7)
SMALL_BLOCK = 8
REDUCE_SCRATCH = 8


def reduce_kernel(*refs):
    n = len(REDUCE_BLOCKS)
    own = MICRO * ROWS
    grads, refs = refs[:n], refs[n:]
    kv_grad, w_ckv, layer_part, hidden, *refs = refs
    alls, refs = refs[: len(COLUMN_BLOCKS)], refs[len(COLUMN_BLOCKS) :]
    gathered, refs = refs[: len(PIECE_BLOCKS)], refs[len(PIECE_BLOCKS) :]
    small_out, kv_all, w_all, layer_out, *refs = refs
    scratch = [refs[REDUCE_SCRATCH * i : REDUCE_SCRATCH * (i + 1)] for i in range(n)]
    refs = refs[REDUCE_SCRATCH * n :]
    (small_far, small_near, core_recv, far_send, far_recv, near_sum, held_kv, held_w) = refs[:8]
    (ring_send, ring_recv, pair_send, pair_recv, rep_send, rep_recv, piece_send, piece_recv, more_send, more_recv,
     local_sems) = refs[8:]
    place = Place()
    at, rep, x, y, z, theirs = place.at, place.rep, place.x, place.y, place.z, place.theirs
    barrier = pltpu.get_barrier_semaphore()
    devices = [place.pair, place.far, place.near, place.across] + place.neighbours()
    for device in devices:
        pl.semaphore_signal(barrier, inc=1, device_id=device, device_id_type=MESH)
    owner = 8 * rep + lax.div(at, 4)
    slot = lax.rem(at, 4)
    stays = owner == at

    def from_self(q):
        return (x == rep) & (4 * lax.rem(at, 8) + q == at)

    for q in range(REP):
        giver = {"rep": x, "shard": 4 * lax.rem(at, 8) + q}

        @pl.when(jnp.logical_not(from_self(q)))
        def _(giver=giver):
            pl.semaphore_signal(barrier, inc=1, device_id=giver, device_id_type=MESH)

    pl.semaphore_wait(barrier, len(devices) + REP - stays.astype(jnp.int32))

    large, small = [], []
    for i, (_, _, on_y, dtype) in enumerate(REDUCE_BLOCKS):
        grad = grads[i]
        first, second, mid, first_small, second_small, low, arrived, result = scratch[i]
        if on_y:

            def half(j, h, a, b, grad=grad):
                return grad[2 * h + a, j, b]

            def whole_half(j, h, grad=grad):
                return grad.at[pl.ds(2 * h, 2), j]
        else:

            def half(j, h, a, b, grad=grad):
                return grad[j, 2 * h + a, b]

            def whole_half(j, h, grad=grad):
                return grad.at[j, pl.ds(2 * h, 2)]

        def half_small(j, h, mid=mid):
            return mid[j, h]

        def whole_half_small(j, h, mid=mid):
            return mid.at[j, h]

        wide = (y, place.on_y) if on_y else (x, place.on_x)
        narrow = (x, place.on_x) if on_y else (y, place.on_y)
        large.append(ReduceRing(half, whole_half, *wide, first, second, ring_send.at[i, 0], ring_recv.at[i, 0]))
        small.append(
            ReduceRing(
                half_small, whole_half_small, *narrow, first_small, second_small, ring_send.at[i, 1], ring_recv.at[i, 1]
            )
        )
    for ring in large:
        ring.start()

    to_core = [
        remote(
            layer_part.at[there * 2 + 1 - place.core], core_recv.at[i], more_send.at[i], more_recv.at[i], place.near
        )
        for i, there in enumerate((1 - place.chip, place.chip))
    ]
    for copy in to_core:
        copy.start()

    def lanes(r):
        return pl.ds(pl.multiple_of(r * 2 * KW, 128), 2 * KW)

    locals_ = [
        (
            pltpu.make_async_copy(kv_grad.at[rep], held_kv, local_sems.at[0]),
            pltpu.make_async_copy(held_kv, kv_all.at[:, lanes(rep)], local_sems.at[1]),
        ),
        (
            pltpu.make_async_copy(w_ckv, held_w, local_sems.at[2]),
            pltpu.make_async_copy(held_w, w_all.at[:, lanes(rep)], local_sems.at[3]),
        ),
    ]
    for inward, _ in locals_:
        inward.start()

    to_core[0].wait_recv()
    far_send[...] = (layer_part[theirs].astype(f32) + core_recv[0].astype(f32)).astype(bf16)
    to_far = remote(far_send, far_recv, more_send.at[2], more_recv.at[2], place.far)
    to_far.start()
    exchanged = [
        remote(w_ckv, w_all.at[:, lanes(rep)], more_send.at[3], more_recv.at[3], place.far),
        remote(w_ckv, w_all.at[:, lanes(rep)], more_send.at[4], more_recv.at[4], place.near),
    ]
    passed_on = remote(
        w_all.at[:, lanes(theirs)], w_all.at[:, lanes(theirs)], more_send.at[5], more_recv.at[5], place.near
    )
    for i, there in enumerate((place.far, place.across, place.near)):
        exchanged.append(
            remote(
                kv_grad.at[there["rep"]], kv_all.at[:, lanes(rep)], more_send.at[6 + i], more_recv.at[6 + i], there
            )
        )
    for copy in exchanged:
        copy.start()
    for inward, outward in locals_:
        inward.wait()
        outward.start()
    to_core[1].wait_recv()
    near_sum[...] = hidden[...] + layer_part[rep].astype(f32) + core_recv[1].astype(f32)

    for ring in large:
        ring.middle(each_of_four)
    for i, ring in enumerate(large):
        mid = scratch[i][2]

        def store(h, a, b, total, mid=mid):
            mid[2 * h + a, b] = total.astype(mid.dtype)

        ring.finish(each_of_four, store)
        small[i].start()
    exchanged[0].wait_recv()
    passed_on.start()
    to_far.wait_recv()
    layer_out[...] = (near_sum[...] + far_recv[...].astype(f32)).astype(bf16)
    for ring in small:
        ring.middle(just_once)
    pairs = []
    for i, ring in enumerate(small):
        low = scratch[i][5]

        def store(h, total, low=low):
            low[h] = total.astype(low.dtype)

        ring.finish(just_once, store)
        pairs.append(remote(low.at[1 - z], scratch[i][6], pair_send.at[i], pair_recv.at[i], place.pair))
        pairs[i].start()
    spread, onward, given = [], [], []
    for i in range(n):
        low, arrived, result = scratch[i][5:8]
        pairs[i].wait_recv()
        total = (low[z].astype(f32) + arrived[...].astype(f32)).astype(low.dtype)
        if i in COLUMN_BLOCKS:
            j = COLUMN_BLOCKS.index(i)
            alls[j][rep] = total
            mine, other = alls[j].at[rep], alls[j].at[theirs]
            spread.append(
                [
                    remote(mine, mine, rep_send.at[j, 0], rep_recv.at[j, 0], place.far),
                    remote(mine, mine, rep_send.at[j, 1], rep_recv.at[j, 1], place.near),
                ]
            )
            onward.append(remote(other, other, rep_send.at[j, 2], rep_recv.at[j, 2], place.near))
            for copy in spread[j]:
                copy.start()
        elif i in PIECE_BLOCKS:
            j = PIECE_BLOCKS.index(i)
            result[...] = total
            for k in range(REP):
                copy = remote(
                    result,
                    gathered[j].at[slot],
                    piece_send.at[j, k],
                    piece_recv.at[j, slot],
                    {"rep": jnp.int32(k), "shard": owner},
                )
                own_piece = stays & (rep == k)
                given.append((own_piece, copy))
                pl.when(jnp.logical_not(own_piece))(copy.start)

            @pl.when(stays)
            def _(j=j, total=total):
                gathered[j][slot] = total
        else:
            result[...] = total
    result = scratch[SMALL_BLOCK][7]
    small_first = remote(result, small_far, more_send.at[9], more_recv.at[9], place.far)
    small_first.start()
    for j in range(len(onward)):
        spread[j][0].wait_recv()
        onward[j].start()
    small_first.wait()
    result[...] = result[...] + small_far[...]
    small_second = remote(result, small_near, more_send.at[10], more_recv.at[10], place.near)
    small_second.start()
    small_second.wait()
    small_out[...] = result[...] + small_near[...]
    for j in range(len(onward)):
        spread[j][1].wait_recv()
        onward[j].wait_recv()
    for j in range(len(PIECE_BLOCKS)):
        for q in range(REP):
            landed = gathered[j].at[q]
            arrival = remote(
                landed, landed, piece_send.at[j, q], piece_recv.at[j, q], {"rep": x, "shard": 4 * lax.rem(at, 8) + q}
            )
            pl.when(jnp.logical_not(from_self(q)))(arrival.wait_recv)
    for copy in exchanged[1:]:
        copy.wait_recv()
    passed_on.wait_recv()
    for _, outward in locals_:
        outward.wait()
    for ring in large + small:
        ring.drain()
    for own_piece, copy in given:
        pl.when(jnp.logical_not(own_piece))(copy.wait_send)
    for copy in to_core + [to_far, passed_on] + exchanged + pairs + onward + [one for two in spread for one in two]:
        copy.wait_send()


def reduce_grads(grads, kv_grad, w_ckv, layer_part, hidden):
    n = len(REDUCE_BLOCKS)
    own = MICRO * ROWS
    enc_rows = kv_grad.shape[1]
    shapes = [jax.ShapeDtypeStruct((REP,) + REDUCE_BLOCKS[i][:2], bf16) for i in COLUMN_BLOCKS + PIECE_BLOCKS]
    shapes += [
        jax.ShapeDtypeStruct((8, 128), f32),
        jax.ShapeDtypeStruct((enc_rows, REP * 2 * KW), bf16),
        jax.ShapeDtypeStruct((D, REP * 2 * KW), bf16),
        jax.ShapeDtypeStruct((own, D), bf16),
    ]
    anywhere = pl.BlockSpec(memory_space=pltpu.HBM)
    here = pl.BlockSpec(memory_space=pltpu.VMEM)
    dma = pltpu.SemaphoreType.DMA
    scratch = []
    for rows, width, _, dtype in REDUCE_BLOCKS:
        for lead in ((2, 2, 2), (2, 2, 2, 2), (4, 2), (2,), (2, 2), (2,), (), ()):
            scratch.append(pltpu.VMEM(lead + (rows, width), dtype))
    scratch += [
        pltpu.VMEM((8, 128), f32),
        pltpu.VMEM((8, 128), f32),
        pltpu.VMEM((2, own, D), bf16),
        pltpu.VMEM((own, D), bf16),
        pltpu.VMEM((own, D), bf16),
        pltpu.VMEM((own, D), f32),
        pltpu.VMEM((enc_rows, 2 * KW), bf16),
        pltpu.VMEM((D, 2 * KW), bf16),
    ]
    scratch += [dma((n, 2, 6)), dma((n, 2, 6)), dma((n,)), dma((n,)), dma((5, 3)), dma((5, 3))]
    scratch += [dma((3, REP)), dma((3, REP)), dma((11,)), dma((11,)), dma((4,))]
    results = pl.pallas_call(
        reduce_kernel,
        name="reduce_grads",
        in_specs=[here] * n + [anywhere, anywhere, here, here],
        out_specs=[here] * (len(COLUMN_BLOCKS) + len(PIECE_BLOCKS) + 1) + [anywhere, anywhere, here],
        out_shape=shapes,
        scratch_shapes=scratch,
        compiler_params=pltpu.CompilerParams(
            collective_id=6, has_side_effects=True, vmem_limit_bytes=30 * mebibyte
        ),
        cost_estimate=estimate(0, 128 << 20, 0),
    )(*grads, kv_grad, w_ckv, layer_part, hidden)
    return results


def norm_parts(values):
    return lax.rsqrt(jnp.mean(values * values, axis=-1, keepdims=True) + epsilon)


def boundary_kernel(n_pairs, turned, forward, gathers, *refs):
    pairs = [(refs[2 * i], refs[2 * i + 1]) for i in range(n_pairs)]
    rest = refs[2 * n_pairs :]
    if forward:
        hidden_ref, gain_ref, out_ref, *rest = rest
    else:
        values_ref, hidden_ref, gain_ref, out_ref, acc_ref, *rest = rest
    if gathers:
        all_ref, *rest = rest
    core_send, core_recv, far_send, far_recv, near_sum, send_sems, recv_sems = rest
    rep = lax.axis_index("rep")
    chip, core = lax.div(rep, 2), lax.rem(rep, 2)
    theirs = (1 - chip) * 2 + core
    far = {"rep": theirs}
    near = {"rep": chip * 2 + 1 - core}
    barrier = pltpu.get_barrier_semaphore()
    for device in (far, near):
        pl.semaphore_signal(barrier, inc=1, device_id=device, device_id_type=MESH)

    def partial(r):
        product = right_contract if turned else matmul
        total = product(pairs[0][0][r], pairs[0][1][...])
        for left, right in pairs[1:]:
            total = total + product(left[r], right[...])
        return total

    def copy(source, target, i, device):
        return remote(source, target, send_sems.at[i], recv_sems.at[i], device)

    half = ROWS
    chunks = [pl.ds(c * half, half) for c in range(MICRO)]
    to_core = []
    for i, there in enumerate((1 - chip, chip)):
        core_send[i] = partial(there * 2 + 1 - core).astype(bf16)
        to_core.append(copy(core_send.at[i], core_recv.at[i], i, near))
        if i == 0:
            pl.semaphore_wait(barrier, 2)
        to_core[i].start()
    far_own = partial(theirs)
    to_core[0].wait_recv()
    far_send[...] = (far_own + core_recv[0].astype(f32)).astype(bf16)
    to_far = [copy(far_send.at[rows], far_recv.at[rows], 2 + c, far) for c, rows in enumerate(chunks)]
    for sent in to_far:
        sent.start()
    near_own = partial(rep)
    to_core[1].wait_recv()
    near_sum[...] = near_own + core_recv[1].astype(f32)
    spread, onward = [], []
    acc = None
    for c, rows in enumerate(chunks):
        to_far[c].wait_recv()
        total = near_sum[rows, :] + far_recv[rows, :].astype(f32)
        gain = gain_ref[...]
        if forward:
            fresh = hidden_ref[rows, :].astype(f32) + total
            sent = (fresh * norm_parts(fresh) * gain).astype(bf16)
        else:
            values = values_ref[rows, :].astype(f32)
            rho = norm_parts(values)
            scaled = gain * total
            inner = jnp.mean(values * scaled, axis=-1, keepdims=True)
            fresh = hidden_ref[rows, :].astype(f32) + rho * scaled - values * (rho * rho * rho * inner)
            part = jnp.sum(values * rho * total, axis=0, keepdims=True)
            acc = part if acc is None else acc + part
            sent = fresh.astype(bf16)
        out_ref[rows, :] = fresh
        if gathers:
            all_ref[rep, rows, :] = sent
            mine = all_ref.at[rep, rows]
            other = all_ref.at[theirs, rows]
            spread.append((copy(mine, mine, 4 + c, far), copy(mine, mine, 6 + c, near)))
            onward.append(copy(other, other, 8 + c, near))
            for one in spread[c]:
                one.start()
    if not forward:
        acc_ref[...] = acc
    for c in range(len(onward)):
        spread[c][0].wait_recv()
        onward[c].start()
    for c in range(len(onward)):
        spread[c][1].wait_recv()
        onward[c].wait_recv()
    for sent in to_core + to_far + [one for two in spread for one in two] + onward:
        sent.wait_send()


def boundary(name, identity, pairs, turned, hidden, gain, values=None, gathers=True):
    own = MICRO * ROWS
    forward = values is None
    operands = [a.reshape(REP, own, -1) if i == 0 else a for pair in pairs for i, a in enumerate(pair)]
    operands += ([] if forward else [values]) + [hidden, gain.reshape(1, D)]
    shapes = [jax.ShapeDtypeStruct((own, D), f32)]
    if not forward:
        shapes.append(jax.ShapeDtypeStruct((1, D), f32))
    if gathers:
        shapes.append(jax.ShapeDtypeStruct((REP, own, D), bf16))
    here = pl.BlockSpec(memory_space=pltpu.VMEM)
    dma = pltpu.SemaphoreType.DMA
    return pl.pallas_call(
        lambda *refs: boundary_kernel(len(pairs), turned, forward, gathers, *refs),
        name=name,
        in_specs=[here] * len(operands),
        out_specs=[here] * len(shapes),
        out_shape=shapes,
        scratch_shapes=[
            pltpu.VMEM((2, own, D), bf16),
            pltpu.VMEM((2, own, D), bf16),
            pltpu.VMEM((own, D), bf16),
            pltpu.VMEM((own, D), bf16),
            pltpu.VMEM((own, D), f32),
            dma((10,)),
            dma((10,)),
        ],
        compiler_params=pltpu.CompilerParams(
            collective_id=identity, has_side_effects=True, vmem_limit_bytes=22 * mebibyte
        ),
        cost_estimate=estimate(1 << 30, 32 << 20, 0),
    )(*operands)


FINAL_COLUMNS = (
    (0, 0, QW),
    (0, QW, KW),
    (0, QW + KW, KW),
    (1, 0, KW),
    (1, KW, KW),
    (2, 0, QW),
    (3, 0, OWN_FF),
    (4, 0, OWN_FF),
)


def finish_kernel(*refs):
    n = len(COLUMN_BLOCKS) + len(PIECE_BLOCKS)
    columns, pieces = refs[: len(COLUMN_BLOCKS)], refs[len(COLUMN_BLOCKS) : n]
    kv_ref, w_ref = refs[n : n + 2]
    finals, enc_ref = refs[n + 2 : -1], refs[-1]
    enc_ref[...] = right_contract(kv_ref[...], w_ref[...])

    @pl.when(pl.program_id(0) == 0)
    def _():
        for final, (source, first, width) in zip(finals, FINAL_COLUMNS):
            parts = [columns[source][r, :, first : first + width].astype(f32) for r in range(REP)]
            final[...] = jnp.concatenate(parts, axis=1)
        for final, piece in zip(finals[len(FINAL_COLUMNS) :], pieces):
            rows = piece.shape[1]
            for q in range(REP):
                skip = REP * rows - final.shape[0] if q == REP - 1 else 0
                final[q * rows : (q + 1) * rows - skip, :] = piece[q, skip:, :].astype(f32)


def finish(columns, pieces, kv_all, w_all):
    shapes = [jax.ShapeDtypeStruct((columns[i].shape[1], REP * width), f32) for i, _, width in FINAL_COLUMNS]
    shapes += [jax.ShapeDtypeStruct((tall, D), f32) for tall in (FF // SHARDS, 32, 32)]
    shapes.append(jax.ShapeDtypeStruct((kv_all.shape[0], D), f32))
    tall = kv_all.shape[0] // 4
    some = pl.BlockSpec((tall, D), lambda i: (i, 0))
    return pl.pallas_call(
        finish_kernel,
        name="finish",
        grid=(4,),
        in_specs=[fixed_block(value.shape) for value in columns + pieces] + [some, fixed_block(w_all.shape)],
        out_specs=[fixed_block(shape.shape) for shape in shapes[:-1]] + [some],
        out_shape=shapes,
        compiler_params=pltpu.CompilerParams(vmem_limit_bytes=24 * mebibyte),
        cost_estimate=estimate(2 << 30, 12 << 20, 0),
    )(*columns, *pieces, kv_all, w_all)


def local(
    tokens,
    out_cotangent,
    encoded,
    segment_ids,
    doc_block,
    bucket_table,
    self_gain,
    query_weight,
    key_weight,
    value_weight,
    out_weight,
    bias_table,
    cross_gain,
    cross_query,
    cross_key,
    cross_value,
    cross_out,
    feed_gain,
    gate_weight,
    up_weight,
    down_weight,
):
    rep = lax.axis_index("rep")
    own = MICRO * ROWS
    enc_rows = MICRO * DOCS * ENC // REP

    def columns(weight, width):
        return lax.dynamic_slice_in_dim(weight, rep * width, width, 1)

    small = jnp.concatenate([self_gain, cross_gain, feed_gain, bias_table[0], jnp.zeros((16,), bf16)])
    small = jnp.broadcast_to(small[None], (8, 128))
    own_tokens = tokens.reshape(own, D)
    own_cotangent = out_cotangent.reshape(own, D)
    wholes, (all_tokens, all_enc, all_grad) = gather_weights(
        [
            query_weight,
            key_weight,
            value_weight,
            cross_key,
            cross_value,
            cross_query,
            columns(gate_weight, OWN_FF),
            small,
            columns(up_weight, OWN_FF),
            down_weight,
            out_weight,
            cross_out,
        ],
        [own_tokens, encoded.reshape(enc_rows, D), own_cotangent],
    )
    w_qkv, w_ckv, w_cq, w_gate, small, w_up, w_down, w_out, w_cout = wholes
    w_qkv = w_qkv.reshape(D, QW + 2 * KW)
    small = small.reshape(SHARDS, 8, 128)[:, 0]
    w_out = w_out.reshape(QW, D)
    w_ckv = w_ckv.reshape(D, 2 * KW)
    w_cq = w_cq.reshape(D, QW)
    w_cout = w_cout.reshape(QW, D)
    w_gate = w_gate.reshape(D, OWN_FF)
    w_up = w_up.reshape(D, OWN_FF)
    w_down = w_down.reshape(8, 96, D)
    w_down = jnp.concatenate([w_down[:, :72], w_down[:, 80:]], axis=1).reshape(OWN_FF, D)
    self_factor = small[:, 0:32].reshape(D).astype(f32)
    cross_factor = small[:, 32:64].reshape(D).astype(f32)
    feed_factor = small[:, 64:96].reshape(D).astype(f32)
    table = small[:, 96:112]

    segments = segment_ids[:, 0]
    seg_col = segments[:, :, None]
    seg_row = segments[:, None, :]
    blocks = doc_block[:, 0].reshape(-1)
    doc_ids = jnp.arange(DOCS, dtype=jnp.int32)
    starts = jnp.sum((segments[:, None, :] < doc_ids[None, :, None]).astype(jnp.int32), axis=2)
    sizes = jnp.sum((segments[:, None, :] == doc_ids[None, :, None]).astype(jnp.int32), axis=2)
    wides = (sizes > NARROW - 16).astype(jnp.int32)
    starts = jnp.minimum(starts // 16 * 16, jnp.where(wides == 0, SEQ - NARROW, SEQ - WINDOW)).reshape(-1)
    wides = wides.reshape(-1)
    turned = jnp.roll(bucket_table[::-1], 1)
    hot = (turned[None, :] == jnp.arange(BUCKETS, dtype=jnp.int32)[:, None]).astype(bf16)
    own_table = lax.dynamic_slice_in_dim(table, rep * OWN_HEADS, OWN_HEADS, 1)
    curve = left_contract(own_table, hot)
    curve = jnp.pad(curve, ((0, 4), (0, 0)))

    all_tokens = all_tokens.reshape(REP * own, D).astype(f32)
    all_enc = all_enc.reshape(REP * enc_rows, D)
    all_grad = all_grad.reshape(REP * own, D)

    normed = (all_tokens * norm_parts(all_tokens) * self_factor).astype(bf16)
    qkv = matmul(normed, w_qkv).astype(bf16).reshape(REP, MICRO, ROWS, QW + 2 * KW)
    kv = matmul(all_enc, w_ckv).astype(bf16).reshape(REP, MICRO, DOCS, ENC // REP, 2 * KW)
    context = self_forward(qkv, seg_col, seg_row, curve).reshape(REP * own, QW)
    hidden, cross_normed = boundary("after_self", 1, [(context, w_out)], False, own_tokens, cross_factor)
    cross_normed = cross_normed.reshape(REP * own, D)
    cross_queries = matmul(cross_normed, w_cq).astype(bf16).reshape(REP, MICRO, ROWS, QW)
    cross_context = cross_forward(blocks, starts, wides, cross_queries, kv, seg_col).reshape(REP * own, QW)
    hidden_two, feed_normed = boundary("after_cross", 2, [(cross_context, w_cout)], False, hidden, feed_factor)
    feed_normed = feed_normed.reshape(REP * own, D)
    gate = matmul(feed_normed, w_gate)
    up_part = matmul(feed_normed, w_up)
    inner_grad = right_contract(all_grad, w_down)

    def gated(gate, up_part):
        return jax.nn.gelu(gate, approximate=True) * up_part

    inner, gated_back = jax.vjp(gated, gate, up_part)
    inner = inner.astype(bf16)
    gate_low, up_low = (grad.astype(bf16) for grad in gated_back(inner_grad))

    hidden_grad, feed_acc, branch = boundary(
        "before_feed", 3, [(gate_low, w_gate), (up_low, w_up)], True, own_cotangent, feed_factor, hidden_two
    )
    branch = branch.reshape(REP * own, D)
    layer_part = matmul(inner, w_down).astype(bf16).reshape(REP, own, D)
    gate_part = left_contract(feed_normed, gate_low)
    up_part = left_contract(feed_normed, up_low)
    down_part = left_contract(inner, all_grad).astype(bf16).reshape(8, 88, D)
    down_part = jnp.concatenate([down_part[:, :72], down_part[:, 64:]], axis=1)

    context_grad = right_contract(branch, w_cout).astype(bf16).reshape(REP, MICRO, ROWS, QW)
    cq_grad, kv_grad = cross_backward(blocks, starts, wides, cross_queries, kv, context_grad, seg_col)
    cq_grad = cq_grad.reshape(REP * own, QW)
    hidden_grad, cross_acc, first_branch = boundary(
        "before_cross", 4, [(cq_grad, w_cq)], True, hidden_grad, cross_factor, hidden
    )
    first_branch = first_branch.reshape(REP * own, D)
    cout_part = left_contract(cross_context, branch)
    cq_part = left_contract(cross_normed, cq_grad)
    kv_grad = kv_grad.reshape(REP, enc_rows, 2 * KW)
    ckv_part = left_contract(all_enc, kv_grad.reshape(REP * enc_rows, 2 * KW))

    context_grad = right_contract(first_branch, w_out).astype(bf16).reshape(REP, MICRO, ROWS, QW)
    qkv_grad, curve_grad = self_backward(qkv, context_grad, seg_col, seg_row, curve)
    qkv_grad = qkv_grad.reshape(REP * own, QW + 2 * KW)
    out_part = left_contract(context, first_branch)
    qkv_part = left_contract(normed, qkv_grad)
    tokens_grad, self_acc = boundary(
        "before_self", 5, [(qkv_grad, w_qkv)], True, hidden_grad, self_factor, own_tokens, False
    )

    table_part = lax.dot_general(
        hot.astype(f32), curve_grad[:OWN_HEADS], (((1,), (1,)), ((), ())), precision=lax.Precision.HIGHEST
    )
    table_part = lax.dynamic_update_slice(jnp.zeros((BUCKETS, HEADS), f32), table_part, (0, rep * OWN_HEADS))
    small_part = jnp.concatenate(
        [
            self_acc.reshape(SHARDS, 32),
            cross_acc.reshape(SHARDS, 32),
            feed_acc.reshape(SHARDS, 32),
            table_part,
            jnp.zeros((SHARDS, 16), f32),
        ],
        axis=1,
    )
    small_part = jnp.broadcast_to(small_part[:, None], (SHARDS, 8, 128))

    parts = [qkv_part, ckv_part, cq_part, gate_part, up_part, down_part, out_part, cout_part, small_part]
    parts = [
        part.astype(dtype).reshape(4, 4, 2, rows, width)
        for part, (rows, width, _, dtype) in zip(parts, REDUCE_BLOCKS)
    ]
    *whole, small_sum, kv_all, w_all, layer_out = reduce_grads(parts, kv_grad, w_ckv, layer_part, hidden_two)
    *finals, encoder_grad = finish(whole[: len(COLUMN_BLOCKS)], whole[len(COLUMN_BLOCKS) :], kv_all, w_all)
    query_grad, key_grad, value_grad, ck_grad, cv_grad, cq_grad, gate_grad, up_grad, down_grad, out_grad, cout_grad = finals
    small_sum = small_sum[0]
    return (
        layer_out.reshape(tokens.shape),
        tokens_grad.reshape(tokens.shape),
        encoder_grad.reshape(encoded.shape),
        small_sum[0:32],
        query_grad,
        key_grad,
        value_grad,
        out_grad,
        small_sum[96:112].reshape(1, HEADS),
        small_sum[32:64],
        cq_grad,
        ck_grad,
        cv_grad,
        cout_grad,
        small_sum[64:96],
        gate_grad,
        up_grad,
        down_grad,
    )


def solution(mesh):
    rows = P("shard", None)
    gain = P("shard")
    acts = P(None, "shard", "rep", None)
    encs = P(None, "shard", None, "rep", None)
    ids = P(None, "shard", None)
    weights = (gain, rows, rows, rows, rows, rows, gain, rows, rows, rows, rows, gain, rows, rows, rows)
    return jax.shard_map(
        local,
        mesh=mesh,
        in_specs=(acts, acts, encs, ids, ids, P()) + weights,
        out_specs=(acts, acts, encs) + weights,
        check_vma=False,
    )
```

```python
import jax
import jax.numpy as jnp
from jax import lax
from jax.experimental import pallas as pl
from jax.experimental.pallas import tpu as pltpu
from jax.sharding import PartitionSpec as P

D = 1024
HEADS = 16
HEAD_DIM = 64
KV_GROUPS = 8
FF = 2816
BUCKETS = 32
ENC = 512
SEQ = 256
DOCS = 4
MICRO = 2

REP = 4
SHARDS = 32
ROWS = SEQ // REP
OWN_HEADS = HEADS // REP
OWN_GROUPS = KV_GROUPS // REP
QW = OWN_HEADS * HEAD_DIM
KW = OWN_GROUPS * HEAD_DIM
OWN_FF = FF // REP
WINDOW = 144
NARROW = 80

epsilon = 1e-06
neg_big = -1e30
gelu_scale = 0.7978845608028654
gelu_cube = 0.044715
f32 = jnp.float32
bf16 = jnp.bfloat16
mebibyte = 1024 * 1024


def matmul(left, right):
    return jnp.dot(left, right, preferred_element_type=f32)


def left_contract(left, right):
    return lax.dot_general(left, right, (((0,), (0,)), ((), ())), preferred_element_type=f32)


def right_contract(left, right):
    return lax.dot_general(left, right, (((1,), (1,)), ((), ())), preferred_element_type=f32)


def skewed(row):
    n = row.shape[1]
    out = jnp.broadcast_to(row, (n, n))
    at = lax.broadcasted_iota(jnp.int32, (n, n), 0)
    step = 1
    while step < n:
        out = jnp.where((at & step) != 0, pltpu.roll(out, step, 1), out)
        step *= 2
    return out


def unskewed_sum(square):
    n = square.shape[1]
    at = lax.broadcasted_iota(jnp.int32, (n, n), 0)
    step = 1
    while step < n:
        square = jnp.where((at & step) != 0, pltpu.roll(square, n - step, 1), square)
        step *= 2
    return jnp.sum(square, axis=0, keepdims=True)


def raised_parts(scores):
    raised = jnp.exp(scores - jnp.max(scores, axis=-1, keepdims=True))
    return raised, 1.0 / jnp.sum(raised, axis=-1, keepdims=True)


def group_rows(rows, group):
    first = group * OWN_HEADS // OWN_GROUPS
    heads = range(first, first + OWN_HEADS // OWN_GROUPS)
    return jnp.concatenate([rows[:, h * HEAD_DIM : (h + 1) * HEAD_DIM] for h in heads], axis=0)


def group_lanes(stacked):
    n = stacked.shape[0] * OWN_GROUPS // OWN_HEADS
    return [stacked[i * n : (i + 1) * n] for i in range(OWN_HEADS // OWN_GROUPS)]


def lanes_of(values, first, group):
    return values[:, first + group * HEAD_DIM : first + (group + 1) * HEAD_DIM]


def stacked_twice(value):
    return jnp.concatenate([value] * (OWN_HEADS // OWN_GROUPS), axis=0)


def attend_back(scores, query, key, value, grad):
    raised, shrink = raised_parts(scores)
    grad = (grad.astype(f32) * shrink).astype(bf16)
    prob_grad = right_contract(grad, value)
    centre = jnp.sum(raised * prob_grad, axis=-1, keepdims=True) * shrink
    score_grad = (raised * (prob_grad - centre)).astype(bf16)
    return score_grad, matmul(score_grad, key), left_contract(score_grad, query), left_contract(raised.astype(bf16), grad)


def self_mask(seg_col, seg_row):
    at_query = lax.broadcasted_iota(jnp.int32, (SEQ, SEQ), 0)
    at_key = lax.broadcasted_iota(jnp.int32, (SEQ, SEQ), 1)
    return (at_key <= at_query) & (seg_col == seg_row)


def fill_bias(curve_ref, bias_ref):
    for head in range(OWN_HEADS):
        bias_ref[head] = skewed(curve_ref[head : head + 1, :])


def self_forward_kernel(
    tokens_ref, gain_ref, weight_ref, seg_col_ref, seg_row_ref, curve_ref, normed_ref, qkv_ref, out_ref, bias_ref
):
    @pl.when(pl.program_id(0) == 0)
    def _():
        fill_bias(curve_ref, bias_ref)

    values = tokens_ref[...].reshape(SEQ, D).astype(f32)
    normed = (values * norm_parts(values) * gain_ref[...]).astype(bf16)
    whole = matmul(normed, weight_ref[...]).astype(bf16)
    normed_ref[...] = normed.reshape(normed_ref.shape)
    qkv_ref[...] = whole.reshape(qkv_ref.shape)
    allowed = stacked_twice(self_mask(seg_col_ref[0], seg_row_ref[0]).astype(jnp.int32)) != 0
    mixed = []
    for group in range(OWN_GROUPS):
        query = group_rows(whole, group)
        scores = right_contract(query, lanes_of(whole, QW, group))
        scores = jnp.where(allowed, scores + bias_ref[2 * group : 2 * group + 2].reshape(2 * SEQ, SEQ), neg_big)
        raised, shrink = raised_parts(scores)
        mixed += group_lanes(matmul(raised.astype(bf16), lanes_of(whole, QW + KW, group)) * shrink)
    out_ref[...] = jnp.concatenate(mixed, axis=1).astype(bf16).reshape(out_ref.shape)


def self_backward_kernel(
    qkv_ref, grad_ref, seg_col_ref, seg_row_ref, curve_ref, out_ref, curve_grad_ref, bias_ref, sum_ref
):
    @pl.when(pl.program_id(0) == 0)
    def _():
        fill_bias(curve_ref, bias_ref)
        sum_ref[...] = jnp.zeros_like(sum_ref)

    whole = qkv_ref[...].reshape(SEQ, QW + 2 * KW)
    grads = grad_ref[...].reshape(SEQ, QW)
    allowed = stacked_twice(self_mask(seg_col_ref[0], seg_row_ref[0]).astype(jnp.int32)) != 0
    query_grads, key_grads, value_grads = [], [], []
    for group in range(OWN_GROUPS):
        query = group_rows(whole, group)
        key = lanes_of(whole, QW, group)
        scores = right_contract(query, key)
        scores = jnp.where(allowed, scores + bias_ref[2 * group : 2 * group + 2].reshape(2 * SEQ, SEQ), neg_big)
        score_grad, query_grad, key_grad, value_grad = attend_back(
            scores, query, key, lanes_of(whole, QW + KW, group), group_rows(grads, group)
        )
        sum_ref[2 * group : 2 * group + 2] += score_grad.astype(f32).reshape(2, SEQ, SEQ)
        query_grads += group_lanes(query_grad)
        key_grads.append(key_grad)
        value_grads.append(value_grad)
    joined = jnp.concatenate(query_grads + key_grads + value_grads, axis=1)
    out_ref[...] = joined.astype(bf16).reshape(out_ref.shape)

    @pl.when(pl.program_id(0) == MICRO - 1)
    def _():
        curve_grad_ref[...] = jnp.zeros_like(curve_grad_ref)
        for head in range(OWN_HEADS):
            curve_grad_ref[head : head + 1, :] = unskewed_sum(sum_ref[head])


def by_window(at, wide_ref, body):
    pl.when(wide_ref[at] == 0)(lambda: body(NARROW))
    pl.when(wide_ref[at] != 0)(lambda: body(WINDOW))


def cross_forward_kernel(block_ref, start_ref, wide_ref, q_ref, kv_ref, seg_ref, out_ref, query_ref, mixed_ref):
    at = pl.program_id(0) * DOCS + pl.program_id(1)

    @pl.when(pl.program_id(1) == 0)
    def _():
        query_ref[...] = q_ref[...].reshape(SEQ, QW)

    start = pl.multiple_of(start_ref[at], 16)

    def body(window):
        rows = query_ref[pl.ds(start, window), :]
        mine = seg_ref[0, pl.ds(start, window), :] == pl.program_id(1)
        both = kv_ref[...].reshape(ENC, 2 * KW)
        mixed = []
        for group in range(OWN_GROUPS):
            raised, shrink = raised_parts(right_contract(group_rows(rows, group), lanes_of(both, 0, group)))
            mixed += group_lanes(matmul(raised.astype(bf16), lanes_of(both, KW, group)) * shrink)
        fresh = jnp.concatenate(mixed, axis=1)
        mixed_ref[pl.ds(start, window), :] = jnp.where(mine, fresh, mixed_ref[pl.ds(start, window), :])

    by_window(at, wide_ref, body)

    @pl.when(pl.program_id(1) == DOCS - 1)
    def _():
        out_ref[...] = mixed_ref[...].astype(bf16).reshape(out_ref.shape)


def cross_backward_kernel(
    block_ref, start_ref, wide_ref, q_ref, kv_ref, grad_ref, seg_ref, out_ref, kv_grad_ref, query_ref, given_ref, mixed_ref
):
    at = pl.program_id(0) * DOCS + pl.program_id(1)

    @pl.when(pl.program_id(1) == 0)
    def _():
        query_ref[...] = q_ref[...].reshape(SEQ, QW)
        given_ref[...] = grad_ref[...].reshape(SEQ, QW)

    start = pl.multiple_of(start_ref[at], 16)

    def body(window):
        rows = query_ref[pl.ds(start, window), :]
        mine = seg_ref[0, pl.ds(start, window), :] == pl.program_id(1)
        grads = jnp.where(mine, given_ref[pl.ds(start, window), :].astype(f32), 0.0)
        both = kv_ref[...].reshape(ENC, 2 * KW)
        query_grads, key_grads, value_grads = [], [], []
        for group in range(OWN_GROUPS):
            query, key = group_rows(rows, group), lanes_of(both, 0, group)
            _, query_grad, key_grad, value_grad = attend_back(
                right_contract(query, key), query, key, lanes_of(both, KW, group), group_rows(grads, group)
            )
            query_grads += group_lanes(query_grad)
            key_grads.append(key_grad)
            value_grads.append(value_grad)
        fresh = jnp.concatenate(query_grads, axis=1)
        mixed_ref[pl.ds(start, window), :] = jnp.where(mine, fresh, mixed_ref[pl.ds(start, window), :])
        joined = jnp.concatenate(key_grads + value_grads, axis=1)
        kv_grad_ref[...] = joined.astype(bf16).reshape(kv_grad_ref.shape)

    by_window(at, wide_ref, body)

    @pl.when(pl.program_id(1) == DOCS - 1)
    def _():
        out_ref[...] = mixed_ref[...].astype(bf16).reshape(out_ref.shape)


def feed_kernel(normed_ref, grad_ref, gate_w_ref, up_w_ref, pieces_ref, inner_ref, gate_ref, up_ref, part_ref, down_ref):
    @pl.when(pl.program_id(0) == 0)
    def _():
        for i in range(4):
            pieces = []
            for k in range(8 * i, 8 * i + 8):
                piece = pieces_ref[k].astype(f32)
                pieces.append(piece[8:] if k % REP == REP - 1 else piece)
            down_ref[i * 176 : (i + 1) * 176, :] = jnp.concatenate(pieces, axis=0).astype(bf16)

    normed = normed_ref[...].reshape(-1, D)
    gate = matmul(normed, gate_w_ref[...])
    up_part = matmul(normed, up_w_ref[...])
    inner_grad = right_contract(grad_ref[...].reshape(-1, D), down_ref[...])
    square = gate * gate
    bent = jnp.tanh(gelu_scale * gate * (1.0 + gelu_cube * square))
    rising = 0.5 * (1.0 + bent)
    slope = rising + 0.5 * gate * (1.0 - bent * bent) * (gelu_scale * (1.0 + 3.0 * gelu_cube * square))
    passed = gate * rising
    inner = (passed * up_part).astype(bf16)
    inner_ref[...] = inner.reshape(inner_ref.shape)
    gate_ref[...] = (inner_grad * up_part * slope).astype(bf16).reshape(gate_ref.shape)
    up_ref[...] = (inner_grad * passed).astype(bf16).reshape(up_ref.shape)
    part_ref[...] = matmul(inner, down_ref[...]).astype(bf16).reshape(part_ref.shape)


def feed(normed, grads, w_gate, w_up, down_pieces):
    own = MICRO * ROWS

    def some(width):
        return pl.BlockSpec((2, own, width), lambda i: (i, 0, 0))

    units = jax.ShapeDtypeStruct((REP, own, OWN_FF), bf16)
    return pl.pallas_call(
        feed_kernel,
        name="feed",
        grid=(REP // 2,),
        in_specs=[
            some(D),
            some(D),
            fixed_block(w_gate.shape),
            fixed_block(w_up.shape),
            fixed_block(down_pieces.shape),
        ],
        out_specs=[some(OWN_FF)] * 3 + [some(D)],
        out_shape=[units, units, units, jax.ShapeDtypeStruct((REP, own, D), bf16)],
        scratch_shapes=[pltpu.VMEM((OWN_FF, D), bf16)],
        compiler_params=pltpu.CompilerParams(vmem_limit_bytes=32 * mebibyte),
        cost_estimate=estimate(3 << 30, 8 << 20, 1 << 19),
    )(normed, grads, w_gate, w_up, down_pieces)


def rows_block(width):
    return pl.BlockSpec((REP, 1, ROWS, width), lambda m, *rest: (0, m, 0, 0))


def fixed_block(shape):
    return pl.BlockSpec(shape, lambda *at: (0,) * len(shape))


def micro_block(shape):
    return pl.BlockSpec((1,) + shape, lambda m, *rest: (m,) + (0,) * len(shape))


def estimate(flops, moved, raised):
    return pl.CostEstimate(flops=flops, bytes_accessed=moved, transcendentals=raised)


self_pairs = MICRO * OWN_HEADS * SEQ * SEQ
cross_pairs = MICRO * OWN_HEADS * DOCS * WINDOW * ENC


def self_forward(tokens, gain, weight, seg_col, seg_row, curve):
    return pl.pallas_call(
        self_forward_kernel,
        name="self_forward",
        grid=(MICRO,),
        in_specs=[
            rows_block(D),
            fixed_block((1, D)),
            fixed_block((D, QW + 2 * KW)),
            micro_block((SEQ, 1)),
            micro_block((1, SEQ)),
            fixed_block((8, SEQ)),
        ],
        out_specs=[rows_block(D), rows_block(QW + 2 * KW), rows_block(QW)],
        out_shape=[jax.ShapeDtypeStruct((REP, MICRO, ROWS, width), bf16) for width in (D, QW + 2 * KW, QW)],
        scratch_shapes=[pltpu.VMEM((OWN_HEADS, SEQ, SEQ), f32)],
        compiler_params=pltpu.CompilerParams(vmem_limit_bytes=18 * mebibyte),
        cost_estimate=estimate(self_pairs * 256, 2 << 20, self_pairs),
    )(tokens, gain, weight, seg_col, seg_row, curve)


def self_backward(qkv, grads, seg_col, seg_row, curve):
    return pl.pallas_call(
        self_backward_kernel,
        name="self_backward",
        grid=(MICRO,),
        in_specs=[
            rows_block(QW + 2 * KW),
            rows_block(QW),
            micro_block((SEQ, 1)),
            micro_block((1, SEQ)),
            fixed_block((8, SEQ)),
        ],
        out_specs=[rows_block(QW + 2 * KW), fixed_block((8, SEQ))],
        out_shape=[
            jax.ShapeDtypeStruct((REP, MICRO, ROWS, QW + 2 * KW), bf16),
            jax.ShapeDtypeStruct((8, SEQ), f32),
        ],
        scratch_shapes=[
            pltpu.VMEM((OWN_HEADS, SEQ, SEQ), f32),
            pltpu.VMEM((OWN_HEADS, SEQ, SEQ), f32),
        ],
        compiler_params=pltpu.CompilerParams(vmem_limit_bytes=18 * mebibyte),
        cost_estimate=estimate(self_pairs * 640, 3 << 20, self_pairs),
    )(qkv, grads, seg_col, seg_row, curve)


def cross_rows():
    return pl.BlockSpec((REP, 1, ROWS, QW), lambda m, d, block, start, wide: (0, m, 0, 0))


def cross_keys():
    return pl.BlockSpec(
        (REP, 1, 1, ENC // REP, 2 * KW),
        lambda m, d, block, start, wide: (0, m, block[m * DOCS + d], 0, 0),
    )


def cross_segs():
    return pl.BlockSpec((1, SEQ, 1), lambda m, d, block, start, wide: (m, 0, 0))


def cross_forward(blocks, starts, wides, queries, kv, seg_col):
    return pl.pallas_call(
        cross_forward_kernel,
        name="cross_forward",
        grid_spec=pltpu.PrefetchScalarGridSpec(
            num_scalar_prefetch=3,
            grid=(MICRO, DOCS),
            in_specs=[cross_rows(), cross_keys(), cross_segs()],
            out_specs=cross_rows(),
            scratch_shapes=[pltpu.VMEM((SEQ, QW), bf16), pltpu.VMEM((SEQ, QW), f32)],
        ),
        out_shape=jax.ShapeDtypeStruct((REP, MICRO, ROWS, QW), bf16),
        compiler_params=pltpu.CompilerParams(vmem_limit_bytes=16 * mebibyte),
        cost_estimate=estimate(cross_pairs * 256, 3 << 20, cross_pairs),
    )(blocks, starts, wides, queries, kv, seg_col)


def cross_backward(blocks, starts, wides, queries, kv, grads, seg_col):
    return pl.pallas_call(
        cross_backward_kernel,
        name="cross_backward",
        grid_spec=pltpu.PrefetchScalarGridSpec(
            num_scalar_prefetch=3,
            grid=(MICRO, DOCS),
            in_specs=[cross_rows(), cross_keys(), cross_rows(), cross_segs()],
            out_specs=[cross_rows(), cross_keys()],
            scratch_shapes=[
                pltpu.VMEM((SEQ, QW), bf16),
                pltpu.VMEM((SEQ, QW), bf16),
                pltpu.VMEM((SEQ, QW), f32),
            ],
        ),
        out_shape=[
            jax.ShapeDtypeStruct((REP, MICRO, ROWS, QW), bf16),
            jax.ShapeDtypeStruct((REP, MICRO, DOCS, ENC // REP, 2 * KW), bf16),
        ],
        compiler_params=pltpu.CompilerParams(vmem_limit_bytes=20 * mebibyte),
        cost_estimate=estimate(cross_pairs * 640, 6 << 20, cross_pairs),
    )(blocks, starts, wides, queries, kv, grads, seg_col)


MESH = pl.DeviceIdType.MESH

swap_core = [(i, i ^ 1) for i in range(REP)]
swap_chip = [(i, i ^ 2) for i in range(REP)]
swap_both = [(i, i ^ 3) for i in range(REP)]


def remote(source, target, send_sem, recv_sem, device):
    return pltpu.make_async_remote_copy(
        src_ref=source,
        dst_ref=target,
        send_sem=send_sem,
        recv_sem=recv_sem,
        device_id=device,
        device_id_type=MESH,
    )


class Ring:
    def __init__(self, group, half, me, device_at, send_sems, recv_sems):
        right, left = lax.rem(me + 1, 4), lax.rem(me + 3, 4)
        to_right, to_left = device_at(right), device_at(left)

        def copy(ref, device, i):
            return remote(ref, ref, send_sems.at[i], recv_sems.at[i], device)

        self.direct = [copy(group(me), to_right, 0), copy(group(me), to_left, 1)]
        self.passed = [copy(half(left, 0), to_right, 2), copy(half(right, 1), to_left, 3)]

    def start(self):
        for copy in self.direct:
            copy.start()

    def forward(self):
        for arrived, onward in zip(self.direct, self.passed):
            arrived.wait_recv()
            onward.start()

    def finish(self):
        for copy in self.passed:
            copy.wait_recv()

    def drain(self):
        for copy in self.direct + self.passed:
            copy.wait_send()


class Place:
    def __init__(self):
        self.at = at = lax.axis_index("shard")
        self.rep = rep = lax.axis_index("rep")
        self.x, self.y, self.z = lax.div(at, 8), lax.rem(lax.div(at, 2), 4), lax.rem(at, 2)
        self.chip, self.core = chip, core = lax.div(rep, 2), lax.rem(rep, 2)
        self.pair = {"shard": at + 1 - 2 * self.z}
        self.theirs = (1 - chip) * 2 + core
        self.far = {"rep": self.theirs}
        self.near = {"rep": chip * 2 + 1 - core}

    def on_x(self, i):
        return {"shard": i * 8 + self.y * 2 + self.z}

    def on_y(self, i):
        return {"shard": self.x * 8 + i * 2 + self.z}

    def neighbours(self):
        return [self.on_x(lax.rem(self.x + d, 4)) for d in (1, 3)] + [
            self.on_y(lax.rem(self.y + d, 4)) for d in (1, 3)
        ]


class Gather:
    def __init__(self, place, block, whole, first_x, sems):
        x, y, z = place.x, place.y, place.z
        pair_send, pair_recv, ring_send, ring_recv = sems
        slot = whole.at[x, y, z]
        self.pair = remote(slot if block is None else block, slot, pair_send, pair_recv, place.pair)

        def x_small(j):
            return whole.at[j, y]

        def x_small_half(j, h):
            return whole.at[j, y, h]

        def y_small(j):
            return whole.at[x, j]

        def y_small_half(j, h):
            return whole.at[x, j, h]

        def x_large(j):
            return whole.at[j]

        def x_large_half(j, h):
            return whole.at[j, pl.ds(2 * h, 2)]

        def y_large(j):
            return whole.at[:, j]

        def y_large_half(j, h):
            return whole.at[pl.ds(2 * h, 2), j]

        near, wide = (ring_send.at[0], ring_recv.at[0]), (ring_send.at[1], ring_recv.at[1])
        if first_x:
            self.small = Ring(x_small, x_small_half, x, place.on_x, *near)
            self.large = Ring(y_large, y_large_half, y, place.on_y, *wide)
        else:
            self.small = Ring(y_small, y_small_half, y, place.on_y, *near)
            self.large = Ring(x_large, x_large_half, x, place.on_x, *wide)

    def drain(self):
        self.pair.wait_send()
        self.small.drain()
        self.large.drain()


GATHER_BLOCKS = (
    (32, QW + 2 * KW, True),
    (32, REP * KW, True),
    (32, QW, True),
    (8, 128, True),
    (32, OWN_FF, True),
    (32, OWN_FF, False),
    (24, D, False),
    (8, D, False),
    (8, D, False),
)
GATHER_HELD = 6
GATHER_ROWS = (1, 4, 1)
GATHER_CHUNKS = sum(GATHER_ROWS)


def gather_kernel(*refs):
    query, key, value, cross_key, cross_value, cross_query, small, gate, up, down, out, cross_out = refs[:12]
    n, n_rows = len(GATHER_BLOCKS), len(GATHER_ROWS)
    own_rows = refs[12 : 12 + n_rows]
    wholes = refs[12 + n_rows : 12 + n_rows + n]
    all_rows = refs[12 + n_rows + n : 12 + 2 * n_rows + n]
    (local_sems, out_sems, piece_send, piece_recv, pair_send, pair_recv, ring_send, ring_recv, rep_send, rep_recv,
     *held) = refs[12 + 2 * n_rows + n :]
    held, held_rows = held[:GATHER_HELD], held[GATHER_HELD:]
    place = Place()
    at, rep, x, y, z = place.at, place.rep, place.x, place.y, place.z
    barrier = pltpu.get_barrier_semaphore()
    devices = [place.pair, place.far, place.near] + place.neighbours()
    for device in devices:
        pl.semaphore_signal(barrier, inc=1, device_id=device, device_id_type=MESH)
    goal = 4 * lax.rem(at, 8) + rep
    stays = (x == rep) & (goal == at)
    source = {"rep": lax.rem(at, 4), "shard": 8 * rep + lax.div(at, 4)}

    @pl.when(jnp.logical_not(stays))
    def _():
        pl.semaphore_signal(barrier, inc=1, device_id=source, device_id_type=MESH)

    pl.semaphore_wait(barrier, len(devices) + 1 - stays.astype(jnp.int32))

    wholes = list(wholes)
    halves = wholes[1]
    wholes[1] = halves.at[place.core]
    slots = [whole.at[x, y, z] for whole in wholes]
    count = [0]

    def own(source_ref, target):
        count[0] += 1
        return pltpu.make_async_copy(source_ref, target, local_sems.at[count[0] - 1])

    def part(ref, width, r=rep):
        return ref.at[:, pl.ds(pl.multiple_of(r * width, 128), width)]

    fills = [
        [
            own(part(query, QW), held[0].at[:, pl.ds(0, QW)]),
            own(part(key, KW), held[0].at[:, pl.ds(QW, KW)]),
            own(part(value, KW), held[0].at[:, pl.ds(QW + KW, KW)]),
        ],
        [
            own(part(cross_key, KW, place.core), held[1].at[:, pl.ds(0, KW)]),
            own(part(cross_value, KW, place.core), held[1].at[:, pl.ds(KW, KW)]),
            own(part(cross_key, KW, 2 + place.core), held[1].at[:, pl.ds(2 * KW, KW)]),
            own(part(cross_value, KW, 2 + place.core), held[1].at[:, pl.ds(3 * KW, KW)]),
        ],
        [own(part(cross_query, QW), held[2])],
        [own(small, held[3])],
        [own(gate, held[4])],
        [own(up, held[5])],
    ]
    firsts = [pl.multiple_of(24 * rep - 8 * lax.div(rep, 3), 8)] + [pl.multiple_of(8 * rep, 8)] * 2
    pieces = []
    for i, ref in enumerate((down, out, cross_out)):
        whole = wholes[GATHER_HELD + i]
        rows = ref.at[pl.ds(firsts[i], GATHER_BLOCKS[GATHER_HELD + i][0])]
        landing = whole.at[lax.div(goal, 8), lax.rem(lax.div(goal, 2), 4), lax.rem(goal, 2)]
        sent = remote(rows, landing, piece_send.at[i], piece_recv.at[i], {"rep": x, "shard": goal})
        pieces.append((sent, own(rows, landing)))
    for sent, stay in pieces:
        pl.when(jnp.logical_not(stays))(sent.start)
        pl.when(stays)(stay.start)
    for fill in fills:
        for copy in fill:
            copy.start()

    rep_first, rep_second, rep_local = [], [], []
    for i, parts in enumerate(GATHER_ROWS):
        whole = all_rows[i]
        rows = own_rows[i].shape[0] // parts
        first, second = (0, 1) if i == 1 else (rep, rep)
        third, fourth = (2, 3) if i == 1 else (place.theirs, place.theirs)
        landing = 2 if i == 1 else rep
        rep_local.append((own(own_rows[i], held_rows[i]), pltpu.make_async_copy(held_rows[i], whole.at[first], out_sems.at[n + i])))
        rep_local[i][0].start()
        for p in range(parts):
            span = pl.ds(p * rows, rows)
            j = len(rep_first)
            mine = own_rows[i].at[span]
            rep_first.append(remote(mine, whole.at[landing, span], rep_send.at[j, 0], rep_recv.at[j, 0], place.far))
            direct = remote(mine, whole.at[second, span], rep_send.at[j, 1], rep_recv.at[j, 1], place.near)
            onward = remote(whole.at[third, span], whole.at[fourth, span], rep_send.at[j, 2], rep_recv.at[j, 2], place.near)
            rep_second.append((direct, onward))

    gathers = []
    for i, (_, _, first_x) in enumerate(GATHER_BLOCKS):
        block = held[i] if i < GATHER_HELD else None
        sems = pair_send.at[i], pair_recv.at[i], ring_send.at[i], ring_recv.at[i]
        gathers.append(Gather(place, block, wholes[i], first_x, sems))
    settled = []
    for i in range(n):
        if i < GATHER_HELD:
            for copy in fills[i]:
                copy.wait()
            settled.append(pltpu.make_async_copy(held[i], slots[i], out_sems.at[i]))
            settled[i].start()
        else:
            sent, stay = pieces[i - GATHER_HELD]
            pl.when(jnp.logical_not(stays))(sent.wait_recv)
            pl.when(stays)(stay.wait)
        gathers[i].pair.start()
    for first, (direct, _) in zip(rep_first, rep_second):
        first.start()
        direct.start()
    for inward, outward in rep_local:
        inward.wait()
        outward.start()
    for i in range(n):
        if i < GATHER_HELD:
            settled[i].wait()
        gathers[i].pair.wait_recv()
        gathers[i].small.start()
    for one in gathers:
        one.small.forward()
    for one in gathers:
        one.small.finish()
        one.large.start()
    for j in range(2):
        rep_first[j].wait_recv()
        rep_second[j][1].start()
    for one in gathers:
        one.large.forward()
    gathers[1].large.finish()
    half = halves.at[place.core]
    swap = remote(half, half, rep_send.at[GATHER_CHUNKS, 0], rep_recv.at[GATHER_CHUNKS, 0], place.near)
    swap.start()
    for i in range(n):
        if i != 1:
            gathers[i].large.finish()
    for j in range(2, GATHER_CHUNKS):
        rep_first[j].wait_recv()
        rep_second[j][1].start()
    for sent, _ in pieces:
        pl.when(jnp.logical_not(stays))(sent.wait_send)
    for one in gathers:
        one.drain()
    for _, outward in rep_local:
        outward.wait()
    for first, second in zip(rep_first, rep_second):
        first.wait_send()
        for copy in second:
            copy.wait()
    swap.wait()


def gather_weights(weights, rows):
    n = len(GATHER_BLOCKS)
    shapes = [
        jax.ShapeDtypeStruct(((2,) if i == 1 else ()) + (4, 4, 2, r, c), bf16)
        for i, (r, c, _) in enumerate(GATHER_BLOCKS)
    ]
    shapes += [jax.ShapeDtypeStruct((REP,) + value.shape, value.dtype) for value in rows]
    anywhere = pl.BlockSpec(memory_space=pltpu.HBM)
    dma = pltpu.SemaphoreType.DMA
    results = pl.pallas_call(
        gather_kernel,
        name="gather_weights",
        in_specs=[anywhere] * (len(weights) + len(rows)),
        out_specs=[anywhere] * len(shapes),
        out_shape=shapes,
        scratch_shapes=[
            dma((11 + 3 + len(rows),)),
            dma((n + len(rows),)),
            dma((3,)),
            dma((3,)),
            dma((n,)),
            dma((n,)),
            dma((n, 2, 4)),
            dma((n, 2, 4)),
            dma((GATHER_CHUNKS + 1, 3)),
            dma((GATHER_CHUNKS + 1, 3)),
        ]
        + [pltpu.VMEM((r, c), bf16) for r, c, _ in GATHER_BLOCKS[:GATHER_HELD]]
        + [pltpu.VMEM(value.shape, value.dtype) for value in rows],
        compiler_params=pltpu.CompilerParams(
            collective_id=0, has_side_effects=True, vmem_limit_bytes=56 * mebibyte
        ),
        cost_estimate=estimate(0, 128 << 20, 0),
    )(*weights, *rows)
    return results[:n], results[n:]


class ReduceRing:
    def __init__(self, half, whole_half, me, device_at, first, second, send_sems, recv_sems):
        right, left, far = lax.rem(me + 1, 4), lax.rem(me + 3, 4), lax.rem(me + 2, 4)
        to_right, to_left = device_at(right), device_at(left)

        def copy(source, target, device, i):
            return remote(source, target, send_sems.at[i], recv_sems.at[i], device)

        self.half, self.me, self.right, self.left = half, me, right, left
        self.first, self.second = first, second
        self.opening = [
            copy(whole_half(far, 0), first.at[0], to_right, 0),
            copy(whole_half(far, 1), first.at[1], to_left, 1),
        ]
        self.plain = [
            copy(whole_half(right, 1), second.at[0, 1], to_right, 2),
            copy(whole_half(left, 0), second.at[1, 0], to_left, 3),
        ]
        self.summed = [
            copy(first.at[0], second.at[0, 0], to_right, 4),
            copy(first.at[1], second.at[1, 1], to_left, 5),
        ]

    def start(self):
        for copy in self.opening + self.plain:
            copy.start()

    def middle(self, each):
        for h, group in enumerate((self.right, self.left)):
            self.opening[h].wait_recv()

            def add(*k, h=h, group=group):
                mixed = self.first[(h, *k)].astype(f32) + self.half(group, h, *k).astype(f32)
                self.first[(h, *k)] = mixed.astype(self.first.dtype)

            each(add)
            self.summed[h].start()

    def finish(self, each, store):
        for h in range(2):
            (self.plain[1] if h == 0 else self.plain[0]).wait_recv()
            self.summed[h].wait_recv()

            def add(*k, h=h):
                mixed = self.second[(0, h, *k)].astype(f32) + self.second[(1, h, *k)].astype(f32)
                store(h, *k, mixed + self.half(self.me, h, *k).astype(f32))

            each(add)

    def drain(self):
        for copy in self.opening + self.plain + self.summed:
            copy.wait_send()


def each_of_four(body):
    def step(i, carry):
        body(lax.div(i, 2), lax.rem(i, 2))
        return carry

    lax.fori_loop(0, 4, step, 0)


def just_once(body):
    body()


def grad_halves(grad, on_y):
    if on_y:
        return (lambda j, h, a, b: grad[2 * h + a, j, b]), (lambda j, h: grad.at[pl.ds(2 * h, 2), j])
    return (lambda j, h, a, b: grad[j, 2 * h + a, b]), (lambda j, h: grad.at[j, pl.ds(2 * h, 2)])


def large_ring(place, grad, on_y, first, second, sems):
    half, whole_half = grad_halves(grad, on_y)
    axis = (place.y, place.on_y) if on_y else (place.x, place.on_x)
    return ReduceRing(half, whole_half, *axis, first, second, *sems)


def large_store(mid):
    def store(h, a, b, total):
        mid[2 * h + a, b] = total.astype(mid.dtype)

    return store


def large_scratch(rows, width, dtype):
    return [pltpu.VMEM((2, 2, 2, rows, width), dtype), pltpu.VMEM((2, 2, 2, 2, rows, width), dtype)]


REDUCE_BLOCKS = (
    (32, QW + 2 * KW, True, bf16, True),
    (32, 2 * KW, False, bf16, True),
    (32, QW, False, bf16, True),
    (32, OWN_FF, True, bf16, True),
    (32, OWN_FF, False, bf16, True),
    (24, D, True, bf16, True),
    (8, D, False, bf16, True),
    (8, D, False, bf16, True),
    (8, 128, False, f32, False),
)
COLUMN_BLOCKS = (0, 1, 2, 3, 4)
PIECE_BLOCKS = (5, 6, 7)
SMALL_BLOCK = 8
BLOCK_ROWS = D // 4


def fill_columns(left, right, grad):
    def step(j, carry):
        lanes = pl.ds(pl.multiple_of(j * BLOCK_ROWS, BLOCK_ROWS), BLOCK_ROWS)
        part = left_contract(left[:, lanes], right[...])
        grad[j] = part.astype(grad.dtype).reshape(grad.shape[1:])
        return carry

    lax.fori_loop(0, 4, step, 0)


def in_thirds(value):
    parts = []
    for _ in range(3):
        parts.append(value.astype(bf16))
        value = value - parts[-1].astype(f32)
    return parts


def exact_matmul(value, ones):
    return sum(matmul(part, ones) for part in in_thirds(value))


def fill_small(rep, accs, curve_grad, hot, blocks):
    owner = lax.broadcasted_iota(jnp.int32, (SHARDS, D), 0)
    entry = lax.broadcasted_iota(jnp.int32, (SHARDS, D), 1)
    column = lax.broadcasted_iota(jnp.int32, (D, 128), 0)
    lane = lax.broadcasted_iota(jnp.int32, (D, 128), 1)
    per = D // SHARDS
    total = None
    for i, acc in enumerate(accs):
        picked = jnp.where(lax.div(entry, per) == owner, acc[...], 0.0)
        ones = (lax.rem(column, per) == lane - per * i).astype(f32).astype(bf16)
        part = exact_matmul(picked, ones)
        total = part if total is None else total + part
    rows = sum(right_contract(hot[...], part) for part in in_thirds(curve_grad[...]))
    head = lax.broadcasted_iota(jnp.int32, (8, 128), 0)
    place = lax.broadcasted_iota(jnp.int32, (8, 128), 1)
    ones = ((head < OWN_HEADS) & (place == 3 * per + OWN_HEADS * rep + head)).astype(f32).astype(bf16)
    total = total + exact_matmul(rows, ones)
    for i in range(SHARDS):
        blocks[i // 8, i // 2 % 4, i % 2] = jnp.broadcast_to(total[i : i + 1, :], (8, 128))


def fill_rows(left, right, grad):
    grad[...] = left_contract(left[...], right[...]).reshape(grad.shape).astype(grad.dtype)


def fill_stream(left, right, grad, held, room, sems):
    n = left.shape[0]
    loads = [pltpu.make_async_copy(left.at[i], held.at[i % 2], sems.at[i]) for i in range(n)]
    loads[0].start()
    loads[1].start()
    for i in range(n):
        loads[i].wait()
        part = left_contract(right[i], held[i % 2])
        room[...] = part if i == 0 else room[...] + part
        if i + 2 < n:
            loads[i + 2].start()

    def turn(j, carry):
        lanes = pl.ds(pl.multiple_of(j * BLOCK_ROWS, BLOCK_ROWS), BLOCK_ROWS)
        grad[j] = room[:, lanes].T.astype(grad.dtype).reshape(grad.shape[1:])
        return carry

    lax.fori_loop(0, 4, turn, 0)


def fill_down(left, right, grad, room):
    def step(j, carry):
        lanes = pl.ds(pl.multiple_of(j * BLOCK_ROWS, BLOCK_ROWS), BLOCK_ROWS)
        room[:, lanes] = left_contract(left[...], right[:, lanes])
        return carry

    lax.fori_loop(0, 4, step, 0)

    def place(a, carry):
        for q in range(REP):
            rows = pl.ds(pl.multiple_of(a * 88 + min(24 * q, 64), 8), 24)
            grad[lax.div(a, 2), 2 * lax.rem(a, 2) + q // 2, q % 2] = room[rows, :].astype(grad.dtype)
        return carry

    lax.fori_loop(0, 8, place, 0)


def reduce_kernel(*refs):
    n = len(REDUCE_BLOCKS)
    own = MICRO * ROWS
    layer_part, hidden, self_acc, cross_acc, feed_acc, curve_grad, hot, *refs = refs
    given = [i for i in range(n) if REDUCE_BLOCKS[i][4]]
    mids, refs = refs[: len(given)], refs[len(given) :]
    alls, refs = refs[: len(COLUMN_BLOCKS)], refs[len(COLUMN_BLOCKS) :]
    gathered, refs = refs[: len(PIECE_BLOCKS)], refs[len(PIECE_BLOCKS) :]
    small_out, layer_out, *refs = refs
    small_blocks, *refs = refs
    grads = {SMALL_BLOCK: small_blocks}
    scratch = []
    for i in range(n):
        extra = 0 if REDUCE_BLOCKS[i][4] else 3
        scratch.append(([None, None, mids[given.index(i)]] if extra == 0 else refs[:3]) + refs[extra : extra + 5])
        refs = refs[extra + 5 :]
    (small_far, small_near, core_recv, far_send, far_recv, near_sum) = refs[:6]
    ring_send, ring_recv, pair_send, pair_recv, rep_send, rep_recv, piece_send, piece_recv, more_send, more_recv = (
        refs[6:]
    )
    place = Place()
    at, rep, x, y, z, theirs = place.at, place.rep, place.x, place.y, place.z, place.theirs
    barrier = pltpu.get_barrier_semaphore()
    devices = [place.pair, place.far, place.near] + place.neighbours()
    for device in devices:
        pl.semaphore_signal(barrier, inc=1, device_id=device, device_id_type=MESH)
    owner = 8 * rep + lax.div(at, 4)
    slot = lax.rem(at, 4)
    stays = owner == at

    def from_self(q):
        return (x == rep) & (4 * lax.rem(at, 8) + q == at)

    for q in range(REP):
        giver = {"rep": x, "shard": 4 * lax.rem(at, 8) + q}

        @pl.when(jnp.logical_not(from_self(q)))
        def _(giver=giver):
            pl.semaphore_signal(barrier, inc=1, device_id=giver, device_id_type=MESH)

    fill_small(rep, (self_acc, cross_acc, feed_acc), curve_grad, hot, small_blocks)
    pl.semaphore_wait(barrier, len(devices) + REP - stays.astype(jnp.int32))

    large, small = [], []
    for i, (_, _, on_y, _, done) in enumerate(REDUCE_BLOCKS):
        first, second, mid, first_small, second_small = scratch[i][:5]

        def half_small(j, h, mid=mid):
            return mid[j, h]

        def whole_half_small(j, h, mid=mid):
            return mid.at[j, h]

        if not done:
            large.append((i, large_ring(place, grads[i], on_y, first, second, (ring_send.at[i, 0], ring_recv.at[i, 0]))))
        narrow = (x, place.on_x) if on_y else (y, place.on_y)
        small.append(
            ReduceRing(
                half_small, whole_half_small, *narrow, first_small, second_small, ring_send.at[i, 1], ring_recv.at[i, 1]
            )
        )
    for i, ring in enumerate(small):
        if REDUCE_BLOCKS[i][4]:
            ring.start()
    for _, ring in large:
        ring.start()

    to_core = [
        remote(
            layer_part.at[there * 2 + 1 - place.core], core_recv.at[i], more_send.at[i], more_recv.at[i], place.near
        )
        for i, there in enumerate((1 - place.chip, place.chip))
    ]
    for copy in to_core:
        copy.start()
    to_core[0].wait_recv()
    far_send[...] = (layer_part[theirs].astype(f32) + core_recv[0].astype(f32)).astype(bf16)
    to_far = remote(far_send, far_recv, more_send.at[2], more_recv.at[2], place.far)
    to_far.start()
    to_core[1].wait_recv()
    near_sum[...] = hidden[...] + layer_part[rep].astype(f32) + core_recv[1].astype(f32)

    for i, ring in enumerate(small):
        if REDUCE_BLOCKS[i][4]:
            ring.middle(just_once)
    for _, ring in large:
        ring.middle(each_of_four)
    for i, ring in large:
        ring.finish(each_of_four, large_store(scratch[i][2]))
        small[i].start()
    to_far.wait_recv()
    layer_out[...] = (near_sum[...] + far_recv[...].astype(f32)).astype(bf16)
    for i, ring in enumerate(small):
        if not REDUCE_BLOCKS[i][4]:
            ring.middle(just_once)
    pairs = []
    for i, ring in enumerate(small):
        low = scratch[i][5]

        def store(h, total, low=low):
            low[h] = total.astype(low.dtype)

        ring.finish(just_once, store)
        pairs.append(remote(low.at[1 - z], scratch[i][6], pair_send.at[i], pair_recv.at[i], place.pair))
        pairs[i].start()
    spread, onward, handed = [], [], []
    for i in range(n):
        low, arrived, result = scratch[i][5:8]
        pairs[i].wait_recv()
        total = (low[z].astype(f32) + arrived[...].astype(f32)).astype(low.dtype)
        if i in COLUMN_BLOCKS:
            j = COLUMN_BLOCKS.index(i)
            alls[j][rep] = total
            mine, other = alls[j].at[rep], alls[j].at[theirs]
            spread.append(
                [
                    remote(mine, mine, rep_send.at[j, 0], rep_recv.at[j, 0], place.far),
                    remote(mine, mine, rep_send.at[j, 1], rep_recv.at[j, 1], place.near),
                ]
            )
            onward.append(remote(other, other, rep_send.at[j, 2], rep_recv.at[j, 2], place.near))
            for copy in spread[j]:
                copy.start()
        elif i in PIECE_BLOCKS:
            j = PIECE_BLOCKS.index(i)
            result[...] = total
            for k in range(REP):
                copy = remote(
                    result,
                    gathered[j].at[slot],
                    piece_send.at[j, k],
                    piece_recv.at[j, slot],
                    {"rep": jnp.int32(k), "shard": owner},
                )
                own_piece = stays & (rep == k)
                handed.append((own_piece, copy))
                pl.when(jnp.logical_not(own_piece))(copy.start)

            @pl.when(stays)
            def _(j=j, total=total):
                gathered[j][slot] = total
        else:
            result[...] = total
    result = scratch[SMALL_BLOCK][7]
    small_first = remote(result, small_far, more_send.at[9], more_recv.at[9], place.far)
    small_first.start()
    for j in range(len(onward)):
        spread[j][0].wait_recv()
        onward[j].start()
    small_first.wait()
    result[...] = result[...] + small_far[...]
    small_second = remote(result, small_near, more_send.at[10], more_recv.at[10], place.near)
    small_second.start()
    small_second.wait()
    small_out[...] = result[...] + small_near[...]
    for j in range(len(onward)):
        spread[j][1].wait_recv()
        onward[j].wait_recv()
    for j in range(len(PIECE_BLOCKS)):
        for q in range(REP):
            landed = gathered[j].at[q]
            arrival = remote(
                landed, landed, piece_send.at[j, q], piece_recv.at[j, q], {"rep": x, "shard": 4 * lax.rem(at, 8) + q}
            )
            pl.when(jnp.logical_not(from_self(q)))(arrival.wait_recv)
    for _, ring in large:
        ring.drain()
    for ring in small:
        ring.drain()
    for own_piece, copy in handed:
        pl.when(jnp.logical_not(own_piece))(copy.wait_send)
    for copy in to_core + [to_far] + pairs + onward + [one for two in spread for one in two]:
        copy.wait_send()


def reduce_grads(layer_part, hidden, accs, curve_grad, hot, mids):
    n = len(REDUCE_BLOCKS)
    own = MICRO * ROWS
    shapes = [jax.ShapeDtypeStruct((REP,) + REDUCE_BLOCKS[i][:2], bf16) for i in COLUMN_BLOCKS + PIECE_BLOCKS]
    shapes += [jax.ShapeDtypeStruct((8, 128), f32), jax.ShapeDtypeStruct((own, D), bf16)]
    here = pl.BlockSpec(memory_space=pltpu.VMEM)
    dma = pltpu.SemaphoreType.DMA
    scratch = [pltpu.VMEM((4, 4, 2) + REDUCE_BLOCKS[SMALL_BLOCK][:2], f32)]
    for rows, width, _, dtype, done in REDUCE_BLOCKS:
        if not done:
            scratch += large_scratch(rows, width, dtype) + [pltpu.VMEM((4, 2, rows, width), dtype)]
        for lead in ((2,), (2, 2), (2,), (), ()):
            scratch.append(pltpu.VMEM(lead + (rows, width), dtype))
    scratch += [
        pltpu.VMEM((8, 128), f32),
        pltpu.VMEM((8, 128), f32),
        pltpu.VMEM((2, own, D), bf16),
        pltpu.VMEM((own, D), bf16),
        pltpu.VMEM((own, D), bf16),
        pltpu.VMEM((own, D), f32),
    ]
    scratch += [dma((n, 2, 6)), dma((n, 2, 6)), dma((n,)), dma((n,)), dma((5, 3)), dma((5, 3))]
    scratch += [dma((3, REP)), dma((3, REP)), dma((11,)), dma((11,))]
    return pl.pallas_call(
        reduce_kernel,
        name="reduce_grads",
        in_specs=[here] * (7 + len(mids)),
        out_specs=[here] * len(shapes),
        out_shape=shapes,
        scratch_shapes=scratch,
        compiler_params=pltpu.CompilerParams(
            collective_id=6, has_side_effects=True, vmem_limit_bytes=56 * mebibyte
        ),
        cost_estimate=estimate(0, 128 << 20, 0),
    )(layer_part, hidden, *accs, curve_grad, hot, *mids)


def norm_parts(values):
    return lax.rsqrt(jnp.mean(values * values, axis=-1, keepdims=True) + epsilon)


class ReduceRider:
    def __init__(self, jobs):
        self.jobs = [(i, fill) for i, fill, _, _ in jobs]
        self.operands, self.uses = [], []
        for _, _, left, right in jobs:
            use = []
            for value in (left, right):
                found = [k for k, other in enumerate(self.operands) if other is value]
                if not found:
                    self.operands.append(value)
                use.append(found[0] if found else len(self.operands) - 1)
            self.uses.append(use)
        n = len(jobs)
        dma = pltpu.SemaphoreType.DMA
        self.shapes, self.scratch = [], [dma((n, 6)), dma((n, 6))]
        for i, fill in self.jobs:
            rows, width, _, dtype, _ = REDUCE_BLOCKS[i]
            self.shapes.append(jax.ShapeDtypeStruct((4, 2, rows, width), dtype))
            self.scratch += [pltpu.VMEM((4, 4, 2, rows, width), dtype)] + large_scratch(rows, width, dtype)
        here, there = pl.BlockSpec(memory_space=pltpu.VMEM), pl.BlockSpec(memory_space=pltpu.HBM)
        self.in_specs = [here] * len(self.operands)
        for (_, fill), use in zip(self.jobs, self.uses):
            if fill is fill_down:
                self.scratch.append(pltpu.VMEM((OWN_FF, D), f32))
            if fill is fill_stream:
                self.in_specs[use[0]] = there
                left, right = (self.operands[u] for u in use)
                self.scratch += [pltpu.VMEM((2,) + left.shape[1:], bf16), pltpu.VMEM((right.shape[2], D), f32), dma((REP,))]
        self.out_specs = [pl.BlockSpec(memory_space=pltpu.VMEM)] * n

    def steps(self, place, operands, mids, scratch):
        send, recv, *rooms = scratch
        rings, fills = [], []
        for k, (i, fill) in enumerate(self.jobs):
            grad, first, second = rooms[3 * k : 3 * k + 3]
            rings.append(large_ring(place, grad, REDUCE_BLOCKS[i][2], first, second, (send.at[k], recv.at[k])))
            extra = rooms[3 * len(self.jobs) :]
            more = extra if fill in (fill_down, fill_stream) else []
            left, right = (operands[u] for u in self.uses[k])
            fills.append(lambda fill=fill, left=left, right=right, grad=grad, more=more: fill(left, right, grad, *more))

        def begin():
            fills[0]()
            rings[0].start()

        def rest():
            for fill, ring in zip(fills[1:], rings[1:]):
                fill()
                ring.start()

        def nothing():
            pass

        def middle():
            for ring in rings:
                ring.middle(each_of_four)

        def end():
            for ring, mid in zip(rings, mids):
                ring.finish(each_of_four, large_store(mid))
            for ring in rings:
                ring.drain()

        return [begin, rest, nothing, middle, end]


def boundary_kernel(n_pairs, turned, forward, gathers, rider, *refs):
    pairs = [(refs[2 * i], refs[2 * i + 1]) for i in range(n_pairs)]
    rest = refs[2 * n_pairs :]
    if forward:
        hidden_ref, gain_ref, *rest = rest
    else:
        values_ref, hidden_ref, gain_ref, *rest = rest
    n_ride = len(rider.operands) if rider else 0
    riding, rest = rest[:n_ride], rest[n_ride:]
    out_ref, *rest = rest
    if not forward:
        acc_ref, *rest = rest
    if gathers:
        all_ref, *rest = rest
    n_ridden = len(rider.shapes) if rider else 0
    ridden, rest = rest[:n_ridden], rest[n_ridden:]
    core_send, core_recv, far_send, far_recv, near_sum, send_sems, recv_sems, *rest = rest
    place = Place()
    rep, chip, core, theirs, far, near = place.rep, place.chip, place.core, place.theirs, place.far, place.near
    barrier = pltpu.get_barrier_semaphore()
    devices = [far, near]
    steps = []
    if rider:
        devices += [place.pair] + place.neighbours()
        steps = rider.steps(place, riding, ridden, rest)

    def ride():
        if steps:
            steps.pop(0)()

    for device in devices:
        pl.semaphore_signal(barrier, inc=1, device_id=device, device_id_type=MESH)

    def partial(r):
        product = right_contract if turned else matmul
        total = product(pairs[0][0][r], pairs[0][1][...])
        for left, right in pairs[1:]:
            total = total + product(left[r], right[...])
        return total

    def copy(source, target, i, device):
        return remote(source, target, send_sems.at[i], recv_sems.at[i], device)

    half = ROWS
    chunks = [pl.ds(c * half, half) for c in range(MICRO)]
    to_core = []
    for i, there in enumerate((1 - chip, chip)):
        core_send[i] = partial(there * 2 + 1 - core).astype(bf16)
        to_core.append(copy(core_send.at[i], core_recv.at[i], i, near))
        if i == 0:
            pl.semaphore_wait(barrier, len(devices))
        to_core[i].start()
    far_own = partial(theirs)
    to_core[0].wait_recv()
    far_send[...] = (far_own + core_recv[0].astype(f32)).astype(bf16)
    to_far = [copy(far_send.at[rows], far_recv.at[rows], 2 + c, far) for c, rows in enumerate(chunks)]
    for sent in to_far:
        sent.start()
    near_own = partial(rep)
    to_core[1].wait_recv()
    near_sum[...] = near_own + core_recv[1].astype(f32)
    ride()
    spread, onward = [], []
    acc = None
    for c, rows in enumerate(chunks):
        to_far[c].wait_recv()
        total = near_sum[rows, :] + far_recv[rows, :].astype(f32)
        gain = gain_ref[...]
        if forward:
            fresh = hidden_ref[rows, :].astype(f32) + total
            sent = (fresh * norm_parts(fresh) * gain).astype(bf16)
        else:
            values = values_ref[rows, :].astype(f32)
            rho = norm_parts(values)
            scaled = gain * total
            inner = jnp.mean(values * scaled, axis=-1, keepdims=True)
            fresh = hidden_ref[rows, :].astype(f32) + rho * scaled - values * (rho * rho * rho * inner)
            part = jnp.sum(values * rho * total, axis=0, keepdims=True)
            acc = part if acc is None else acc + part
            sent = fresh.astype(bf16)
        out_ref[rows, :] = fresh
        if gathers:
            all_ref[rep, rows, :] = sent
            mine = all_ref.at[rep, rows]
            other = all_ref.at[theirs, rows]
            spread.append((copy(mine, mine, 4 + c, far), copy(mine, mine, 6 + c, near)))
            onward.append(copy(other, other, 8 + c, near))
            for one in spread[c]:
                one.start()
        ride()
    if not forward:
        acc_ref[...] = acc
    for c in range(len(onward)):
        spread[c][0].wait_recv()
        onward[c].start()
    ride()
    for c in range(len(onward)):
        spread[c][1].wait_recv()
        onward[c].wait_recv()
    ride()
    for sent in to_core + to_far + [one for two in spread for one in two] + onward:
        sent.wait_send()


def boundary(name, identity, pairs, turned, hidden, gain, values=None, gathers=True, rider=None):
    own = MICRO * ROWS
    forward = values is None
    operands = [a.reshape(REP, own, -1) if i == 0 else a for pair in pairs for i, a in enumerate(pair)]
    operands += ([] if forward else [values]) + [hidden, gain.reshape(1, D)]
    in_specs = [pl.BlockSpec(memory_space=pltpu.VMEM)] * len(operands)
    shapes = [jax.ShapeDtypeStruct((own, D), f32)]
    if not forward:
        shapes.append(jax.ShapeDtypeStruct((1, D), f32))
    if gathers:
        shapes.append(jax.ShapeDtypeStruct((REP, own, D), bf16))
    here = pl.BlockSpec(memory_space=pltpu.VMEM)
    out_specs = [here] * len(shapes)
    if rider:
        operands += rider.operands
        in_specs += rider.in_specs
        shapes += rider.shapes
        out_specs += rider.out_specs
    dma = pltpu.SemaphoreType.DMA
    return pl.pallas_call(
        lambda *refs: boundary_kernel(len(pairs), turned, forward, gathers, rider, *refs),
        name=name,
        in_specs=in_specs,
        out_specs=out_specs,
        out_shape=shapes,
        scratch_shapes=[
            pltpu.VMEM((2, own, D), bf16),
            pltpu.VMEM((2, own, D), bf16),
            pltpu.VMEM((own, D), bf16),
            pltpu.VMEM((own, D), bf16),
            pltpu.VMEM((own, D), f32),
            dma((10,)),
            dma((10,)),
        ]
        + (rider.scratch if rider else []),
        compiler_params=pltpu.CompilerParams(
            collective_id=identity, has_side_effects=True, vmem_limit_bytes=(36 if identity == 5 else 24) * mebibyte
        ),
        cost_estimate=estimate(1 << 30, 32 << 20, 0),
    )(*operands)


FINAL_COLUMNS = (
    (0, 0, QW),
    (0, QW, KW),
    (0, QW + KW, KW),
    (1, 0, KW),
    (1, KW, KW),
    (2, 0, QW),
    (3, 0, OWN_FF),
    (4, 0, OWN_FF),
)


def finish_kernel(*refs):
    n = len(COLUMN_BLOCKS) + len(PIECE_BLOCKS)
    columns, pieces = refs[: len(COLUMN_BLOCKS)], refs[len(COLUMN_BLOCKS) : n]
    kv_refs, w_ref = refs[n : n + REP], refs[n + REP]
    finals, enc_ref = refs[n + REP + 1 : -1], refs[-1]
    rep = lax.axis_index("rep")
    chip, core = lax.div(rep, 2), lax.rem(rep, 2)
    total = None
    for i, kv_ref in enumerate(kv_refs):
        there, which = (1 - chip if i // 2 else chip), (1 - core if i % 2 else core)
        lanes = pl.ds(pl.multiple_of(there * 2 * KW, 2 * KW), 2 * KW)
        part = right_contract(kv_ref[...], w_ref[which, :, lanes])
        total = part if total is None else total + part
    enc_ref[...] = total

    @pl.when(pl.program_id(0) == 0)
    def _():
        for final, (source, first, width) in zip(finals, FINAL_COLUMNS):
            parts = [columns[source][r, :, first : first + width].astype(f32) for r in range(REP)]
            final[...] = jnp.concatenate(parts, axis=1)
        for final, piece in zip(finals[len(FINAL_COLUMNS) :], pieces):
            rows = piece.shape[1]
            for q in range(REP):
                skip = REP * rows - final.shape[0] if q == REP - 1 else 0
                final[q * rows : (q + 1) * rows - skip, :] = piece[q, skip:, :].astype(f32)


def finish(columns, pieces, kv_parts, w_ckv):
    shapes = [jax.ShapeDtypeStruct((columns[i].shape[1], REP * width), f32) for i, _, width in FINAL_COLUMNS]
    shapes += [jax.ShapeDtypeStruct((tall, D), f32) for tall in (FF // SHARDS, 32, 32)]
    shapes.append(jax.ShapeDtypeStruct((kv_parts[0].shape[0], D), f32))
    tall = kv_parts[0].shape[0] // 4
    some = pl.BlockSpec((tall, D), lambda i: (i, 0))
    return pl.pallas_call(
        finish_kernel,
        name="finish",
        grid=(4,),
        in_specs=[fixed_block(value.shape) for value in columns + pieces]
        + [pl.BlockSpec((tall, 2 * KW), lambda i: (i, 0))] * REP
        + [fixed_block(w_ckv.shape)],
        out_specs=[fixed_block(shape.shape) for shape in shapes[:-1]] + [some],
        out_shape=shapes,
        compiler_params=pltpu.CompilerParams(vmem_limit_bytes=56 * mebibyte),
        cost_estimate=estimate(2 << 30, 12 << 20, 0),
    )(*columns, *pieces, *kv_parts, w_ckv)


def local(
    tokens,
    out_cotangent,
    encoded,
    segment_ids,
    doc_block,
    bucket_table,
    self_gain,
    query_weight,
    key_weight,
    value_weight,
    out_weight,
    bias_table,
    cross_gain,
    cross_query,
    cross_key,
    cross_value,
    cross_out,
    feed_gain,
    gate_weight,
    up_weight,
    down_weight,
):
    rep = lax.axis_index("rep")
    own = MICRO * ROWS
    enc_rows = MICRO * DOCS * ENC // REP

    def columns(weight, width):
        return lax.dynamic_slice_in_dim(weight, rep * width, width, 1)

    small = sum(
        jnp.pad(value.reshape(1, -1), ((0, 7), (32 * i, 128 - 32 * i - value.size)))
        for i, value in enumerate((self_gain, cross_gain, feed_gain, bias_table))
    )
    own_tokens = tokens.reshape(own, D)
    own_cotangent = out_cotangent.reshape(own, D)
    wholes, (all_tokens, all_enc, all_grad) = gather_weights(
        [
            query_weight,
            key_weight,
            value_weight,
            cross_key,
            cross_value,
            cross_query,
            small,
            columns(gate_weight, OWN_FF),
            columns(up_weight, OWN_FF),
            down_weight,
            out_weight,
            cross_out,
        ],
        [own_tokens, encoded.reshape(enc_rows, D), own_cotangent],
    )
    w_qkv, w_ckv, w_cq, small, w_gate, w_up, w_down, w_out, w_cout = wholes
    w_gate = w_gate.reshape(D, OWN_FF)
    w_up = w_up.reshape(D, OWN_FF)
    w_qkv = w_qkv.reshape(D, QW + 2 * KW)
    small = small.reshape(SHARDS, 8, 128)[:, 0]
    w_out = w_out.reshape(QW, D)
    w_ckv = w_ckv.reshape(2, D, REP * KW)
    own_ckv = lax.dynamic_slice(w_ckv, (rep % 2, 0, rep // 2 * 2 * KW), (1, D, 2 * KW))[0]
    w_cq = w_cq.reshape(D, QW)
    w_cout = w_cout.reshape(QW, D)
    w_down = w_down.reshape(SHARDS, 24, D)
    self_factor = small[:, 0:32].reshape(D).astype(f32)
    cross_factor = small[:, 32:64].reshape(D).astype(f32)
    feed_factor = small[:, 64:96].reshape(D).astype(f32)
    table = small[:, 96:112]

    segments = segment_ids[:, 0]
    seg_col = segments[:, :, None]
    seg_row = segments[:, None, :]
    blocks = doc_block[:, 0].reshape(-1)
    doc_ids = jnp.arange(DOCS, dtype=jnp.int32)
    starts = jnp.sum((segments[:, None, :] < doc_ids[None, :, None]).astype(jnp.int32), axis=2)
    sizes = jnp.sum((segments[:, None, :] == doc_ids[None, :, None]).astype(jnp.int32), axis=2)
    wides = (sizes > NARROW - 16).astype(jnp.int32)
    starts = jnp.minimum(starts // 16 * 16, jnp.where(wides == 0, SEQ - NARROW, SEQ - WINDOW)).reshape(-1)
    wides = wides.reshape(-1)
    turned = jnp.roll(bucket_table[::-1], 1)
    hot = (turned[None, :] == jnp.arange(BUCKETS, dtype=jnp.int32)[:, None]).astype(bf16)
    own_table = lax.dynamic_slice_in_dim(table, rep * OWN_HEADS, OWN_HEADS, 1)
    curve = left_contract(own_table, hot)
    curve = jnp.pad(curve, ((0, 4), (0, 0)))

    all_tokens = all_tokens.reshape(REP, MICRO, ROWS, D)
    all_grad = all_grad.reshape(REP * own, D)

    all_enc = all_enc.reshape(REP * enc_rows, D)

    normed, qkv, context = self_forward(all_tokens, self_factor.reshape(1, D), w_qkv, seg_col, seg_row, curve)
    normed = normed.reshape(REP * own, D)
    context = context.reshape(REP * own, QW)
    hidden, cross_normed = boundary("after_self", 1, [(context, w_out)], False, own_tokens, cross_factor)
    kv = matmul(all_enc, own_ckv).astype(bf16).reshape(REP, MICRO, DOCS, ENC // REP, 2 * KW)
    cross_normed = cross_normed.reshape(REP * own, D)
    cross_queries = matmul(cross_normed, w_cq).astype(bf16).reshape(REP, MICRO, ROWS, QW)
    cross_context = cross_forward(blocks, starts, wides, cross_queries, kv, seg_col).reshape(REP * own, QW)
    hidden_two, feed_normed = boundary("after_cross", 2, [(cross_context, w_cout)], False, hidden, feed_factor)
    feed_normed = feed_normed.reshape(REP * own, D)
    inner, gate_low, up_low, layer_part = feed(feed_normed.reshape(REP, own, D), all_grad.reshape(REP, own, D), w_gate, w_up, w_down)
    inner = inner.reshape(REP * own, OWN_FF)
    gate_low = gate_low.reshape(REP * own, OWN_FF)
    up_low = up_low.reshape(REP * own, OWN_FF)

    hidden_grad, feed_acc, branch, gate_mid, up_mid = boundary(
        "before_feed",
        3,
        [(gate_low, w_gate), (up_low, w_up)],
        True,
        own_cotangent,
        feed_factor,
        hidden_two,
        rider=ReduceRider([(3, fill_columns, feed_normed, gate_low), (4, fill_columns, feed_normed, up_low)]),
    )
    branch = branch.reshape(REP * own, D)
    context_grad = right_contract(branch, w_cout).astype(bf16).reshape(REP, MICRO, ROWS, QW)
    cq_grad, kv_grad = cross_backward(blocks, starts, wides, cross_queries, kv, context_grad, seg_col)
    cq_grad = cq_grad.reshape(REP * own, QW)
    kv_grad = kv_grad.reshape(REP, enc_rows, 2 * KW)
    hidden_grad, cross_acc, first_branch, down_mid, cq_mid, cout_mid = boundary(
        "before_cross",
        4,
        [(cq_grad, w_cq)],
        True,
        hidden_grad,
        cross_factor,
        hidden,
        rider=ReduceRider(
            [
                (5, fill_down, inner, all_grad),
                (2, fill_columns, cross_normed, cq_grad),
                (7, fill_rows, cross_context, branch),
            ]
        ),
    )
    first_branch = first_branch.reshape(REP * own, D)
    sent, first_branch = lax.optimization_barrier((kv_grad, first_branch))
    kv_parts = [
        kv_grad[0],
        lax.ppermute(sent[1], "rep", swap_core),
        lax.ppermute(sent[2], "rep", swap_chip),
        lax.ppermute(sent[3], "rep", swap_both),
    ]

    context_grad = right_contract(first_branch, w_out).astype(bf16).reshape(REP, MICRO, ROWS, QW)
    qkv_grad, curve_grad = self_backward(qkv, context_grad, seg_col, seg_row, curve)
    qkv_grad = qkv_grad.reshape(REP * own, QW + 2 * KW)
    tokens_grad, self_acc, qkv_mid, out_mid, ckv_mid = boundary(
        "before_self",
        5,
        [(qkv_grad, w_qkv)],
        True,
        hidden_grad,
        self_factor,
        own_tokens,
        False,
        ReduceRider(
            [
                (0, fill_columns, normed, qkv_grad),
                (6, fill_rows, context, first_branch),
                (1, fill_stream, all_enc.reshape(REP, enc_rows, D), kv_grad),
            ]
        ),
    )

    mids = [qkv_mid, ckv_mid, cq_mid, gate_mid, up_mid, down_mid, out_mid, cout_mid]
    *whole, small_sum, layer_out = reduce_grads(
        layer_part,
        hidden_two,
        [self_acc, cross_acc, feed_acc],
        curve_grad,
        hot,
        mids,
    )
    *finals, encoder_grad = finish(whole[: len(COLUMN_BLOCKS)], whole[len(COLUMN_BLOCKS) :], kv_parts, w_ckv)
    query_grad, key_grad, value_grad, ck_grad, cv_grad, cq_grad, gate_grad, up_grad, down_grad, out_grad, cout_grad = finals
    small_sum = small_sum[0]
    return (
        layer_out.reshape(tokens.shape),
        tokens_grad.reshape(tokens.shape),
        encoder_grad.reshape(encoded.shape),
        small_sum[0:32],
        query_grad,
        key_grad,
        value_grad,
        out_grad,
        small_sum[96:112].reshape(1, HEADS),
        small_sum[32:64],
        cq_grad,
        ck_grad,
        cv_grad,
        cout_grad,
        small_sum[64:96],
        gate_grad,
        up_grad,
        down_grad,
    )


def solution(mesh):
    rows = P("shard", None)
    gain = P("shard")
    acts = P(None, "shard", "rep", None)
    encs = P(None, "shard", None, "rep", None)
    ids = P(None, "shard", None)
    weights = (gain, rows, rows, rows, rows, rows, gain, rows, rows, rows, rows, gain, rows, rows, rows)
    return jax.shard_map(
        local,
        mesh=mesh,
        in_specs=(acts, acts, encs, ids, ids, P()) + weights,
        out_specs=(acts, acts, encs) + weights,
        check_vma=False,
    )
```

```python
import jax
import jax.numpy as jnp
from jax import lax
from jax.experimental import pallas as pl
from jax.experimental.pallas import tpu as pltpu
from jax.sharding import PartitionSpec as P

D = 1024
HEADS = 16
HEAD_DIM = 64
KV_GROUPS = 8
FF = 2816
BUCKETS = 32
ENC = 512
SEQ = 256
DOCS = 4
MICRO = 2

REP = 4
SHARDS = 32
ROWS = SEQ // REP
OWN_HEADS = HEADS // REP
OWN_GROUPS = KV_GROUPS // REP
QW = OWN_HEADS * HEAD_DIM
KW = OWN_GROUPS * HEAD_DIM
OWN_FF = FF // REP
WINDOW = 144
NARROW = 80

epsilon = 1e-06
neg_big = -1e30
gelu_scale = 0.7978845608028654
gelu_cube = 0.044715
f32 = jnp.float32
bf16 = jnp.bfloat16
mebibyte = 1024 * 1024


def matmul(left, right):
    return jnp.dot(left, right, preferred_element_type=f32)


def left_contract(left, right):
    return lax.dot_general(left, right, (((0,), (0,)), ((), ())), preferred_element_type=f32)


def right_contract(left, right):
    return lax.dot_general(left, right, (((1,), (1,)), ((), ())), preferred_element_type=f32)


def skewed(row):
    n = row.shape[1]
    out = jnp.broadcast_to(row, (n, n))
    at = lax.broadcasted_iota(jnp.int32, (n, n), 0)
    step = 1
    while step < n:
        out = jnp.where((at & step) != 0, pltpu.roll(out, step, 1), out)
        step *= 2
    return out


def unskewed_sum(square):
    n = square.shape[1]
    at = lax.broadcasted_iota(jnp.int32, (n, n), 0)
    step = 1
    while step < n:
        square = jnp.where((at & step) != 0, pltpu.roll(square, n - step, 1), square)
        step *= 2
    return jnp.sum(square, axis=0, keepdims=True)


def raised_parts(scores):
    raised = jnp.exp(scores - jnp.max(scores, axis=-1, keepdims=True))
    return raised, 1.0 / jnp.sum(raised, axis=-1, keepdims=True)


def group_rows(rows, group):
    first = group * OWN_HEADS // OWN_GROUPS
    heads = range(first, first + OWN_HEADS // OWN_GROUPS)
    return jnp.concatenate([rows[:, h * HEAD_DIM : (h + 1) * HEAD_DIM] for h in heads], axis=0)


def group_lanes(stacked):
    n = stacked.shape[0] * OWN_GROUPS // OWN_HEADS
    return [stacked[i * n : (i + 1) * n] for i in range(OWN_HEADS // OWN_GROUPS)]


def lanes_of(values, first, group):
    return values[:, first + group * HEAD_DIM : first + (group + 1) * HEAD_DIM]


def stacked_twice(value):
    return jnp.concatenate([value] * (OWN_HEADS // OWN_GROUPS), axis=0)


def attend_back(scores, query, key, value, grad):
    raised, shrink = raised_parts(scores)
    grad = (grad.astype(f32) * shrink).astype(bf16)
    prob_grad = right_contract(grad, value)
    centre = jnp.sum(raised * prob_grad, axis=-1, keepdims=True) * shrink
    score_grad = (raised * (prob_grad - centre)).astype(bf16)
    return score_grad, matmul(score_grad, key), left_contract(score_grad, query), left_contract(raised.astype(bf16), grad)


def self_mask(seg_row):
    at_query = lax.broadcasted_iota(jnp.int32, (SEQ, SEQ), 0)
    at_key = lax.broadcasted_iota(jnp.int32, (SEQ, SEQ), 1)
    of_key = jnp.broadcast_to(seg_row.astype(f32), (SEQ, SEQ))
    return (at_key <= at_query) & (of_key == of_key.T)


def bucket_hot(buckets):
    at = lax.broadcasted_iota(jnp.int32, (BUCKETS, SEQ), 0)
    return (at == buckets).astype(f32).astype(bf16)


def fill_bias(curve_ref, bias_ref):
    for head in range(OWN_HEADS):
        bias_ref[head] = skewed(curve_ref[head : head + 1, :]).T


def self_attention(values, gain, weight, allowed, bias_ref):
    values = values.astype(f32)
    normed = (values * norm_parts(values) * gain).astype(bf16)
    whole = matmul(normed, weight).astype(bf16)
    allowed = stacked_twice(allowed.astype(jnp.int32)) != 0
    mixed = []
    for group in range(OWN_GROUPS):
        scores = right_contract(group_rows(whole, group), lanes_of(whole, QW, group))
        scores = jnp.where(allowed, scores + bias_ref[2 * group : 2 * group + 2].reshape(2 * SEQ, SEQ), neg_big)
        raised, shrink = raised_parts(scores)
        mixed += group_lanes(matmul(raised.astype(bf16), lanes_of(whole, QW + KW, group)) * shrink)
    return normed, whole, jnp.concatenate(mixed, axis=1).astype(bf16)


def unpack_small(rep, small, hot, gains_ref, curve_ref):
    rows = jnp.sum(small.astype(f32).reshape(SHARDS, 8, 128), axis=1).astype(bf16)
    per = D // SHARDS
    lane = lax.broadcasted_iota(jnp.int32, (128, D), 0)
    column = lax.broadcasted_iota(jnp.int32, (128, D), 1)
    owner = lax.broadcasted_iota(jnp.int32, (SHARDS, D), 0)
    entry = lax.broadcasted_iota(jnp.int32, (SHARDS, D), 1)
    gains_ref[...] = jnp.zeros_like(gains_ref)
    for i in range(3):
        ones = (lax.rem(column, per) == lane - per * i).astype(f32).astype(bf16)
        spread = jnp.where(lax.div(entry, per) == owner, matmul(rows, ones), 0.0)
        gains_ref[i : i + 1, :] = jnp.sum(spread, axis=0, keepdims=True)
    head = lax.broadcasted_iota(jnp.int32, (8, 128), 0)
    place = lax.broadcasted_iota(jnp.int32, (8, 128), 1)
    ones = ((head < OWN_HEADS) & (place == 3 * per + OWN_HEADS * rep + head)).astype(f32).astype(bf16)
    curve_ref[...] = matmul(right_contract(ones, rows).astype(bf16), hot)


def self_backward_kernel(
    qkv_ref, grad_ref, seg_row_ref, curve_ref, out_ref, curve_grad_ref, bias_ref, sum_ref
):
    @pl.when(pl.program_id(0) == 0)
    def _():
        fill_bias(curve_ref, bias_ref)
        sum_ref[...] = jnp.zeros_like(sum_ref)

    whole = qkv_ref[...].reshape(SEQ, QW + 2 * KW)
    grads = grad_ref[...].reshape(SEQ, QW)
    allowed = stacked_twice(self_mask(seg_row_ref[0]).astype(jnp.int32)) != 0
    query_grads, key_grads, value_grads = [], [], []
    for group in range(OWN_GROUPS):
        query = group_rows(whole, group)
        key = lanes_of(whole, QW, group)
        scores = right_contract(query, key)
        scores = jnp.where(allowed, scores + bias_ref[2 * group : 2 * group + 2].reshape(2 * SEQ, SEQ), neg_big)
        score_grad, query_grad, key_grad, value_grad = attend_back(
            scores, query, key, lanes_of(whole, QW + KW, group), group_rows(grads, group)
        )
        sum_ref[2 * group : 2 * group + 2] += score_grad.astype(f32).reshape(2, SEQ, SEQ)
        query_grads += group_lanes(query_grad)
        key_grads.append(key_grad)
        value_grads.append(value_grad)
    joined = jnp.concatenate(query_grads + key_grads + value_grads, axis=1)
    out_ref[...] = joined.astype(bf16).reshape(out_ref.shape)

    @pl.when(pl.program_id(0) == MICRO - 1)
    def _():
        curve_grad_ref[...] = jnp.zeros_like(curve_grad_ref)
        for head in range(OWN_HEADS):
            curve_grad_ref[head : head + 1, :] = unskewed_sum(sum_ref[head].T)


def by_window(at, wide_ref, body):
    pl.when(wide_ref[at] == 0)(lambda: body(NARROW))
    pl.when(wide_ref[at] != 0)(lambda: body(WINDOW))


def cross_forward_kernel(block_ref, start_ref, wide_ref, begin_ref, end_ref, q_ref, kv_ref, out_ref, query_ref, mixed_ref):
    at = pl.program_id(0) * DOCS + pl.program_id(1)

    @pl.when(pl.program_id(1) == 0)
    def _():
        query_ref[...] = q_ref[...].reshape(SEQ, QW)

    start = pl.multiple_of(start_ref[at], 16)

    def body(window):
        rows = query_ref[pl.ds(start, window), :]
        row = start + lax.broadcasted_iota(jnp.int32, (window, 1), 0)
        mine = (row >= begin_ref[at]) & (row < end_ref[at])
        both = kv_ref[...].reshape(ENC, 2 * KW)
        mixed = []
        for group in range(OWN_GROUPS):
            raised, shrink = raised_parts(right_contract(group_rows(rows, group), lanes_of(both, 0, group)))
            mixed += group_lanes(matmul(raised.astype(bf16), lanes_of(both, KW, group)) * shrink)
        fresh = jnp.concatenate(mixed, axis=1)
        mixed_ref[pl.ds(start, window), :] = jnp.where(mine, fresh, mixed_ref[pl.ds(start, window), :])

    by_window(at, wide_ref, body)

    @pl.when(pl.program_id(1) == DOCS - 1)
    def _():
        out_ref[...] = mixed_ref[...].astype(bf16).reshape(out_ref.shape)


def cross_backward_kernel(
    block_ref, start_ref, wide_ref, begin_ref, end_ref, q_ref, kv_ref, grad_ref, out_ref, kv_grad_ref, query_ref, given_ref,
    mixed_ref
):
    at = pl.program_id(0) * DOCS + pl.program_id(1)

    @pl.when(pl.program_id(1) == 0)
    def _():
        query_ref[...] = q_ref[...].reshape(SEQ, QW)
        given_ref[...] = grad_ref[...].reshape(SEQ, QW)

    start = pl.multiple_of(start_ref[at], 16)

    def body(window):
        rows = query_ref[pl.ds(start, window), :]
        row = start + lax.broadcasted_iota(jnp.int32, (window, 1), 0)
        mine = (row >= begin_ref[at]) & (row < end_ref[at])
        grads = jnp.where(mine, given_ref[pl.ds(start, window), :].astype(f32), 0.0)
        both = kv_ref[...].reshape(ENC, 2 * KW)
        query_grads, key_grads, value_grads = [], [], []
        for group in range(OWN_GROUPS):
            query, key = group_rows(rows, group), lanes_of(both, 0, group)
            _, query_grad, key_grad, value_grad = attend_back(
                right_contract(query, key), query, key, lanes_of(both, KW, group), group_rows(grads, group)
            )
            query_grads += group_lanes(query_grad)
            key_grads.append(key_grad)
            value_grads.append(value_grad)
        fresh = jnp.concatenate(query_grads, axis=1)
        mixed_ref[pl.ds(start, window), :] = jnp.where(mine, fresh, mixed_ref[pl.ds(start, window), :])
        joined = jnp.concatenate(key_grads + value_grads, axis=1)
        kv_grad_ref[...] = joined.astype(bf16).reshape(kv_grad_ref.shape)

    by_window(at, wide_ref, body)

    @pl.when(pl.program_id(1) == DOCS - 1)
    def _():
        out_ref[...] = mixed_ref[...].astype(bf16).reshape(out_ref.shape)


def feed_kernel(normed_ref, grad_ref, gate_w_ref, up_w_ref, pieces_ref, inner_ref, gate_ref, up_ref, part_ref, down_ref):
    @pl.when(pl.program_id(0) == 0)
    def _():
        for i in range(4):
            pieces = []
            for k in range(8 * i, 8 * i + 8):
                piece = pieces_ref[k].astype(f32)
                pieces.append(piece[8:] if k % REP == REP - 1 else piece)
            down_ref[i * 176 : (i + 1) * 176, :] = jnp.concatenate(pieces, axis=0).astype(bf16)

    normed = normed_ref[...].reshape(-1, D)
    gate = matmul(normed, gate_w_ref[...])
    up_part = matmul(normed, up_w_ref[...])
    inner_grad = right_contract(grad_ref[...].reshape(-1, D), down_ref[...])
    square = gate * gate
    bent = jnp.tanh(gelu_scale * gate * (1.0 + gelu_cube * square))
    rising = 0.5 * (1.0 + bent)
    slope = rising + 0.5 * gate * (1.0 - bent * bent) * (gelu_scale * (1.0 + 3.0 * gelu_cube * square))
    passed = gate * rising
    inner = (passed * up_part).astype(bf16)
    inner_ref[...] = inner.reshape(inner_ref.shape)
    gate_ref[...] = (inner_grad * up_part * slope).astype(bf16).reshape(gate_ref.shape)
    up_ref[...] = (inner_grad * passed).astype(bf16).reshape(up_ref.shape)
    part_ref[...] = matmul(inner, down_ref[...]).astype(bf16).reshape(part_ref.shape)


def feed(normed, grads, w_gate, w_up, down_pieces):
    own = MICRO * ROWS

    def some(width):
        return pl.BlockSpec((2, own, width), lambda i: (i, 0, 0))

    units = jax.ShapeDtypeStruct((REP, own, OWN_FF), bf16)
    return pl.pallas_call(
        feed_kernel,
        name="feed",
        grid=(REP // 2,),
        in_specs=[
            some(D),
            some(D),
            fixed_block(w_gate.shape),
            fixed_block(w_up.shape),
            fixed_block(down_pieces.shape),
        ],
        out_specs=[some(OWN_FF)] * 3 + [some(D)],
        out_shape=[units, units, units, jax.ShapeDtypeStruct((REP, own, D), bf16)],
        scratch_shapes=[pltpu.VMEM((OWN_FF, D), bf16)],
        compiler_params=pltpu.CompilerParams(vmem_limit_bytes=32 * mebibyte),
        cost_estimate=estimate(3 << 30, 8 << 20, 1 << 19),
    )(normed, grads, w_gate, w_up, down_pieces)


def rows_block(width):
    return pl.BlockSpec((REP, 1, ROWS, width), lambda m, *rest: (0, m, 0, 0))


def fixed_block(shape):
    return pl.BlockSpec(shape, lambda *at: (0,) * len(shape))


def micro_block(shape):
    return pl.BlockSpec((1,) + shape, lambda m, *rest: (m,) + (0,) * len(shape))


def estimate(flops, moved, raised):
    return pl.CostEstimate(flops=flops, bytes_accessed=moved, transcendentals=raised)


self_pairs = MICRO * OWN_HEADS * SEQ * SEQ
cross_pairs = MICRO * OWN_HEADS * DOCS * WINDOW * ENC


def self_backward(qkv, grads, seg_row, curve):
    return pl.pallas_call(
        self_backward_kernel,
        name="self_backward",
        grid=(MICRO,),
        in_specs=[
            rows_block(QW + 2 * KW),
            rows_block(QW),
            micro_block((1, SEQ)),
            fixed_block((8, SEQ)),
        ],
        out_specs=[rows_block(QW + 2 * KW), fixed_block((8, SEQ))],
        out_shape=[
            jax.ShapeDtypeStruct((REP, MICRO, ROWS, QW + 2 * KW), bf16),
            jax.ShapeDtypeStruct((8, SEQ), f32),
        ],
        scratch_shapes=[
            pltpu.VMEM((OWN_HEADS, SEQ, SEQ), f32),
            pltpu.VMEM((OWN_HEADS, SEQ, SEQ), f32),
        ],
        compiler_params=pltpu.CompilerParams(vmem_limit_bytes=18 * mebibyte),
        cost_estimate=estimate(self_pairs * 640, 3 << 20, self_pairs),
    )(qkv, grads, seg_row, curve)


def cross_rows():
    return pl.BlockSpec((REP, 1, ROWS, QW), lambda m, d, block, *rest: (0, m, 0, 0))


def cross_keys():
    return pl.BlockSpec(
        (REP, 1, 1, ENC // REP, 2 * KW),
        lambda m, d, block, *rest: (0, m, block[m * DOCS + d], 0, 0),
    )


def cross_forward(spans, queries, kv):
    return pl.pallas_call(
        cross_forward_kernel,
        name="cross_forward",
        grid_spec=pltpu.PrefetchScalarGridSpec(
            num_scalar_prefetch=5,
            grid=(MICRO, DOCS),
            in_specs=[cross_rows(), cross_keys()],
            out_specs=cross_rows(),
            scratch_shapes=[pltpu.VMEM((SEQ, QW), bf16), pltpu.VMEM((SEQ, QW), f32)],
        ),
        out_shape=jax.ShapeDtypeStruct((REP, MICRO, ROWS, QW), bf16),
        compiler_params=pltpu.CompilerParams(vmem_limit_bytes=16 * mebibyte),
        cost_estimate=estimate(cross_pairs * 256, 3 << 20, cross_pairs),
    )(*spans, queries, kv)


def cross_backward(spans, queries, kv, grads):
    return pl.pallas_call(
        cross_backward_kernel,
        name="cross_backward",
        grid_spec=pltpu.PrefetchScalarGridSpec(
            num_scalar_prefetch=5,
            grid=(MICRO, DOCS),
            in_specs=[cross_rows(), cross_keys(), cross_rows()],
            out_specs=[cross_rows(), cross_keys()],
            scratch_shapes=[
                pltpu.VMEM((SEQ, QW), bf16),
                pltpu.VMEM((SEQ, QW), bf16),
                pltpu.VMEM((SEQ, QW), f32),
            ],
        ),
        out_shape=[
            jax.ShapeDtypeStruct((REP, MICRO, ROWS, QW), bf16),
            jax.ShapeDtypeStruct((REP, MICRO, DOCS, ENC // REP, 2 * KW), bf16),
        ],
        compiler_params=pltpu.CompilerParams(vmem_limit_bytes=20 * mebibyte),
        cost_estimate=estimate(cross_pairs * 640, 6 << 20, cross_pairs),
    )(*spans, queries, kv, grads)


MESH = pl.DeviceIdType.MESH

swap_core = [(i, i ^ 1) for i in range(REP)]
swap_chip = [(i, i ^ 2) for i in range(REP)]
swap_both = [(i, i ^ 3) for i in range(REP)]


def remote(source, target, send_sem, recv_sem, device):
    return pltpu.make_async_remote_copy(
        src_ref=source,
        dst_ref=target,
        send_sem=send_sem,
        recv_sem=recv_sem,
        device_id=device,
        device_id_type=MESH,
    )


class Ring:
    def __init__(self, group, half, me, device_at, send_sems, recv_sems):
        right, left = lax.rem(me + 1, 4), lax.rem(me + 3, 4)
        to_right, to_left = device_at(right), device_at(left)

        def copy(ref, device, i):
            return remote(ref, ref, send_sems.at[i], recv_sems.at[i], device)

        self.direct = [copy(group(me), to_right, 0), copy(group(me), to_left, 1)]
        self.passed = [copy(half(left, 0), to_right, 2), copy(half(right, 1), to_left, 3)]

    def start(self):
        for copy in self.direct:
            copy.start()

    def forward(self):
        for arrived, onward in zip(self.direct, self.passed):
            arrived.wait_recv()
            onward.start()

    def finish(self):
        for copy in self.passed:
            copy.wait_recv()

    def drain(self):
        for copy in self.direct + self.passed:
            copy.wait_send()


class Place:
    def __init__(self):
        self.at = at = lax.axis_index("shard")
        self.rep = rep = lax.axis_index("rep")
        self.x, self.y, self.z = lax.div(at, 8), lax.rem(lax.div(at, 2), 4), lax.rem(at, 2)
        self.chip, self.core = chip, core = lax.div(rep, 2), lax.rem(rep, 2)
        self.pair = {"shard": at + 1 - 2 * self.z}
        self.theirs = (1 - chip) * 2 + core
        self.far = {"rep": self.theirs}
        self.near = {"rep": chip * 2 + 1 - core}

    def on_x(self, i):
        return {"shard": i * 8 + self.y * 2 + self.z}

    def on_y(self, i):
        return {"shard": self.x * 8 + i * 2 + self.z}

    def neighbours(self):
        return [self.on_x(lax.rem(self.x + d, 4)) for d in (1, 3)] + [
            self.on_y(lax.rem(self.y + d, 4)) for d in (1, 3)
        ]


class Gather:
    def __init__(self, place, block, whole, first_x, sems):
        x, y, z = place.x, place.y, place.z
        pair_send, pair_recv, ring_send, ring_recv = sems
        slot = whole.at[x, y, z]
        self.pair = remote(slot if block is None else block, slot, pair_send, pair_recv, place.pair)

        def x_small(j):
            return whole.at[j, y]

        def x_small_half(j, h):
            return whole.at[j, y, h]

        def y_small(j):
            return whole.at[x, j]

        def y_small_half(j, h):
            return whole.at[x, j, h]

        def x_large(j):
            return whole.at[j]

        def x_large_half(j, h):
            return whole.at[j, pl.ds(2 * h, 2)]

        def y_large(j):
            return whole.at[:, j]

        def y_large_half(j, h):
            return whole.at[pl.ds(2 * h, 2), j]

        near, wide = (ring_send.at[0], ring_recv.at[0]), (ring_send.at[1], ring_recv.at[1])
        if first_x:
            self.small = Ring(x_small, x_small_half, x, place.on_x, *near)
            self.large = Ring(y_large, y_large_half, y, place.on_y, *wide)
        else:
            self.small = Ring(y_small, y_small_half, y, place.on_y, *near)
            self.large = Ring(x_large, x_large_half, x, place.on_x, *wide)

    def drain(self):
        self.pair.wait_send()
        self.small.drain()
        self.large.drain()


GATHER_BLOCKS = (
    (32, QW + 2 * KW, True),
    (32, REP * KW, True),
    (32, QW, True),
    (8, 128, True),
    (32, OWN_FF, True),
    (32, OWN_FF, False),
    (24, D, False),
    (8, D, False),
    (8, D, False),
)
GATHER_HELD = 6
GATHER_ROWS = (1, 4, 1)
GATHER_CHUNKS = sum(GATHER_ROWS)


def gather_kernel(*refs):
    query, key, value, cross_key, cross_value, cross_query, small, gate, up, down, out, cross_out = refs[:12]
    seg_row, buckets = refs[12:14]
    n, n_rows = len(GATHER_BLOCKS), len(GATHER_ROWS)
    own_rows, refs = refs[14 : 14 + n_rows], refs[14 + n_rows :]
    wholes, all_rows, refs = refs[:n], refs[n : n + n_rows], refs[n + n_rows :]
    gains_out, curve_out, normed_out, qkv_out, context_out, kv_out, *refs = refs
    (local_sems, out_sems, piece_send, piece_recv, pair_send, pair_recv, ring_send, ring_recv, rep_send, rep_recv,
     load_sems, token_held, qkv_held, small_held, ckv_held, enc_held, bias_ref, *held) = refs
    held, held_rows = held[:GATHER_HELD], held[GATHER_HELD:]
    place = Place()
    at, rep, x, y, z = place.at, place.rep, place.x, place.y, place.z
    barrier = pltpu.get_barrier_semaphore()
    devices = [place.pair, place.far, place.near] + place.neighbours()
    for device in devices:
        pl.semaphore_signal(barrier, inc=1, device_id=device, device_id_type=MESH)
    goal = 4 * lax.rem(at, 8) + rep
    stays = (x == rep) & (goal == at)
    source = {"rep": lax.rem(at, 4), "shard": 8 * rep + lax.div(at, 4)}

    @pl.when(jnp.logical_not(stays))
    def _():
        pl.semaphore_signal(barrier, inc=1, device_id=source, device_id_type=MESH)

    pl.semaphore_wait(barrier, len(devices) + 1 - stays.astype(jnp.int32))

    wholes = list(wholes)
    halves = wholes[1]
    wholes[1] = halves.at[place.core]
    slots = [whole.at[x, y, z] for whole in wholes]
    count = [0]

    def own(source_ref, target):
        count[0] += 1
        return pltpu.make_async_copy(source_ref, target, local_sems.at[count[0] - 1])

    def part(ref, width, r=rep):
        return ref.at[:, pl.ds(pl.multiple_of(r * width, 128), width)]

    fills = [
        [
            own(part(query, QW), held[0].at[:, pl.ds(0, QW)]),
            own(part(key, KW), held[0].at[:, pl.ds(QW, KW)]),
            own(part(value, KW), held[0].at[:, pl.ds(QW + KW, KW)]),
        ],
        [
            own(part(cross_key, KW, place.core), held[1].at[:, pl.ds(0, KW)]),
            own(part(cross_value, KW, place.core), held[1].at[:, pl.ds(KW, KW)]),
            own(part(cross_key, KW, 2 + place.core), held[1].at[:, pl.ds(2 * KW, KW)]),
            own(part(cross_value, KW, 2 + place.core), held[1].at[:, pl.ds(3 * KW, KW)]),
        ],
        [own(part(cross_query, QW), held[2])],
        [own(small, held[3])],
        [own(gate, held[4])],
        [own(up, held[5])],
    ]
    firsts = [pl.multiple_of(24 * rep - 8 * lax.div(rep, 3), 8)] + [pl.multiple_of(8 * rep, 8)] * 2
    pieces = []
    for i, ref in enumerate((down, out, cross_out)):
        whole = wholes[GATHER_HELD + i]
        rows = ref.at[pl.ds(firsts[i], GATHER_BLOCKS[GATHER_HELD + i][0])]
        landing = whole.at[lax.div(goal, 8), lax.rem(lax.div(goal, 2), 4), lax.rem(goal, 2)]
        sent = remote(rows, landing, piece_send.at[i], piece_recv.at[i], {"rep": x, "shard": goal})
        pieces.append((sent, own(rows, landing)))
    for sent, stay in pieces:
        pl.when(jnp.logical_not(stays))(sent.start)
        pl.when(stays)(stay.start)
    for fill in fills:
        for copy in fill:
            copy.start()

    rep_first, rep_second, rep_local = [], [], []
    for i, parts in enumerate(GATHER_ROWS):
        whole = all_rows[i]
        rows = own_rows[i].shape[0] // parts
        first, second = (0, 1) if i == 1 else (rep, rep)
        third, fourth = (2, 3) if i == 1 else (place.theirs, place.theirs)
        landing = 2 if i == 1 else rep
        rep_local.append((own(own_rows[i], held_rows[i]), pltpu.make_async_copy(held_rows[i], whole.at[first], out_sems.at[n + i])))
        rep_local[i][0].start()
        for p in range(parts):
            span = pl.ds(p * rows, rows)
            j = len(rep_first)
            mine = own_rows[i].at[span]
            rep_first.append(remote(mine, whole.at[landing, span], rep_send.at[j, 0], rep_recv.at[j, 0], place.far))
            direct = remote(mine, whole.at[second, span], rep_send.at[j, 1], rep_recv.at[j, 1], place.near)
            onward = remote(whole.at[third, span], whole.at[fourth, span], rep_send.at[j, 2], rep_recv.at[j, 2], place.near)
            rep_second.append((direct, onward))

    gathers = []
    for i, (_, _, first_x) in enumerate(GATHER_BLOCKS):
        block = held[i] if i < GATHER_HELD else None
        sems = pair_send.at[i], pair_recv.at[i], ring_send.at[i], ring_recv.at[i]
        gathers.append(Gather(place, block, wholes[i], first_x, sems))
    settled = []
    for i in range(n):
        if i < GATHER_HELD:
            for copy in fills[i]:
                copy.wait()
            settled.append(pltpu.make_async_copy(held[i], slots[i], out_sems.at[i]))
            settled[i].start()
        else:
            sent, stay = pieces[i - GATHER_HELD]
            pl.when(jnp.logical_not(stays))(sent.wait_recv)
            pl.when(stays)(stay.wait)
        gathers[i].pair.start()
    for first, (direct, _) in zip(rep_first, rep_second):
        first.start()
        direct.start()
    for inward, outward in rep_local:
        inward.wait()
        outward.start()
    for i in range(n):
        if i < GATHER_HELD:
            settled[i].wait()
        gathers[i].pair.wait_recv()
        gathers[i].small.start()
    for one in gathers:
        one.small.forward()
    early, late, sideways = (0, 3, 1, 2), (4,), (7, 8, 6, 5)
    for i in early + sideways:
        gathers[i].small.finish()
        gathers[i].large.start()
    for j in range(2):
        rep_first[j].wait_recv()
        rep_second[j][1].start()
    for i in early:
        gathers[i].large.forward()
    for i in late:
        gathers[i].small.finish()
        gathers[i].large.start()
    gathers[7].large.forward()
    gathers[8].large.forward()
    lanes = pl.ds(pl.multiple_of(place.chip * 2 * KW, 2 * KW), 2 * KW)
    gathers[0].large.finish()
    gathers[3].large.finish()
    gathers[1].large.finish()
    half = halves.at[place.core]
    swap = remote(half, half, rep_send.at[GATHER_CHUNKS, 0], rep_recv.at[GATHER_CHUNKS, 0], place.near)
    swap.start()
    for copy in rep_second[0]:
        copy.wait_recv()
    rep_local[0][1].wait()
    loads = [
        pltpu.make_async_copy(half.at[:, :, :, :, lanes], ckv_held, load_sems.at[0]),
        pltpu.make_async_copy(wholes[0], qkv_held, load_sems.at[1]),
        pltpu.make_async_copy(wholes[3], small_held, load_sems.at[2]),
        pltpu.make_async_copy(all_rows[0], token_held, load_sems.at[3]),
    ]
    for load in loads:
        load.start()
    for load in loads:
        load.wait()
    unpack_small(rep, small_held[...], bucket_hot(buckets[...]), gains_out, curve_out)
    fill_bias(curve_out, bias_ref)
    for micro in range(MICRO):
        rows = slice(micro * ROWS, (micro + 1) * ROWS)
        normed, whole, mixed = self_attention(
            token_held[:, rows, :].reshape(SEQ, D),
            gains_out[0:1, :],
            qkv_held[...].reshape(D, QW + 2 * KW),
            self_mask(seg_row[micro]),
            bias_ref,
        )
        normed_out[:, rows, :] = normed.reshape(REP, ROWS, D)
        qkv_out[:, rows, :] = whole.reshape(REP, ROWS, QW + 2 * KW)
        context_out[:, rows, :] = mixed.reshape(REP, ROWS, QW)
    gathers[6].large.forward()
    gathers[5].large.forward()
    parts = GATHER_ROWS[1]
    tall = own_rows[1].shape[0] // parts

    def project(source_ref, k, p, count=2):
        rows = slice(p * tall, (p + count) * tall)
        kv_out[k, rows, :] = matmul(source_ref[...], ckv_held[...].reshape(D, 2 * KW)).astype(bf16)

    def load_half(k, p, slot):
        for q in (p, p + 1):
            rep_second[1 + q][0 if k == 1 else 1].wait_recv() if k != 2 else None
        load = pltpu.make_async_copy(
            all_rows[1].at[k, pl.ds(p * tall, 2 * tall)], enc_held.at[slot], load_sems.at[4 + slot]
        )
        load.start()
        return load

    first_near = load_half(1, 0, 0)
    project(held_rows[1], 0, 0, parts)
    for i in late:
        gathers[i].large.forward()
    first_near.wait()
    second_near = load_half(1, 2, 1)
    project(enc_held.at[0], 1, 0)
    second_near.wait()
    project(enc_held.at[1], 1, 2)
    for p in (0, 2):
        for q in (p, p + 1):
            if q:
                rep_first[1 + q].wait_recv()
                rep_second[1 + q][1].start()
        far_load = load_half(2, p, 2)
        far_load.wait()
        project(enc_held.at[2], 2, p)
        across_load = load_half(3, p, p // 2)
        across_load.wait()
        project(enc_held.at[p // 2], 3, p)
    for i in late + sideways + early[3:]:
        gathers[i].large.finish()
    rep_first[GATHER_CHUNKS - 1].wait_recv()
    rep_second[GATHER_CHUNKS - 1][1].start()
    for sent, _ in pieces:
        pl.when(jnp.logical_not(stays))(sent.wait_send)
    for one in gathers:
        one.drain()
    for _, outward in rep_local[1:]:
        outward.wait()
    for j, (first, second) in enumerate(zip(rep_first, rep_second)):
        first.wait_send()
        for copy in second:
            copy.wait_send()
            if j == GATHER_CHUNKS - 1:
                copy.wait_recv()
    swap.wait()


def gather_weights(weights, tables, rows):
    n = len(GATHER_BLOCKS)
    shapes = [
        jax.ShapeDtypeStruct(((2,) if i == 1 else ()) + (4, 4, 2, r, c), bf16)
        for i, (r, c, _) in enumerate(GATHER_BLOCKS)
    ]
    shapes += [jax.ShapeDtypeStruct((REP,) + value.shape, value.dtype) for value in rows]
    own = MICRO * ROWS
    n_far = len(shapes)
    shapes += [jax.ShapeDtypeStruct((8, D), f32), jax.ShapeDtypeStruct((8, SEQ), f32)]
    shapes += [jax.ShapeDtypeStruct((REP, own, width), bf16) for width in (D, QW + 2 * KW, QW)]
    shapes.append(jax.ShapeDtypeStruct((REP, rows[1].shape[0], 2 * KW), bf16))
    anywhere = pl.BlockSpec(memory_space=pltpu.HBM)
    here = pl.BlockSpec(memory_space=pltpu.VMEM)
    dma = pltpu.SemaphoreType.DMA
    results = pl.pallas_call(
        gather_kernel,
        name="gather_weights",
        in_specs=[anywhere] * len(weights) + [here] * len(tables) + [anywhere] * len(rows),
        out_specs=[anywhere] * n_far + [here] * (len(shapes) - n_far),
        out_shape=shapes,
        scratch_shapes=[
            dma((11 + 3 + len(rows),)),
            dma((n + len(rows),)),
            dma((3,)),
            dma((3,)),
            dma((n,)),
            dma((n,)),
            dma((n, 2, 4)),
            dma((n, 2, 4)),
            dma((GATHER_CHUNKS + 1, 3)),
            dma((GATHER_CHUNKS + 1, 3)),
            dma((7,)),
            pltpu.VMEM((REP, own, D), bf16),
            pltpu.VMEM((4, 4, 2, 32, QW + 2 * KW), bf16),
            pltpu.VMEM((4, 4, 2, 8, 128), bf16),
            pltpu.VMEM((4, 4, 2, 32, 2 * KW), bf16),
            pltpu.VMEM((3, rows[1].shape[0] // 2, D), bf16),
            pltpu.VMEM((OWN_HEADS, SEQ, SEQ), f32),
        ]
        + [pltpu.VMEM((r, c), bf16) for r, c, _ in GATHER_BLOCKS[:GATHER_HELD]]
        + [pltpu.VMEM(value.shape, value.dtype) for value in rows],
        compiler_params=pltpu.CompilerParams(
            collective_id=0, has_side_effects=True, vmem_limit_bytes=56 * mebibyte
        ),
        cost_estimate=estimate(0, 128 << 20, 0),
    )(*weights, *tables, *rows)
    return results[:n], results[n : n + len(rows)], results[n + len(rows) :]


class ReduceRing:
    def __init__(self, half, whole_half, me, device_at, first, second, send_sems, recv_sems):
        right, left, far = lax.rem(me + 1, 4), lax.rem(me + 3, 4), lax.rem(me + 2, 4)
        to_right, to_left = device_at(right), device_at(left)

        def copy(source, target, device, i):
            return remote(source, target, send_sems.at[i], recv_sems.at[i], device)

        self.half, self.me, self.right, self.left = half, me, right, left
        self.first, self.second = first, second
        self.opening = [
            copy(whole_half(far, 0), first.at[0], to_right, 0),
            copy(whole_half(far, 1), first.at[1], to_left, 1),
        ]
        self.plain = [
            copy(whole_half(right, 1), second.at[0, 1], to_right, 2),
            copy(whole_half(left, 0), second.at[1, 0], to_left, 3),
        ]
        self.summed = [
            copy(first.at[0], second.at[0, 0], to_right, 4),
            copy(first.at[1], second.at[1, 1], to_left, 5),
        ]

    def start(self):
        for copy in self.opening + self.plain:
            copy.start()

    def middle(self, each):
        for h, group in enumerate((self.right, self.left)):
            self.opening[h].wait_recv()

            def add(*k, h=h, group=group):
                mixed = self.first[(h, *k)].astype(f32) + self.half(group, h, *k).astype(f32)
                self.first[(h, *k)] = mixed.astype(self.first.dtype)

            each(add)
            self.summed[h].start()

    def finish(self, each, store):
        for h in range(2):
            (self.plain[1] if h == 0 else self.plain[0]).wait_recv()
            self.summed[h].wait_recv()

            def add(*k, h=h):
                mixed = self.second[(0, h, *k)].astype(f32) + self.second[(1, h, *k)].astype(f32)
                store(h, *k, mixed + self.half(self.me, h, *k).astype(f32))

            each(add)

    def drain(self):
        for copy in self.opening + self.plain + self.summed:
            copy.wait_send()


def each_of_four(body):
    def step(i, carry):
        body(lax.div(i, 2), lax.rem(i, 2))
        return carry

    lax.fori_loop(0, 4, step, 0)


def just_once(body):
    body()


def grad_halves(grad, on_y):
    if on_y:
        return (lambda j, h, a, b: grad[2 * h + a, j, b]), (lambda j, h: grad.at[pl.ds(2 * h, 2), j])
    return (lambda j, h, a, b: grad[j, 2 * h + a, b]), (lambda j, h: grad.at[j, pl.ds(2 * h, 2)])


def large_ring(place, grad, on_y, first, second, sems):
    half, whole_half = grad_halves(grad, on_y)
    axis = (place.y, place.on_y) if on_y else (place.x, place.on_x)
    return ReduceRing(half, whole_half, *axis, first, second, *sems)


def large_store(mid):
    def store(h, a, b, total):
        mid[2 * h + a, b] = total.astype(mid.dtype)

    return store


def large_scratch(rows, width, dtype):
    return [pltpu.VMEM((2, 2, 2, rows, width), dtype), pltpu.VMEM((2, 2, 2, 2, rows, width), dtype)]


REDUCE_BLOCKS = (
    (32, QW + 2 * KW, True, bf16, True),
    (32, 2 * KW, False, bf16, True),
    (32, QW, False, bf16, True),
    (32, OWN_FF, True, bf16, True),
    (32, OWN_FF, False, bf16, True),
    (24, D, True, bf16, True),
    (8, D, False, bf16, True),
    (8, D, False, bf16, True),
    (8, 128, False, f32, False),
)
COLUMN_BLOCKS = (0, 1, 2, 3, 4)
PIECE_BLOCKS = (5, 6, 7)
SMALL_BLOCK = 8
BLOCK_ROWS = D // 4


def fill_columns(left, right, grad):
    def step(j, carry):
        lanes = pl.ds(pl.multiple_of(j * BLOCK_ROWS, BLOCK_ROWS), BLOCK_ROWS)
        part = left_contract(left[:, lanes], right[...])
        grad[j] = part.astype(grad.dtype).reshape(grad.shape[1:])
        return carry

    lax.fori_loop(0, 4, step, 0)


def in_thirds(value):
    parts = []
    for _ in range(3):
        parts.append(value.astype(bf16))
        value = value - parts[-1].astype(f32)
    return parts


def exact_matmul(value, ones):
    return sum(matmul(part, ones) for part in in_thirds(value))


def fill_small(rep, accs, curve_grad, hot, blocks):
    owner = lax.broadcasted_iota(jnp.int32, (SHARDS, D), 0)
    entry = lax.broadcasted_iota(jnp.int32, (SHARDS, D), 1)
    column = lax.broadcasted_iota(jnp.int32, (D, 128), 0)
    lane = lax.broadcasted_iota(jnp.int32, (D, 128), 1)
    per = D // SHARDS
    total = None
    for i, acc in enumerate(accs):
        picked = jnp.where(lax.div(entry, per) == owner, acc[...], 0.0)
        ones = (lax.rem(column, per) == lane - per * i).astype(f32).astype(bf16)
        part = exact_matmul(picked, ones)
        total = part if total is None else total + part
    rows = sum(right_contract(hot, part) for part in in_thirds(curve_grad[...]))
    head = lax.broadcasted_iota(jnp.int32, (8, 128), 0)
    place = lax.broadcasted_iota(jnp.int32, (8, 128), 1)
    ones = ((head < OWN_HEADS) & (place == 3 * per + OWN_HEADS * rep + head)).astype(f32).astype(bf16)
    total = total + exact_matmul(rows, ones)
    for i in range(SHARDS):
        blocks[i // 8, i // 2 % 4, i % 2] = jnp.broadcast_to(total[i : i + 1, :], (8, 128))


def fill_rows(left, right, grad):
    grad[...] = left_contract(left[...], right[...]).reshape(grad.shape).astype(grad.dtype)


def fill_stream(left, right, grad, held, room, sems):
    n = left.shape[0]
    loads = [pltpu.make_async_copy(left.at[i], held.at[i % 2], sems.at[i]) for i in range(n)]
    loads[0].start()
    loads[1].start()
    for i in range(n):
        loads[i].wait()
        part = left_contract(right[i], held[i % 2])
        room[...] = part if i == 0 else room[...] + part
        if i + 2 < n:
            loads[i + 2].start()

    def turn(j, carry):
        lanes = pl.ds(pl.multiple_of(j * BLOCK_ROWS, BLOCK_ROWS), BLOCK_ROWS)
        grad[j] = room[:, lanes].T.astype(grad.dtype).reshape(grad.shape[1:])
        return carry

    lax.fori_loop(0, 4, turn, 0)


def fill_down(left, right, grad, room):
    def step(j, carry):
        lanes = pl.ds(pl.multiple_of(j * BLOCK_ROWS, BLOCK_ROWS), BLOCK_ROWS)
        room[:, lanes] = left_contract(left[...], right[:, lanes])
        return carry

    lax.fori_loop(0, 4, step, 0)

    def place(a, carry):
        for q in range(REP):
            rows = pl.ds(pl.multiple_of(a * 88 + min(24 * q, 64), 8), 24)
            grad[lax.div(a, 2), 2 * lax.rem(a, 2) + q // 2, q % 2] = room[rows, :].astype(grad.dtype)
        return carry

    lax.fori_loop(0, 8, place, 0)


def reduce_kernel(*refs):
    n = len(REDUCE_BLOCKS)
    own = MICRO * ROWS
    layer_part, hidden, self_acc, cross_acc, feed_acc, curve_grad, buckets, *refs = refs
    given = [i for i in range(n) if REDUCE_BLOCKS[i][4]]
    mids, refs = refs[: len(given)], refs[len(given) :]
    alls, refs = refs[: len(COLUMN_BLOCKS)], refs[len(COLUMN_BLOCKS) :]
    gathered, refs = refs[: len(PIECE_BLOCKS)], refs[len(PIECE_BLOCKS) :]
    small_out, layer_out, *refs = refs
    small_blocks, *refs = refs
    grads = {SMALL_BLOCK: small_blocks}
    scratch = []
    for i in range(n):
        extra = 0 if REDUCE_BLOCKS[i][4] else 3
        scratch.append(([None, None, mids[given.index(i)]] if extra == 0 else refs[:3]) + refs[extra : extra + 5])
        refs = refs[extra + 5 :]
    (small_far, small_near, core_recv, far_send, far_recv, near_sum) = refs[:6]
    ring_send, ring_recv, pair_send, pair_recv, rep_send, rep_recv, piece_send, piece_recv, more_send, more_recv = (
        refs[6:]
    )
    place = Place()
    at, rep, x, y, z, theirs = place.at, place.rep, place.x, place.y, place.z, place.theirs
    barrier = pltpu.get_barrier_semaphore()
    devices = [place.pair, place.far, place.near] + place.neighbours()
    for device in devices:
        pl.semaphore_signal(barrier, inc=1, device_id=device, device_id_type=MESH)
    owner = 8 * rep + lax.div(at, 4)
    slot = lax.rem(at, 4)
    stays = owner == at

    def from_self(q):
        return (x == rep) & (4 * lax.rem(at, 8) + q == at)

    for q in range(REP):
        giver = {"rep": x, "shard": 4 * lax.rem(at, 8) + q}

        @pl.when(jnp.logical_not(from_self(q)))
        def _(giver=giver):
            pl.semaphore_signal(barrier, inc=1, device_id=giver, device_id_type=MESH)

    fill_small(rep, (self_acc, cross_acc, feed_acc), curve_grad, bucket_hot(buckets[...]), small_blocks)
    pl.semaphore_wait(barrier, len(devices) + REP - stays.astype(jnp.int32))

    large, small = [], []
    for i, (_, _, on_y, _, done) in enumerate(REDUCE_BLOCKS):
        first, second, mid, first_small, second_small = scratch[i][:5]

        def half_small(j, h, mid=mid):
            return mid[j, h]

        def whole_half_small(j, h, mid=mid):
            return mid.at[j, h]

        if not done:
            large.append((i, large_ring(place, grads[i], on_y, first, second, (ring_send.at[i, 0], ring_recv.at[i, 0]))))
        narrow = (x, place.on_x) if on_y else (y, place.on_y)
        small.append(
            ReduceRing(
                half_small, whole_half_small, *narrow, first_small, second_small, ring_send.at[i, 1], ring_recv.at[i, 1]
            )
        )
    for i, ring in enumerate(small):
        if REDUCE_BLOCKS[i][4]:
            ring.start()
    for _, ring in large:
        ring.start()

    to_core = [
        remote(
            layer_part.at[there * 2 + 1 - place.core], core_recv.at[i], more_send.at[i], more_recv.at[i], place.near
        )
        for i, there in enumerate((1 - place.chip, place.chip))
    ]
    for copy in to_core:
        copy.start()
    to_core[0].wait_recv()
    far_send[...] = (layer_part[theirs].astype(f32) + core_recv[0].astype(f32)).astype(bf16)
    to_far = remote(far_send, far_recv, more_send.at[2], more_recv.at[2], place.far)
    to_far.start()
    to_core[1].wait_recv()
    near_sum[...] = hidden[...] + layer_part[rep].astype(f32) + core_recv[1].astype(f32)

    for i, ring in enumerate(small):
        if REDUCE_BLOCKS[i][4]:
            ring.middle(just_once)
    for _, ring in large:
        ring.middle(each_of_four)
    for i, ring in large:
        ring.finish(each_of_four, large_store(scratch[i][2]))
        small[i].start()
    to_far.wait_recv()
    layer_out[...] = (near_sum[...] + far_recv[...].astype(f32)).astype(bf16)
    for i, ring in enumerate(small):
        if not REDUCE_BLOCKS[i][4]:
            ring.middle(just_once)
    pairs = []
    for i, ring in enumerate(small):
        low = scratch[i][5]

        def store(h, total, low=low):
            low[h] = total.astype(low.dtype)

        ring.finish(just_once, store)
        pairs.append(remote(low.at[1 - z], scratch[i][6], pair_send.at[i], pair_recv.at[i], place.pair))
        pairs[i].start()
    spread, onward, handed = [], [], []
    for i in range(n):
        low, arrived, result = scratch[i][5:8]
        pairs[i].wait_recv()
        total = (low[z].astype(f32) + arrived[...].astype(f32)).astype(low.dtype)
        if i in COLUMN_BLOCKS:
            j = COLUMN_BLOCKS.index(i)
            alls[j][rep] = total
            mine, other = alls[j].at[rep], alls[j].at[theirs]
            spread.append(
                [
                    remote(mine, mine, rep_send.at[j, 0], rep_recv.at[j, 0], place.far),
                    remote(mine, mine, rep_send.at[j, 1], rep_recv.at[j, 1], place.near),
                ]
            )
            onward.append(remote(other, other, rep_send.at[j, 2], rep_recv.at[j, 2], place.near))
            for copy in spread[j]:
                copy.start()
        elif i in PIECE_BLOCKS:
            j = PIECE_BLOCKS.index(i)
            result[...] = total
            for k in range(REP):
                copy = remote(
                    result,
                    gathered[j].at[slot],
                    piece_send.at[j, k],
                    piece_recv.at[j, slot],
                    {"rep": jnp.int32(k), "shard": owner},
                )
                own_piece = stays & (rep == k)
                handed.append((own_piece, copy))
                pl.when(jnp.logical_not(own_piece))(copy.start)

            @pl.when(stays)
            def _(j=j, total=total):
                gathered[j][slot] = total
        else:
            result[...] = total
    result = scratch[SMALL_BLOCK][7]
    small_first = remote(result, small_far, more_send.at[9], more_recv.at[9], place.far)
    small_first.start()
    for j in range(len(onward)):
        spread[j][0].wait_recv()
        onward[j].start()
    small_first.wait()
    result[...] = result[...] + small_far[...]
    small_second = remote(result, small_near, more_send.at[10], more_recv.at[10], place.near)
    small_second.start()
    small_second.wait()
    small_out[...] = result[...] + small_near[...]
    for j in range(len(onward)):
        spread[j][1].wait_recv()
        onward[j].wait_recv()
    for j in range(len(PIECE_BLOCKS)):
        for q in range(REP):
            landed = gathered[j].at[q]
            arrival = remote(
                landed, landed, piece_send.at[j, q], piece_recv.at[j, q], {"rep": x, "shard": 4 * lax.rem(at, 8) + q}
            )
            pl.when(jnp.logical_not(from_self(q)))(arrival.wait_recv)
    for _, ring in large:
        ring.drain()
    for ring in small:
        ring.drain()
    for own_piece, copy in handed:
        pl.when(jnp.logical_not(own_piece))(copy.wait_send)
    for copy in to_core + [to_far] + pairs + onward + [one for two in spread for one in two]:
        copy.wait_send()


def reduce_grads(layer_part, hidden, accs, curve_grad, buckets, mids):
    n = len(REDUCE_BLOCKS)
    own = MICRO * ROWS
    shapes = [jax.ShapeDtypeStruct((REP,) + REDUCE_BLOCKS[i][:2], bf16) for i in COLUMN_BLOCKS + PIECE_BLOCKS]
    shapes += [jax.ShapeDtypeStruct((8, 128), f32), jax.ShapeDtypeStruct((own, D), bf16)]
    here = pl.BlockSpec(memory_space=pltpu.VMEM)
    dma = pltpu.SemaphoreType.DMA
    scratch = [pltpu.VMEM((4, 4, 2) + REDUCE_BLOCKS[SMALL_BLOCK][:2], f32)]
    for rows, width, _, dtype, done in REDUCE_BLOCKS:
        if not done:
            scratch += large_scratch(rows, width, dtype) + [pltpu.VMEM((4, 2, rows, width), dtype)]
        for lead in ((2,), (2, 2), (2,), (), ()):
            scratch.append(pltpu.VMEM(lead + (rows, width), dtype))
    scratch += [
        pltpu.VMEM((8, 128), f32),
        pltpu.VMEM((8, 128), f32),
        pltpu.VMEM((2, own, D), bf16),
        pltpu.VMEM((own, D), bf16),
        pltpu.VMEM((own, D), bf16),
        pltpu.VMEM((own, D), f32),
    ]
    scratch += [dma((n, 2, 6)), dma((n, 2, 6)), dma((n,)), dma((n,)), dma((5, 3)), dma((5, 3))]
    scratch += [dma((3, REP)), dma((3, REP)), dma((11,)), dma((11,))]
    return pl.pallas_call(
        reduce_kernel,
        name="reduce_grads",
        in_specs=[here] * (7 + len(mids)),
        out_specs=[here] * len(shapes),
        out_shape=shapes,
        scratch_shapes=scratch,
        compiler_params=pltpu.CompilerParams(
            collective_id=6, has_side_effects=True, vmem_limit_bytes=56 * mebibyte
        ),
        cost_estimate=estimate(0, 128 << 20, 0),
    )(layer_part, hidden, *accs, curve_grad, buckets, *mids)


def norm_parts(values):
    return lax.rsqrt(jnp.mean(values * values, axis=-1, keepdims=True) + epsilon)


class ReduceRider:
    def __init__(self, jobs):
        self.jobs = [(i, fill) for i, fill, _, _ in jobs]
        self.operands, self.uses = [], []
        for _, _, left, right in jobs:
            use = []
            for value in (left, right):
                found = [k for k, other in enumerate(self.operands) if other is value]
                if not found:
                    self.operands.append(value)
                use.append(found[0] if found else len(self.operands) - 1)
            self.uses.append(use)
        n = len(jobs)
        dma = pltpu.SemaphoreType.DMA
        self.shapes, self.scratch = [], [dma((n, 6)), dma((n, 6))]
        for i, fill in self.jobs:
            rows, width, _, dtype, _ = REDUCE_BLOCKS[i]
            self.shapes.append(jax.ShapeDtypeStruct((4, 2, rows, width), dtype))
            self.scratch += [pltpu.VMEM((4, 4, 2, rows, width), dtype)] + large_scratch(rows, width, dtype)
        here, there = pl.BlockSpec(memory_space=pltpu.VMEM), pl.BlockSpec(memory_space=pltpu.HBM)
        self.in_specs = [here] * len(self.operands)
        for (_, fill), use in zip(self.jobs, self.uses):
            if fill is fill_down:
                self.scratch.append(pltpu.VMEM((OWN_FF, D), f32))
            if fill is fill_stream:
                self.in_specs[use[0]] = there
                left, right = (self.operands[u] for u in use)
                self.scratch += [pltpu.VMEM((2,) + left.shape[1:], bf16), pltpu.VMEM((right.shape[2], D), f32), dma((REP,))]
        self.out_specs = [pl.BlockSpec(memory_space=pltpu.VMEM)] * n

    def steps(self, place, operands, mids, scratch):
        send, recv, *rooms = scratch
        rings, fills = [], []
        for k, (i, fill) in enumerate(self.jobs):
            grad, first, second = rooms[3 * k : 3 * k + 3]
            rings.append(large_ring(place, grad, REDUCE_BLOCKS[i][2], first, second, (send.at[k], recv.at[k])))
            extra = rooms[3 * len(self.jobs) :]
            more = extra if fill in (fill_down, fill_stream) else []
            left, right = (operands[u] for u in self.uses[k])
            fills.append(lambda fill=fill, left=left, right=right, grad=grad, more=more: fill(left, right, grad, *more))

        def begin():
            fills[0]()
            rings[0].start()

        def rest():
            for fill, ring in zip(fills[1:], rings[1:]):
                fill()
                ring.start()

        def nothing():
            pass

        def middle():
            for ring in rings:
                ring.middle(each_of_four)

        def end():
            for ring, mid in zip(rings, mids):
                ring.finish(each_of_four, large_store(mid))
            for ring in rings:
                ring.drain()

        return [begin, rest, nothing, middle, end]


def boundary_kernel(n_pairs, turned, forward, gathers, rider, which, *refs):
    pairs = [(refs[2 * i], refs[2 * i + 1]) for i in range(n_pairs)]
    rest = refs[2 * n_pairs :]
    if forward:
        hidden_ref, gain_ref, *rest = rest
    else:
        values_ref, hidden_ref, gain_ref, *rest = rest
    n_ride = len(rider.operands) if rider else 0
    riding, rest = rest[:n_ride], rest[n_ride:]
    out_ref, *rest = rest
    if not forward:
        acc_ref, *rest = rest
    if gathers:
        all_ref, *rest = rest
    n_ridden = len(rider.shapes) if rider else 0
    ridden, rest = rest[:n_ridden], rest[n_ridden:]
    core_send, core_recv, far_send, far_recv, near_sum, send_sems, recv_sems, *rest = rest
    place = Place()
    rep, chip, core, theirs, far, near = place.rep, place.chip, place.core, place.theirs, place.far, place.near
    barrier = pltpu.get_barrier_semaphore()
    devices = [far, near]
    steps = []
    if rider:
        devices += [place.pair] + place.neighbours()
        steps = rider.steps(place, riding, ridden, rest)

    def ride():
        if steps:
            steps.pop(0)()

    for device in devices:
        pl.semaphore_signal(barrier, inc=1, device_id=device, device_id_type=MESH)

    def partial(r):
        product = right_contract if turned else matmul
        total = product(pairs[0][0][r], pairs[0][1][...])
        for left, right in pairs[1:]:
            total = total + product(left[r], right[...])
        return total

    def copy(source, target, i, device):
        return remote(source, target, send_sems.at[i], recv_sems.at[i], device)

    half = ROWS
    chunks = [pl.ds(c * half, half) for c in range(MICRO)]
    to_core = []
    for i, there in enumerate((1 - chip, chip)):
        core_send[i] = partial(there * 2 + 1 - core).astype(bf16)
        to_core.append(copy(core_send.at[i], core_recv.at[i], i, near))
        if i == 0:
            pl.semaphore_wait(barrier, len(devices))
        to_core[i].start()
    far_own = partial(theirs)
    to_core[0].wait_recv()
    far_send[...] = (far_own + core_recv[0].astype(f32)).astype(bf16)
    to_far = [copy(far_send.at[rows], far_recv.at[rows], 2 + c, far) for c, rows in enumerate(chunks)]
    for sent in to_far:
        sent.start()
    near_own = partial(rep)
    to_core[1].wait_recv()
    near_sum[...] = near_own + core_recv[1].astype(f32)
    ride()
    spread, onward = [], []
    acc = None
    for c, rows in enumerate(chunks):
        to_far[c].wait_recv()
        total = near_sum[rows, :] + far_recv[rows, :].astype(f32)
        gain = gain_ref[which : which + 1, :]
        if forward:
            fresh = hidden_ref[rows, :].astype(f32) + total
            sent = (fresh * norm_parts(fresh) * gain).astype(bf16)
        else:
            values = values_ref[rows, :].astype(f32)
            rho = norm_parts(values)
            scaled = gain * total
            inner = jnp.mean(values * scaled, axis=-1, keepdims=True)
            fresh = hidden_ref[rows, :].astype(f32) + rho * scaled - values * (rho * rho * rho * inner)
            part = jnp.sum(values * rho * total, axis=0, keepdims=True)
            acc = part if acc is None else acc + part
            sent = fresh.astype(bf16)
        out_ref[rows, :] = fresh
        if gathers:
            all_ref[rep, rows, :] = sent
            mine = all_ref.at[rep, rows]
            other = all_ref.at[theirs, rows]
            spread.append((copy(mine, mine, 4 + c, far), copy(mine, mine, 6 + c, near)))
            onward.append(copy(other, other, 8 + c, near))
            for one in spread[c]:
                one.start()
        ride()
    if not forward:
        acc_ref[...] = acc
    for c in range(len(onward)):
        spread[c][0].wait_recv()
        onward[c].start()
    ride()
    for c in range(len(onward)):
        spread[c][1].wait_recv()
        onward[c].wait_recv()
    ride()
    for sent in to_core + to_far + [one for two in spread for one in two] + onward:
        sent.wait_send()


def boundary(name, identity, pairs, turned, hidden, gains, which, values=None, gathers=True, rider=None):
    own = MICRO * ROWS
    forward = values is None
    operands = [a.reshape(REP, own, -1) if i == 0 else a for pair in pairs for i, a in enumerate(pair)]
    operands += ([] if forward else [values]) + [hidden, gains]
    in_specs = [pl.BlockSpec(memory_space=pltpu.VMEM)] * len(operands)
    shapes = [jax.ShapeDtypeStruct((own, D), f32)]
    if not forward:
        shapes.append(jax.ShapeDtypeStruct((1, D), f32))
    if gathers:
        shapes.append(jax.ShapeDtypeStruct((REP, own, D), bf16))
    here = pl.BlockSpec(memory_space=pltpu.VMEM)
    out_specs = [here] * len(shapes)
    if rider:
        operands += rider.operands
        in_specs += rider.in_specs
        shapes += rider.shapes
        out_specs += rider.out_specs
    dma = pltpu.SemaphoreType.DMA
    return pl.pallas_call(
        lambda *refs: boundary_kernel(len(pairs), turned, forward, gathers, rider, which, *refs),
        name=name,
        in_specs=in_specs,
        out_specs=out_specs,
        out_shape=shapes,
        scratch_shapes=[
            pltpu.VMEM((2, own, D), bf16),
            pltpu.VMEM((2, own, D), bf16),
            pltpu.VMEM((own, D), bf16),
            pltpu.VMEM((own, D), bf16),
            pltpu.VMEM((own, D), f32),
            dma((10,)),
            dma((10,)),
        ]
        + (rider.scratch if rider else []),
        compiler_params=pltpu.CompilerParams(
            collective_id=identity, has_side_effects=True, vmem_limit_bytes=(36 if identity == 5 else 24) * mebibyte
        ),
        cost_estimate=estimate(1 << 30, 32 << 20, 0),
    )(*operands)


FINAL_COLUMNS = (
    (0, 0, QW),
    (0, QW, KW),
    (0, QW + KW, KW),
    (1, 0, KW),
    (1, KW, KW),
    (2, 0, QW),
    (3, 0, OWN_FF),
    (4, 0, OWN_FF),
)


def finish_kernel(*refs):
    n = len(COLUMN_BLOCKS) + len(PIECE_BLOCKS)
    columns, pieces = refs[: len(COLUMN_BLOCKS)], refs[len(COLUMN_BLOCKS) : n]
    kv_refs, w_ref = refs[n : n + REP], refs[n + REP]
    finals, enc_ref = refs[n + REP + 1 : -1], refs[-1]
    rep = lax.axis_index("rep")
    chip, core = lax.div(rep, 2), lax.rem(rep, 2)
    total = None
    for i, kv_ref in enumerate(kv_refs):
        there, which = (1 - chip if i // 2 else chip), (1 - core if i % 2 else core)
        lanes = pl.ds(pl.multiple_of(there * 2 * KW, 2 * KW), 2 * KW)
        part = right_contract(kv_ref[...], w_ref[which, :, lanes])
        total = part if total is None else total + part
    enc_ref[...] = total

    @pl.when(pl.program_id(0) == 0)
    def _():
        for final, (source, first, width) in zip(finals, FINAL_COLUMNS):
            parts = [columns[source][r, :, first : first + width].astype(f32) for r in range(REP)]
            final[...] = jnp.concatenate(parts, axis=1)
        for final, piece in zip(finals[len(FINAL_COLUMNS) :], pieces):
            rows = piece.shape[1]
            for q in range(REP):
                skip = REP * rows - final.shape[0] if q == REP - 1 else 0
                final[q * rows : (q + 1) * rows - skip, :] = piece[q, skip:, :].astype(f32)


def finish(columns, pieces, kv_parts, w_ckv):
    shapes = [jax.ShapeDtypeStruct((columns[i].shape[1], REP * width), f32) for i, _, width in FINAL_COLUMNS]
    shapes += [jax.ShapeDtypeStruct((tall, D), f32) for tall in (FF // SHARDS, 32, 32)]
    shapes.append(jax.ShapeDtypeStruct((kv_parts[0].shape[0], D), f32))
    tall = kv_parts[0].shape[0] // 4
    some = pl.BlockSpec((tall, D), lambda i: (i, 0))
    return pl.pallas_call(
        finish_kernel,
        name="finish",
        grid=(4,),
        in_specs=[fixed_block(value.shape) for value in columns + pieces]
        + [pl.BlockSpec((tall, 2 * KW), lambda i: (i, 0))] * REP
        + [fixed_block(w_ckv.shape)],
        out_specs=[fixed_block(shape.shape) for shape in shapes[:-1]] + [some],
        out_shape=shapes,
        compiler_params=pltpu.CompilerParams(vmem_limit_bytes=56 * mebibyte),
        cost_estimate=estimate(2 << 30, 12 << 20, 0),
    )(*columns, *pieces, *kv_parts, w_ckv)


def local(
    tokens,
    out_cotangent,
    encoded,
    segment_ids,
    doc_block,
    bucket_table,
    self_gain,
    query_weight,
    key_weight,
    value_weight,
    out_weight,
    bias_table,
    cross_gain,
    cross_query,
    cross_key,
    cross_value,
    cross_out,
    feed_gain,
    gate_weight,
    up_weight,
    down_weight,
):
    rep = lax.axis_index("rep")
    own = MICRO * ROWS
    enc_rows = MICRO * DOCS * ENC // REP

    def columns(weight, width):
        return lax.dynamic_slice_in_dim(weight, rep * width, width, 1)

    segments = segment_ids[:, 0]
    seg_row = segments[:, None, :]
    buckets = bucket_table.reshape(1, SEQ)
    doc_ids = jnp.arange(DOCS, dtype=jnp.int32)
    ends = jnp.sum((segments[:, None, :] <= doc_ids[None, :, None]).astype(jnp.int32), axis=2)
    begins = jnp.pad(ends[:, :-1], ((0, 0), (1, 0)))
    wides = (ends - begins > NARROW - 16).astype(jnp.int32)
    starts = jnp.minimum(begins // 16 * 16, jnp.where(wides == 0, SEQ - NARROW, SEQ - WINDOW))
    spans = [value.reshape(-1) for value in (doc_block[:, 0], starts, wides, begins, ends)]

    small = sum(
        jnp.pad(value.reshape(1, -1), ((0, 7), (32 * i, 128 - 32 * i - value.size)))
        for i, value in enumerate((self_gain, cross_gain, feed_gain, bias_table))
    )
    own_tokens = tokens.reshape(own, D)
    own_cotangent = out_cotangent.reshape(own, D)
    wholes, (all_tokens, all_enc, all_grad), ready = gather_weights(
        [
            query_weight,
            key_weight,
            value_weight,
            cross_key,
            cross_value,
            cross_query,
            small,
            columns(gate_weight, OWN_FF),
            columns(up_weight, OWN_FF),
            down_weight,
            out_weight,
            cross_out,
        ],
        [seg_row, buckets],
        [own_tokens, encoded.reshape(enc_rows, D), own_cotangent],
    )
    w_qkv, w_ckv, w_cq, small, w_gate, w_up, w_down, w_out, w_cout = wholes
    w_gate = w_gate.reshape(D, OWN_FF)
    w_up = w_up.reshape(D, OWN_FF)
    gains, curve, normed, qkv, context, kv = ready
    w_qkv = w_qkv.reshape(D, QW + 2 * KW)
    w_out = w_out.reshape(QW, D)
    w_ckv = w_ckv.reshape(2, D, REP * KW)
    w_cq = w_cq.reshape(D, QW)
    w_cout = w_cout.reshape(QW, D)
    w_down = w_down.reshape(SHARDS, 24, D)
    all_grad = all_grad.reshape(REP * own, D)

    all_enc = all_enc.reshape(REP * enc_rows, D)

    qkv = qkv.reshape(REP, MICRO, ROWS, QW + 2 * KW)
    normed = normed.reshape(REP * own, D)
    context = context.reshape(REP * own, QW)
    hidden, cross_normed = boundary("after_self", 1, [(context, w_out)], False, own_tokens, gains, 1)
    kv = kv.reshape(REP, MICRO, DOCS, ENC // REP, 2 * KW)
    cross_normed = cross_normed.reshape(REP * own, D)
    cross_queries = matmul(cross_normed, w_cq).astype(bf16).reshape(REP, MICRO, ROWS, QW)
    cross_context = cross_forward(spans, cross_queries, kv).reshape(REP * own, QW)
    hidden_two, feed_normed = boundary("after_cross", 2, [(cross_context, w_cout)], False, hidden, gains, 2)
    feed_normed = feed_normed.reshape(REP * own, D)
    inner, gate_low, up_low, layer_part = feed(feed_normed.reshape(REP, own, D), all_grad.reshape(REP, own, D), w_gate, w_up, w_down)
    inner = inner.reshape(REP * own, OWN_FF)
    gate_low = gate_low.reshape(REP * own, OWN_FF)
    up_low = up_low.reshape(REP * own, OWN_FF)

    hidden_grad, feed_acc, branch, gate_mid, up_mid = boundary(
        "before_feed",
        3,
        [(gate_low, w_gate), (up_low, w_up)],
        True,
        own_cotangent,
        gains,
        2,
        hidden_two,
        rider=ReduceRider([(3, fill_columns, feed_normed, gate_low), (4, fill_columns, feed_normed, up_low)]),
    )
    branch = branch.reshape(REP * own, D)
    context_grad = right_contract(branch, w_cout).astype(bf16).reshape(REP, MICRO, ROWS, QW)
    cq_grad, kv_grad = cross_backward(spans, cross_queries, kv, context_grad)
    cq_grad = cq_grad.reshape(REP * own, QW)
    kv_grad = kv_grad.reshape(REP, enc_rows, 2 * KW)
    hidden_grad, cross_acc, first_branch, down_mid, cq_mid, cout_mid = boundary(
        "before_cross",
        4,
        [(cq_grad, w_cq)],
        True,
        hidden_grad,
        gains,
        1,
        hidden,
        rider=ReduceRider(
            [
                (5, fill_down, inner, all_grad),
                (2, fill_columns, cross_normed, cq_grad),
                (7, fill_rows, cross_context, branch),
            ]
        ),
    )
    first_branch = first_branch.reshape(REP * own, D)
    sent, first_branch = lax.optimization_barrier((kv_grad, first_branch))
    kv_parts = [
        kv_grad[0],
        lax.ppermute(sent[1], "rep", swap_core),
        lax.ppermute(sent[2], "rep", swap_chip),
        lax.ppermute(sent[3], "rep", swap_both),
    ]

    context_grad = right_contract(first_branch, w_out).astype(bf16).reshape(REP, MICRO, ROWS, QW)
    qkv_grad, curve_grad = self_backward(qkv, context_grad, seg_row, curve)
    qkv_grad = qkv_grad.reshape(REP * own, QW + 2 * KW)
    tokens_grad, self_acc, qkv_mid, out_mid, ckv_mid = boundary(
        "before_self",
        5,
        [(qkv_grad, w_qkv)],
        True,
        hidden_grad,
        gains,
        0,
        own_tokens,
        False,
        ReduceRider(
            [
                (0, fill_columns, normed, qkv_grad),
                (6, fill_rows, context, first_branch),
                (1, fill_stream, all_enc.reshape(REP, enc_rows, D), kv_grad),
            ]
        ),
    )

    mids = [qkv_mid, ckv_mid, cq_mid, gate_mid, up_mid, down_mid, out_mid, cout_mid]
    *whole, small_sum, layer_out = reduce_grads(
        layer_part,
        hidden_two,
        [self_acc, cross_acc, feed_acc],
        curve_grad,
        buckets,
        mids,
    )
    *finals, encoder_grad = finish(whole[: len(COLUMN_BLOCKS)], whole[len(COLUMN_BLOCKS) :], kv_parts, w_ckv)
    query_grad, key_grad, value_grad, ck_grad, cv_grad, cq_grad, gate_grad, up_grad, down_grad, out_grad, cout_grad = finals
    small_sum = small_sum[0]
    return (
        layer_out.reshape(tokens.shape),
        tokens_grad.reshape(tokens.shape),
        encoder_grad.reshape(encoded.shape),
        small_sum[0:32],
        query_grad,
        key_grad,
        value_grad,
        out_grad,
        small_sum[96:112].reshape(1, HEADS),
        small_sum[32:64],
        cq_grad,
        ck_grad,
        cv_grad,
        cout_grad,
        small_sum[64:96],
        gate_grad,
        up_grad,
        down_grad,
    )


def solution(mesh):
    rows = P("shard", None)
    gain = P("shard")
    acts = P(None, "shard", "rep", None)
    encs = P(None, "shard", None, "rep", None)
    ids = P(None, "shard", None)
    weights = (gain, rows, rows, rows, rows, rows, gain, rows, rows, rows, rows, gain, rows, rows, rows)
    return jax.shard_map(
        local,
        mesh=mesh,
        in_specs=(acts, acts, encs, ids, ids, P()) + weights,
        out_specs=(acts, acts, encs) + weights,
        check_vma=False,
    )
```

```python
import jax
import jax.numpy as jnp
from jax import lax
from jax.experimental import pallas as pl
from jax.experimental.pallas import tpu as pltpu
from jax.sharding import PartitionSpec as P

D = 1024
HEADS = 16
HEAD_DIM = 64
KV_GROUPS = 8
FF = 2816
BUCKETS = 32
ENC = 512
SEQ = 256
DOCS = 4
MICRO = 2

REP = 4
SHARDS = 32
ROWS = SEQ // REP
OWN_HEADS = HEADS // REP
OWN_GROUPS = KV_GROUPS // REP
QW = OWN_HEADS * HEAD_DIM
KW = OWN_GROUPS * HEAD_DIM
OWN_FF = FF // REP
WINDOW = 144
NARROW = 80

epsilon = 1e-06
neg_big = -1e30
gelu_scale = 0.7978845608028654
gelu_cube = 0.044715
f32 = jnp.float32
bf16 = jnp.bfloat16
mebibyte = 1024 * 1024


def matmul(left, right):
    return jnp.dot(left, right, preferred_element_type=f32)


def left_contract(left, right):
    return lax.dot_general(left, right, (((0,), (0,)), ((), ())), preferred_element_type=f32)


def right_contract(left, right):
    return lax.dot_general(left, right, (((1,), (1,)), ((), ())), preferred_element_type=f32)


def skewed(row):
    n = row.shape[1]
    out = jnp.broadcast_to(row, (n, n))
    at = lax.broadcasted_iota(jnp.int32, (n, n), 0)
    step = 1
    while step < n:
        out = jnp.where((at & step) != 0, pltpu.roll(out, step, 1), out)
        step *= 2
    return out


def unskewed_sum(square):
    n = square.shape[1]
    at = lax.broadcasted_iota(jnp.int32, (n, n), 0)
    step = 1
    while step < n:
        square = jnp.where((at & step) != 0, pltpu.roll(square, n - step, 1), square)
        step *= 2
    return jnp.sum(square, axis=0, keepdims=True)


def raised_parts(scores):
    raised = jnp.exp(scores - jnp.max(scores, axis=-1, keepdims=True))
    return raised, 1.0 / jnp.sum(raised, axis=-1, keepdims=True)


def group_rows(rows, group):
    first = group * OWN_HEADS // OWN_GROUPS
    heads = range(first, first + OWN_HEADS // OWN_GROUPS)
    return jnp.concatenate([rows[:, h * HEAD_DIM : (h + 1) * HEAD_DIM] for h in heads], axis=0)


def group_lanes(stacked):
    n = stacked.shape[0] * OWN_GROUPS // OWN_HEADS
    return [stacked[i * n : (i + 1) * n] for i in range(OWN_HEADS // OWN_GROUPS)]


def lanes_of(values, first, group):
    return values[:, first + group * HEAD_DIM : first + (group + 1) * HEAD_DIM]


def stacked_twice(value):
    return jnp.concatenate([value] * (OWN_HEADS // OWN_GROUPS), axis=0)


def attend_back(scores, query, key, value, grad):
    raised, shrink = raised_parts(scores)
    grad = (grad.astype(f32) * shrink).astype(bf16)
    prob_grad = right_contract(grad, value)
    centre = jnp.sum(raised * prob_grad, axis=-1, keepdims=True) * shrink
    score_grad = (raised * (prob_grad - centre)).astype(bf16)
    return score_grad, matmul(score_grad, key), left_contract(score_grad, query), left_contract(raised.astype(bf16), grad)


def self_mask(seg_row):
    at_query = lax.broadcasted_iota(jnp.int32, (SEQ, SEQ), 0)
    at_key = lax.broadcasted_iota(jnp.int32, (SEQ, SEQ), 1)
    of_key = jnp.broadcast_to(seg_row.astype(f32), (SEQ, SEQ))
    return (at_key <= at_query) & (of_key == of_key.T)


def bucket_hot(buckets):
    at = lax.broadcasted_iota(jnp.int32, (BUCKETS, SEQ), 0)
    return (at == buckets).astype(f32).astype(bf16)


def fill_bias(curve_ref, bias_ref):
    for head in range(OWN_HEADS):
        bias_ref[head] = skewed(curve_ref[head : head + 1, :]).T


def self_attention(values, gain, weight, allowed, bias_ref):
    values = values.astype(f32)
    normed = (values * norm_parts(values) * gain).astype(bf16)
    whole = matmul(normed, weight).astype(bf16)
    allowed = stacked_twice(allowed.astype(jnp.int32)) != 0
    mixed = []
    for group in range(OWN_GROUPS):
        scores = right_contract(group_rows(whole, group), lanes_of(whole, QW, group))
        scores = jnp.where(allowed, scores + bias_ref[2 * group : 2 * group + 2].reshape(2 * SEQ, SEQ), neg_big)
        raised, shrink = raised_parts(scores)
        mixed += group_lanes(matmul(raised.astype(bf16), lanes_of(whole, QW + KW, group)) * shrink)
    return normed, whole, jnp.concatenate(mixed, axis=1).astype(bf16)


def unpack_small(rep, small, hot, gains_ref, curve_ref):
    rows = jnp.sum(small.astype(f32).reshape(SHARDS, 8, 128), axis=1).astype(bf16)
    per = D // SHARDS
    lane = lax.broadcasted_iota(jnp.int32, (128, D), 0)
    column = lax.broadcasted_iota(jnp.int32, (128, D), 1)
    owner = lax.broadcasted_iota(jnp.int32, (SHARDS, D), 0)
    entry = lax.broadcasted_iota(jnp.int32, (SHARDS, D), 1)
    gains_ref[...] = jnp.zeros_like(gains_ref)
    for i in range(3):
        ones = (lax.rem(column, per) == lane - per * i).astype(f32).astype(bf16)
        spread = jnp.where(lax.div(entry, per) == owner, matmul(rows, ones), 0.0)
        gains_ref[i : i + 1, :] = jnp.sum(spread, axis=0, keepdims=True)
    head = lax.broadcasted_iota(jnp.int32, (8, 128), 0)
    place = lax.broadcasted_iota(jnp.int32, (8, 128), 1)
    ones = ((head < OWN_HEADS) & (place == 3 * per + OWN_HEADS * rep + head)).astype(f32).astype(bf16)
    curve_ref[...] = matmul(right_contract(ones, rows).astype(bf16), hot)


def self_backward_kernel(
    qkv_ref, grad_ref, seg_row_ref, curve_ref, out_ref, curve_grad_ref, bias_ref, sum_ref
):
    @pl.when(pl.program_id(0) == 0)
    def _():
        fill_bias(curve_ref, bias_ref)
        sum_ref[...] = jnp.zeros_like(sum_ref)

    whole = qkv_ref[...].reshape(SEQ, QW + 2 * KW)
    grads = grad_ref[...].reshape(SEQ, QW)
    allowed = stacked_twice(self_mask(seg_row_ref[0]).astype(jnp.int32)) != 0
    query_grads, key_grads, value_grads = [], [], []
    for group in range(OWN_GROUPS):
        query = group_rows(whole, group)
        key = lanes_of(whole, QW, group)
        scores = right_contract(query, key)
        scores = jnp.where(allowed, scores + bias_ref[2 * group : 2 * group + 2].reshape(2 * SEQ, SEQ), neg_big)
        score_grad, query_grad, key_grad, value_grad = attend_back(
            scores, query, key, lanes_of(whole, QW + KW, group), group_rows(grads, group)
        )
        sum_ref[2 * group : 2 * group + 2] += score_grad.astype(f32).reshape(2, SEQ, SEQ)
        query_grads += group_lanes(query_grad)
        key_grads.append(key_grad)
        value_grads.append(value_grad)
    joined = jnp.concatenate(query_grads + key_grads + value_grads, axis=1)
    out_ref[...] = joined.astype(bf16).reshape(out_ref.shape)

    @pl.when(pl.program_id(0) == MICRO - 1)
    def _():
        curve_grad_ref[...] = jnp.zeros_like(curve_grad_ref)
        for head in range(OWN_HEADS):
            curve_grad_ref[head : head + 1, :] = unskewed_sum(sum_ref[head].T)


def by_window(at, wide_ref, body):
    pl.when(wide_ref[at] == 0)(lambda: body(NARROW))
    pl.when(wide_ref[at] != 0)(lambda: body(WINDOW))


def cross_forward_kernel(block_ref, start_ref, wide_ref, begin_ref, end_ref, q_ref, kv_ref, out_ref, query_ref, mixed_ref):
    at = pl.program_id(0) * DOCS + pl.program_id(1)

    @pl.when(pl.program_id(1) == 0)
    def _():
        query_ref[...] = q_ref[...].reshape(SEQ, QW)

    start = pl.multiple_of(start_ref[at], 16)

    def body(window):
        rows = query_ref[pl.ds(start, window), :]
        row = start + lax.broadcasted_iota(jnp.int32, (window, 1), 0)
        mine = (row >= begin_ref[at]) & (row < end_ref[at])
        both = kv_ref[...].reshape(ENC, 2 * KW)
        mixed = []
        for group in range(OWN_GROUPS):
            raised, shrink = raised_parts(right_contract(group_rows(rows, group), lanes_of(both, 0, group)))
            mixed += group_lanes(matmul(raised.astype(bf16), lanes_of(both, KW, group)) * shrink)
        fresh = jnp.concatenate(mixed, axis=1)
        mixed_ref[pl.ds(start, window), :] = jnp.where(mine, fresh, mixed_ref[pl.ds(start, window), :])

    by_window(at, wide_ref, body)

    @pl.when(pl.program_id(1) == DOCS - 1)
    def _():
        out_ref[...] = mixed_ref[...].astype(bf16).reshape(out_ref.shape)


def cross_backward_kernel(
    block_ref, start_ref, wide_ref, begin_ref, end_ref, q_ref, kv_ref, grad_ref, out_ref, kv_grad_ref, query_ref, given_ref,
    mixed_ref
):
    at = pl.program_id(0) * DOCS + pl.program_id(1)

    @pl.when(pl.program_id(1) == 0)
    def _():
        query_ref[...] = q_ref[...].reshape(SEQ, QW)
        given_ref[...] = grad_ref[...].reshape(SEQ, QW)

    start = pl.multiple_of(start_ref[at], 16)

    def body(window):
        rows = query_ref[pl.ds(start, window), :]
        row = start + lax.broadcasted_iota(jnp.int32, (window, 1), 0)
        mine = (row >= begin_ref[at]) & (row < end_ref[at])
        grads = jnp.where(mine, given_ref[pl.ds(start, window), :].astype(f32), 0.0)
        both = kv_ref[...].reshape(ENC, 2 * KW)
        query_grads, key_grads, value_grads = [], [], []
        for group in range(OWN_GROUPS):
            query, key = group_rows(rows, group), lanes_of(both, 0, group)
            _, query_grad, key_grad, value_grad = attend_back(
                right_contract(query, key), query, key, lanes_of(both, KW, group), group_rows(grads, group)
            )
            query_grads += group_lanes(query_grad)
            key_grads.append(key_grad)
            value_grads.append(value_grad)
        fresh = jnp.concatenate(query_grads, axis=1)
        mixed_ref[pl.ds(start, window), :] = jnp.where(mine, fresh, mixed_ref[pl.ds(start, window), :])
        joined = jnp.concatenate(key_grads + value_grads, axis=1)
        kv_grad_ref[...] = joined.astype(bf16).reshape(kv_grad_ref.shape)

    by_window(at, wide_ref, body)

    @pl.when(pl.program_id(1) == DOCS - 1)
    def _():
        out_ref[...] = mixed_ref[...].astype(bf16).reshape(out_ref.shape)


def feed_kernel(normed_ref, grad_ref, gate_w_ref, up_w_ref, pieces_ref, inner_ref, gate_ref, up_ref, part_ref, down_ref):
    @pl.when(pl.program_id(0) == 0)
    def _():
        for i in range(4):
            pieces = []
            for k in range(8 * i, 8 * i + 8):
                piece = pieces_ref[k].astype(f32)
                pieces.append(piece[8:] if k % REP == REP - 1 else piece)
            down_ref[i * 176 : (i + 1) * 176, :] = jnp.concatenate(pieces, axis=0).astype(bf16)

    normed = normed_ref[...].reshape(-1, D)
    gate = matmul(normed, gate_w_ref[...])
    up_part = matmul(normed, up_w_ref[...])
    inner_grad = right_contract(grad_ref[...].reshape(-1, D), down_ref[...])
    square = gate * gate
    bent = jnp.tanh(gelu_scale * gate * (1.0 + gelu_cube * square))
    rising = 0.5 * (1.0 + bent)
    slope = rising + 0.5 * gate * (1.0 - bent * bent) * (gelu_scale * (1.0 + 3.0 * gelu_cube * square))
    passed = gate * rising
    inner = (passed * up_part).astype(bf16)
    inner_ref[...] = inner.reshape(inner_ref.shape)
    gate_ref[...] = (inner_grad * up_part * slope).astype(bf16).reshape(gate_ref.shape)
    up_ref[...] = (inner_grad * passed).astype(bf16).reshape(up_ref.shape)
    part_ref[...] = matmul(inner, down_ref[...]).astype(bf16).reshape(part_ref.shape)


def feed(normed, grads, w_gate, w_up, down_pieces):
    own = MICRO * ROWS

    def some(width):
        return pl.BlockSpec((2, own, width), lambda i: (i, 0, 0))

    units = jax.ShapeDtypeStruct((REP, own, OWN_FF), bf16)
    return pl.pallas_call(
        feed_kernel,
        name="feed",
        grid=(REP // 2,),
        in_specs=[
            some(D),
            some(D),
            fixed_block(w_gate.shape),
            fixed_block(w_up.shape),
            fixed_block(down_pieces.shape),
        ],
        out_specs=[some(OWN_FF)] * 3 + [some(D)],
        out_shape=[units, units, units, jax.ShapeDtypeStruct((REP, own, D), bf16)],
        scratch_shapes=[pltpu.VMEM((OWN_FF, D), bf16)],
        compiler_params=pltpu.CompilerParams(vmem_limit_bytes=32 * mebibyte),
        cost_estimate=estimate(3 << 30, 8 << 20, 1 << 19),
    )(normed, grads, w_gate, w_up, down_pieces)


def rows_block(width):
    return pl.BlockSpec((REP, 1, ROWS, width), lambda m, *rest: (0, m, 0, 0))


def fixed_block(shape):
    return pl.BlockSpec(shape, lambda *at: (0,) * len(shape))


def micro_block(shape):
    return pl.BlockSpec((1,) + shape, lambda m, *rest: (m,) + (0,) * len(shape))


def estimate(flops, moved, raised):
    return pl.CostEstimate(flops=flops, bytes_accessed=moved, transcendentals=raised)


self_pairs = MICRO * OWN_HEADS * SEQ * SEQ
cross_pairs = MICRO * OWN_HEADS * DOCS * WINDOW * ENC


def self_backward(qkv, grads, seg_row, curve):
    return pl.pallas_call(
        self_backward_kernel,
        name="self_backward",
        grid=(MICRO,),
        in_specs=[
            rows_block(QW + 2 * KW),
            rows_block(QW),
            micro_block((1, SEQ)),
            fixed_block((8, SEQ)),
        ],
        out_specs=[rows_block(QW + 2 * KW), fixed_block((8, SEQ))],
        out_shape=[
            jax.ShapeDtypeStruct((REP, MICRO, ROWS, QW + 2 * KW), bf16),
            jax.ShapeDtypeStruct((8, SEQ), f32),
        ],
        scratch_shapes=[
            pltpu.VMEM((OWN_HEADS, SEQ, SEQ), f32),
            pltpu.VMEM((OWN_HEADS, SEQ, SEQ), f32),
        ],
        compiler_params=pltpu.CompilerParams(vmem_limit_bytes=18 * mebibyte),
        cost_estimate=estimate(self_pairs * 640, 3 << 20, self_pairs),
    )(qkv, grads, seg_row, curve)


def cross_rows():
    return pl.BlockSpec((REP, 1, ROWS, QW), lambda m, d, block, *rest: (0, m, 0, 0))


def cross_keys():
    return pl.BlockSpec(
        (REP, 1, 1, ENC // REP, 2 * KW),
        lambda m, d, block, *rest: (0, m, block[m * DOCS + d], 0, 0),
    )


def cross_forward(spans, queries, kv):
    return pl.pallas_call(
        cross_forward_kernel,
        name="cross_forward",
        grid_spec=pltpu.PrefetchScalarGridSpec(
            num_scalar_prefetch=5,
            grid=(MICRO, DOCS),
            in_specs=[cross_rows(), cross_keys()],
            out_specs=cross_rows(),
            scratch_shapes=[pltpu.VMEM((SEQ, QW), bf16), pltpu.VMEM((SEQ, QW), f32)],
        ),
        out_shape=jax.ShapeDtypeStruct((REP, MICRO, ROWS, QW), bf16),
        compiler_params=pltpu.CompilerParams(vmem_limit_bytes=16 * mebibyte),
        cost_estimate=estimate(cross_pairs * 256, 3 << 20, cross_pairs),
    )(*spans, queries, kv)


def cross_backward(spans, queries, kv, grads):
    return pl.pallas_call(
        cross_backward_kernel,
        name="cross_backward",
        grid_spec=pltpu.PrefetchScalarGridSpec(
            num_scalar_prefetch=5,
            grid=(MICRO, DOCS),
            in_specs=[cross_rows(), cross_keys(), cross_rows()],
            out_specs=[cross_rows(), cross_keys()],
            scratch_shapes=[
                pltpu.VMEM((SEQ, QW), bf16),
                pltpu.VMEM((SEQ, QW), bf16),
                pltpu.VMEM((SEQ, QW), f32),
            ],
        ),
        out_shape=[
            jax.ShapeDtypeStruct((REP, MICRO, ROWS, QW), bf16),
            jax.ShapeDtypeStruct((REP, MICRO, DOCS, ENC // REP, 2 * KW), bf16),
        ],
        compiler_params=pltpu.CompilerParams(vmem_limit_bytes=20 * mebibyte),
        cost_estimate=estimate(cross_pairs * 640, 6 << 20, cross_pairs),
    )(*spans, queries, kv, grads)


MESH = pl.DeviceIdType.MESH

swap_core = [(i, i ^ 1) for i in range(REP)]
swap_chip = [(i, i ^ 2) for i in range(REP)]
swap_both = [(i, i ^ 3) for i in range(REP)]


def remote(source, target, send_sem, recv_sem, device):
    return pltpu.make_async_remote_copy(
        src_ref=source,
        dst_ref=target,
        send_sem=send_sem,
        recv_sem=recv_sem,
        device_id=device,
        device_id_type=MESH,
    )


class Ring:
    def __init__(self, group, half, me, device_at, send_sems, recv_sems):
        right, left = lax.rem(me + 1, 4), lax.rem(me + 3, 4)
        to_right, to_left = device_at(right), device_at(left)

        def copy(ref, device, i):
            return remote(ref, ref, send_sems.at[i], recv_sems.at[i], device)

        self.direct = [copy(group(me), to_right, 0), copy(group(me), to_left, 1)]
        self.passed = [copy(half(left, 0), to_right, 2), copy(half(right, 1), to_left, 3)]

    def start(self):
        for copy in self.direct:
            copy.start()

    def forward(self):
        for arrived, onward in zip(self.direct, self.passed):
            arrived.wait_recv()
            onward.start()

    def finish(self):
        for copy in self.passed:
            copy.wait_recv()

    def drain(self):
        for copy in self.direct + self.passed:
            copy.wait_send()


class Place:
    def __init__(self):
        self.at = at = lax.axis_index("shard")
        self.rep = rep = lax.axis_index("rep")
        self.x, self.y, self.z = lax.div(at, 8), lax.rem(lax.div(at, 2), 4), lax.rem(at, 2)
        self.chip, self.core = chip, core = lax.div(rep, 2), lax.rem(rep, 2)
        self.pair = {"shard": at + 1 - 2 * self.z}
        self.theirs = (1 - chip) * 2 + core
        self.far = {"rep": self.theirs}
        self.near = {"rep": chip * 2 + 1 - core}

    def on_x(self, i):
        return {"shard": i * 8 + self.y * 2 + self.z}

    def on_y(self, i):
        return {"shard": self.x * 8 + i * 2 + self.z}

    def neighbours(self):
        return [self.on_x(lax.rem(self.x + d, 4)) for d in (1, 3)] + [
            self.on_y(lax.rem(self.y + d, 4)) for d in (1, 3)
        ]


class Gather:
    def __init__(self, place, block, whole, first_x, sems):
        x, y, z = place.x, place.y, place.z
        pair_send, pair_recv, ring_send, ring_recv = sems
        slot = whole.at[x, y, z]
        self.pair = remote(slot if block is None else block, slot, pair_send, pair_recv, place.pair)

        def x_small(j):
            return whole.at[j, y]

        def x_small_half(j, h):
            return whole.at[j, y, h]

        def y_small(j):
            return whole.at[x, j]

        def y_small_half(j, h):
            return whole.at[x, j, h]

        def x_large(j):
            return whole.at[j]

        def x_large_half(j, h):
            return whole.at[j, pl.ds(2 * h, 2)]

        def y_large(j):
            return whole.at[:, j]

        def y_large_half(j, h):
            return whole.at[pl.ds(2 * h, 2), j]

        near, wide = (ring_send.at[0], ring_recv.at[0]), (ring_send.at[1], ring_recv.at[1])
        if first_x:
            self.small = Ring(x_small, x_small_half, x, place.on_x, *near)
            self.large = Ring(y_large, y_large_half, y, place.on_y, *wide)
        else:
            self.small = Ring(y_small, y_small_half, y, place.on_y, *near)
            self.large = Ring(x_large, x_large_half, x, place.on_x, *wide)

    def drain(self):
        self.pair.wait_send()
        self.small.drain()
        self.large.drain()


GATHER_BLOCKS = (
    (32, QW + 2 * KW, True),
    (32, REP * KW, True),
    (32, QW, True),
    (8, 128, True),
    (32, OWN_FF, True),
    (32, OWN_FF, False),
    (24, D, False),
    (8, D, False),
    (8, D, False),
)
GATHER_HELD = 6
GATHER_ROWS = (1, 4, 1)
GATHER_CHUNKS = sum(GATHER_ROWS)


def gather_kernel(*refs):
    query, key, value, cross_key, cross_value, cross_query, small, gate, up, down, out, cross_out = refs[:12]
    seg_row, buckets = refs[12:14]
    n, n_rows = len(GATHER_BLOCKS), len(GATHER_ROWS)
    own_rows, refs = refs[14 : 14 + n_rows], refs[14 + n_rows :]
    wholes, all_rows, refs = refs[:n], refs[n : n + n_rows], refs[n + n_rows :]
    gains_out, curve_out, normed_out, qkv_out, context_out, kv_out, *refs = refs
    (local_sems, out_sems, piece_send, piece_recv, pair_send, pair_recv, ring_send, ring_recv, rep_send, rep_recv,
     load_sems, token_held, qkv_held, small_held, ckv_held, enc_held, bias_ref, *held) = refs
    held, held_rows = held[:GATHER_HELD], held[GATHER_HELD:]
    place = Place()
    at, rep, x, y, z = place.at, place.rep, place.x, place.y, place.z
    barrier = pltpu.get_barrier_semaphore()
    devices = [place.pair, place.far, place.near] + place.neighbours()
    for device in devices:
        pl.semaphore_signal(barrier, inc=1, device_id=device, device_id_type=MESH)
    goal = 4 * lax.rem(at, 8) + rep
    stays = (x == rep) & (goal == at)
    source = {"rep": lax.rem(at, 4), "shard": 8 * rep + lax.div(at, 4)}

    @pl.when(jnp.logical_not(stays))
    def _():
        pl.semaphore_signal(barrier, inc=1, device_id=source, device_id_type=MESH)

    pl.semaphore_wait(barrier, len(devices) + 1 - stays.astype(jnp.int32))

    wholes = list(wholes)
    halves = wholes[1]
    wholes[1] = halves.at[place.core]
    slots = [whole.at[x, y, z] for whole in wholes]
    count = [0]

    def own(source_ref, target):
        count[0] += 1
        return pltpu.make_async_copy(source_ref, target, local_sems.at[count[0] - 1])

    def part(ref, width, r=rep):
        return ref.at[:, pl.ds(pl.multiple_of(r * width, 128), width)]

    fills = [
        [
            own(part(query, QW), held[0].at[:, pl.ds(0, QW)]),
            own(part(key, KW), held[0].at[:, pl.ds(QW, KW)]),
            own(part(value, KW), held[0].at[:, pl.ds(QW + KW, KW)]),
        ],
        [
            own(part(cross_key, KW, place.core), held[1].at[:, pl.ds(0, KW)]),
            own(part(cross_value, KW, place.core), held[1].at[:, pl.ds(KW, KW)]),
            own(part(cross_key, KW, 2 + place.core), held[1].at[:, pl.ds(2 * KW, KW)]),
            own(part(cross_value, KW, 2 + place.core), held[1].at[:, pl.ds(3 * KW, KW)]),
        ],
        [own(part(cross_query, QW), held[2])],
        [own(small, held[3])],
        [own(gate, held[4])],
        [own(up, held[5])],
    ]
    firsts = [pl.multiple_of(24 * rep - 8 * lax.div(rep, 3), 8)] + [pl.multiple_of(8 * rep, 8)] * 2
    pieces = []
    for i, ref in enumerate((down, out, cross_out)):
        whole = wholes[GATHER_HELD + i]
        rows = ref.at[pl.ds(firsts[i], GATHER_BLOCKS[GATHER_HELD + i][0])]
        landing = whole.at[lax.div(goal, 8), lax.rem(lax.div(goal, 2), 4), lax.rem(goal, 2)]
        sent = remote(rows, landing, piece_send.at[i], piece_recv.at[i], {"rep": x, "shard": goal})
        pieces.append((sent, own(rows, landing)))
    for sent, stay in pieces:
        pl.when(jnp.logical_not(stays))(sent.start)
        pl.when(stays)(stay.start)
    for fill in fills:
        for copy in fill:
            copy.start()

    rep_first, rep_second, rep_local = [], [], []
    for i, parts in enumerate(GATHER_ROWS):
        whole = all_rows[i]
        rows = own_rows[i].shape[0] // parts
        first, second = (0, 1) if i == 1 else (rep, rep)
        third, fourth = (2, 3) if i == 1 else (place.theirs, place.theirs)
        landing = 2 if i == 1 else rep
        rep_local.append((own(own_rows[i], held_rows[i]), pltpu.make_async_copy(held_rows[i], whole.at[first], out_sems.at[n + i])))
        rep_local[i][0].start()
        for p in range(parts):
            span = pl.ds(p * rows, rows)
            j = len(rep_first)
            mine = own_rows[i].at[span]
            rep_first.append(remote(mine, whole.at[landing, span], rep_send.at[j, 0], rep_recv.at[j, 0], place.far))
            direct = remote(mine, whole.at[second, span], rep_send.at[j, 1], rep_recv.at[j, 1], place.near)
            onward = remote(whole.at[third, span], whole.at[fourth, span], rep_send.at[j, 2], rep_recv.at[j, 2], place.near)
            rep_second.append((direct, onward))

    gathers = []
    for i, (_, _, first_x) in enumerate(GATHER_BLOCKS):
        block = held[i] if i < GATHER_HELD else None
        sems = pair_send.at[i], pair_recv.at[i], ring_send.at[i], ring_recv.at[i]
        gathers.append(Gather(place, block, wholes[i], first_x, sems))
    settled = []
    for i in range(n):
        if i < GATHER_HELD:
            for copy in fills[i]:
                copy.wait()
            settled.append(pltpu.make_async_copy(held[i], slots[i], out_sems.at[i]))
            settled[i].start()
        else:
            sent, stay = pieces[i - GATHER_HELD]
            pl.when(jnp.logical_not(stays))(sent.wait_recv)
            pl.when(stays)(stay.wait)
        gathers[i].pair.start()
    for first, (direct, _) in zip(rep_first, rep_second):
        first.start()
        direct.start()
    for inward, outward in rep_local:
        inward.wait()
        outward.start()
    for i in range(n):
        if i < GATHER_HELD:
            settled[i].wait()
        gathers[i].pair.wait_recv()
        gathers[i].small.start()
    for one in gathers:
        one.small.forward()
    early, late, sideways = (0, 3, 1, 2), (4,), (7, 8, 6, 5)
    for i in early + sideways:
        gathers[i].small.finish()
        gathers[i].large.start()
    for j in range(2):
        rep_first[j].wait_recv()
        rep_second[j][1].start()
    for i in early:
        gathers[i].large.forward()
    for i in late:
        gathers[i].small.finish()
        gathers[i].large.start()
    gathers[7].large.forward()
    gathers[8].large.forward()
    lanes = pl.ds(pl.multiple_of(place.chip * 2 * KW, 2 * KW), 2 * KW)
    gathers[0].large.finish()
    gathers[3].large.finish()
    gathers[1].large.finish()
    half = halves.at[place.core]
    swap = remote(half, half, rep_send.at[GATHER_CHUNKS, 0], rep_recv.at[GATHER_CHUNKS, 0], place.near)
    swap.start()
    for copy in rep_second[0]:
        copy.wait_recv()
    rep_local[0][1].wait()
    loads = [
        pltpu.make_async_copy(half.at[:, :, :, :, lanes], ckv_held, load_sems.at[0]),
        pltpu.make_async_copy(wholes[0], qkv_held, load_sems.at[1]),
        pltpu.make_async_copy(wholes[3], small_held, load_sems.at[2]),
        pltpu.make_async_copy(all_rows[0], token_held, load_sems.at[3]),
    ]
    for load in loads:
        load.start()
    for load in loads:
        load.wait()
    unpack_small(rep, small_held[...], bucket_hot(buckets[...]), gains_out, curve_out)
    fill_bias(curve_out, bias_ref)
    for micro in range(MICRO):
        rows = slice(micro * ROWS, (micro + 1) * ROWS)
        normed, whole, mixed = self_attention(
            token_held[:, rows, :].reshape(SEQ, D),
            gains_out[0:1, :],
            qkv_held[...].reshape(D, QW + 2 * KW),
            self_mask(seg_row[micro]),
            bias_ref,
        )
        normed_out[:, rows, :] = normed.reshape(REP, ROWS, D)
        qkv_out[:, rows, :] = whole.reshape(REP, ROWS, QW + 2 * KW)
        context_out[:, rows, :] = mixed.reshape(REP, ROWS, QW)
    gathers[6].large.forward()
    gathers[5].large.forward()
    parts = GATHER_ROWS[1]
    tall = own_rows[1].shape[0] // parts

    def project(source_ref, k, p, count=2):
        rows = slice(p * tall, (p + count) * tall)
        kv_out[k, rows, :] = matmul(source_ref[...], ckv_held[...].reshape(D, 2 * KW)).astype(bf16)

    def load_half(k, p, slot):
        for q in (p, p + 1):
            rep_second[1 + q][0 if k == 1 else 1].wait_recv() if k != 2 else None
        load = pltpu.make_async_copy(
            all_rows[1].at[k, pl.ds(p * tall, 2 * tall)], enc_held.at[slot], load_sems.at[4 + slot]
        )
        load.start()
        return load

    first_near = load_half(1, 0, 0)
    project(held_rows[1], 0, 0, parts)
    for i in late:
        gathers[i].large.forward()
    first_near.wait()
    second_near = load_half(1, 2, 1)
    project(enc_held.at[0], 1, 0)
    second_near.wait()
    project(enc_held.at[1], 1, 2)
    for p in (0, 2):
        for q in (p, p + 1):
            if q:
                rep_first[1 + q].wait_recv()
                rep_second[1 + q][1].start()
        far_load = load_half(2, p, 2)
        far_load.wait()
        project(enc_held.at[2], 2, p)
        across_load = load_half(3, p, p // 2)
        across_load.wait()
        project(enc_held.at[p // 2], 3, p)
    for i in late + sideways + early[3:]:
        gathers[i].large.finish()
    rep_first[GATHER_CHUNKS - 1].wait_recv()
    rep_second[GATHER_CHUNKS - 1][1].start()
    for sent, _ in pieces:
        pl.when(jnp.logical_not(stays))(sent.wait_send)
    for one in gathers:
        one.drain()
    for _, outward in rep_local[1:]:
        outward.wait()
    for j, (first, second) in enumerate(zip(rep_first, rep_second)):
        first.wait_send()
        for copy in second:
            copy.wait_send()
            if j == GATHER_CHUNKS - 1:
                copy.wait_recv()
    swap.wait()


def gather_weights(weights, tables, rows):
    n = len(GATHER_BLOCKS)
    shapes = [
        jax.ShapeDtypeStruct(((2,) if i == 1 else ()) + (4, 4, 2, r, c), bf16)
        for i, (r, c, _) in enumerate(GATHER_BLOCKS)
    ]
    shapes += [jax.ShapeDtypeStruct((REP,) + value.shape, value.dtype) for value in rows]
    own = MICRO * ROWS
    n_far = len(shapes)
    shapes += [jax.ShapeDtypeStruct((8, D), f32), jax.ShapeDtypeStruct((8, SEQ), f32)]
    shapes += [jax.ShapeDtypeStruct((REP, own, width), bf16) for width in (D, QW + 2 * KW, QW)]
    shapes.append(jax.ShapeDtypeStruct((REP, rows[1].shape[0], 2 * KW), bf16))
    anywhere = pl.BlockSpec(memory_space=pltpu.HBM)
    here = pl.BlockSpec(memory_space=pltpu.VMEM)
    dma = pltpu.SemaphoreType.DMA
    results = pl.pallas_call(
        gather_kernel,
        name="gather_weights",
        in_specs=[anywhere] * len(weights) + [here] * len(tables) + [anywhere] * len(rows),
        out_specs=[anywhere] * n_far + [here] * (len(shapes) - n_far),
        out_shape=shapes,
        scratch_shapes=[
            dma((11 + 3 + len(rows),)),
            dma((n + len(rows),)),
            dma((3,)),
            dma((3,)),
            dma((n,)),
            dma((n,)),
            dma((n, 2, 4)),
            dma((n, 2, 4)),
            dma((GATHER_CHUNKS + 1, 3)),
            dma((GATHER_CHUNKS + 1, 3)),
            dma((7,)),
            pltpu.VMEM((REP, own, D), bf16),
            pltpu.VMEM((4, 4, 2, 32, QW + 2 * KW), bf16),
            pltpu.VMEM((4, 4, 2, 8, 128), bf16),
            pltpu.VMEM((4, 4, 2, 32, 2 * KW), bf16),
            pltpu.VMEM((3, rows[1].shape[0] // 2, D), bf16),
            pltpu.VMEM((OWN_HEADS, SEQ, SEQ), f32),
        ]
        + [pltpu.VMEM((r, c), bf16) for r, c, _ in GATHER_BLOCKS[:GATHER_HELD]]
        + [pltpu.VMEM(value.shape, value.dtype) for value in rows],
        compiler_params=pltpu.CompilerParams(
            collective_id=0, has_side_effects=True, vmem_limit_bytes=56 * mebibyte
        ),
        cost_estimate=estimate(0, 128 << 20, 0),
    )(*weights, *tables, *rows)
    return results[:n], results[n : n + len(rows)], results[n + len(rows) :]


class ReduceRing:
    def __init__(self, half, whole_half, me, device_at, first, second, send_sems, recv_sems):
        right, left, far = lax.rem(me + 1, 4), lax.rem(me + 3, 4), lax.rem(me + 2, 4)
        to_right, to_left = device_at(right), device_at(left)

        def copy(source, target, device, i):
            return remote(source, target, send_sems.at[i], recv_sems.at[i], device)

        self.half, self.me, self.right, self.left = half, me, right, left
        self.first, self.second = first, second
        self.opening = [
            copy(whole_half(far, 0), first.at[0], to_right, 0),
            copy(whole_half(far, 1), first.at[1], to_left, 1),
        ]
        self.plain = [
            copy(whole_half(right, 1), second.at[0, 1], to_right, 2),
            copy(whole_half(left, 0), second.at[1, 0], to_left, 3),
        ]
        self.summed = [
            copy(first.at[0], second.at[0, 0], to_right, 4),
            copy(first.at[1], second.at[1, 1], to_left, 5),
        ]

    def start(self):
        for copy in self.opening + self.plain:
            copy.start()

    def middle(self, each):
        for h, group in enumerate((self.right, self.left)):
            self.opening[h].wait_recv()

            def add(*k, h=h, group=group):
                mixed = self.first[(h, *k)].astype(f32) + self.half(group, h, *k).astype(f32)
                self.first[(h, *k)] = mixed.astype(self.first.dtype)

            each(add)
            self.summed[h].start()

    def finish(self, each, store):
        for h in range(2):
            (self.plain[1] if h == 0 else self.plain[0]).wait_recv()
            self.summed[h].wait_recv()

            def add(*k, h=h):
                mixed = self.second[(0, h, *k)].astype(f32) + self.second[(1, h, *k)].astype(f32)
                store(h, *k, mixed + self.half(self.me, h, *k).astype(f32))

            each(add)

    def drain(self):
        for copy in self.opening + self.plain + self.summed:
            copy.wait_send()


def each_of_four(body):
    def step(i, carry):
        body(lax.div(i, 2), lax.rem(i, 2))
        return carry

    lax.fori_loop(0, 4, step, 0)


def just_once(body):
    body()


def grad_halves(grad, on_y):
    if on_y:
        return (lambda j, h, a, b: grad[2 * h + a, j, b]), (lambda j, h: grad.at[pl.ds(2 * h, 2), j])
    return (lambda j, h, a, b: grad[j, 2 * h + a, b]), (lambda j, h: grad.at[j, pl.ds(2 * h, 2)])


def large_ring(place, grad, on_y, first, second, sems):
    half, whole_half = grad_halves(grad, on_y)
    axis = (place.y, place.on_y) if on_y else (place.x, place.on_x)
    return ReduceRing(half, whole_half, *axis, first, second, *sems)


def large_store(mid):
    def store(h, a, b, total):
        mid[2 * h + a, b] = total.astype(mid.dtype)

    return store


def large_scratch(rows, width, dtype):
    return [pltpu.VMEM((2, 2, 2, rows, width), dtype), pltpu.VMEM((2, 2, 2, 2, rows, width), dtype)]


REDUCE_BLOCKS = (
    (32, QW + 2 * KW, True, bf16, True),
    (32, 2 * KW, False, bf16, True),
    (32, QW, False, bf16, True),
    (32, OWN_FF, True, bf16, True),
    (32, OWN_FF, False, bf16, True),
    (24, D, True, bf16, True),
    (8, D, False, bf16, True),
    (8, D, False, bf16, True),
    (8, 128, False, f32, False),
)
COLUMN_BLOCKS = (0, 1, 2, 3, 4)
PIECE_BLOCKS = (5, 6, 7)
SMALL_BLOCK = 8
BLOCK_ROWS = D // 4


def fill_columns(left, right, grad):
    def step(j, carry):
        lanes = pl.ds(pl.multiple_of(j * BLOCK_ROWS, BLOCK_ROWS), BLOCK_ROWS)
        part = left_contract(left[:, lanes], right[...])
        grad[j] = part.astype(grad.dtype).reshape(grad.shape[1:])
        return carry

    lax.fori_loop(0, 4, step, 0)


def in_thirds(value):
    parts = []
    for _ in range(3):
        parts.append(value.astype(bf16))
        value = value - parts[-1].astype(f32)
    return parts


def exact_matmul(value, ones):
    return sum(matmul(part, ones) for part in in_thirds(value))


def fill_small(rep, accs, curve_grad, hot, blocks):
    owner = lax.broadcasted_iota(jnp.int32, (SHARDS, D), 0)
    entry = lax.broadcasted_iota(jnp.int32, (SHARDS, D), 1)
    column = lax.broadcasted_iota(jnp.int32, (D, 128), 0)
    lane = lax.broadcasted_iota(jnp.int32, (D, 128), 1)
    per = D // SHARDS
    total = None
    for i, acc in enumerate(accs):
        picked = jnp.where(lax.div(entry, per) == owner, acc[...], 0.0)
        ones = (lax.rem(column, per) == lane - per * i).astype(f32).astype(bf16)
        part = exact_matmul(picked, ones)
        total = part if total is None else total + part
    rows = sum(right_contract(hot, part) for part in in_thirds(curve_grad[...]))
    head = lax.broadcasted_iota(jnp.int32, (8, 128), 0)
    place = lax.broadcasted_iota(jnp.int32, (8, 128), 1)
    ones = ((head < OWN_HEADS) & (place == 3 * per + OWN_HEADS * rep + head)).astype(f32).astype(bf16)
    total = total + exact_matmul(rows, ones)
    for i in range(SHARDS):
        blocks[i // 8, i // 2 % 4, i % 2] = jnp.broadcast_to(total[i : i + 1, :], (8, 128))


def fill_rows(left, right, grad):
    grad[...] = left_contract(left[...], right[...]).reshape(grad.shape).astype(grad.dtype)


def fill_stream(left, right, grad, held, room, sems):
    n = left.shape[0]
    loads = [pltpu.make_async_copy(left.at[i], held.at[i % 2], sems.at[i]) for i in range(n)]
    loads[0].start()
    loads[1].start()
    for i in range(n):
        loads[i].wait()
        part = left_contract(right[i], held[i % 2])
        room[...] = part if i == 0 else room[...] + part
        if i + 2 < n:
            loads[i + 2].start()

    def turn(j, carry):
        lanes = pl.ds(pl.multiple_of(j * BLOCK_ROWS, BLOCK_ROWS), BLOCK_ROWS)
        grad[j] = room[:, lanes].T.astype(grad.dtype).reshape(grad.shape[1:])
        return carry

    lax.fori_loop(0, 4, turn, 0)


def fill_down(left, right, grad, room):
    def step(j, carry):
        lanes = pl.ds(pl.multiple_of(j * BLOCK_ROWS, BLOCK_ROWS), BLOCK_ROWS)
        room[:, lanes] = left_contract(left[...], right[:, lanes])
        return carry

    lax.fori_loop(0, 4, step, 0)

    def place(a, carry):
        for q in range(REP):
            rows = pl.ds(pl.multiple_of(a * 88 + min(24 * q, 64), 8), 24)
            grad[lax.div(a, 2), 2 * lax.rem(a, 2) + q // 2, q % 2] = room[rows, :].astype(grad.dtype)
        return carry

    lax.fori_loop(0, 8, place, 0)


def reduce_kernel(*refs):
    n = len(REDUCE_BLOCKS)
    own = MICRO * ROWS
    layer_part, hidden, self_acc, cross_acc, feed_acc, curve_grad, buckets, *refs = refs
    given = [i for i in range(n) if REDUCE_BLOCKS[i][4]]
    mids, refs = refs[: len(given)], refs[len(given) :]
    alls, refs = refs[: len(COLUMN_BLOCKS)], refs[len(COLUMN_BLOCKS) :]
    gathered, refs = refs[: len(PIECE_BLOCKS)], refs[len(PIECE_BLOCKS) :]
    small_out, layer_out, *refs = refs
    small_blocks, *refs = refs
    grads = {SMALL_BLOCK: small_blocks}
    scratch = []
    for i in range(n):
        extra = 0 if REDUCE_BLOCKS[i][4] else 3
        scratch.append(([None, None, mids[given.index(i)]] if extra == 0 else refs[:3]) + refs[extra : extra + 5])
        refs = refs[extra + 5 :]
    (small_far, small_near, core_recv, far_send, far_recv, near_sum) = refs[:6]
    ring_send, ring_recv, pair_send, pair_recv, rep_send, rep_recv, piece_send, piece_recv, more_send, more_recv = (
        refs[6:]
    )
    place = Place()
    at, rep, x, y, z, theirs = place.at, place.rep, place.x, place.y, place.z, place.theirs
    barrier = pltpu.get_barrier_semaphore()
    devices = [place.pair, place.far, place.near] + place.neighbours()
    for device in devices:
        pl.semaphore_signal(barrier, inc=1, device_id=device, device_id_type=MESH)
    owner = 8 * rep + lax.div(at, 4)
    slot = lax.rem(at, 4)
    stays = owner == at

    def from_self(q):
        return (x == rep) & (4 * lax.rem(at, 8) + q == at)

    for q in range(REP):
        giver = {"rep": x, "shard": 4 * lax.rem(at, 8) + q}

        @pl.when(jnp.logical_not(from_self(q)))
        def _(giver=giver):
            pl.semaphore_signal(barrier, inc=1, device_id=giver, device_id_type=MESH)

    fill_small(rep, (self_acc, cross_acc, feed_acc), curve_grad, bucket_hot(buckets[...]), small_blocks)
    pl.semaphore_wait(barrier, len(devices) + REP - stays.astype(jnp.int32))

    large, small = [], []
    for i, (_, _, on_y, _, done) in enumerate(REDUCE_BLOCKS):
        first, second, mid, first_small, second_small = scratch[i][:5]

        def half_small(j, h, mid=mid):
            return mid[j, h]

        def whole_half_small(j, h, mid=mid):
            return mid.at[j, h]

        if not done:
            large.append((i, large_ring(place, grads[i], on_y, first, second, (ring_send.at[i, 0], ring_recv.at[i, 0]))))
        narrow = (x, place.on_x) if on_y else (y, place.on_y)
        small.append(
            ReduceRing(
                half_small, whole_half_small, *narrow, first_small, second_small, ring_send.at[i, 1], ring_recv.at[i, 1]
            )
        )
    for i, ring in enumerate(small):
        if REDUCE_BLOCKS[i][4]:
            ring.start()
    for _, ring in large:
        ring.start()

    to_core = [
        remote(
            layer_part.at[there * 2 + 1 - place.core], core_recv.at[i], more_send.at[i], more_recv.at[i], place.near
        )
        for i, there in enumerate((1 - place.chip, place.chip))
    ]
    for copy in to_core:
        copy.start()
    to_core[0].wait_recv()
    far_send[...] = (layer_part[theirs].astype(f32) + core_recv[0].astype(f32)).astype(bf16)
    to_far = remote(far_send, far_recv, more_send.at[2], more_recv.at[2], place.far)
    to_far.start()
    to_core[1].wait_recv()
    near_sum[...] = hidden[...] + layer_part[rep].astype(f32) + core_recv[1].astype(f32)

    for i, ring in enumerate(small):
        if REDUCE_BLOCKS[i][4]:
            ring.middle(just_once)
    for _, ring in large:
        ring.middle(each_of_four)
    for i, ring in large:
        ring.finish(each_of_four, large_store(scratch[i][2]))
        small[i].start()
    to_far.wait_recv()
    layer_out[...] = (near_sum[...] + far_recv[...].astype(f32)).astype(bf16)
    for i, ring in enumerate(small):
        if not REDUCE_BLOCKS[i][4]:
            ring.middle(just_once)
    pairs = []
    for i, ring in enumerate(small):
        low = scratch[i][5]

        def store(h, total, low=low):
            low[h] = total.astype(low.dtype)

        ring.finish(just_once, store)
        pairs.append(remote(low.at[1 - z], scratch[i][6], pair_send.at[i], pair_recv.at[i], place.pair))
        pairs[i].start()
    spread, onward, handed = [], [], []
    for i in range(n):
        low, arrived, result = scratch[i][5:8]
        pairs[i].wait_recv()
        total = (low[z].astype(f32) + arrived[...].astype(f32)).astype(low.dtype)
        if i in COLUMN_BLOCKS:
            j = COLUMN_BLOCKS.index(i)
            alls[j][rep] = total
            mine, other = alls[j].at[rep], alls[j].at[theirs]
            spread.append(
                [
                    remote(mine, mine, rep_send.at[j, 0], rep_recv.at[j, 0], place.far),
                    remote(mine, mine, rep_send.at[j, 1], rep_recv.at[j, 1], place.near),
                ]
            )
            onward.append(remote(other, other, rep_send.at[j, 2], rep_recv.at[j, 2], place.near))
            for copy in spread[j]:
                copy.start()
        elif i in PIECE_BLOCKS:
            j = PIECE_BLOCKS.index(i)
            result[...] = total
            for k in range(REP):
                copy = remote(
                    result,
                    gathered[j].at[slot],
                    piece_send.at[j, k],
                    piece_recv.at[j, slot],
                    {"rep": jnp.int32(k), "shard": owner},
                )
                own_piece = stays & (rep == k)
                handed.append((own_piece, copy))
                pl.when(jnp.logical_not(own_piece))(copy.start)

            @pl.when(stays)
            def _(j=j, total=total):
                gathered[j][slot] = total
        else:
            result[...] = total
    result = scratch[SMALL_BLOCK][7]
    small_first = remote(result, small_far, more_send.at[9], more_recv.at[9], place.far)
    small_first.start()
    for j in range(len(onward)):
        spread[j][0].wait_recv()
        onward[j].start()
    small_first.wait()
    result[...] = result[...] + small_far[...]
    small_second = remote(result, small_near, more_send.at[10], more_recv.at[10], place.near)
    small_second.start()
    small_second.wait()
    small_out[...] = result[...] + small_near[...]
    for j in range(len(onward)):
        spread[j][1].wait_recv()
        onward[j].wait_recv()
    for j in range(len(PIECE_BLOCKS)):
        for q in range(REP):
            landed = gathered[j].at[q]
            arrival = remote(
                landed, landed, piece_send.at[j, q], piece_recv.at[j, q], {"rep": x, "shard": 4 * lax.rem(at, 8) + q}
            )
            pl.when(jnp.logical_not(from_self(q)))(arrival.wait_recv)
    for _, ring in large:
        ring.drain()
    for ring in small:
        ring.drain()
    for own_piece, copy in handed:
        pl.when(jnp.logical_not(own_piece))(copy.wait_send)
    for copy in to_core + [to_far] + pairs + onward + [one for two in spread for one in two]:
        copy.wait_send()


def reduce_grads(layer_part, hidden, accs, curve_grad, buckets, mids):
    n = len(REDUCE_BLOCKS)
    own = MICRO * ROWS
    shapes = [jax.ShapeDtypeStruct((REP,) + REDUCE_BLOCKS[i][:2], bf16) for i in COLUMN_BLOCKS + PIECE_BLOCKS]
    shapes += [jax.ShapeDtypeStruct((8, 128), f32), jax.ShapeDtypeStruct((own, D), bf16)]
    here = pl.BlockSpec(memory_space=pltpu.VMEM)
    dma = pltpu.SemaphoreType.DMA
    scratch = [pltpu.VMEM((4, 4, 2) + REDUCE_BLOCKS[SMALL_BLOCK][:2], f32)]
    for rows, width, _, dtype, done in REDUCE_BLOCKS:
        if not done:
            scratch += large_scratch(rows, width, dtype) + [pltpu.VMEM((4, 2, rows, width), dtype)]
        for lead in ((2,), (2, 2), (2,), (), ()):
            scratch.append(pltpu.VMEM(lead + (rows, width), dtype))
    scratch += [
        pltpu.VMEM((8, 128), f32),
        pltpu.VMEM((8, 128), f32),
        pltpu.VMEM((2, own, D), bf16),
        pltpu.VMEM((own, D), bf16),
        pltpu.VMEM((own, D), bf16),
        pltpu.VMEM((own, D), f32),
    ]
    scratch += [dma((n, 2, 6)), dma((n, 2, 6)), dma((n,)), dma((n,)), dma((5, 3)), dma((5, 3))]
    scratch += [dma((3, REP)), dma((3, REP)), dma((11,)), dma((11,))]
    return pl.pallas_call(
        reduce_kernel,
        name="reduce_grads",
        in_specs=[here] * (7 + len(mids)),
        out_specs=[here] * len(shapes),
        out_shape=shapes,
        scratch_shapes=scratch,
        compiler_params=pltpu.CompilerParams(
            collective_id=6, has_side_effects=True, vmem_limit_bytes=20 * mebibyte
        ),
        cost_estimate=estimate(0, 128 << 20, 0),
    )(layer_part, hidden, *accs, curve_grad, buckets, *mids)


def norm_parts(values):
    return lax.rsqrt(jnp.mean(values * values, axis=-1, keepdims=True) + epsilon)


class ReduceRider:
    def __init__(self, jobs):
        self.jobs = [(i, fill) for i, fill, _, _ in jobs]
        self.operands, self.uses = [], []
        for _, _, left, right in jobs:
            use = []
            for value in (left, right):
                found = [k for k, other in enumerate(self.operands) if other is value]
                if not found:
                    self.operands.append(value)
                use.append(found[0] if found else len(self.operands) - 1)
            self.uses.append(use)
        n = len(jobs)
        dma = pltpu.SemaphoreType.DMA
        self.shapes, self.scratch = [], [dma((n, 6)), dma((n, 6))]
        for i, fill in self.jobs:
            rows, width, _, dtype, _ = REDUCE_BLOCKS[i]
            self.shapes.append(jax.ShapeDtypeStruct((4, 2, rows, width), dtype))
            self.scratch += [pltpu.VMEM((4, 4, 2, rows, width), dtype)] + large_scratch(rows, width, dtype)
        here, there = pl.BlockSpec(memory_space=pltpu.VMEM), pl.BlockSpec(memory_space=pltpu.HBM)
        self.in_specs = [here] * len(self.operands)
        for (_, fill), use in zip(self.jobs, self.uses):
            if fill is fill_down:
                self.scratch.append(pltpu.VMEM((OWN_FF, D), f32))
            if fill is fill_stream:
                self.in_specs[use[0]] = there
                left, right = (self.operands[u] for u in use)
                self.scratch += [pltpu.VMEM((2,) + left.shape[1:], bf16), pltpu.VMEM((right.shape[2], D), f32), dma((REP,))]
        self.out_specs = [pl.BlockSpec(memory_space=pltpu.VMEM)] * n

    def steps(self, place, operands, mids, scratch):
        send, recv, *rooms = scratch
        rings, fills = [], []
        for k, (i, fill) in enumerate(self.jobs):
            grad, first, second = rooms[3 * k : 3 * k + 3]
            rings.append(large_ring(place, grad, REDUCE_BLOCKS[i][2], first, second, (send.at[k], recv.at[k])))
            extra = rooms[3 * len(self.jobs) :]
            more = extra if fill in (fill_down, fill_stream) else []
            left, right = (operands[u] for u in self.uses[k])
            fills.append(lambda fill=fill, left=left, right=right, grad=grad, more=more: fill(left, right, grad, *more))

        def begin():
            fills[0]()
            rings[0].start()

        def rest():
            for fill, ring in zip(fills[1:], rings[1:]):
                fill()
                ring.start()

        def nothing():
            pass

        def middle():
            for ring in rings:
                ring.middle(each_of_four)

        def end():
            for ring, mid in zip(rings, mids):
                ring.finish(each_of_four, large_store(mid))
            for ring in rings:
                ring.drain()

        return [begin, rest, nothing, middle, end]


def boundary_kernel(n_pairs, turned, forward, gathers, rider, which, *refs):
    pairs = [(refs[2 * i], refs[2 * i + 1]) for i in range(n_pairs)]
    rest = refs[2 * n_pairs :]
    if forward:
        hidden_ref, gain_ref, *rest = rest
    else:
        values_ref, hidden_ref, gain_ref, *rest = rest
    n_ride = len(rider.operands) if rider else 0
    riding, rest = rest[:n_ride], rest[n_ride:]
    out_ref, *rest = rest
    if not forward:
        acc_ref, *rest = rest
    if gathers:
        all_ref, *rest = rest
    n_ridden = len(rider.shapes) if rider else 0
    ridden, rest = rest[:n_ridden], rest[n_ridden:]
    core_send, core_recv, far_send, far_recv, near_sum, send_sems, recv_sems, *rest = rest
    place = Place()
    rep, chip, core, theirs, far, near = place.rep, place.chip, place.core, place.theirs, place.far, place.near
    barrier = pltpu.get_barrier_semaphore()
    devices = [far, near]
    steps = []
    if rider:
        devices += [place.pair] + place.neighbours()
        steps = rider.steps(place, riding, ridden, rest)

    def ride():
        if steps:
            steps.pop(0)()

    for device in devices:
        pl.semaphore_signal(barrier, inc=1, device_id=device, device_id_type=MESH)

    def partial(r):
        product = right_contract if turned else matmul
        total = product(pairs[0][0][r], pairs[0][1][...])
        for left, right in pairs[1:]:
            total = total + product(left[r], right[...])
        return total

    def copy(source, target, i, device):
        return remote(source, target, send_sems.at[i], recv_sems.at[i], device)

    half = ROWS
    chunks = [pl.ds(c * half, half) for c in range(MICRO)]
    to_core = []
    for i, there in enumerate((1 - chip, chip)):
        core_send[i] = partial(there * 2 + 1 - core).astype(bf16)
        to_core.append(copy(core_send.at[i], core_recv.at[i], i, near))
        if i == 0:
            pl.semaphore_wait(barrier, len(devices))
        to_core[i].start()
    far_own = partial(theirs)
    to_core[0].wait_recv()
    far_send[...] = (far_own + core_recv[0].astype(f32)).astype(bf16)
    to_far = [copy(far_send.at[rows], far_recv.at[rows], 2 + c, far) for c, rows in enumerate(chunks)]
    for sent in to_far:
        sent.start()
    near_own = partial(rep)
    to_core[1].wait_recv()
    near_sum[...] = near_own + core_recv[1].astype(f32)
    ride()
    spread, onward = [], []
    acc = None
    for c, rows in enumerate(chunks):
        to_far[c].wait_recv()
        total = near_sum[rows, :] + far_recv[rows, :].astype(f32)
        gain = gain_ref[which : which + 1, :]
        if forward:
            fresh = hidden_ref[rows, :].astype(f32) + total
            sent = (fresh * norm_parts(fresh) * gain).astype(bf16)
        else:
            values = values_ref[rows, :].astype(f32)
            rho = norm_parts(values)
            scaled = gain * total
            inner = jnp.mean(values * scaled, axis=-1, keepdims=True)
            fresh = hidden_ref[rows, :].astype(f32) + rho * scaled - values * (rho * rho * rho * inner)
            part = jnp.sum(values * rho * total, axis=0, keepdims=True)
            acc = part if acc is None else acc + part
            sent = fresh.astype(bf16)
        out_ref[rows, :] = fresh
        if gathers:
            all_ref[rep, rows, :] = sent
            mine = all_ref.at[rep, rows]
            other = all_ref.at[theirs, rows]
            spread.append((copy(mine, mine, 4 + c, far), copy(mine, mine, 6 + c, near)))
            onward.append(copy(other, other, 8 + c, near))
            for one in spread[c]:
                one.start()
        ride()
    if not forward:
        acc_ref[...] = acc
    for c in range(len(onward)):
        spread[c][0].wait_recv()
        onward[c].start()
    ride()
    for c in range(len(onward)):
        spread[c][1].wait_recv()
        onward[c].wait_recv()
    ride()
    for sent in to_core + to_far + [one for two in spread for one in two] + onward:
        sent.wait_send()


def boundary(name, identity, pairs, turned, hidden, gains, which, values=None, gathers=True, rider=None):
    own = MICRO * ROWS
    forward = values is None
    operands = [a.reshape(REP, own, -1) if i == 0 else a for pair in pairs for i, a in enumerate(pair)]
    operands += ([] if forward else [values]) + [hidden, gains]
    in_specs = [pl.BlockSpec(memory_space=pltpu.VMEM)] * len(operands)
    shapes = [jax.ShapeDtypeStruct((own, D), f32)]
    if not forward:
        shapes.append(jax.ShapeDtypeStruct((1, D), f32))
    if gathers:
        shapes.append(jax.ShapeDtypeStruct((REP, own, D), bf16))
    here = pl.BlockSpec(memory_space=pltpu.VMEM)
    out_specs = [here] * len(shapes)
    if rider:
        operands += rider.operands
        in_specs += rider.in_specs
        shapes += rider.shapes
        out_specs += rider.out_specs
    dma = pltpu.SemaphoreType.DMA
    return pl.pallas_call(
        lambda *refs: boundary_kernel(len(pairs), turned, forward, gathers, rider, which, *refs),
        name=name,
        in_specs=in_specs,
        out_specs=out_specs,
        out_shape=shapes,
        scratch_shapes=[
            pltpu.VMEM((2, own, D), bf16),
            pltpu.VMEM((2, own, D), bf16),
            pltpu.VMEM((own, D), bf16),
            pltpu.VMEM((own, D), bf16),
            pltpu.VMEM((own, D), f32),
            dma((10,)),
            dma((10,)),
        ]
        + (rider.scratch if rider else []),
        compiler_params=pltpu.CompilerParams(
            collective_id=identity, has_side_effects=True, vmem_limit_bytes=(36 if identity == 5 else 24 if rider else 14) * mebibyte
        ),
        cost_estimate=estimate(1 << 30, 32 << 20, 0),
    )(*operands)


FINAL_COLUMNS = (
    (0, 0, QW),
    (0, QW, KW),
    (0, QW + KW, KW),
    (1, 0, KW),
    (1, KW, KW),
    (2, 0, QW),
    (3, 0, OWN_FF),
    (4, 0, OWN_FF),
)


def finish_kernel(*refs):
    n = len(COLUMN_BLOCKS) + len(PIECE_BLOCKS)
    columns, pieces = refs[: len(COLUMN_BLOCKS)], refs[len(COLUMN_BLOCKS) : n]
    kv_refs, w_ref = refs[n : n + REP], refs[n + REP]
    finals, enc_ref = refs[n + REP + 1 : -1], refs[-1]
    rep = lax.axis_index("rep")
    chip, core = lax.div(rep, 2), lax.rem(rep, 2)
    total = None
    for i, kv_ref in enumerate(kv_refs):
        there, which = (1 - chip if i // 2 else chip), (1 - core if i % 2 else core)
        lanes = pl.ds(pl.multiple_of(there * 2 * KW, 2 * KW), 2 * KW)
        part = right_contract(kv_ref[...], w_ref[which, :, lanes])
        total = part if total is None else total + part
    enc_ref[...] = total

    @pl.when(pl.program_id(0) == 0)
    def _():
        for final, (source, first, width) in zip(finals, FINAL_COLUMNS):
            parts = [columns[source][r, :, first : first + width].astype(f32) for r in range(REP)]
            final[...] = jnp.concatenate(parts, axis=1)
        for final, piece in zip(finals[len(FINAL_COLUMNS) :], pieces):
            rows = piece.shape[1]
            for q in range(REP):
                skip = REP * rows - final.shape[0] if q == REP - 1 else 0
                final[q * rows : (q + 1) * rows - skip, :] = piece[q, skip:, :].astype(f32)


def finish(columns, pieces, kv_parts, w_ckv):
    shapes = [jax.ShapeDtypeStruct((columns[i].shape[1], REP * width), f32) for i, _, width in FINAL_COLUMNS]
    shapes += [jax.ShapeDtypeStruct((tall, D), f32) for tall in (FF // SHARDS, 32, 32)]
    shapes.append(jax.ShapeDtypeStruct((kv_parts[0].shape[0], D), f32))
    tall = kv_parts[0].shape[0] // 4
    some = pl.BlockSpec((tall, D), lambda i: (i, 0))
    return pl.pallas_call(
        finish_kernel,
        name="finish",
        grid=(4,),
        in_specs=[fixed_block(value.shape) for value in columns + pieces]
        + [pl.BlockSpec((tall, 2 * KW), lambda i: (i, 0))] * REP
        + [fixed_block(w_ckv.shape)],
        out_specs=[fixed_block(shape.shape) for shape in shapes[:-1]] + [some],
        out_shape=shapes,
        compiler_params=pltpu.CompilerParams(vmem_limit_bytes=24 * mebibyte),
        cost_estimate=estimate(2 << 30, 12 << 20, 0),
    )(*columns, *pieces, *kv_parts, w_ckv)


def local(
    tokens,
    out_cotangent,
    encoded,
    segment_ids,
    doc_block,
    bucket_table,
    self_gain,
    query_weight,
    key_weight,
    value_weight,
    out_weight,
    bias_table,
    cross_gain,
    cross_query,
    cross_key,
    cross_value,
    cross_out,
    feed_gain,
    gate_weight,
    up_weight,
    down_weight,
):
    rep = lax.axis_index("rep")
    own = MICRO * ROWS
    enc_rows = MICRO * DOCS * ENC // REP

    def columns(weight, width):
        return lax.dynamic_slice_in_dim(weight, rep * width, width, 1)

    segments = segment_ids[:, 0]
    seg_row = segments[:, None, :]
    buckets = bucket_table.reshape(1, SEQ)
    doc_ids = jnp.arange(DOCS, dtype=jnp.int32)
    ends = jnp.sum((segments[:, None, :] <= doc_ids[None, :, None]).astype(jnp.int32), axis=2)
    begins = jnp.pad(ends[:, :-1], ((0, 0), (1, 0)))
    wides = (ends - begins > NARROW - 16).astype(jnp.int32)
    starts = jnp.minimum(begins // 16 * 16, jnp.where(wides == 0, SEQ - NARROW, SEQ - WINDOW))
    spans = [value.reshape(-1) for value in (doc_block[:, 0], starts, wides, begins, ends)]

    small = sum(
        jnp.pad(value.reshape(1, -1), ((0, 7), (32 * i, 128 - 32 * i - value.size)))
        for i, value in enumerate((self_gain, cross_gain, feed_gain, bias_table))
    )
    own_tokens = tokens.reshape(own, D)
    own_cotangent = out_cotangent.reshape(own, D)
    wholes, (all_tokens, all_enc, all_grad), ready = gather_weights(
        [
            query_weight,
            key_weight,
            value_weight,
            cross_key,
            cross_value,
            cross_query,
            small,
            columns(gate_weight, OWN_FF),
            columns(up_weight, OWN_FF),
            down_weight,
            out_weight,
            cross_out,
        ],
        [seg_row, buckets],
        [own_tokens, encoded.reshape(enc_rows, D), own_cotangent],
    )
    w_qkv, w_ckv, w_cq, small, w_gate, w_up, w_down, w_out, w_cout = wholes
    w_gate = w_gate.reshape(D, OWN_FF)
    w_up = w_up.reshape(D, OWN_FF)
    gains, curve, normed, qkv, context, kv = ready
    w_qkv = w_qkv.reshape(D, QW + 2 * KW)
    w_out = w_out.reshape(QW, D)
    w_ckv = w_ckv.reshape(2, D, REP * KW)
    w_cq = w_cq.reshape(D, QW)
    w_cout = w_cout.reshape(QW, D)
    w_down = w_down.reshape(SHARDS, 24, D)
    all_grad = all_grad.reshape(REP * own, D)

    all_enc = all_enc.reshape(REP * enc_rows, D)

    qkv = qkv.reshape(REP, MICRO, ROWS, QW + 2 * KW)
    normed = normed.reshape(REP * own, D)
    context = context.reshape(REP * own, QW)
    hidden, cross_normed = boundary("after_self", 1, [(context, w_out)], False, own_tokens, gains, 1)
    kv = kv.reshape(REP, MICRO, DOCS, ENC // REP, 2 * KW)
    cross_normed = cross_normed.reshape(REP * own, D)
    cross_queries = matmul(cross_normed, w_cq).astype(bf16).reshape(REP, MICRO, ROWS, QW)
    cross_context = cross_forward(spans, cross_queries, kv).reshape(REP * own, QW)
    hidden_two, feed_normed = boundary("after_cross", 2, [(cross_context, w_cout)], False, hidden, gains, 2)
    feed_normed = feed_normed.reshape(REP * own, D)
    inner, gate_low, up_low, layer_part = feed(feed_normed.reshape(REP, own, D), all_grad.reshape(REP, own, D), w_gate, w_up, w_down)
    inner = inner.reshape(REP * own, OWN_FF)
    gate_low = gate_low.reshape(REP * own, OWN_FF)
    up_low = up_low.reshape(REP * own, OWN_FF)

    hidden_grad, feed_acc, branch, gate_mid, up_mid = boundary(
        "before_feed",
        3,
        [(gate_low, w_gate), (up_low, w_up)],
        True,
        own_cotangent,
        gains,
        2,
        hidden_two,
        rider=ReduceRider([(3, fill_columns, feed_normed, gate_low), (4, fill_columns, feed_normed, up_low)]),
    )
    branch = branch.reshape(REP * own, D)
    context_grad = right_contract(branch, w_cout).astype(bf16).reshape(REP, MICRO, ROWS, QW)
    cq_grad, kv_grad = cross_backward(spans, cross_queries, kv, context_grad)
    cq_grad = cq_grad.reshape(REP * own, QW)
    kv_grad = kv_grad.reshape(REP, enc_rows, 2 * KW)
    hidden_grad, cross_acc, first_branch, down_mid, cq_mid, cout_mid = boundary(
        "before_cross",
        4,
        [(cq_grad, w_cq)],
        True,
        hidden_grad,
        gains,
        1,
        hidden,
        rider=ReduceRider(
            [
                (5, fill_down, inner, all_grad),
                (2, fill_columns, cross_normed, cq_grad),
                (7, fill_rows, cross_context, branch),
            ]
        ),
    )
    first_branch = first_branch.reshape(REP * own, D)
    sent, first_branch = lax.optimization_barrier((kv_grad, first_branch))
    kv_parts = [
        kv_grad[0],
        lax.ppermute(sent[1], "rep", swap_core),
        lax.ppermute(sent[2], "rep", swap_chip),
        lax.ppermute(sent[3], "rep", swap_both),
    ]

    context_grad = right_contract(first_branch, w_out).astype(bf16).reshape(REP, MICRO, ROWS, QW)
    qkv_grad, curve_grad = self_backward(qkv, context_grad, seg_row, curve)
    qkv_grad = qkv_grad.reshape(REP * own, QW + 2 * KW)
    tokens_grad, self_acc, qkv_mid, out_mid, ckv_mid = boundary(
        "before_self",
        5,
        [(qkv_grad, w_qkv)],
        True,
        hidden_grad,
        gains,
        0,
        own_tokens,
        False,
        ReduceRider(
            [
                (0, fill_columns, normed, qkv_grad),
                (6, fill_rows, context, first_branch),
                (1, fill_stream, all_enc.reshape(REP, enc_rows, D), kv_grad),
            ]
        ),
    )

    mids = [qkv_mid, ckv_mid, cq_mid, gate_mid, up_mid, down_mid, out_mid, cout_mid]
    *whole, small_sum, layer_out = reduce_grads(
        layer_part,
        hidden_two,
        [self_acc, cross_acc, feed_acc],
        curve_grad,
        buckets,
        mids,
    )
    *finals, encoder_grad = finish(whole[: len(COLUMN_BLOCKS)], whole[len(COLUMN_BLOCKS) :], kv_parts, w_ckv)
    query_grad, key_grad, value_grad, ck_grad, cv_grad, cq_grad, gate_grad, up_grad, down_grad, out_grad, cout_grad = finals
    small_sum = small_sum[0]
    return (
        layer_out.reshape(tokens.shape),
        tokens_grad.reshape(tokens.shape),
        encoder_grad.reshape(encoded.shape),
        small_sum[0:32],
        query_grad,
        key_grad,
        value_grad,
        out_grad,
        small_sum[96:112].reshape(1, HEADS),
        small_sum[32:64],
        cq_grad,
        ck_grad,
        cv_grad,
        cout_grad,
        small_sum[64:96],
        gate_grad,
        up_grad,
        down_grad,
    )


def solution(mesh):
    rows = P("shard", None)
    gain = P("shard")
    acts = P(None, "shard", "rep", None)
    encs = P(None, "shard", None, "rep", None)
    ids = P(None, "shard", None)
    weights = (gain, rows, rows, rows, rows, rows, gain, rows, rows, rows, rows, gain, rows, rows, rows)
    return jax.shard_map(
        local,
        mesh=mesh,
        in_specs=(acts, acts, encs, ids, ids, P()) + weights,
        out_specs=(acts, acts, encs) + weights,
        check_vma=False,
    )
```

```python
import jax
import jax.numpy as jnp
from jax import lax
from jax.experimental import pallas as pl
from jax.experimental.pallas import tpu as pltpu
from jax.sharding import PartitionSpec as P

D = 1024
HEADS = 16
HEAD_DIM = 64
KV_GROUPS = 8
FF = 2816
BUCKETS = 32
ENC = 512
SEQ = 256
DOCS = 4
MICRO = 2

REP = 4
SHARDS = 32
ROWS = SEQ // REP
OWN_HEADS = HEADS // REP
OWN_GROUPS = KV_GROUPS // REP
QW = OWN_HEADS * HEAD_DIM
KW = OWN_GROUPS * HEAD_DIM
OWN_FF = FF // REP
WINDOWS = (64, 96, 144)

epsilon = 1e-06
neg_big = -1e30
gelu_scale = 0.7978845608028654
gelu_cube = 0.044715
f32 = jnp.float32
bf16 = jnp.bfloat16
mebibyte = 1024 * 1024


def matmul(left, right):
    return jnp.dot(left, right, preferred_element_type=f32)


def left_contract(left, right):
    return lax.dot_general(left, right, (((0,), (0,)), ((), ())), preferred_element_type=f32)


def right_contract(left, right):
    return lax.dot_general(left, right, (((1,), (1,)), ((), ())), preferred_element_type=f32)


def skewed(row):
    n = row.shape[1]
    out = jnp.broadcast_to(row, (n, n))
    at = lax.broadcasted_iota(jnp.int32, (n, n), 0)
    step = 1
    while step < n:
        out = jnp.where((at & step) != 0, pltpu.roll(out, step, 1), out)
        step *= 2
    return out


def unskewed_sum(square):
    n = square.shape[1]
    at = lax.broadcasted_iota(jnp.int32, (n, n), 0)
    step = 1
    while step < n:
        square = jnp.where((at & step) != 0, pltpu.roll(square, n - step, 1), square)
        step *= 2
    return jnp.sum(square, axis=0, keepdims=True)


def raised_parts(scores):
    raised = jnp.exp(scores - jnp.max(scores, axis=-1, keepdims=True))
    return raised, 1.0 / jnp.sum(raised, axis=-1, keepdims=True)


def group_rows(rows, group):
    first = group * OWN_HEADS // OWN_GROUPS
    heads = range(first, first + OWN_HEADS // OWN_GROUPS)
    return jnp.concatenate([rows[:, h * HEAD_DIM : (h + 1) * HEAD_DIM] for h in heads], axis=0)


def group_lanes(stacked):
    n = stacked.shape[0] * OWN_GROUPS // OWN_HEADS
    return [stacked[i * n : (i + 1) * n] for i in range(OWN_HEADS // OWN_GROUPS)]


def lanes_of(values, first, group):
    return values[:, first + group * HEAD_DIM : first + (group + 1) * HEAD_DIM]


def stacked_twice(value):
    return jnp.concatenate([value] * (OWN_HEADS // OWN_GROUPS), axis=0)


def attend_back(scores, query, key, value, grad):
    raised, shrink = raised_parts(scores)
    grad = (grad.astype(f32) * shrink).astype(bf16)
    prob_grad = right_contract(grad, value)
    centre = jnp.sum(raised * prob_grad, axis=-1, keepdims=True) * shrink
    score_grad = (raised * (prob_grad - centre)).astype(bf16)
    return score_grad, matmul(score_grad, key), left_contract(score_grad, query), left_contract(raised.astype(bf16), grad)


def self_mask(seg_row):
    at_query = lax.broadcasted_iota(jnp.int32, (SEQ, SEQ), 0)
    at_key = lax.broadcasted_iota(jnp.int32, (SEQ, SEQ), 1)
    of_key = jnp.broadcast_to(seg_row.astype(f32), (SEQ, SEQ))
    return (at_key <= at_query) & (of_key == of_key.T)


def bucket_hot(buckets):
    at = lax.broadcasted_iota(jnp.int32, (BUCKETS, SEQ), 0)
    return (at == buckets).astype(f32).astype(bf16)


def fill_bias(curve_ref, bias_ref):
    for head in range(OWN_HEADS):
        bias_ref[head] = skewed(curve_ref[head : head + 1, :]).T


def self_attention(values, gain, weight, allowed, bias_ref):
    values = values.astype(f32)
    normed = (values * norm_parts(values) * gain).astype(bf16)
    whole = matmul(normed, weight).astype(bf16)
    allowed = stacked_twice(allowed.astype(jnp.int32)) != 0
    mixed = []
    for group in range(OWN_GROUPS):
        scores = right_contract(group_rows(whole, group), lanes_of(whole, QW, group))
        scores = jnp.where(allowed, scores + bias_ref[2 * group : 2 * group + 2].reshape(2 * SEQ, SEQ), neg_big)
        raised, shrink = raised_parts(scores)
        mixed += group_lanes(matmul(raised.astype(bf16), lanes_of(whole, QW + KW, group)) * shrink)
    return normed, whole, jnp.concatenate(mixed, axis=1).astype(bf16)


def unpack_small(rep, small, hot, gains_ref, curve_ref):
    rows = jnp.sum(small.astype(f32).reshape(SHARDS, 8, 128), axis=1).astype(bf16)
    per = D // SHARDS
    lane = lax.broadcasted_iota(jnp.int32, (128, D), 0)
    column = lax.broadcasted_iota(jnp.int32, (128, D), 1)
    owner = lax.broadcasted_iota(jnp.int32, (SHARDS, D), 0)
    entry = lax.broadcasted_iota(jnp.int32, (SHARDS, D), 1)
    gains_ref[...] = jnp.zeros_like(gains_ref)
    for i in range(3):
        ones = (lax.rem(column, per) == lane - per * i).astype(f32).astype(bf16)
        spread = jnp.where(lax.div(entry, per) == owner, matmul(rows, ones), 0.0)
        gains_ref[i : i + 1, :] = jnp.sum(spread, axis=0, keepdims=True)
    head = lax.broadcasted_iota(jnp.int32, (8, 128), 0)
    place = lax.broadcasted_iota(jnp.int32, (8, 128), 1)
    ones = ((head < OWN_HEADS) & (place == 3 * per + OWN_HEADS * rep + head)).astype(f32).astype(bf16)
    curve_ref[...] = matmul(right_contract(ones, rows).astype(bf16), hot)


def self_backward_kernel(
    qkv_ref, grad_ref, seg_row_ref, curve_ref, out_ref, curve_grad_ref, bias_ref, sum_ref
):
    @pl.when(pl.program_id(0) == 0)
    def _():
        fill_bias(curve_ref, bias_ref)
        sum_ref[...] = jnp.zeros_like(sum_ref)

    whole = qkv_ref[...].reshape(SEQ, QW + 2 * KW)
    grads = grad_ref[...].reshape(SEQ, QW)
    allowed = stacked_twice(self_mask(seg_row_ref[0]).astype(jnp.int32)) != 0
    query_grads, key_grads, value_grads = [], [], []
    for group in range(OWN_GROUPS):
        query = group_rows(whole, group)
        key = lanes_of(whole, QW, group)
        scores = right_contract(query, key)
        scores = jnp.where(allowed, scores + bias_ref[2 * group : 2 * group + 2].reshape(2 * SEQ, SEQ), neg_big)
        score_grad, query_grad, key_grad, value_grad = attend_back(
            scores, query, key, lanes_of(whole, QW + KW, group), group_rows(grads, group)
        )
        sum_ref[2 * group : 2 * group + 2] += score_grad.astype(f32).reshape(2, SEQ, SEQ)
        query_grads += group_lanes(query_grad)
        key_grads.append(key_grad)
        value_grads.append(value_grad)
    joined = jnp.concatenate(query_grads + key_grads + value_grads, axis=1)
    out_ref[...] = joined.astype(bf16).reshape(out_ref.shape)

    @pl.when(pl.program_id(0) == MICRO - 1)
    def _():
        curve_grad_ref[...] = jnp.zeros_like(curve_grad_ref)
        for head in range(OWN_HEADS):
            curve_grad_ref[head : head + 1, :] = unskewed_sum(sum_ref[head].T)


def by_window(at, wide_ref, body):
    for level, window in enumerate(WINDOWS):
        pl.when(wide_ref[at] == level)(lambda window=window: body(window))


def cross_forward_kernel(block_ref, start_ref, wide_ref, begin_ref, end_ref, q_ref, kv_ref, out_ref, query_ref, mixed_ref):
    at = pl.program_id(0) * DOCS + pl.program_id(1)

    @pl.when(pl.program_id(1) == 0)
    def _():
        query_ref[...] = q_ref[...].reshape(SEQ, QW)

    start = pl.multiple_of(start_ref[at], 16)

    def body(window):
        rows = query_ref[pl.ds(start, window), :]
        row = start + lax.broadcasted_iota(jnp.int32, (window, 1), 0)
        mine = (row >= begin_ref[at]) & (row < end_ref[at])
        both = kv_ref[...].reshape(ENC, 2 * KW)
        mixed = []
        for group in range(OWN_GROUPS):
            raised, shrink = raised_parts(right_contract(group_rows(rows, group), lanes_of(both, 0, group)))
            mixed += group_lanes(matmul(raised.astype(bf16), lanes_of(both, KW, group)) * shrink)
        fresh = jnp.concatenate(mixed, axis=1)
        mixed_ref[pl.ds(start, window), :] = jnp.where(mine, fresh, mixed_ref[pl.ds(start, window), :])

    by_window(at, wide_ref, body)

    @pl.when(pl.program_id(1) == DOCS - 1)
    def _():
        out_ref[...] = mixed_ref[...].astype(bf16).reshape(out_ref.shape)


def cross_backward_kernel(
    block_ref, start_ref, wide_ref, begin_ref, end_ref, q_ref, kv_ref, grad_ref, out_ref, kv_grad_ref, query_ref, given_ref,
    mixed_ref
):
    at = pl.program_id(0) * DOCS + pl.program_id(1)

    @pl.when(pl.program_id(1) == 0)
    def _():
        query_ref[...] = q_ref[...].reshape(SEQ, QW)
        given_ref[...] = grad_ref[...].reshape(SEQ, QW)

    start = pl.multiple_of(start_ref[at], 16)

    def body(window):
        rows = query_ref[pl.ds(start, window), :]
        row = start + lax.broadcasted_iota(jnp.int32, (window, 1), 0)
        mine = (row >= begin_ref[at]) & (row < end_ref[at])
        grads = jnp.where(mine, given_ref[pl.ds(start, window), :].astype(f32), 0.0)
        both = kv_ref[...].reshape(ENC, 2 * KW)
        query_grads, key_grads, value_grads = [], [], []
        for group in range(OWN_GROUPS):
            query, key = group_rows(rows, group), lanes_of(both, 0, group)
            _, query_grad, key_grad, value_grad = attend_back(
                right_contract(query, key), query, key, lanes_of(both, KW, group), group_rows(grads, group)
            )
            query_grads += group_lanes(query_grad)
            key_grads.append(key_grad)
            value_grads.append(value_grad)
        fresh = jnp.concatenate(query_grads, axis=1)
        mixed_ref[pl.ds(start, window), :] = jnp.where(mine, fresh, mixed_ref[pl.ds(start, window), :])
        joined = jnp.concatenate(key_grads + value_grads, axis=1)
        kv_grad_ref[...] = joined.astype(bf16).reshape(kv_grad_ref.shape)

    by_window(at, wide_ref, body)

    @pl.when(pl.program_id(1) == DOCS - 1)
    def _():
        out_ref[...] = mixed_ref[...].astype(bf16).reshape(out_ref.shape)


def feed_kernel(normed_ref, grad_ref, gate_w_ref, up_w_ref, pieces_ref, inner_ref, gate_ref, up_ref, part_ref, down_ref):
    @pl.when(pl.program_id(0) == 0)
    def _():
        for i in range(4):
            pieces = []
            for k in range(8 * i, 8 * i + 8):
                piece = pieces_ref[k].astype(f32)
                pieces.append(piece[8:] if k % REP == REP - 1 else piece)
            down_ref[i * 176 : (i + 1) * 176, :] = jnp.concatenate(pieces, axis=0).astype(bf16)

    normed = normed_ref[...].reshape(-1, D)
    gate = matmul(normed, gate_w_ref[...])
    up_part = matmul(normed, up_w_ref[...])
    inner_grad = right_contract(grad_ref[...].reshape(-1, D), down_ref[...])
    square = gate * gate
    bent = jnp.tanh(gelu_scale * gate * (1.0 + gelu_cube * square))
    rising = 0.5 * (1.0 + bent)
    slope = rising + 0.5 * gate * (1.0 - bent * bent) * (gelu_scale * (1.0 + 3.0 * gelu_cube * square))
    passed = gate * rising
    inner = (passed * up_part).astype(bf16)
    inner_ref[...] = inner.reshape(inner_ref.shape)
    gate_ref[...] = (inner_grad * up_part * slope).astype(bf16).reshape(gate_ref.shape)
    up_ref[...] = (inner_grad * passed).astype(bf16).reshape(up_ref.shape)
    part_ref[...] = matmul(inner, down_ref[...]).astype(bf16).reshape(part_ref.shape)


def feed(normed, grads, w_gate, w_up, down_pieces):
    own = MICRO * ROWS

    def some(width):
        return pl.BlockSpec((2, own, width), lambda i: (i, 0, 0))

    units = jax.ShapeDtypeStruct((REP, own, OWN_FF), bf16)
    return pl.pallas_call(
        feed_kernel,
        name="feed",
        grid=(REP // 2,),
        in_specs=[
            some(D),
            some(D),
            fixed_block(w_gate.shape),
            fixed_block(w_up.shape),
            fixed_block(down_pieces.shape),
        ],
        out_specs=[some(OWN_FF)] * 3 + [some(D)],
        out_shape=[units, units, units, jax.ShapeDtypeStruct((REP, own, D), bf16)],
        scratch_shapes=[pltpu.VMEM((OWN_FF, D), bf16)],
        compiler_params=pltpu.CompilerParams(vmem_limit_bytes=32 * mebibyte),
        cost_estimate=estimate(3 << 30, 8 << 20, 1 << 19),
    )(normed, grads, w_gate, w_up, down_pieces)


def rows_block(width):
    return pl.BlockSpec((REP, 1, ROWS, width), lambda m, *rest: (0, m, 0, 0))


def fixed_block(shape):
    return pl.BlockSpec(shape, lambda *at: (0,) * len(shape))


def micro_block(shape):
    return pl.BlockSpec((1,) + shape, lambda m, *rest: (m,) + (0,) * len(shape))


def estimate(flops, moved, raised):
    return pl.CostEstimate(flops=flops, bytes_accessed=moved, transcendentals=raised)


self_pairs = MICRO * OWN_HEADS * SEQ * SEQ
cross_pairs = MICRO * OWN_HEADS * DOCS * WINDOWS[1] * ENC


def self_backward(qkv, grads, seg_row, curve):
    return pl.pallas_call(
        self_backward_kernel,
        name="self_backward",
        grid=(MICRO,),
        in_specs=[
            rows_block(QW + 2 * KW),
            rows_block(QW),
            micro_block((1, SEQ)),
            fixed_block((8, SEQ)),
        ],
        out_specs=[rows_block(QW + 2 * KW), fixed_block((8, SEQ))],
        out_shape=[
            jax.ShapeDtypeStruct((REP, MICRO, ROWS, QW + 2 * KW), bf16),
            jax.ShapeDtypeStruct((8, SEQ), f32),
        ],
        scratch_shapes=[
            pltpu.VMEM((OWN_HEADS, SEQ, SEQ), f32),
            pltpu.VMEM((OWN_HEADS, SEQ, SEQ), f32),
        ],
        compiler_params=pltpu.CompilerParams(vmem_limit_bytes=18 * mebibyte),
        cost_estimate=estimate(self_pairs * 640, 3 << 20, self_pairs),
    )(qkv, grads, seg_row, curve)


def cross_rows():
    return pl.BlockSpec((REP, 1, ROWS, QW), lambda m, d, block, *rest: (0, m, 0, 0))


def cross_keys():
    return pl.BlockSpec(
        (REP, 1, 1, ENC // REP, 2 * KW),
        lambda m, d, block, *rest: (0, m, block[m * DOCS + d], 0, 0),
    )


def cross_forward(spans, queries, kv):
    return pl.pallas_call(
        cross_forward_kernel,
        name="cross_forward",
        grid_spec=pltpu.PrefetchScalarGridSpec(
            num_scalar_prefetch=5,
            grid=(MICRO, DOCS),
            in_specs=[cross_rows(), cross_keys()],
            out_specs=cross_rows(),
            scratch_shapes=[pltpu.VMEM((SEQ, QW), bf16), pltpu.VMEM((SEQ, QW), f32)],
        ),
        out_shape=jax.ShapeDtypeStruct((REP, MICRO, ROWS, QW), bf16),
        compiler_params=pltpu.CompilerParams(vmem_limit_bytes=16 * mebibyte),
        cost_estimate=estimate(cross_pairs * 256, 3 << 20, cross_pairs),
    )(*spans, queries, kv)


def cross_backward(spans, queries, kv, grads):
    return pl.pallas_call(
        cross_backward_kernel,
        name="cross_backward",
        grid_spec=pltpu.PrefetchScalarGridSpec(
            num_scalar_prefetch=5,
            grid=(MICRO, DOCS),
            in_specs=[cross_rows(), cross_keys(), cross_rows()],
            out_specs=[cross_rows(), cross_keys()],
            scratch_shapes=[
                pltpu.VMEM((SEQ, QW), bf16),
                pltpu.VMEM((SEQ, QW), bf16),
                pltpu.VMEM((SEQ, QW), f32),
            ],
        ),
        out_shape=[
            jax.ShapeDtypeStruct((REP, MICRO, ROWS, QW), bf16),
            jax.ShapeDtypeStruct((REP, MICRO, DOCS, ENC // REP, 2 * KW), bf16),
        ],
        compiler_params=pltpu.CompilerParams(vmem_limit_bytes=20 * mebibyte),
        cost_estimate=estimate(cross_pairs * 640, 6 << 20, cross_pairs),
    )(*spans, queries, kv, grads)


MESH = pl.DeviceIdType.MESH

swap_core = [(i, i ^ 1) for i in range(REP)]
swap_chip = [(i, i ^ 2) for i in range(REP)]
swap_both = [(i, i ^ 3) for i in range(REP)]


def remote(source, target, send_sem, recv_sem, device):
    return pltpu.make_async_remote_copy(
        src_ref=source,
        dst_ref=target,
        send_sem=send_sem,
        recv_sem=recv_sem,
        device_id=device,
        device_id_type=MESH,
    )


class Ring:
    def __init__(self, group, half, me, device_at, send_sems, recv_sems):
        right, left = lax.rem(me + 1, 4), lax.rem(me + 3, 4)
        to_right, to_left = device_at(right), device_at(left)

        def copy(ref, device, i):
            return remote(ref, ref, send_sems.at[i], recv_sems.at[i], device)

        self.direct = [copy(group(me), to_right, 0), copy(group(me), to_left, 1)]
        self.passed = [copy(half(left, 0), to_right, 2), copy(half(right, 1), to_left, 3)]

    def start(self):
        for copy in self.direct:
            copy.start()

    def forward(self):
        for arrived, onward in zip(self.direct, self.passed):
            arrived.wait_recv()
            onward.start()

    def finish(self):
        for copy in self.passed:
            copy.wait_recv()

    def drain(self):
        for copy in self.direct + self.passed:
            copy.wait_send()


class Place:
    def __init__(self):
        self.at = at = lax.axis_index("shard")
        self.rep = rep = lax.axis_index("rep")
        self.x, self.y, self.z = lax.div(at, 8), lax.rem(lax.div(at, 2), 4), lax.rem(at, 2)
        self.chip, self.core = chip, core = lax.div(rep, 2), lax.rem(rep, 2)
        self.pair = {"shard": at + 1 - 2 * self.z}
        self.theirs = (1 - chip) * 2 + core
        self.far = {"rep": self.theirs}
        self.near = {"rep": chip * 2 + 1 - core}

    def on_x(self, i):
        return {"shard": i * 8 + self.y * 2 + self.z}

    def on_y(self, i):
        return {"shard": self.x * 8 + i * 2 + self.z}

    def neighbours(self):
        return [self.on_x(lax.rem(self.x + d, 4)) for d in (1, 3)] + [
            self.on_y(lax.rem(self.y + d, 4)) for d in (1, 3)
        ]


class Gather:
    def __init__(self, place, block, whole, first_x, sems):
        x, y, z = place.x, place.y, place.z
        pair_send, pair_recv, ring_send, ring_recv = sems
        slot = whole.at[x, y, z]
        self.pair = remote(slot if block is None else block, slot, pair_send, pair_recv, place.pair)

        def x_small(j):
            return whole.at[j, y]

        def x_small_half(j, h):
            return whole.at[j, y, h]

        def y_small(j):
            return whole.at[x, j]

        def y_small_half(j, h):
            return whole.at[x, j, h]

        def x_large(j):
            return whole.at[j]

        def x_large_half(j, h):
            return whole.at[j, pl.ds(2 * h, 2)]

        def y_large(j):
            return whole.at[:, j]

        def y_large_half(j, h):
            return whole.at[pl.ds(2 * h, 2), j]

        near, wide = (ring_send.at[0], ring_recv.at[0]), (ring_send.at[1], ring_recv.at[1])
        if first_x:
            self.small = Ring(x_small, x_small_half, x, place.on_x, *near)
            self.large = Ring(y_large, y_large_half, y, place.on_y, *wide)
        else:
            self.small = Ring(y_small, y_small_half, y, place.on_y, *near)
            self.large = Ring(x_large, x_large_half, x, place.on_x, *wide)

    def drain(self):
        self.pair.wait_send()
        self.small.drain()
        self.large.drain()


GATHER_BLOCKS = (
    (32, QW + 2 * KW, True),
    (32, REP * KW, True),
    (32, QW, True),
    (8, 128, True),
    (32, OWN_FF, True),
    (32, OWN_FF, False),
    (24, D, False),
    (8, D, False),
    (8, D, False),
)
GATHER_HELD = 6
GATHER_ROWS = (1, 4, 1)
GATHER_CHUNKS = sum(GATHER_ROWS)


def gather_kernel(*refs):
    query, key, value, cross_key, cross_value, cross_query, small, gate, up, down, out, cross_out = refs[:12]
    seg_row, buckets = refs[12:14]
    n, n_rows = len(GATHER_BLOCKS), len(GATHER_ROWS)
    own_rows, refs = refs[14 : 14 + n_rows], refs[14 + n_rows :]
    wholes, all_rows, refs = refs[:n], refs[n : n + n_rows], refs[n + n_rows :]
    gains_out, curve_out, normed_out, qkv_out, context_out, kv_out, *refs = refs
    (local_sems, out_sems, piece_send, piece_recv, pair_send, pair_recv, ring_send, ring_recv, rep_send, rep_recv,
     load_sems, token_held, qkv_held, small_held, ckv_held, enc_held, bias_ref, *held) = refs
    held, held_rows = held[:GATHER_HELD], held[GATHER_HELD:]
    place = Place()
    at, rep, x, y, z = place.at, place.rep, place.x, place.y, place.z
    barrier = pltpu.get_barrier_semaphore()
    devices = [place.pair, place.far, place.near] + place.neighbours()
    for device in devices:
        pl.semaphore_signal(barrier, inc=1, device_id=device, device_id_type=MESH)
    goal = 4 * lax.rem(at, 8) + rep
    stays = (x == rep) & (goal == at)
    source = {"rep": lax.rem(at, 4), "shard": 8 * rep + lax.div(at, 4)}

    @pl.when(jnp.logical_not(stays))
    def _():
        pl.semaphore_signal(barrier, inc=1, device_id=source, device_id_type=MESH)

    pl.semaphore_wait(barrier, len(devices) + 1 - stays.astype(jnp.int32))

    wholes = list(wholes)
    halves = wholes[1]
    wholes[1] = halves.at[place.core]
    slots = [whole.at[x, y, z] for whole in wholes]
    count = [0]

    def own(source_ref, target):
        count[0] += 1
        return pltpu.make_async_copy(source_ref, target, local_sems.at[count[0] - 1])

    def part(ref, width, r=rep):
        return ref.at[:, pl.ds(pl.multiple_of(r * width, 128), width)]

    fills = [
        [
            own(part(query, QW), held[0].at[:, pl.ds(0, QW)]),
            own(part(key, KW), held[0].at[:, pl.ds(QW, KW)]),
            own(part(value, KW), held[0].at[:, pl.ds(QW + KW, KW)]),
        ],
        [
            own(part(cross_key, KW, place.core), held[1].at[:, pl.ds(0, KW)]),
            own(part(cross_value, KW, place.core), held[1].at[:, pl.ds(KW, KW)]),
            own(part(cross_key, KW, 2 + place.core), held[1].at[:, pl.ds(2 * KW, KW)]),
            own(part(cross_value, KW, 2 + place.core), held[1].at[:, pl.ds(3 * KW, KW)]),
        ],
        [own(part(cross_query, QW), held[2])],
        [own(small, held[3])],
        [own(gate, held[4])],
        [own(up, held[5])],
    ]
    firsts = [pl.multiple_of(24 * rep - 8 * lax.div(rep, 3), 8)] + [pl.multiple_of(8 * rep, 8)] * 2
    pieces = []
    for i, ref in enumerate((down, out, cross_out)):
        whole = wholes[GATHER_HELD + i]
        rows = ref.at[pl.ds(firsts[i], GATHER_BLOCKS[GATHER_HELD + i][0])]
        landing = whole.at[lax.div(goal, 8), lax.rem(lax.div(goal, 2), 4), lax.rem(goal, 2)]
        sent = remote(rows, landing, piece_send.at[i], piece_recv.at[i], {"rep": x, "shard": goal})
        pieces.append((sent, own(rows, landing)))
    for sent, stay in pieces:
        pl.when(jnp.logical_not(stays))(sent.start)
        pl.when(stays)(stay.start)
    for fill in fills:
        for copy in fill:
            copy.start()

    rep_first, rep_second, rep_local = [], [], []
    for i, parts in enumerate(GATHER_ROWS):
        whole = all_rows[i]
        rows = own_rows[i].shape[0] // parts
        first, second = (0, 1) if i == 1 else (rep, rep)
        third, fourth = (2, 3) if i == 1 else (place.theirs, place.theirs)
        landing = 2 if i == 1 else rep
        rep_local.append((own(own_rows[i], held_rows[i]), pltpu.make_async_copy(held_rows[i], whole.at[first], out_sems.at[n + i])))
        rep_local[i][0].start()
        for p in range(parts):
            span = pl.ds(p * rows, rows)
            j = len(rep_first)
            mine = own_rows[i].at[span]
            rep_first.append(remote(mine, whole.at[landing, span], rep_send.at[j, 0], rep_recv.at[j, 0], place.far))
            direct = remote(mine, whole.at[second, span], rep_send.at[j, 1], rep_recv.at[j, 1], place.near)
            onward = remote(whole.at[third, span], whole.at[fourth, span], rep_send.at[j, 2], rep_recv.at[j, 2], place.near)
            rep_second.append((direct, onward))

    gathers = []
    for i, (_, _, first_x) in enumerate(GATHER_BLOCKS):
        block = held[i] if i < GATHER_HELD else None
        sems = pair_send.at[i], pair_recv.at[i], ring_send.at[i], ring_recv.at[i]
        gathers.append(Gather(place, block, wholes[i], first_x, sems))
    settled = []
    for i in range(n):
        if i < GATHER_HELD:
            for copy in fills[i]:
                copy.wait()
            settled.append(pltpu.make_async_copy(held[i], slots[i], out_sems.at[i]))
            settled[i].start()
        else:
            sent, stay = pieces[i - GATHER_HELD]
            pl.when(jnp.logical_not(stays))(sent.wait_recv)
            pl.when(stays)(stay.wait)
        gathers[i].pair.start()
    for first, (direct, _) in zip(rep_first, rep_second):
        first.start()
        direct.start()
    for inward, outward in rep_local:
        inward.wait()
        outward.start()
    for i in range(n):
        if i < GATHER_HELD:
            settled[i].wait()
        gathers[i].pair.wait_recv()
        gathers[i].small.start()
    for one in gathers:
        one.small.forward()
    early, late, sideways = (0, 3, 1, 2), (4,), (7, 8, 6, 5)
    for i in early + sideways:
        gathers[i].small.finish()
        gathers[i].large.start()
    for j in range(2):
        rep_first[j].wait_recv()
        rep_second[j][1].start()
    for i in early:
        gathers[i].large.forward()
    for i in late:
        gathers[i].small.finish()
        gathers[i].large.start()
    gathers[7].large.forward()
    gathers[8].large.forward()
    lanes = pl.ds(pl.multiple_of(place.chip * 2 * KW, 2 * KW), 2 * KW)
    gathers[0].large.finish()
    gathers[3].large.finish()
    gathers[1].large.finish()
    half = halves.at[place.core]
    swap = remote(half, half, rep_send.at[GATHER_CHUNKS, 0], rep_recv.at[GATHER_CHUNKS, 0], place.near)
    swap.start()
    for copy in rep_second[0]:
        copy.wait_recv()
    rep_local[0][1].wait()
    loads = [
        pltpu.make_async_copy(half.at[:, :, :, :, lanes], ckv_held, load_sems.at[0]),
        pltpu.make_async_copy(wholes[0], qkv_held, load_sems.at[1]),
        pltpu.make_async_copy(wholes[3], small_held, load_sems.at[2]),
        pltpu.make_async_copy(all_rows[0], token_held, load_sems.at[3]),
    ]
    for load in loads:
        load.start()
    for load in loads:
        load.wait()
    unpack_small(rep, small_held[...], bucket_hot(buckets[...]), gains_out, curve_out)
    fill_bias(curve_out, bias_ref)
    for micro in range(MICRO):
        rows = slice(micro * ROWS, (micro + 1) * ROWS)
        normed, whole, mixed = self_attention(
            token_held[:, rows, :].reshape(SEQ, D),
            gains_out[0:1, :],
            qkv_held[...].reshape(D, QW + 2 * KW),
            self_mask(seg_row[micro]),
            bias_ref,
        )
        normed_out[:, rows, :] = normed.reshape(REP, ROWS, D)
        qkv_out[:, rows, :] = whole.reshape(REP, ROWS, QW + 2 * KW)
        context_out[:, rows, :] = mixed.reshape(REP, ROWS, QW)
    gathers[6].large.forward()
    gathers[5].large.forward()
    parts = GATHER_ROWS[1]
    tall = own_rows[1].shape[0] // parts

    def project(source_ref, k, p, count=2):
        rows = slice(p * tall, (p + count) * tall)
        kv_out[k, rows, :] = matmul(source_ref[...], ckv_held[...].reshape(D, 2 * KW)).astype(bf16)

    def load_half(k, p, slot):
        for q in (p, p + 1):
            rep_second[1 + q][0 if k == 1 else 1].wait_recv() if k != 2 else None
        load = pltpu.make_async_copy(
            all_rows[1].at[k, pl.ds(p * tall, 2 * tall)], enc_held.at[slot], load_sems.at[4 + slot]
        )
        load.start()
        return load

    first_near = load_half(1, 0, 0)
    project(held_rows[1], 0, 0, parts)
    for i in late:
        gathers[i].large.forward()
    first_near.wait()
    second_near = load_half(1, 2, 1)
    project(enc_held.at[0], 1, 0)
    second_near.wait()
    project(enc_held.at[1], 1, 2)
    for p in (0, 2):
        for q in (p, p + 1):
            if q:
                rep_first[1 + q].wait_recv()
                rep_second[1 + q][1].start()
        far_load = load_half(2, p, 2)
        far_load.wait()
        project(enc_held.at[2], 2, p)
        across_load = load_half(3, p, p // 2)
        across_load.wait()
        project(enc_held.at[p // 2], 3, p)
    for i in late + sideways + early[3:]:
        gathers[i].large.finish()
    rep_first[GATHER_CHUNKS - 1].wait_recv()
    rep_second[GATHER_CHUNKS - 1][1].start()
    for sent, _ in pieces:
        pl.when(jnp.logical_not(stays))(sent.wait_send)
    for one in gathers:
        one.drain()
    for _, outward in rep_local[1:]:
        outward.wait()
    for j, (first, second) in enumerate(zip(rep_first, rep_second)):
        first.wait_send()
        for copy in second:
            copy.wait_send()
            if j == GATHER_CHUNKS - 1:
                copy.wait_recv()
    swap.wait()


def gather_weights(weights, tables, rows):
    n = len(GATHER_BLOCKS)
    shapes = [
        jax.ShapeDtypeStruct(((2,) if i == 1 else ()) + (4, 4, 2, r, c), bf16)
        for i, (r, c, _) in enumerate(GATHER_BLOCKS)
    ]
    shapes += [jax.ShapeDtypeStruct((REP,) + value.shape, value.dtype) for value in rows]
    own = MICRO * ROWS
    n_far = len(shapes)
    shapes += [jax.ShapeDtypeStruct((8, D), f32), jax.ShapeDtypeStruct((8, SEQ), f32)]
    shapes += [jax.ShapeDtypeStruct((REP, own, width), bf16) for width in (D, QW + 2 * KW, QW)]
    shapes.append(jax.ShapeDtypeStruct((REP, rows[1].shape[0], 2 * KW), bf16))
    anywhere = pl.BlockSpec(memory_space=pltpu.HBM)
    here = pl.BlockSpec(memory_space=pltpu.VMEM)
    dma = pltpu.SemaphoreType.DMA
    results = pl.pallas_call(
        gather_kernel,
        name="gather_weights",
        in_specs=[anywhere] * len(weights) + [here] * len(tables) + [anywhere] * len(rows),
        out_specs=[anywhere] * n_far + [here] * (len(shapes) - n_far),
        out_shape=shapes,
        scratch_shapes=[
            dma((11 + 3 + len(rows),)),
            dma((n + len(rows),)),
            dma((3,)),
            dma((3,)),
            dma((n,)),
            dma((n,)),
            dma((n, 2, 4)),
            dma((n, 2, 4)),
            dma((GATHER_CHUNKS + 1, 3)),
            dma((GATHER_CHUNKS + 1, 3)),
            dma((7,)),
            pltpu.VMEM((REP, own, D), bf16),
            pltpu.VMEM((4, 4, 2, 32, QW + 2 * KW), bf16),
            pltpu.VMEM((4, 4, 2, 8, 128), bf16),
            pltpu.VMEM((4, 4, 2, 32, 2 * KW), bf16),
            pltpu.VMEM((3, rows[1].shape[0] // 2, D), bf16),
            pltpu.VMEM((OWN_HEADS, SEQ, SEQ), f32),
        ]
        + [pltpu.VMEM((r, c), bf16) for r, c, _ in GATHER_BLOCKS[:GATHER_HELD]]
        + [pltpu.VMEM(value.shape, value.dtype) for value in rows],
        compiler_params=pltpu.CompilerParams(
            collective_id=0, has_side_effects=True, vmem_limit_bytes=56 * mebibyte
        ),
        cost_estimate=estimate(0, 128 << 20, 0),
    )(*weights, *tables, *rows)
    return results[:n], results[n : n + len(rows)], results[n + len(rows) :]


class ReduceRing:
    def __init__(self, half, whole_half, me, device_at, first, second, send_sems, recv_sems):
        right, left, far = lax.rem(me + 1, 4), lax.rem(me + 3, 4), lax.rem(me + 2, 4)
        to_right, to_left = device_at(right), device_at(left)

        def copy(source, target, device, i):
            return remote(source, target, send_sems.at[i], recv_sems.at[i], device)

        self.half, self.me, self.right, self.left = half, me, right, left
        self.first, self.second = first, second
        self.opening = [
            copy(whole_half(far, 0), first.at[0], to_right, 0),
            copy(whole_half(far, 1), first.at[1], to_left, 1),
        ]
        self.plain = [
            copy(whole_half(right, 1), second.at[0, 1], to_right, 2),
            copy(whole_half(left, 0), second.at[1, 0], to_left, 3),
        ]
        self.summed = [
            copy(first.at[0], second.at[0, 0], to_right, 4),
            copy(first.at[1], second.at[1, 1], to_left, 5),
        ]

    def start(self):
        for copy in self.opening + self.plain:
            copy.start()

    def middle(self, each):
        for h, group in enumerate((self.right, self.left)):
            self.opening[h].wait_recv()

            def add(*k, h=h, group=group):
                mixed = self.first[(h, *k)].astype(f32) + self.half(group, h, *k).astype(f32)
                self.first[(h, *k)] = mixed.astype(self.first.dtype)

            each(add)
            self.summed[h].start()

    def finish(self, each, store):
        for h in range(2):
            (self.plain[1] if h == 0 else self.plain[0]).wait_recv()
            self.summed[h].wait_recv()

            def add(*k, h=h):
                mixed = self.second[(0, h, *k)].astype(f32) + self.second[(1, h, *k)].astype(f32)
                store(h, *k, mixed + self.half(self.me, h, *k).astype(f32))

            each(add)

    def drain(self):
        for copy in self.opening + self.plain + self.summed:
            copy.wait_send()


def each_of_four(body):
    def step(i, carry):
        body(lax.div(i, 2), lax.rem(i, 2))
        return carry

    lax.fori_loop(0, 4, step, 0)


def just_once(body):
    body()


def grad_halves(grad, on_y):
    if on_y:
        return (lambda j, h, a, b: grad[2 * h + a, j, b]), (lambda j, h: grad.at[pl.ds(2 * h, 2), j])
    return (lambda j, h, a, b: grad[j, 2 * h + a, b]), (lambda j, h: grad.at[j, pl.ds(2 * h, 2)])


def large_ring(place, grad, on_y, first, second, sems):
    half, whole_half = grad_halves(grad, on_y)
    axis = (place.y, place.on_y) if on_y else (place.x, place.on_x)
    return ReduceRing(half, whole_half, *axis, first, second, *sems)


def large_store(mid):
    def store(h, a, b, total):
        mid[2 * h + a, b] = total.astype(mid.dtype)

    return store


def large_scratch(rows, width, dtype):
    return [pltpu.VMEM((2, 2, 2, rows, width), dtype), pltpu.VMEM((2, 2, 2, 2, rows, width), dtype)]


REDUCE_BLOCKS = (
    (32, QW + 2 * KW, True, bf16, True),
    (32, 2 * KW, False, bf16, True),
    (32, QW, False, bf16, True),
    (32, OWN_FF, True, bf16, True),
    (32, OWN_FF, False, bf16, True),
    (24, D, True, bf16, True),
    (8, D, False, bf16, True),
    (8, D, False, bf16, True),
    (8, 128, False, f32, False),
)
COLUMN_BLOCKS = (0, 1, 2, 3, 4)
PIECE_BLOCKS = (5, 6, 7)
SMALL_BLOCK = 8
BLOCK_ROWS = D // 4


def fill_columns(left, right, grad):
    def step(j, carry):
        lanes = pl.ds(pl.multiple_of(j * BLOCK_ROWS, BLOCK_ROWS), BLOCK_ROWS)
        part = left_contract(left[:, lanes], right[...])
        grad[j] = part.astype(grad.dtype).reshape(grad.shape[1:])
        return carry

    lax.fori_loop(0, 4, step, 0)


def in_thirds(value):
    parts = []
    for _ in range(3):
        parts.append(value.astype(bf16))
        value = value - parts[-1].astype(f32)
    return parts


def exact_matmul(value, ones):
    return sum(matmul(part, ones) for part in in_thirds(value))


def fill_small(rep, accs, curve_grad, hot, blocks):
    owner = lax.broadcasted_iota(jnp.int32, (SHARDS, D), 0)
    entry = lax.broadcasted_iota(jnp.int32, (SHARDS, D), 1)
    column = lax.broadcasted_iota(jnp.int32, (D, 128), 0)
    lane = lax.broadcasted_iota(jnp.int32, (D, 128), 1)
    per = D // SHARDS
    total = None
    for i, acc in enumerate(accs):
        picked = jnp.where(lax.div(entry, per) == owner, acc[...], 0.0)
        ones = (lax.rem(column, per) == lane - per * i).astype(f32).astype(bf16)
        part = exact_matmul(picked, ones)
        total = part if total is None else total + part
    rows = sum(right_contract(hot, part) for part in in_thirds(curve_grad[...]))
    head = lax.broadcasted_iota(jnp.int32, (8, 128), 0)
    place = lax.broadcasted_iota(jnp.int32, (8, 128), 1)
    ones = ((head < OWN_HEADS) & (place == 3 * per + OWN_HEADS * rep + head)).astype(f32).astype(bf16)
    total = total + exact_matmul(rows, ones)
    for i in range(SHARDS):
        blocks[i // 8, i // 2 % 4, i % 2] = jnp.broadcast_to(total[i : i + 1, :], (8, 128))


def fill_rows(left, right, grad):
    grad[...] = left_contract(left[...], right[...]).reshape(grad.shape).astype(grad.dtype)


def fill_stream(left, right, grad, held, room, sems):
    n = left.shape[0]
    loads = [pltpu.make_async_copy(left.at[i], held.at[i % 2], sems.at[i]) for i in range(n)]
    loads[0].start()
    loads[1].start()
    for i in range(n):
        loads[i].wait()
        part = left_contract(right[i], held[i % 2])
        room[...] = part if i == 0 else room[...] + part
        if i + 2 < n:
            loads[i + 2].start()

    def turn(j, carry):
        lanes = pl.ds(pl.multiple_of(j * BLOCK_ROWS, BLOCK_ROWS), BLOCK_ROWS)
        grad[j] = room[:, lanes].T.astype(grad.dtype).reshape(grad.shape[1:])
        return carry

    lax.fori_loop(0, 4, turn, 0)


def fill_down(left, right, grad, room):
    def step(j, carry):
        lanes = pl.ds(pl.multiple_of(j * BLOCK_ROWS, BLOCK_ROWS), BLOCK_ROWS)
        room[:, lanes] = left_contract(left[...], right[:, lanes])
        return carry

    lax.fori_loop(0, 4, step, 0)

    def place(a, carry):
        for q in range(REP):
            rows = pl.ds(pl.multiple_of(a * 88 + min(24 * q, 64), 8), 24)
            grad[lax.div(a, 2), 2 * lax.rem(a, 2) + q // 2, q % 2] = room[rows, :].astype(grad.dtype)
        return carry

    lax.fori_loop(0, 8, place, 0)


def reduce_kernel(*refs):
    n = len(REDUCE_BLOCKS)
    own = MICRO * ROWS
    layer_part, hidden, self_acc, cross_acc, feed_acc, curve_grad, buckets, *refs = refs
    given = [i for i in range(n) if REDUCE_BLOCKS[i][4]]
    mids, refs = refs[: len(given)], refs[len(given) :]
    alls, refs = refs[: len(COLUMN_BLOCKS)], refs[len(COLUMN_BLOCKS) :]
    gathered, refs = refs[: len(PIECE_BLOCKS)], refs[len(PIECE_BLOCKS) :]
    small_out, layer_out, *refs = refs
    small_blocks, *refs = refs
    grads = {SMALL_BLOCK: small_blocks}
    scratch = []
    for i in range(n):
        extra = 0 if REDUCE_BLOCKS[i][4] else 3
        scratch.append(([None, None, mids[given.index(i)]] if extra == 0 else refs[:3]) + refs[extra : extra + 5])
        refs = refs[extra + 5 :]
    (small_far, small_near, core_recv, far_send, far_recv, near_sum) = refs[:6]
    ring_send, ring_recv, pair_send, pair_recv, rep_send, rep_recv, piece_send, piece_recv, more_send, more_recv = (
        refs[6:]
    )
    place = Place()
    at, rep, x, y, z, theirs = place.at, place.rep, place.x, place.y, place.z, place.theirs
    barrier = pltpu.get_barrier_semaphore()
    devices = [place.pair, place.far, place.near] + place.neighbours()
    for device in devices:
        pl.semaphore_signal(barrier, inc=1, device_id=device, device_id_type=MESH)
    owner = 8 * rep + lax.div(at, 4)
    slot = lax.rem(at, 4)
    stays = owner == at

    def from_self(q):
        return (x == rep) & (4 * lax.rem(at, 8) + q == at)

    for q in range(REP):
        giver = {"rep": x, "shard": 4 * lax.rem(at, 8) + q}

        @pl.when(jnp.logical_not(from_self(q)))
        def _(giver=giver):
            pl.semaphore_signal(barrier, inc=1, device_id=giver, device_id_type=MESH)

    fill_small(rep, (self_acc, cross_acc, feed_acc), curve_grad, bucket_hot(buckets[...]), small_blocks)
    pl.semaphore_wait(barrier, len(devices) + REP - stays.astype(jnp.int32))

    large, small = [], []
    for i, (_, _, on_y, _, done) in enumerate(REDUCE_BLOCKS):
        first, second, mid, first_small, second_small = scratch[i][:5]

        def half_small(j, h, mid=mid):
            return mid[j, h]

        def whole_half_small(j, h, mid=mid):
            return mid.at[j, h]

        if not done:
            large.append((i, large_ring(place, grads[i], on_y, first, second, (ring_send.at[i, 0], ring_recv.at[i, 0]))))
        narrow = (x, place.on_x) if on_y else (y, place.on_y)
        small.append(
            ReduceRing(
                half_small, whole_half_small, *narrow, first_small, second_small, ring_send.at[i, 1], ring_recv.at[i, 1]
            )
        )
    for i, ring in enumerate(small):
        if REDUCE_BLOCKS[i][4]:
            ring.start()
    for _, ring in large:
        ring.start()

    to_core = [
        remote(
            layer_part.at[there * 2 + 1 - place.core], core_recv.at[i], more_send.at[i], more_recv.at[i], place.near
        )
        for i, there in enumerate((1 - place.chip, place.chip))
    ]
    for copy in to_core:
        copy.start()
    to_core[0].wait_recv()
    far_send[...] = (layer_part[theirs].astype(f32) + core_recv[0].astype(f32)).astype(bf16)
    to_far = remote(far_send, far_recv, more_send.at[2], more_recv.at[2], place.far)
    to_far.start()
    to_core[1].wait_recv()
    near_sum[...] = hidden[...] + layer_part[rep].astype(f32) + core_recv[1].astype(f32)

    for i, ring in enumerate(small):
        if REDUCE_BLOCKS[i][4]:
            ring.middle(just_once)
    for _, ring in large:
        ring.middle(each_of_four)
    for i, ring in large:
        ring.finish(each_of_four, large_store(scratch[i][2]))
        small[i].start()
    to_far.wait_recv()
    layer_out[...] = (near_sum[...] + far_recv[...].astype(f32)).astype(bf16)
    for i, ring in enumerate(small):
        if not REDUCE_BLOCKS[i][4]:
            ring.middle(just_once)
    pairs = []
    for i, ring in enumerate(small):
        low = scratch[i][5]

        def store(h, total, low=low):
            low[h] = total.astype(low.dtype)

        ring.finish(just_once, store)
        pairs.append(remote(low.at[1 - z], scratch[i][6], pair_send.at[i], pair_recv.at[i], place.pair))
        pairs[i].start()
    spread, onward, handed = [], [], []
    for i in range(n):
        low, arrived, result = scratch[i][5:8]
        pairs[i].wait_recv()
        total = (low[z].astype(f32) + arrived[...].astype(f32)).astype(low.dtype)
        if i in COLUMN_BLOCKS:
            j = COLUMN_BLOCKS.index(i)
            alls[j][rep] = total
            mine, other = alls[j].at[rep], alls[j].at[theirs]
            spread.append(
                [
                    remote(mine, mine, rep_send.at[j, 0], rep_recv.at[j, 0], place.far),
                    remote(mine, mine, rep_send.at[j, 1], rep_recv.at[j, 1], place.near),
                ]
            )
            onward.append(remote(other, other, rep_send.at[j, 2], rep_recv.at[j, 2], place.near))
            for copy in spread[j]:
                copy.start()
        elif i in PIECE_BLOCKS:
            j = PIECE_BLOCKS.index(i)
            result[...] = total
            for k in range(REP):
                copy = remote(
                    result,
                    gathered[j].at[slot],
                    piece_send.at[j, k],
                    piece_recv.at[j, slot],
                    {"rep": jnp.int32(k), "shard": owner},
                )
                own_piece = stays & (rep == k)
                handed.append((own_piece, copy))
                pl.when(jnp.logical_not(own_piece))(copy.start)

            @pl.when(stays)
            def _(j=j, total=total):
                gathered[j][slot] = total
        else:
            result[...] = total
    result = scratch[SMALL_BLOCK][7]
    small_first = remote(result, small_far, more_send.at[9], more_recv.at[9], place.far)
    small_first.start()
    for j in range(len(onward)):
        spread[j][0].wait_recv()
        onward[j].start()
    small_first.wait()
    result[...] = result[...] + small_far[...]
    small_second = remote(result, small_near, more_send.at[10], more_recv.at[10], place.near)
    small_second.start()
    small_second.wait()
    small_out[...] = result[...] + small_near[...]
    for j in range(len(onward)):
        spread[j][1].wait_recv()
        onward[j].wait_recv()
    for j in range(len(PIECE_BLOCKS)):
        for q in range(REP):
            landed = gathered[j].at[q]
            arrival = remote(
                landed, landed, piece_send.at[j, q], piece_recv.at[j, q], {"rep": x, "shard": 4 * lax.rem(at, 8) + q}
            )
            pl.when(jnp.logical_not(from_self(q)))(arrival.wait_recv)
    for _, ring in large:
        ring.drain()
    for ring in small:
        ring.drain()
    for own_piece, copy in handed:
        pl.when(jnp.logical_not(own_piece))(copy.wait_send)
    for copy in to_core + [to_far] + pairs + onward + [one for two in spread for one in two]:
        copy.wait_send()


def reduce_grads(layer_part, hidden, accs, curve_grad, buckets, mids):
    n = len(REDUCE_BLOCKS)
    own = MICRO * ROWS
    shapes = [jax.ShapeDtypeStruct((REP,) + REDUCE_BLOCKS[i][:2], bf16) for i in COLUMN_BLOCKS + PIECE_BLOCKS]
    shapes += [jax.ShapeDtypeStruct((8, 128), f32), jax.ShapeDtypeStruct((own, D), bf16)]
    here = pl.BlockSpec(memory_space=pltpu.VMEM)
    dma = pltpu.SemaphoreType.DMA
    scratch = [pltpu.VMEM((4, 4, 2) + REDUCE_BLOCKS[SMALL_BLOCK][:2], f32)]
    for rows, width, _, dtype, done in REDUCE_BLOCKS:
        if not done:
            scratch += large_scratch(rows, width, dtype) + [pltpu.VMEM((4, 2, rows, width), dtype)]
        for lead in ((2,), (2, 2), (2,), (), ()):
            scratch.append(pltpu.VMEM(lead + (rows, width), dtype))
    scratch += [
        pltpu.VMEM((8, 128), f32),
        pltpu.VMEM((8, 128), f32),
        pltpu.VMEM((2, own, D), bf16),
        pltpu.VMEM((own, D), bf16),
        pltpu.VMEM((own, D), bf16),
        pltpu.VMEM((own, D), f32),
    ]
    scratch += [dma((n, 2, 6)), dma((n, 2, 6)), dma((n,)), dma((n,)), dma((5, 3)), dma((5, 3))]
    scratch += [dma((3, REP)), dma((3, REP)), dma((11,)), dma((11,))]
    return pl.pallas_call(
        reduce_kernel,
        name="reduce_grads",
        in_specs=[here] * (7 + len(mids)),
        out_specs=[here] * len(shapes),
        out_shape=shapes,
        scratch_shapes=scratch,
        compiler_params=pltpu.CompilerParams(
            collective_id=6, has_side_effects=True, vmem_limit_bytes=20 * mebibyte
        ),
        cost_estimate=estimate(0, 128 << 20, 0),
    )(layer_part, hidden, *accs, curve_grad, buckets, *mids)


def norm_parts(values):
    return lax.rsqrt(jnp.mean(values * values, axis=-1, keepdims=True) + epsilon)


class ReduceRider:
    def __init__(self, jobs):
        self.jobs = [(i, fill) for i, fill, _, _ in jobs]
        self.operands, self.uses = [], []
        for _, _, left, right in jobs:
            use = []
            for value in (left, right):
                found = [k for k, other in enumerate(self.operands) if other is value]
                if not found:
                    self.operands.append(value)
                use.append(found[0] if found else len(self.operands) - 1)
            self.uses.append(use)
        n = len(jobs)
        dma = pltpu.SemaphoreType.DMA
        self.shapes, self.scratch = [], [dma((n, 6)), dma((n, 6))]
        for i, fill in self.jobs:
            rows, width, _, dtype, _ = REDUCE_BLOCKS[i]
            self.shapes.append(jax.ShapeDtypeStruct((4, 2, rows, width), dtype))
            self.scratch += [pltpu.VMEM((4, 4, 2, rows, width), dtype)] + large_scratch(rows, width, dtype)
        here, there = pl.BlockSpec(memory_space=pltpu.VMEM), pl.BlockSpec(memory_space=pltpu.HBM)
        self.in_specs = [here] * len(self.operands)
        for (_, fill), use in zip(self.jobs, self.uses):
            if fill is fill_down:
                self.scratch.append(pltpu.VMEM((OWN_FF, D), f32))
            if fill is fill_stream:
                self.in_specs[use[0]] = there
                left, right = (self.operands[u] for u in use)
                self.scratch += [pltpu.VMEM((2,) + left.shape[1:], bf16), pltpu.VMEM((right.shape[2], D), f32), dma((REP,))]
        self.out_specs = [pl.BlockSpec(memory_space=pltpu.VMEM)] * n

    def steps(self, place, operands, mids, scratch):
        send, recv, *rooms = scratch
        rings, fills = [], []
        for k, (i, fill) in enumerate(self.jobs):
            grad, first, second = rooms[3 * k : 3 * k + 3]
            rings.append(large_ring(place, grad, REDUCE_BLOCKS[i][2], first, second, (send.at[k], recv.at[k])))
            extra = rooms[3 * len(self.jobs) :]
            more = extra if fill in (fill_down, fill_stream) else []
            left, right = (operands[u] for u in self.uses[k])
            fills.append(lambda fill=fill, left=left, right=right, grad=grad, more=more: fill(left, right, grad, *more))

        def begin():
            fills[0]()
            rings[0].start()

        def rest():
            for fill, ring in zip(fills[1:], rings[1:]):
                fill()
                ring.start()

        def nothing():
            pass

        def middle():
            for ring in rings:
                ring.middle(each_of_four)

        def end():
            for ring, mid in zip(rings, mids):
                ring.finish(each_of_four, large_store(mid))
            for ring in rings:
                ring.drain()

        return [begin, rest, nothing, middle, end]


def boundary_kernel(n_pairs, turned, forward, gathers, rider, which, *refs):
    pairs = [(refs[2 * i], refs[2 * i + 1]) for i in range(n_pairs)]
    rest = refs[2 * n_pairs :]
    if forward:
        hidden_ref, gain_ref, *rest = rest
    else:
        values_ref, hidden_ref, gain_ref, *rest = rest
    n_ride = len(rider.operands) if rider else 0
    riding, rest = rest[:n_ride], rest[n_ride:]
    out_ref, *rest = rest
    if not forward:
        acc_ref, *rest = rest
    if gathers:
        all_ref, *rest = rest
    n_ridden = len(rider.shapes) if rider else 0
    ridden, rest = rest[:n_ridden], rest[n_ridden:]
    core_send, core_recv, far_send, far_recv, near_sum, send_sems, recv_sems, *rest = rest
    place = Place()
    rep, chip, core, theirs, far, near = place.rep, place.chip, place.core, place.theirs, place.far, place.near
    barrier = pltpu.get_barrier_semaphore()
    devices = [far, near]
    steps = []
    if rider:
        devices += [place.pair] + place.neighbours()
        steps = rider.steps(place, riding, ridden, rest)

    def ride():
        if steps:
            steps.pop(0)()

    for device in devices:
        pl.semaphore_signal(barrier, inc=1, device_id=device, device_id_type=MESH)

    def partial(r):
        product = right_contract if turned else matmul
        total = product(pairs[0][0][r], pairs[0][1][...])
        for left, right in pairs[1:]:
            total = total + product(left[r], right[...])
        return total

    def copy(source, target, i, device):
        return remote(source, target, send_sems.at[i], recv_sems.at[i], device)

    half = ROWS
    chunks = [pl.ds(c * half, half) for c in range(MICRO)]
    to_core = []
    for i, there in enumerate((1 - chip, chip)):
        core_send[i] = partial(there * 2 + 1 - core).astype(bf16)
        to_core.append(copy(core_send.at[i], core_recv.at[i], i, near))
        if i == 0:
            pl.semaphore_wait(barrier, len(devices))
        to_core[i].start()
    far_own = partial(theirs)
    to_core[0].wait_recv()
    far_send[...] = (far_own + core_recv[0].astype(f32)).astype(bf16)
    to_far = [copy(far_send.at[rows], far_recv.at[rows], 2 + c, far) for c, rows in enumerate(chunks)]
    for sent in to_far:
        sent.start()
    near_own = partial(rep)
    to_core[1].wait_recv()
    near_sum[...] = near_own + core_recv[1].astype(f32)
    ride()
    spread, onward = [], []
    acc = None
    for c, rows in enumerate(chunks):
        to_far[c].wait_recv()
        total = near_sum[rows, :] + far_recv[rows, :].astype(f32)
        gain = gain_ref[which : which + 1, :]
        if forward:
            fresh = hidden_ref[rows, :].astype(f32) + total
            sent = (fresh * norm_parts(fresh) * gain).astype(bf16)
        else:
            values = values_ref[rows, :].astype(f32)
            rho = norm_parts(values)
            scaled = gain * total
            inner = jnp.mean(values * scaled, axis=-1, keepdims=True)
            fresh = hidden_ref[rows, :].astype(f32) + rho * scaled - values * (rho * rho * rho * inner)
            part = jnp.sum(values * rho * total, axis=0, keepdims=True)
            acc = part if acc is None else acc + part
            sent = fresh.astype(bf16)
        out_ref[rows, :] = fresh
        if gathers:
            all_ref[rep, rows, :] = sent
            mine = all_ref.at[rep, rows]
            other = all_ref.at[theirs, rows]
            spread.append((copy(mine, mine, 4 + c, far), copy(mine, mine, 6 + c, near)))
            onward.append(copy(other, other, 8 + c, near))
            for one in spread[c]:
                one.start()
        ride()
    if not forward:
        acc_ref[...] = acc
    for c in range(len(onward)):
        spread[c][0].wait_recv()
        onward[c].start()
    ride()
    for c in range(len(onward)):
        spread[c][1].wait_recv()
        onward[c].wait_recv()
    ride()
    for sent in to_core + to_far + [one for two in spread for one in two] + onward:
        sent.wait_send()


def boundary(name, identity, pairs, turned, hidden, gains, which, values=None, gathers=True, rider=None):
    own = MICRO * ROWS
    forward = values is None
    operands = [a.reshape(REP, own, -1) if i == 0 else a for pair in pairs for i, a in enumerate(pair)]
    operands += ([] if forward else [values]) + [hidden, gains]
    in_specs = [pl.BlockSpec(memory_space=pltpu.VMEM)] * len(operands)
    shapes = [jax.ShapeDtypeStruct((own, D), f32)]
    if not forward:
        shapes.append(jax.ShapeDtypeStruct((1, D), f32))
    if gathers:
        shapes.append(jax.ShapeDtypeStruct((REP, own, D), bf16))
    here = pl.BlockSpec(memory_space=pltpu.VMEM)
    out_specs = [here] * len(shapes)
    if rider:
        operands += rider.operands
        in_specs += rider.in_specs
        shapes += rider.shapes
        out_specs += rider.out_specs
    dma = pltpu.SemaphoreType.DMA
    return pl.pallas_call(
        lambda *refs: boundary_kernel(len(pairs), turned, forward, gathers, rider, which, *refs),
        name=name,
        in_specs=in_specs,
        out_specs=out_specs,
        out_shape=shapes,
        scratch_shapes=[
            pltpu.VMEM((2, own, D), bf16),
            pltpu.VMEM((2, own, D), bf16),
            pltpu.VMEM((own, D), bf16),
            pltpu.VMEM((own, D), bf16),
            pltpu.VMEM((own, D), f32),
            dma((10,)),
            dma((10,)),
        ]
        + (rider.scratch if rider else []),
        compiler_params=pltpu.CompilerParams(
            collective_id=identity, has_side_effects=True, vmem_limit_bytes=(36 if identity == 5 else 24 if rider else 14) * mebibyte
        ),
        cost_estimate=estimate(1 << 30, 32 << 20, 0),
    )(*operands)


FINAL_COLUMNS = (
    (0, 0, QW),
    (0, QW, KW),
    (0, QW + KW, KW),
    (1, 0, KW),
    (1, KW, KW),
    (2, 0, QW),
    (3, 0, OWN_FF),
    (4, 0, OWN_FF),
)


def finish_kernel(*refs):
    n = len(COLUMN_BLOCKS) + len(PIECE_BLOCKS)
    columns, pieces = refs[: len(COLUMN_BLOCKS)], refs[len(COLUMN_BLOCKS) : n]
    kv_refs, w_ref = refs[n : n + REP], refs[n + REP]
    finals, enc_ref = refs[n + REP + 1 : -1], refs[-1]
    rep = lax.axis_index("rep")
    chip, core = lax.div(rep, 2), lax.rem(rep, 2)
    total = None
    for i, kv_ref in enumerate(kv_refs):
        there, which = (1 - chip if i // 2 else chip), (1 - core if i % 2 else core)
        lanes = pl.ds(pl.multiple_of(there * 2 * KW, 2 * KW), 2 * KW)
        part = right_contract(kv_ref[...], w_ref[which, :, lanes])
        total = part if total is None else total + part
    enc_ref[...] = total

    @pl.when(pl.program_id(0) == 0)
    def _():
        for final, (source, first, width) in zip(finals, FINAL_COLUMNS):
            parts = [columns[source][r, :, first : first + width].astype(f32) for r in range(REP)]
            final[...] = jnp.concatenate(parts, axis=1)
        for final, piece in zip(finals[len(FINAL_COLUMNS) :], pieces):
            rows = piece.shape[1]
            for q in range(REP):
                skip = REP * rows - final.shape[0] if q == REP - 1 else 0
                final[q * rows : (q + 1) * rows - skip, :] = piece[q, skip:, :].astype(f32)


def finish(columns, pieces, kv_parts, w_ckv):
    shapes = [jax.ShapeDtypeStruct((columns[i].shape[1], REP * width), f32) for i, _, width in FINAL_COLUMNS]
    shapes += [jax.ShapeDtypeStruct((tall, D), f32) for tall in (FF // SHARDS, 32, 32)]
    shapes.append(jax.ShapeDtypeStruct((kv_parts[0].shape[0], D), f32))
    tall = kv_parts[0].shape[0] // 4
    some = pl.BlockSpec((tall, D), lambda i: (i, 0))
    return pl.pallas_call(
        finish_kernel,
        name="finish",
        grid=(4,),
        in_specs=[fixed_block(value.shape) for value in columns + pieces]
        + [pl.BlockSpec((tall, 2 * KW), lambda i: (i, 0))] * REP
        + [fixed_block(w_ckv.shape)],
        out_specs=[fixed_block(shape.shape) for shape in shapes[:-1]] + [some],
        out_shape=shapes,
        compiler_params=pltpu.CompilerParams(vmem_limit_bytes=24 * mebibyte),
        cost_estimate=estimate(2 << 30, 12 << 20, 0),
    )(*columns, *pieces, *kv_parts, w_ckv)


def local(
    tokens,
    out_cotangent,
    encoded,
    segment_ids,
    doc_block,
    bucket_table,
    self_gain,
    query_weight,
    key_weight,
    value_weight,
    out_weight,
    bias_table,
    cross_gain,
    cross_query,
    cross_key,
    cross_value,
    cross_out,
    feed_gain,
    gate_weight,
    up_weight,
    down_weight,
):
    rep = lax.axis_index("rep")
    own = MICRO * ROWS
    enc_rows = MICRO * DOCS * ENC // REP

    def columns(weight, width):
        return lax.dynamic_slice_in_dim(weight, rep * width, width, 1)

    segments = segment_ids[:, 0]
    seg_row = segments[:, None, :]
    buckets = bucket_table.reshape(1, SEQ)
    doc_ids = jnp.arange(DOCS, dtype=jnp.int32)
    ends = jnp.sum((segments[:, None, :] <= doc_ids[None, :, None]).astype(jnp.int32), axis=2)
    begins = jnp.pad(ends[:, :-1], ((0, 0), (1, 0)))
    sizes = ends - begins
    wides = sum((sizes > window - 16).astype(jnp.int32) for window in WINDOWS[:-1])
    last = jnp.where(wides == 0, SEQ - WINDOWS[0], jnp.where(wides == 1, SEQ - WINDOWS[1], SEQ - WINDOWS[2]))
    starts = jnp.minimum(begins // 16 * 16, last)
    spans = [value.reshape(-1) for value in (doc_block[:, 0], starts, wides, begins, ends)]

    small = sum(
        jnp.pad(value.reshape(1, -1), ((0, 7), (32 * i, 128 - 32 * i - value.size)))
        for i, value in enumerate((self_gain, cross_gain, feed_gain, bias_table))
    )
    own_tokens = tokens.reshape(own, D)
    own_cotangent = out_cotangent.reshape(own, D)
    wholes, (all_tokens, all_enc, all_grad), ready = gather_weights(
        [
            query_weight,
            key_weight,
            value_weight,
            cross_key,
            cross_value,
            cross_query,
            small,
            columns(gate_weight, OWN_FF),
            columns(up_weight, OWN_FF),
            down_weight,
            out_weight,
            cross_out,
        ],
        [seg_row, buckets],
        [own_tokens, encoded.reshape(enc_rows, D), own_cotangent],
    )
    w_qkv, w_ckv, w_cq, small, w_gate, w_up, w_down, w_out, w_cout = wholes
    w_gate = w_gate.reshape(D, OWN_FF)
    w_up = w_up.reshape(D, OWN_FF)
    gains, curve, normed, qkv, context, kv = ready
    w_qkv = w_qkv.reshape(D, QW + 2 * KW)
    w_out = w_out.reshape(QW, D)
    w_ckv = w_ckv.reshape(2, D, REP * KW)
    w_cq = w_cq.reshape(D, QW)
    w_cout = w_cout.reshape(QW, D)
    w_down = w_down.reshape(SHARDS, 24, D)
    all_grad = all_grad.reshape(REP * own, D)

    all_enc = all_enc.reshape(REP * enc_rows, D)

    qkv = qkv.reshape(REP, MICRO, ROWS, QW + 2 * KW)
    normed = normed.reshape(REP * own, D)
    context = context.reshape(REP * own, QW)
    hidden, cross_normed = boundary("after_self", 1, [(context, w_out)], False, own_tokens, gains, 1)
    kv = kv.reshape(REP, MICRO, DOCS, ENC // REP, 2 * KW)
    cross_normed = cross_normed.reshape(REP * own, D)
    cross_queries = matmul(cross_normed, w_cq).astype(bf16).reshape(REP, MICRO, ROWS, QW)
    cross_context = cross_forward(spans, cross_queries, kv).reshape(REP * own, QW)
    hidden_two, feed_normed = boundary("after_cross", 2, [(cross_context, w_cout)], False, hidden, gains, 2)
    feed_normed = feed_normed.reshape(REP * own, D)
    inner, gate_low, up_low, layer_part = feed(feed_normed.reshape(REP, own, D), all_grad.reshape(REP, own, D), w_gate, w_up, w_down)
    inner = inner.reshape(REP * own, OWN_FF)
    gate_low = gate_low.reshape(REP * own, OWN_FF)
    up_low = up_low.reshape(REP * own, OWN_FF)

    hidden_grad, feed_acc, branch, gate_mid, up_mid = boundary(
        "before_feed",
        3,
        [(gate_low, w_gate), (up_low, w_up)],
        True,
        own_cotangent,
        gains,
        2,
        hidden_two,
        rider=ReduceRider([(3, fill_columns, feed_normed, gate_low), (4, fill_columns, feed_normed, up_low)]),
    )
    branch = branch.reshape(REP * own, D)
    context_grad = right_contract(branch, w_cout).astype(bf16).reshape(REP, MICRO, ROWS, QW)
    cq_grad, kv_grad = cross_backward(spans, cross_queries, kv, context_grad)
    cq_grad = cq_grad.reshape(REP * own, QW)
    kv_grad = kv_grad.reshape(REP, enc_rows, 2 * KW)
    hidden_grad, cross_acc, first_branch, down_mid, cq_mid, cout_mid = boundary(
        "before_cross",
        4,
        [(cq_grad, w_cq)],
        True,
        hidden_grad,
        gains,
        1,
        hidden,
        rider=ReduceRider(
            [
                (5, fill_down, inner, all_grad),
                (2, fill_columns, cross_normed, cq_grad),
                (7, fill_rows, cross_context, branch),
            ]
        ),
    )
    first_branch = first_branch.reshape(REP * own, D)
    sent, first_branch = lax.optimization_barrier((kv_grad, first_branch))
    kv_parts = [
        kv_grad[0],
        lax.ppermute(sent[1], "rep", swap_core),
        lax.ppermute(sent[2], "rep", swap_chip),
        lax.ppermute(sent[3], "rep", swap_both),
    ]

    context_grad = right_contract(first_branch, w_out).astype(bf16).reshape(REP, MICRO, ROWS, QW)
    qkv_grad, curve_grad = self_backward(qkv, context_grad, seg_row, curve)
    qkv_grad = qkv_grad.reshape(REP * own, QW + 2 * KW)
    tokens_grad, self_acc, qkv_mid, out_mid, ckv_mid = boundary(
        "before_self",
        5,
        [(qkv_grad, w_qkv)],
        True,
        hidden_grad,
        gains,
        0,
        own_tokens,
        False,
        ReduceRider(
            [
                (0, fill_columns, normed, qkv_grad),
                (6, fill_rows, context, first_branch),
                (1, fill_stream, all_enc.reshape(REP, enc_rows, D), kv_grad),
            ]
        ),
    )

    mids = [qkv_mid, ckv_mid, cq_mid, gate_mid, up_mid, down_mid, out_mid, cout_mid]
    *whole, small_sum, layer_out = reduce_grads(
        layer_part,
        hidden_two,
        [self_acc, cross_acc, feed_acc],
        curve_grad,
        buckets,
        mids,
    )
    *finals, encoder_grad = finish(whole[: len(COLUMN_BLOCKS)], whole[len(COLUMN_BLOCKS) :], kv_parts, w_ckv)
    query_grad, key_grad, value_grad, ck_grad, cv_grad, cq_grad, gate_grad, up_grad, down_grad, out_grad, cout_grad = finals
    small_sum = small_sum[0]
    return (
        layer_out.reshape(tokens.shape),
        tokens_grad.reshape(tokens.shape),
        encoder_grad.reshape(encoded.shape),
        small_sum[0:32],
        query_grad,
        key_grad,
        value_grad,
        out_grad,
        small_sum[96:112].reshape(1, HEADS),
        small_sum[32:64],
        cq_grad,
        ck_grad,
        cv_grad,
        cout_grad,
        small_sum[64:96],
        gate_grad,
        up_grad,
        down_grad,
    )


def solution(mesh):
    rows = P("shard", None)
    gain = P("shard")
    acts = P(None, "shard", "rep", None)
    encs = P(None, "shard", None, "rep", None)
    ids = P(None, "shard", None)
    weights = (gain, rows, rows, rows, rows, rows, gain, rows, rows, rows, rows, gain, rows, rows, rows)
    return jax.shard_map(
        local,
        mesh=mesh,
        in_specs=(acts, acts, encs, ids, ids, P()) + weights,
        out_specs=(acts, acts, encs) + weights,
        check_vma=False,
    )
```
